32 devices in a mesh: grp: 2 (over y), ctx: 4 (over z), kvh: 2 (over x), sub: 2 (over core).
Axes of the slice: x: 2, y: 2, z: 4, core: 2. Of those that a mesh axis runs over, the one named last changes fastest.
Arguments:
- queries: bfloat16 [1024, 8, 8, 128], P(('grp', 'ctx'), 'kvh', 'sub'), parts along dimension 0
- new_keys: bfloat16 [1024, 8, 128], P(('grp', 'ctx'), 'kvh'), parts along dimension 0
- new_values: bfloat16 [1024, 8, 128], P(('grp', 'ctx'), 'kvh'), parts along dimension 0, may hold values from -6 to 6
- cache_keys: bfloat16 [16384, 8, 128], P(('grp', 'ctx'), 'kvh'), parts along dimension 0, may hold values from -16 to 16
- cache_values: bfloat16 [16384, 8, 128], P(('grp', 'ctx'), 'kvh'), parts along dimension 0, may hold values from -6 to 6
- vertical_pool: int32 [16], P(('grp', 'ctx')), parts along dimension 0, may hold values from 0 to 15, as said below
- vertical_lists: int32 [8, 6], P(('grp', 'ctx')), parts along dimension 0, may hold values from 0 to 7, as said below
- slash_lists: int32 [8, 2], P(('grp', 'ctx')), parts along dimension 0, may hold values from 0 to 1, as said below
- list_counts: int32 [8, 2], P(('grp', 'ctx')), parts along dimension 0, may hold values from 1 to 6, as said below
Outputs:
- attention: bfloat16 [1024, 8, 8, 128], P(('grp', 'ctx'), 'kvh', 'sub'), parts along dimension 0
The draws below stay inside these ranges and needn't reach their ends.
There are 2 independent parts, one for each index of `grp`. The reference program is written for one: setup_inputs(seed, part) draws one part's arguments, and reference() takes and returns one part's arrays. A program takes and returns all parts, laid end to end along the dimension named above; each array names one. Nothing has to cross between parts.
Inputs may be any that keep to these rules, and one draw needn't show every extreme that they name: `vertical_pool`: the 2 entries of one index of ctx are distinct. `vertical_lists`: in row b the first list_counts[b, 0] entries are distinct; later entries are never read. `slash_lists`: row b begins with 0; its first list_counts[b, 1] entries are distinct and none exceeds b or 1 plus b modulo 1; later entries are never read. `list_counts`: column 0 lies between 1 and 6, column 1 between 1 and 2, each reached in every draw.
All inputs are finite; a program needn't handle non-finite values.
Results may differ from the reference program's by a relative error of at most 0.014.
Values may be sent and summed in bfloat16 or wider, within the bound.
A program may use at most 64 MiB of HBM per device.

```python
import jax
import jax.numpy as jnp
from jax import lax

KVH = 8
HD = 128
GROUPS = 8
BLK = 128
P_DEV = 2048
VD = 2
QB_DEV = 1
NQB = 4
QTOT = 512
PREFIX = 8192
POOL = 8
VMAX = 6
SMAX = 2


def draw_queries(key, part):
    drawn = jnp.clip(jax.random.normal(key, (QTOT, KVH, GROUPS, HD), jnp.float32), -8.0, 8.0)
    return drawn.astype(jnp.bfloat16)


def draw_new_keys(key, part):
    drawn = jnp.clip(2.5 * jax.random.normal(key, (QTOT, KVH, HD), jnp.float32), -16.0, 16.0)
    return drawn.astype(jnp.bfloat16)


def draw_vertical_pool(key, part):
    blocks_dev = P_DEV // BLK
    owners = POOL // VD
    subkeys = jax.random.split(jax.random.fold_in(key, 11), owners)
    rows = jax.vmap(lambda subkey: jax.random.permutation(subkey, blocks_dev)[:VD])(subkeys).astype(jnp.int32)
    chosen = jax.random.randint(jax.random.fold_in(key, 12), (), 0, owners)
    position = jnp.arange(VD, dtype=jnp.int32)
    ends = jnp.where(position == VD - 1, blocks_dev - 1, position).astype(jnp.int32)
    rows = jnp.where(jnp.arange(owners)[:, None] == chosen, ends[None, :], rows)
    return rows.reshape(POOL).astype(jnp.int32)


def list_tables(key):
    drawn = jax.random.fold_in(key, 21)
    subkeys = jax.random.split(drawn, 4)
    blocks = jnp.arange(NQB, dtype=jnp.int32)
    jitter = jax.random.randint(subkeys[0], (NQB,), 0, VMAX // 8 + 1)
    jitter = jnp.where(blocks == NQB - 1, 0, jitter)
    vertical_count = jnp.maximum(VMAX * (blocks + 1) // NQB - jitter, 1)
    vertical = jax.vmap(lambda subkey: jax.random.permutation(subkey, POOL)[:VMAX])(jax.random.split(subkeys[1], NQB))
    local_index = blocks % QB_DEV
    reach_limit = jnp.minimum(blocks, QB_DEV + local_index)
    slash_count = jax.random.randint(subkeys[2], (NQB,), 1, reach_limit + 2)
    slash_count = jnp.where(blocks == NQB - 1, reach_limit + 1, slash_count)
    candidates = jax.vmap(lambda subkey: jax.random.permutation(subkey, SMAX - 1) + 1)(jax.random.split(subkeys[3], NQB))
    position = jnp.arange(SMAX - 1, dtype=jnp.int32)
    order_key = (candidates > reach_limit[:, None]).astype(jnp.int32) * SMAX + position[None, :]
    ordering = jnp.argsort(order_key, axis=1)
    ordered = jnp.take_along_axis(candidates, ordering, axis=1)
    slash_rows = jnp.concatenate([jnp.zeros((NQB, 1), jnp.int32), ordered.astype(jnp.int32)], axis=1)
    counts = jnp.stack([vertical_count, slash_count], axis=1)
    return (vertical.astype(jnp.int32), slash_rows.astype(jnp.int32), counts.astype(jnp.int32))


def draw_vertical_lists(key, part):
    return list_tables(key)[0]


def draw_slash_lists(key, part):
    return list_tables(key)[1]


def draw_list_counts(key, part):
    return list_tables(key)[2]


def levels(own_key, extent, pieces, least, high):
    factor_of = 1.0
    for axis_at, parts in pieces:
        heights = jax.random.uniform(jax.random.fold_in(jax.random.fold_in(own_key, 6), axis_at), (parts,), jnp.float32, least / len(pieces), high / len(pieces))
        factor_of = factor_of * jnp.repeat(jnp.exp(heights), extent[axis_at] // parts).reshape((-1,) + (1,) * (len(extent) - 1 - axis_at))
    return factor_of


def bell_draw(rng, dims, width, bound, pieces=(), kind=jnp.bfloat16):
    values = jax.random.normal(rng, dims, jnp.float32) * width
    if len(pieces) > 0:
        values = levels(rng, dims, pieces, -0.22, 0.18) * values
    return jnp.clip(values, min=-bound, max=bound).astype(kind)


def setup_inputs(seed: int = 0, part: int = 0) -> dict:
    arg_keys = jax.random.split(jax.random.key(seed), 10)
    own_keys = jax.random.split(jax.random.fold_in(arg_keys[9], part), 10)
    queries = draw_queries(jax.random.fold_in(jax.random.fold_in(arg_keys[9], part), 71), part)
    new_keys = draw_new_keys(jax.random.fold_in(jax.random.fold_in(arg_keys[9], part), 71), part)
    new_values = bell_draw(own_keys[2], (QTOT, KVH, HD), 1.0, 6.0, ((0, 4), (1, 2)))
    cache_keys = bell_draw(own_keys[3], (PREFIX, KVH, HD), 2.5, 16.0, ((0, 4), (1, 2)))
    cache_values = bell_draw(own_keys[4], (PREFIX, KVH, HD), 1.0, 6.0, ((0, 4), (1, 2)))
    vertical_pool = draw_vertical_pool(jax.random.fold_in(jax.random.fold_in(arg_keys[9], part), 71), part)
    vertical_lists = draw_vertical_lists(jax.random.fold_in(jax.random.fold_in(arg_keys[9], part), 71), part)
    slash_lists = draw_slash_lists(jax.random.fold_in(jax.random.fold_in(arg_keys[9], part), 71), part)
    list_counts = draw_list_counts(jax.random.fold_in(jax.random.fold_in(arg_keys[9], part), 71), part)
    return dict(queries=queries, new_keys=new_keys, new_values=new_values, cache_keys=cache_keys, cache_values=cache_values, vertical_pool=vertical_pool, vertical_lists=vertical_lists, slash_lists=slash_lists, list_counts=list_counts)


def block_update(carry_state, query_block, block_keys, block_values, visible):
    row_peak, row_total, numerator = carry_state
    score_scale = query_block.shape[-1] ** -0.5
    scores = jnp.einsum("rkgd,ckd->rkgc", query_block.astype(jnp.float32), block_keys.astype(jnp.float32)) * score_scale
    scores = jnp.where(visible, scores, -jnp.inf)
    new_peak = jnp.maximum(row_peak, jnp.max(scores, axis=3))
    factor = jnp.exp(row_peak - new_peak)
    weights = jnp.exp(scores - new_peak[..., None])
    row_total = row_total * factor + jnp.sum(weights, axis=3)
    rounded = lax.optimization_barrier(weights.astype(jnp.bfloat16)).astype(jnp.float32)
    numerator = numerator * factor[..., None] + jnp.einsum("rkgc,ckd->rkgd", rounded, block_values.astype(jnp.float32))
    return new_peak, row_total, numerator


def reference(queries, new_keys, new_values, cache_keys, cache_values, vertical_pool, vertical_lists, slash_lists, list_counts):
    blocks_dev = P_DEV // BLK
    owners = jnp.arange(POOL, dtype=jnp.int32) // VD
    pool_sources = (owners * blocks_dev + vertical_pool).astype(jnp.int32)
    cached_keys = cache_keys.reshape(PREFIX // BLK, BLK, KVH, HD)
    cached_values = cache_values.reshape(PREFIX // BLK, BLK, KVH, HD)
    fresh_keys = new_keys.reshape(NQB, BLK, KVH, HD)
    fresh_values = new_values.reshape(NQB, BLK, KVH, HD)
    query_grid = queries.reshape(NQB, BLK, KVH, GROUPS, HD)
    row_ids = lax.broadcasted_iota(jnp.int32, (BLK, 1, 1, BLK), 0)
    col_ids = lax.broadcasted_iota(jnp.int32, (BLK, 1, 1, BLK), 3)
    causal = col_ids <= row_ids

    def one_block(block_index):
        query_block = query_grid[block_index]
        blank_state = (jnp.full((BLK, KVH, GROUPS), -jnp.inf, jnp.float32),
                       jnp.zeros((BLK, KVH, GROUPS), jnp.float32),
                       jnp.zeros((BLK, KVH, GROUPS, HD), jnp.float32))

        def vertical_step(step_index, carry_state):
            source = pool_sources[vertical_lists[block_index, step_index]]
            return block_update(carry_state, query_block, cached_keys[source], cached_values[source], True)

        carry_state = lax.fori_loop(0, list_counts[block_index, 0], vertical_step, blank_state)

        def slash_step(step_index, carry_state):
            offset = slash_lists[block_index, step_index]
            target = block_index - offset
            return block_update(carry_state, query_block, fresh_keys[target], fresh_values[target], causal | (offset > 0))

        carry_state = lax.fori_loop(0, list_counts[block_index, 1], slash_step, carry_state)
        return (carry_state[2] / carry_state[1][..., None]).astype(jnp.bfloat16)

    result = lax.map(one_block, jnp.arange(NQB, dtype=jnp.int32))
    return result.reshape(QTOT, KVH, GROUPS, HD)
```

```python
import functools
import math

import jax
import jax.numpy as jnp
from jax import lax
from jax.experimental import pallas as pl
from jax.experimental.pallas import tpu as pltpu
from jax.sharding import PartitionSpec as P

BLK = 128
MESH = pl.DeviceIdType.MESH


def attend(n, q_hbm, nk_hbm, nv_hbm, ck_hbm, cv_hbm, vp_ref, vl_ref, sl_ref, cnt_ref, o_ref,
           q_raw, nk_raw, nv_raw, ck_raw, cv_raw, q_ref, own_ref, new_ref, sort_kv, sort_q,
           pool, slash_raw, slash, acc, peak, total, rounded, fade,
           hop_send, hop_recv, sib_send, sib_recv, sl_sem, in_sem):
    z = lax.axis_index("ctx")
    s = lax.axis_index("sub")
    heads, rows, head_dim = q_ref.shape
    groups = rows // BLK
    wide = heads * BLK
    loads = [pltpu.make_async_copy(src, dst, in_sem.at[i]) for i, (src, dst) in enumerate(
        [(ck_hbm, ck_raw), (cv_hbm, cv_raw), (nk_hbm, nk_raw), (nv_hbm, nv_raw), (q_hbm, q_raw)])]
    loads[0].start()
    c = math.log2(math.e) / math.sqrt(head_dim)
    has_left = z > 0
    has_right = z < n - 1
    sib_id = {"sub": 1 - s}

    barrier = pltpu.get_barrier_semaphore()
    pl.semaphore_signal(barrier, inc=1, device_id=sib_id, device_id_type=MESH)

    @pl.when(has_left)
    def _():
        pl.semaphore_signal(barrier, inc=1, device_id={"ctx": z - 1}, device_id_type=MESH)

    @pl.when(has_right)
    def _():
        pl.semaphore_signal(barrier, inc=1, device_id={"ctx": z + 1}, device_id_type=MESH)

    ids = lax.broadcasted_iota(jnp.int32, (wide, wide), 0)
    at = lax.broadcasted_iota(jnp.int32, (wide, wide), 1)
    sort_kv[...] = jnp.where(at == (ids % BLK) * heads + ids // BLK, 1.0, 0.0).astype(jnp.bfloat16)
    token = (ids % BLK) // groups
    sort_q[...] = jnp.where(at == (token * heads + ids // BLK) * groups + ids % groups,
                            1.0, 0.0).astype(jnp.bfloat16)

    def by_head(raw):
        return jnp.dot(sort_kv[...], raw, preferred_element_type=jnp.float32).astype(jnp.bfloat16)

    def put_keys(dst, raw):
        ordered = by_head(raw)
        for h in range(heads):
            dst[h] = ordered[h * BLK:(h + 1) * BLK]

    def put_values(dst, raw):
        ordered = lax.dot_general(raw, sort_kv[...], (((0,), (1,)), ((), ())),
                                  preferred_element_type=jnp.float32).astype(jnp.bfloat16)
        for h in range(heads):
            dst[h] = ordered[:, h * BLK:(h + 1) * BLK]

    def chosen(cache, b):
        return cache[vp_ref[b]]

    pl.semaphore_wait(barrier, 1 + has_left.astype(jnp.int32) + has_right.astype(jnp.int32))

    def hop(src_ref, src, kv, right):
        return pltpu.make_async_remote_copy(
            src_ref=src_ref, dst_ref=pool.at[src, s, kv],
            send_sem=hop_send.at[src, int(right), kv], recv_sem=hop_recv.at[src, kv],
            device_id={"ctx": z + 1 if right else z - 1}, device_id_type=MESH)

    def sib(src, kv):
        return pltpu.make_async_remote_copy(
            src_ref=pool.at[src, s, kv], dst_ref=pool.at[src, s, kv],
            send_sem=sib_send.at[src, kv], recv_sem=sib_recv.at[src, kv],
            device_id=sib_id, device_id_type=MESH)

    def sib_in(src, kv):
        return pltpu.make_async_remote_copy(
            src_ref=pool.at[src, 1 - s, kv], dst_ref=pool.at[src, 1 - s, kv],
            send_sem=sib_send.at[src, kv], recv_sem=sib_recv.at[src, kv],
            device_id=sib_id, device_id_type=MESH)

    def slash_hop(src_ref=nk_hbm):
        return pltpu.make_async_remote_copy(
            src_ref=src_ref, dst_ref=slash_raw.at[s],
            send_sem=sl_sem.at[0], recv_sem=sl_sem.at[1],
            device_id={"ctx": z + 1}, device_id_type=MESH)

    def slash_sib(part):
        return pltpu.make_async_remote_copy(
            src_ref=slash_raw.at[part], dst_ref=slash_raw.at[part],
            send_sem=sl_sem.at[2], recv_sem=sl_sem.at[3],
            device_id=sib_id, device_id_type=MESH)

    for part, src_ref in enumerate((nk_hbm, nv_hbm)):
        @pl.when(has_right & (s == part))
        def _():
            slash_hop(src_ref).start()

    def send_own(kv):
        @pl.when(has_right)
        def _():
            hop(own_ref.at[s, kv], z, kv, True).start()

        @pl.when(has_left)
        def _():
            hop(own_ref.at[s, kv], z, kv, False).start()

    loads[0].wait()
    loads[1].start()
    put_keys(own_ref.at[s, 0], chosen(ck_raw, s))
    for load in loads[2:]:
        load.start()
    send_own(0)
    loads[1].wait()
    put_values(own_ref.at[s, 1], chosen(cv_raw, s))
    send_own(1)
    loads[2].wait()
    loads[3].wait()
    put_keys(new_ref.at[0], nk_raw[...])
    put_values(new_ref.at[1], nv_raw[...])
    put_keys(own_ref.at[1 - s, 0], chosen(ck_raw, 1 - s))
    put_values(own_ref.at[1 - s, 1], chosen(cv_raw, 1 - s))
    loads[4].wait()
    for part in range(rows // BLK):
        ordered = jnp.dot(sort_q[...], q_raw[part * wide:(part + 1) * wide],
                          preferred_element_type=jnp.float32).astype(jnp.bfloat16)
        for h in range(heads):
            q_ref[h, part * BLK:(part + 1) * BLK] = ordered[h * BLK:(h + 1) * BLK]

    def listed(slot):
        count = cnt_ref[0, 0]
        width = vl_ref.shape[1]
        if width <= 8:
            hit = jnp.int32(0)
            for i in range(width):
                hit = hit | jnp.where((vl_ref[0, i] == slot) & (i < count), 1, 0)
            return hit

        def one(i, hit):
            return hit | jnp.where((vl_ref[0, i] == slot) & (i < count), 1, 0)

        return lax.fori_loop(0, width, one, jnp.int32(0))

    def score(keys, q):
        return lax.dot_general(keys, q, (((1,), (1,)), ((), ())),
                               preferred_element_type=jnp.float32)

    def take_keys(side, blocks, first=False):
        for h in range(heads):
            q = q_ref[h]
            raw = []
            tops = []
            for keys, seen in blocks:
                scores = score(keys[h], q)
                if seen is None:
                    key_id = lax.broadcasted_iota(jnp.int32, scores.shape, 0)
                    row_id = lax.broadcasted_iota(jnp.int32, scores.shape, 1) // groups
                    scores = jnp.where(key_id <= row_id, scores, -jnp.inf)
                top = jnp.max(scores, axis=0, keepdims=True)
                if seen is not None:
                    top = jnp.where(seen > 0, top, -jnp.inf)
                raw.append(scores)
                tops.append(top)
            high = functools.reduce(jnp.maximum, tops)
            if not first:
                old = peak[h]
                high = jnp.maximum(old, high)
                factor = jnp.exp2((old - high) * c)
                fade[side, h] = factor
            peak[h] = high
            sums = []
            for i, ((_, seen), scores) in enumerate(zip(blocks, raw)):
                base = high if seen is None else jnp.where(seen > 0, high, jnp.inf)
                weights = jnp.exp2((scores - base) * c)
                sums.append(jnp.sum(weights, axis=0, keepdims=True))
                rounded[side, h, i * BLK:(i + 1) * BLK] = weights.astype(jnp.bfloat16)
            add = sum(sums[1:], sums[0])
            total[h] = add if first else total[h] * fade[side, h] + add

    def take_values(side, blocks, first=False):
        depth = len(blocks) * BLK
        for h in range(heads):
            values = jnp.concatenate([values[h] for values in blocks], 1)
            add = jnp.dot(values, rounded[side, h, :depth], preferred_element_type=jnp.float32)
            acc[h] = add if first else acc[h] * fade[side, h] + add

    take_keys(0, [(new_ref.at[0], None)]
              + [(own_ref.at[b, 0], listed(2 * z + b)) for b in range(2)], first=True)
    take_values(0, [new_ref.at[1]] + [own_ref.at[b, 1] for b in range(2)], first=True)

    @pl.when(has_left)
    def _():
        slash_hop().wait_recv()
        slash_sib(s).start()

    def arrive(src, kv, right):
        hop(own_ref.at[s, kv], src, kv, right).wait_recv()

        @pl.when(has_right if right else has_left)
        def _():
            hop(pool.at[src, s, kv], src, kv, right).start()

        sib(src, kv).start()

    def step(d, carry):
        sides = ((z + d, z + d < n, False), (z - d, z - d >= 0, True))
        for kv in range(2):
            for src, there, right in sides:
                @pl.when(there)
                def _():
                    arrive(src, kv, right)

            for side, (src, there, right) in enumerate(sides):
                @pl.when(there)
                def _():
                    sib_in(src, kv).wait_recv()
                    if kv == 0:
                        take_keys(side, [(pool.at[src, b, 0], listed(2 * src + b))
                                         for b in range(2)])
                    else:
                        take_values(side, [pool.at[src, b, 1] for b in range(2)])

        @pl.when((d == 1) & has_left)
        def _():
            slash_sib(1 - s).wait_recv()
            put_keys(slash.at[0], slash_raw[0])
            put_values(slash.at[1], slash_raw[1])
            back = jnp.int32(0)
            for i in range(sl_ref.shape[1]):
                back = back | jnp.where((sl_ref[0, i] == 1) & (i < cnt_ref[0, 1]), 1, 0)
            take_keys(0, [(slash.at[0], back)])
            take_values(0, [slash.at[1]])

        return carry

    lax.fori_loop(1, n, step, 0)

    for part in range(rows // BLK):
        lanes = slice(part * BLK, (part + 1) * BLK)
        done = jnp.concatenate(
            [(acc[h, :, lanes] / total[h, :, lanes]).astype(jnp.bfloat16) for h in range(heads)], 1)
        o_ref[part * wide:(part + 1) * wide] = lax.dot_general(
            sort_q[...], done, (((0,), (1,)), ((), ())),
            preferred_element_type=jnp.float32).astype(o_ref.dtype)

    def drain(src, carry):
        for kv in range(2):
            @pl.when(has_right & (src <= z))
            def _():
                hop(own_ref.at[s, kv], src, kv, True).wait_send()

            @pl.when(has_left & (src >= z))
            def _():
                hop(own_ref.at[s, kv], src, kv, False).wait_send()

            @pl.when(src != z)
            def _():
                sib(src, kv).wait_send()
        return carry

    lax.fori_loop(0, n, drain, 0)

    @pl.when(has_right)
    def _():
        slash_hop().wait_send()

    @pl.when(has_left)
    def _():
        slash_sib(s).wait_send()


def plan():
    def kv(src, h):
        return (1, src * 4 + h)

    def step(recv=(0, 0), unit=None, wait=True, half=None, result=0, extra=0):
        code, block = 0, 0
        if unit is not None:
            slot, src, h = unit
            code, block = slot + 1 + (0 if wait else 8), src * 4 + h
        return (recv[0], recv[1], code, block, 0 if half is None else half + 1, result, extra)

    def own(z, count=4):
        return [step(unit=(h, z, h), wait=False) for h in range(count)]

    def lagged(messages, steps):
        late = None
        for recv, extra in messages:
            steps.append(step(recv, None if late is None else (late % 4, late // 4, late % 4), extra=extra))
            late = recv[1] if recv[0] == 1 else None
        if late is not None:
            steps.append(step(unit=(late % 4, late // 4, late % 4)))
        return steps

    slash = (3, 0)
    roles = [lagged([(kv(src, h), 0) for src in (1, 2, 3) for h in range(4)], own(0))]
    one = lagged([(kv(0, 0), 0), (kv(2, 0), 0), (kv(0, 2), 0), (kv(2, 1), 0), (kv(0, 1), 1), (kv(2, 2), 0),
                  (kv(0, 3), 2), (kv(2, 3), 0), (kv(3, 0), 0), (slash, 0), (kv(3, 1), 0), (kv(3, 2), 0),
                  (kv(3, 3), 0)], own(1))
    for h in range(4):
        at = len(one) - 4 + h
        one[at] = one[at][:4] + (h + 1,) + one[at][5:]
    roles.append(one)
    roles.append(own(2, 2) + [
        step(kv(1, 0), (2, 2, 2), wait=False), step(kv(3, 0), (3, 2, 3), wait=False),
        step(kv(1, 2), (0, 1, 0)), step(kv(1, 1), (0, 3, 0)), step((2, 0), (2, 1, 2)),
        step(kv(0, 0), (4, 2, 2), wait=False, half=4), step(kv(3, 1), (1, 1, 1)),
        step(kv(0, 2), (4, 1, 2), wait=False), step(unit=(0, 0, 0)),
        step(unit=(4, 0, 2), result=1), step(kv(0, 1), (1, 3, 1)), step((2, 1), (2, 0, 2), wait=False),
        step(kv(1, 3), (5, 2, 3), wait=False, half=5), step(kv(3, 2), (1, 0, 1)),
        step(kv(0, 3), (5, 1, 3)), step(kv(3, 3), (3, 1, 3), wait=False),
        step(unit=(5, 0, 3), result=2), step(unit=(2, 3, 2)), step(slash, (3, 0, 3), wait=False),
        step(unit=(3, 3, 3), half=0), step(half=1), step(half=2), step(half=3)])
    roles.append(own(3) + [
        step(kv(2, 0)), step(slash, (0, 2, 0)), step(kv(2, 1), half=0), step(unit=(1, 2, 1), half=1),
        step(kv(1, 0)), step(kv(1, 1), (0, 1, 0)), step(kv(0, 0), (1, 1, 1)), step((4, 0), (0, 0, 0)),
        step(kv(0, 1)), step(unit=(1, 0, 1)), step((4, 1))])
    return roles


def chain(n, q_hbm, nk_hbm, nv_hbm, ck_hbm, cv_hbm, vp_ref, vl_ref, sl_ref, cnt_ref, o_ref,
          q_raw, nk_raw, nv_raw, ck_raw, cv_raw, q_ref, slab, sort_kv, sort_q,
          pool, acc, peak, total, mask, part_acc, part_stat,
          hop_send, hop_recv, sib_send, sib_recv, sl_sem, q_sem, part_sem, in_sem):
    z = lax.axis_index("ctx")
    s = lax.axis_index("sub")
    heads = pool.shape[1]
    rows, head_dim = q_ref.shape[1:]
    groups = rows // BLK
    wide = heads * BLK
    last = n - 1
    guests = heads // 2
    loads = [pltpu.make_async_copy(src, dst, in_sem.at[i]) for i, (src, dst) in enumerate(
        [(ck_hbm, ck_raw), (cv_hbm, cv_raw), (nk_hbm, nk_raw), (nv_hbm, nv_raw), (q_hbm, q_raw)])]
    for load in loads:
        load.start()
    c = math.log2(math.e) / math.sqrt(head_dim)
    has_left = z > 0
    has_right = z < last
    sib_id = {"sub": 1 - s}

    barrier = pltpu.get_barrier_semaphore()
    pl.semaphore_signal(barrier, inc=1, device_id=sib_id, device_id_type=MESH)

    @pl.when(has_left)
    def _():
        pl.semaphore_signal(barrier, inc=1, device_id={"ctx": z - 1}, device_id_type=MESH)

    @pl.when(has_right)
    def _():
        pl.semaphore_signal(barrier, inc=1, device_id={"ctx": z + 1}, device_id_type=MESH)

    ids = lax.broadcasted_iota(jnp.int32, (wide, wide), 0)
    at = lax.broadcasted_iota(jnp.int32, (wide, wide), 1)
    sort_kv[...] = jnp.where(at == (ids % BLK) * heads + ids // BLK, 1.0, 0.0).astype(jnp.bfloat16)
    token = (ids % BLK) // groups
    sort_q[...] = jnp.where(at == (token * heads + ids // BLK) * groups + ids % groups,
                            1.0, 0.0).astype(jnp.bfloat16)

    def unseen(hit):
        return jnp.full((1, BLK), jnp.where(hit > 0, 0.0, jnp.inf), jnp.float32)

    for slot in range(2 * n):
        hit = jnp.int32(0)
        for i in range(vl_ref.shape[1]):
            hit = hit | jnp.where((vl_ref[0, i] == slot) & (i < cnt_ref[0, 0]), 1, 0)
        mask[0, slot:slot + 1] = unseen(hit)
    hit = jnp.int32(0)
    for i in range(sl_ref.shape[1]):
        hit = hit | jnp.where((sl_ref[0, i] == 1) & (i < cnt_ref[0, 1]), 1, 0)
    mask[0, 2 * n:2 * n + 1] = unseen(hit)

    def put_keys(raw, put):
        ordered = jnp.dot(sort_kv[...], raw, preferred_element_type=jnp.float32).astype(jnp.bfloat16)
        for h in range(heads):
            put(h, ordered[h * BLK:(h + 1) * BLK])

    def put_values(raw, put):
        ordered = lax.dot_general(raw, sort_kv[...], (((0,), (1,)), ((), ())),
                                  preferred_element_type=jnp.float32).astype(jnp.bfloat16)
        for h in range(heads):
            put(h, ordered[:, h * BLK:(h + 1) * BLK])

    def put_pool(b, kv):
        def put(h, block):
            pool[z, h, b, kv] = block
        return put

    def put_slab(kv):
        def put(h, block):
            slab[0, kv, h] = block
        return put

    def hop(src, h, right):
        return pltpu.make_async_remote_copy(
            src_ref=pool.at[src, h, s], dst_ref=pool.at[src, h, s],
            send_sem=hop_send.at[src, h, int(right)], recv_sem=hop_recv.at[src, h],
            device_id={"ctx": z + 1 if right else z - 1}, device_id_type=MESH)

    def sib(src, h, part=s):
        return pltpu.make_async_remote_copy(
            src_ref=pool.at[src, h, part], dst_ref=pool.at[src, h, part],
            send_sem=sib_send.at[src, h], recv_sem=sib_recv.at[src, h],
            device_id=sib_id, device_id_type=MESH)

    def slash_hop(count):
        return pltpu.make_async_remote_copy(
            src_ref=slab.at[0, s, pl.ds(0, count)], dst_ref=slab.at[1, s, pl.ds(0, count)],
            send_sem=sl_sem.at[0], recv_sem=sl_sem.at[1],
            device_id={"ctx": z + 1}, device_id_type=MESH)

    def slash_sib(count, part):
        return pltpu.make_async_remote_copy(
            src_ref=slab.at[1, part, pl.ds(0, count)], dst_ref=slab.at[1, part, pl.ds(0, count)],
            send_sem=sl_sem.at[2], recv_sem=sl_sem.at[3],
            device_id=sib_id, device_id_type=MESH)

    def guest_q(g):
        return pltpu.make_async_remote_copy(
            src_ref=q_ref.at[heads - guests + g], dst_ref=q_ref.at[heads + g],
            send_sem=q_sem.at[0, g], recv_sem=q_sem.at[1, g],
            device_id={"ctx": z - 1}, device_id_type=MESH)

    def guest_mask():
        return pltpu.make_async_remote_copy(
            src_ref=mask.at[0], dst_ref=mask.at[1],
            send_sem=q_sem.at[0, guests], recv_sem=q_sem.at[1, guests],
            device_id={"ctx": z - 1}, device_id_type=MESH)

    def guest_part(g):
        return [pltpu.make_async_remote_copy(
            src_ref=ref.at[g], dst_ref=ref.at[g],
            send_sem=part_sem.at[0, g, i], recv_sem=part_sem.at[1, g, i],
            device_id={"ctx": z + 1}, device_id_type=MESH)
            for i, ref in enumerate((part_acc, part_stat))]

    loads[0].wait()
    put_keys(ck_raw[vp_ref[s]], put_pool(s, 0))
    loads[1].wait()
    put_values(cv_raw[vp_ref[s]], put_pool(s, 1))
    pl.semaphore_wait(barrier, 1 + has_left.astype(jnp.int32) + has_right.astype(jnp.int32))

    @pl.when(z == 0)
    def _():
        for h in (0, 2, 1, 3):
            hop(z, h, True).start()

    @pl.when(z == 1)
    def _():
        for h in (0, 2, 1):
            hop(z, h, True).start()

    @pl.when(z == 2)
    def _():
        hop(z, 0, True).start()

    @pl.when((z == 1) | (z == 2))
    def _():
        for h in range(heads):
            hop(z, h, False).start()

    @pl.when(z == last)
    def _():
        hop(z, 0, False).start()
        guest_mask().start()

    loads[2].wait()
    loads[3].wait()
    put_keys(nk_raw[...], put_slab(0))
    put_values(nv_raw[...], put_slab(1))

    @pl.when(z == 0)
    def _():
        slash_hop(heads).start()

    @pl.when(z == 2)
    def _():
        slash_hop(heads - guests).start()
        hop(z, 1, True).start()

    loads[4].wait()
    for part in range(rows // BLK):
        ordered = jnp.dot(sort_q[...], q_raw[part * wide:(part + 1) * wide],
                          preferred_element_type=jnp.float32).astype(jnp.bfloat16)
        for h in range(heads):
            q_ref[h, part * BLK:(part + 1) * BLK] = ordered[h * BLK:(h + 1) * BLK]

    @pl.when(z == last)
    def _():
        guest_q(0).start()
        hop(z, 1, False).start()
        guest_q(1).start()
        hop(z, 2, False).start()
        hop(z, 3, False).start()

    put_keys(ck_raw[vp_ref[1 - s]], put_pool(1 - s, 0))
    put_values(cv_raw[vp_ref[1 - s]], put_pool(1 - s, 1))

    @pl.when(z == last - 1)
    def _():
        for g in range(guests):
            acc[heads + g] = jnp.zeros_like(acc[heads + g])
            total[heads + g] = jnp.zeros_like(total[heads + g])
            peak[heads + g] = jnp.full_like(peak[heads + g], -1e30)

    def score(keys, q):
        return lax.dot_general(keys, q, (((1,), (1,)), ((), ())),
                               preferred_element_type=jnp.float32)

    def diagonal(h, carry):
        scores = score(slab[0, 0, h], q_ref[h])
        key_id = lax.broadcasted_iota(jnp.int32, scores.shape, 0)
        row_id = lax.broadcasted_iota(jnp.int32, scores.shape, 1) // groups
        scores = jnp.where(key_id <= row_id, scores, -jnp.inf)
        high = jnp.max(scores, axis=0, keepdims=True)
        weights = jnp.exp2((scores - high) * c)
        peak[h] = high
        total[h] = jnp.sum(weights, axis=0, keepdims=True)
        acc[h] = jnp.dot(slab[0, 1, h], weights.astype(jnp.bfloat16), preferred_element_type=jnp.float32)
        return carry

    lax.fori_loop(0, heads, diagonal, 0)

    def spread(row):
        return jnp.concatenate([row] * groups, 1)

    def update(slot, blocks):
        q = q_ref[slot]
        old = peak[slot]
        raw = [score(keys, q) for keys, _, _ in blocks]
        hide = [spread(row) for _, _, row in blocks]
        high = old
        for scores, row in zip(raw, hide):
            high = jnp.maximum(high, jnp.max(scores, axis=0, keepdims=True) - row)
        factor = jnp.exp2((old - high) * c)
        peak[slot] = high
        weights = [jnp.exp2((scores - (high + row)) * c) for scores, row in zip(raw, hide)]
        add = functools.reduce(jnp.add, [jnp.sum(w, axis=0, keepdims=True) for w in weights])
        total[slot] = total[slot] * factor + add
        rounded = jnp.concatenate([w.astype(jnp.bfloat16) for w in weights], 0)
        values = jnp.concatenate([values for _, values, _ in blocks], 1)
        acc[slot] = acc[slot] * factor + jnp.dot(values, rounded, preferred_element_type=jnp.float32)

    roles = plan()
    steps = max(len(role) for role in roles)

    def by_role(values):
        out = jnp.int32(values[-1])
        for i in reversed(range(len(values) - 1)):
            out = jnp.where(z == i, jnp.int32(values[i]), out)
        return out

    words = []
    for field in range(7):
        chunks = []
        for start in range(0, steps, 7):
            chunks.append(by_role([sum(step[field] << (4 * i) for i, step in enumerate(role[start:start + 7]))
                                   for role in roles]))
        words.append(chunks)

    def step(t, carry):
        group = t // 7
        shift = 4 * (t % 7)

        def look(field):
            word = words[field][-1]
            for i in reversed(range(len(words[field]) - 1)):
                word = jnp.where(group == i, words[field][i], word)
            return lax.shift_right_logical(word, shift) & 15

        kind, message, unit, block, half, result, extra = [look(field) for field in range(7)]
        src, h = message // 4, message % 4

        @pl.when(kind == 1)
        def _():
            hop(src, h, True).wait_recv()

            @pl.when((src < z) & ((z == 1) | ((z == 2) & (h < heads - guests))))
            def _():
                hop(src, h, True).start()

            @pl.when((src > z) & has_left)
            def _():
                hop(src, h, False).start()

            sib(src, h).start()

            @pl.when(extra == 1)
            def _():
                hop(z, 3, True).start()

            @pl.when(extra == 2)
            def _():
                slash_hop(heads).start()

        @pl.when(kind == 2)
        def _():
            @pl.when(h == 0)
            def _():
                guest_mask().wait_recv()

            guest_q(h).wait_recv()

        @pl.when((kind == 3) & has_right)
        def _():
            slash_hop(heads).wait_recv()
            slash_sib(heads, s).start()

        @pl.when((kind == 3) & (z == last))
        def _():
            slash_hop(heads - guests).wait_recv()
            slash_sib(heads - guests, s).start()

        @pl.when(kind == 4)
        def _():
            for copy in guest_part(h):
                copy.wait_recv()
            slot = heads - guests + h
            old, new = peak[slot], part_stat[h, 0:1]
            high = jnp.maximum(old, new)
            mine, theirs = jnp.exp2((old - high) * c), jnp.exp2((new - high) * c)
            acc[slot] = acc[slot] * mine + part_acc[h].astype(jnp.float32) * theirs
            total[slot] = total[slot] * mine + part_stat[h, 1:2] * theirs

        @pl.when(unit > 0)
        def _():
            slot = (unit - 1) % 8
            src, h = block // 4, block % 4

            @pl.when(unit < 8)
            def _():
                sib(src, h, 1 - s).wait_recv()

            guest = slot // heads
            update(slot, [(pool[src, h, b, 0], pool[src, h, b, 1], mask[guest, pl.ds(2 * src + b, 1)])
                          for b in range(2)])

        @pl.when(half > 0)
        def _():
            slot = half - 1
            guest = slot // heads

            @pl.when((slot == 0) & has_right)
            def _():
                slash_sib(heads, 1 - s).wait_recv()

            @pl.when((slot == 0) & (z == last))
            def _():
                slash_sib(heads - guests, 1 - s).wait_recv()

            h = slot - guest * guests
            update(slot, [(slab[1 - guest, 0, h], slab[1 - guest, 1, h], mask[guest, 2 * n:2 * n + 1])])

        @pl.when(result > 0)
        def _():
            g = result - 1
            part_acc[g] = acc[heads + g].astype(jnp.bfloat16)
            part_stat[g, 0:1] = peak[heads + g]
            part_stat[g, 1:2] = total[heads + g]
            for copy in guest_part(g):
                copy.start()

        return carry

    lax.fori_loop(0, by_role([len(role) for role in roles]), step, 0)

    for part in range(rows // BLK):
        lanes = slice(part * BLK, (part + 1) * BLK)
        done = jnp.concatenate(
            [(acc[h, :, lanes] / total[h, :, lanes]).astype(jnp.bfloat16) for h in range(heads)], 1)
        o_ref[part * wide:(part + 1) * wide] = lax.dot_general(
            sort_q[...], done, (((0,), (1,)), ((), ())),
            preferred_element_type=jnp.float32).astype(o_ref.dtype)

    def drain(i, carry):
        src, h = i // heads, i % heads

        @pl.when((src <= z) & (z < last) & ((z < last - 1) | (h < heads - guests)))
        def _():
            hop(src, h, True).wait_send()

        @pl.when((src >= z) & has_left)
        def _():
            hop(src, h, False).wait_send()

        @pl.when((src != z) & ((z < last) | (h < heads - guests)))
        def _():
            sib(src, h).wait_send()
        return carry

    lax.fori_loop(0, n * heads, drain, 0)

    @pl.when(z < last - 1)
    def _():
        slash_hop(heads).wait_send()

    @pl.when(z == last - 1)
    def _():
        slash_hop(heads - guests).wait_send()
        for g in range(guests):
            for copy in guest_part(g):
                copy.wait_send()

    @pl.when(has_left & has_right)
    def _():
        slash_sib(heads, s).wait_send()

    @pl.when(z == last)
    def _():
        slash_sib(heads - guests, s).wait_send()
        guest_mask().wait_send()
        for g in range(guests):
            guest_q(g).wait_send()


def store(o_vmem, o_hbm, sem):
    copy = pltpu.make_async_copy(o_vmem, o_hbm, sem)
    copy.start()
    copy.wait()


def chain_call(n, q, nk, nv, ck, cv, tables, heads, rows, head_dim):
    def vmem(*shape):
        return pltpu.VMEM(shape, jnp.bfloat16)

    hbm = pl.BlockSpec(memory_space=pltpu.HBM)
    smem = pl.BlockSpec(memory_space=pltpu.SMEM)
    in_vmem = pl.BlockSpec(memory_space=pltpu.VMEM)
    dma = pltpu.SemaphoreType.DMA
    cached, wide = ck.shape[:2]
    guests = heads // 2
    f32 = jnp.float32
    out = pl.pallas_call(
        functools.partial(chain, n),
        out_shape=pltpu.VMEM((heads * rows, head_dim), jnp.bfloat16),
        in_specs=[hbm] * 5 + [smem] * 4,
        out_specs=in_vmem,
        scratch_shapes=[
            vmem(heads * rows, head_dim), vmem(wide, head_dim), vmem(wide, head_dim),
            vmem(cached, wide, head_dim), vmem(cached, wide, head_dim),
            vmem(heads + guests, rows, head_dim), vmem(2, 2, heads, BLK, head_dim),
            vmem(wide, wide), vmem(wide, wide),
            vmem(n, heads, 2, 2, BLK, head_dim),
            pltpu.VMEM((heads + guests, head_dim, rows), f32),
            pltpu.VMEM((heads + guests, 1, rows), f32),
            pltpu.VMEM((heads + guests, 1, rows), f32),
            pltpu.VMEM((2, 16, BLK), f32),
            vmem(guests, head_dim, rows), pltpu.VMEM((guests, 8, rows), f32),
            dma((n, heads, 2)), dma((n, heads)), dma((n, heads)), dma((n, heads)), dma((4,)),
            dma((2, guests + 1)), dma((2, guests, 2)), dma((5,)),
        ],
        compiler_params=pltpu.CompilerParams(
            collective_id=0, has_side_effects=True, vmem_limit_bytes=40 * 2**20),
    )(q, nk, nv, ck, cv, *tables)
    return pl.pallas_call(
        store,
        out_shape=jax.ShapeDtypeStruct(out.shape, out.dtype),
        in_specs=[in_vmem],
        out_specs=hbm,
        scratch_shapes=[dma],
        compiler_params=pltpu.CompilerParams(vmem_limit_bytes=2**20),
    )(out)


def shards(n, queries, new_keys, new_values, cache_keys, cache_values,
           vertical_pool, vertical_lists, slash_lists, list_counts):
    tokens, heads, groups, head_dim = queries.shape
    rows = tokens * groups
    picked = vertical_pool.shape[0]

    def flat(x):
        return x.reshape(-1, head_dim)

    def vmem(*shape):
        return pltpu.VMEM(shape, jnp.bfloat16)

    hbm = pl.BlockSpec(memory_space=pltpu.HBM)
    smem = pl.BlockSpec(memory_space=pltpu.SMEM)
    dma = pltpu.SemaphoreType.DMA
    wide = heads * BLK
    cached = cache_keys.shape[0] // BLK
    if n == 4 and heads == 4 and picked == 2:
        out = chain_call(n, flat(queries), flat(new_keys), flat(new_values),
                         cache_keys.reshape(cached, wide, head_dim), cache_values.reshape(cached, wide, head_dim),
                         (vertical_pool, vertical_lists, slash_lists, list_counts), heads, rows, head_dim)
        return out.reshape(tokens, heads, groups, head_dim)
    out = pl.pallas_call(
        functools.partial(attend, n),
        out_shape=jax.ShapeDtypeStruct((tokens * heads * groups, head_dim), jnp.bfloat16),
        in_specs=[hbm] * 5 + [smem] * 4,
        out_specs=pl.BlockSpec(memory_space=pltpu.VMEM),
        scratch_shapes=[
            vmem(heads * rows, head_dim), vmem(wide, head_dim), vmem(wide, head_dim),
            vmem(cached, wide, head_dim), vmem(cached, wide, head_dim),
            vmem(heads, rows, head_dim), vmem(picked, 2, heads, BLK, head_dim),
            vmem(2, heads, BLK, head_dim), vmem(wide, wide), vmem(wide, wide),
            vmem(n, picked, 2, heads, BLK, head_dim),
            vmem(2, wide, head_dim), vmem(2, heads, BLK, head_dim),
            pltpu.VMEM((heads, head_dim, rows), jnp.float32),
            pltpu.VMEM((heads, 1, rows), jnp.float32),
            pltpu.VMEM((heads, 1, rows), jnp.float32),
            vmem(2, heads, 3 * BLK, rows), pltpu.VMEM((2, heads, 1, rows), jnp.float32),
            dma((n, 2, 2)), dma((n, 2)), dma((n, 2)), dma((n, 2)), dma((4,)), dma((5,)),
        ],
        compiler_params=pltpu.CompilerParams(
            collective_id=0, has_side_effects=True, vmem_limit_bytes=60 * 2**20),
    )(flat(queries), flat(new_keys), flat(new_values), cache_keys.reshape(cached, wide, head_dim),
      cache_values.reshape(cached, wide, head_dim),
      vertical_pool, vertical_lists, slash_lists, list_counts)
    return out.reshape(tokens, heads, groups, head_dim)


def solution(mesh):
    in_specs = (
        P(("grp", "ctx"), "kvh", "sub", None),
        P(("grp", "ctx"), "kvh", None),
        P(("grp", "ctx"), "kvh", None),
        P(("grp", "ctx"), "kvh", None),
        P(("grp", "ctx"), "kvh", None),
        P(("grp", "ctx")),
        P(("grp", "ctx"), None),
        P(("grp", "ctx"), None),
        P(("grp", "ctx"), None),
    )
    out_specs = P(("grp", "ctx"), "kvh", "sub", None)
    return jax.shard_map(functools.partial(shards, mesh.shape["ctx"]), mesh=mesh,
                         in_specs=in_specs, out_specs=out_specs, check_vma=False)
```

```python
import functools
import math

import jax
import jax.numpy as jnp
from jax import lax
from jax.experimental import pallas as pl
from jax.experimental.pallas import tpu as pltpu
from jax.sharding import PartitionSpec as P

BLK = 128
MESH = pl.DeviceIdType.MESH


def attend(n, q_hbm, nk_hbm, nv_hbm, ck_hbm, cv_hbm, vp_ref, vl_ref, sl_ref, cnt_ref, o_ref,
           q_raw, nk_raw, nv_raw, ck_raw, cv_raw, q_ref, own_ref, new_ref, sort_kv, sort_q,
           pool, slash_raw, slash, acc, peak, total, rounded, fade,
           hop_send, hop_recv, sib_send, sib_recv, sl_sem, in_sem):
    z = lax.axis_index("ctx")
    s = lax.axis_index("sub")
    heads, rows, head_dim = q_ref.shape
    groups = rows // BLK
    wide = heads * BLK
    loads = [pltpu.make_async_copy(src, dst, in_sem.at[i]) for i, (src, dst) in enumerate(
        [(ck_hbm, ck_raw), (cv_hbm, cv_raw), (nk_hbm, nk_raw), (nv_hbm, nv_raw), (q_hbm, q_raw)])]
    loads[0].start()
    c = math.log2(math.e) / math.sqrt(head_dim)
    has_left = z > 0
    has_right = z < n - 1
    sib_id = {"sub": 1 - s}

    barrier = pltpu.get_barrier_semaphore()
    pl.semaphore_signal(barrier, inc=1, device_id=sib_id, device_id_type=MESH)

    @pl.when(has_left)
    def _():
        pl.semaphore_signal(barrier, inc=1, device_id={"ctx": z - 1}, device_id_type=MESH)

    @pl.when(has_right)
    def _():
        pl.semaphore_signal(barrier, inc=1, device_id={"ctx": z + 1}, device_id_type=MESH)

    ids = lax.broadcasted_iota(jnp.int32, (wide, wide), 0)
    at = lax.broadcasted_iota(jnp.int32, (wide, wide), 1)
    sort_kv[...] = jnp.where(at == (ids % BLK) * heads + ids // BLK, 1.0, 0.0).astype(jnp.bfloat16)
    token = (ids % BLK) // groups
    sort_q[...] = jnp.where(at == (token * heads + ids // BLK) * groups + ids % groups,
                            1.0, 0.0).astype(jnp.bfloat16)

    def by_head(raw):
        return jnp.dot(sort_kv[...], raw, preferred_element_type=jnp.float32).astype(jnp.bfloat16)

    def put_keys(dst, raw):
        ordered = by_head(raw)
        for h in range(heads):
            dst[h] = ordered[h * BLK:(h + 1) * BLK]

    def put_values(dst, raw):
        ordered = lax.dot_general(raw, sort_kv[...], (((0,), (1,)), ((), ())),
                                  preferred_element_type=jnp.float32).astype(jnp.bfloat16)
        for h in range(heads):
            dst[h] = ordered[:, h * BLK:(h + 1) * BLK]

    def chosen(cache, b):
        return cache[vp_ref[b]]

    pl.semaphore_wait(barrier, 1 + has_left.astype(jnp.int32) + has_right.astype(jnp.int32))

    def hop(src_ref, src, kv, right):
        return pltpu.make_async_remote_copy(
            src_ref=src_ref, dst_ref=pool.at[src, s, kv],
            send_sem=hop_send.at[src, int(right), kv], recv_sem=hop_recv.at[src, kv],
            device_id={"ctx": z + 1 if right else z - 1}, device_id_type=MESH)

    def sib(src, kv):
        return pltpu.make_async_remote_copy(
            src_ref=pool.at[src, s, kv], dst_ref=pool.at[src, s, kv],
            send_sem=sib_send.at[src, kv], recv_sem=sib_recv.at[src, kv],
            device_id=sib_id, device_id_type=MESH)

    def sib_in(src, kv):
        return pltpu.make_async_remote_copy(
            src_ref=pool.at[src, 1 - s, kv], dst_ref=pool.at[src, 1 - s, kv],
            send_sem=sib_send.at[src, kv], recv_sem=sib_recv.at[src, kv],
            device_id=sib_id, device_id_type=MESH)

    def slash_hop(src_ref=nk_hbm):
        return pltpu.make_async_remote_copy(
            src_ref=src_ref, dst_ref=slash_raw.at[s],
            send_sem=sl_sem.at[0], recv_sem=sl_sem.at[1],
            device_id={"ctx": z + 1}, device_id_type=MESH)

    def slash_sib(part):
        return pltpu.make_async_remote_copy(
            src_ref=slash_raw.at[part], dst_ref=slash_raw.at[part],
            send_sem=sl_sem.at[2], recv_sem=sl_sem.at[3],
            device_id=sib_id, device_id_type=MESH)

    for part, src_ref in enumerate((nk_hbm, nv_hbm)):
        @pl.when(has_right & (s == part))
        def _():
            slash_hop(src_ref).start()

    def send_own(kv):
        @pl.when(has_right)
        def _():
            hop(own_ref.at[s, kv], z, kv, True).start()

        @pl.when(has_left)
        def _():
            hop(own_ref.at[s, kv], z, kv, False).start()

    loads[0].wait()
    loads[1].start()
    put_keys(own_ref.at[s, 0], chosen(ck_raw, s))
    for load in loads[2:]:
        load.start()
    send_own(0)
    loads[1].wait()
    put_values(own_ref.at[s, 1], chosen(cv_raw, s))
    send_own(1)
    loads[2].wait()
    loads[3].wait()
    put_keys(new_ref.at[0], nk_raw[...])
    put_values(new_ref.at[1], nv_raw[...])
    put_keys(own_ref.at[1 - s, 0], chosen(ck_raw, 1 - s))
    put_values(own_ref.at[1 - s, 1], chosen(cv_raw, 1 - s))
    loads[4].wait()
    for part in range(rows // BLK):
        ordered = jnp.dot(sort_q[...], q_raw[part * wide:(part + 1) * wide],
                          preferred_element_type=jnp.float32).astype(jnp.bfloat16)
        for h in range(heads):
            q_ref[h, part * BLK:(part + 1) * BLK] = ordered[h * BLK:(h + 1) * BLK]

    def listed(slot):
        count = cnt_ref[0, 0]
        width = vl_ref.shape[1]
        if width <= 8:
            hit = jnp.int32(0)
            for i in range(width):
                hit = hit | jnp.where((vl_ref[0, i] == slot) & (i < count), 1, 0)
            return hit

        def one(i, hit):
            return hit | jnp.where((vl_ref[0, i] == slot) & (i < count), 1, 0)

        return lax.fori_loop(0, width, one, jnp.int32(0))

    def score(keys, q):
        return lax.dot_general(keys, q, (((1,), (1,)), ((), ())),
                               preferred_element_type=jnp.float32)

    def take_keys(side, blocks, first=False):
        for h in range(heads):
            q = q_ref[h]
            raw = []
            tops = []
            for keys, seen in blocks:
                scores = score(keys[h], q)
                if seen is None:
                    key_id = lax.broadcasted_iota(jnp.int32, scores.shape, 0)
                    row_id = lax.broadcasted_iota(jnp.int32, scores.shape, 1) // groups
                    scores = jnp.where(key_id <= row_id, scores, -jnp.inf)
                top = jnp.max(scores, axis=0, keepdims=True)
                if seen is not None:
                    top = jnp.where(seen > 0, top, -jnp.inf)
                raw.append(scores)
                tops.append(top)
            high = functools.reduce(jnp.maximum, tops)
            if not first:
                old = peak[h]
                high = jnp.maximum(old, high)
                factor = jnp.exp2((old - high) * c)
                fade[side, h] = factor
            peak[h] = high
            sums = []
            for i, ((_, seen), scores) in enumerate(zip(blocks, raw)):
                base = high if seen is None else jnp.where(seen > 0, high, jnp.inf)
                weights = jnp.exp2((scores - base) * c)
                sums.append(jnp.sum(weights, axis=0, keepdims=True))
                rounded[side, h, i * BLK:(i + 1) * BLK] = weights.astype(jnp.bfloat16)
            add = sum(sums[1:], sums[0])
            total[h] = add if first else total[h] * fade[side, h] + add

    def take_values(side, blocks, first=False):
        depth = len(blocks) * BLK
        for h in range(heads):
            values = jnp.concatenate([values[h] for values in blocks], 1)
            add = jnp.dot(values, rounded[side, h, :depth], preferred_element_type=jnp.float32)
            acc[h] = add if first else acc[h] * fade[side, h] + add

    take_keys(0, [(new_ref.at[0], None)]
              + [(own_ref.at[b, 0], listed(2 * z + b)) for b in range(2)], first=True)
    take_values(0, [new_ref.at[1]] + [own_ref.at[b, 1] for b in range(2)], first=True)

    @pl.when(has_left)
    def _():
        slash_hop().wait_recv()
        slash_sib(s).start()

    def arrive(src, kv, right):
        hop(own_ref.at[s, kv], src, kv, right).wait_recv()

        @pl.when(has_right if right else has_left)
        def _():
            hop(pool.at[src, s, kv], src, kv, right).start()

        sib(src, kv).start()

    def step(d, carry):
        sides = ((z + d, z + d < n, False), (z - d, z - d >= 0, True))
        for kv in range(2):
            for src, there, right in sides:
                @pl.when(there)
                def _():
                    arrive(src, kv, right)

            for side, (src, there, right) in enumerate(sides):
                @pl.when(there)
                def _():
                    sib_in(src, kv).wait_recv()
                    if kv == 0:
                        take_keys(side, [(pool.at[src, b, 0], listed(2 * src + b))
                                         for b in range(2)])
                    else:
                        take_values(side, [pool.at[src, b, 1] for b in range(2)])

        @pl.when((d == 1) & has_left)
        def _():
            slash_sib(1 - s).wait_recv()
            put_keys(slash.at[0], slash_raw[0])
            put_values(slash.at[1], slash_raw[1])
            back = jnp.int32(0)
            for i in range(sl_ref.shape[1]):
                back = back | jnp.where((sl_ref[0, i] == 1) & (i < cnt_ref[0, 1]), 1, 0)
            take_keys(0, [(slash.at[0], back)])
            take_values(0, [slash.at[1]])

        return carry

    lax.fori_loop(1, n, step, 0)

    for part in range(rows // BLK):
        lanes = slice(part * BLK, (part + 1) * BLK)
        done = jnp.concatenate(
            [(acc[h, :, lanes] / total[h, :, lanes]).astype(jnp.bfloat16) for h in range(heads)], 1)
        o_ref[part * wide:(part + 1) * wide] = lax.dot_general(
            sort_q[...], done, (((0,), (1,)), ((), ())),
            preferred_element_type=jnp.float32).astype(o_ref.dtype)

    def drain(src, carry):
        for kv in range(2):
            @pl.when(has_right & (src <= z))
            def _():
                hop(own_ref.at[s, kv], src, kv, True).wait_send()

            @pl.when(has_left & (src >= z))
            def _():
                hop(own_ref.at[s, kv], src, kv, False).wait_send()

            @pl.when(src != z)
            def _():
                sib(src, kv).wait_send()
        return carry

    lax.fori_loop(0, n, drain, 0)

    @pl.when(has_right)
    def _():
        slash_hop().wait_send()

    @pl.when(has_left)
    def _():
        slash_sib(s).wait_send()

BITS = 5
PACK = 6
OWN, GUEST, ALONE = 4, 5, 6
IDLE = (6, 4 * GUEST)
GUESTS = 1


def plan(heads):
    def kv(src, h):
        return (1, src * 4 + h)

    def unit(slot, src, h, wait=True):
        return (slot + (8 if wait else 0), src * 4 + h)

    def mine(h, src):
        return unit(h, src, h)

    def early(z):
        return [(None, unit(h, z, h, False)) for h in range(heads)]

    def build(steps):
        out, before = [], None
        for recv, now, *more in steps + [(None, None)]:
            busy = now is not None or before is not None
            code = now if now is not None else IDLE
            out.append((recv or (0, 0)) + code + (int(busy) | sum(more),))
            before = now
        return out

    quest, slash, part = (2, 0), (3, 0), (4, 0)

    def local(h, src=OWN):
        return unit(h, src, h, src == OWN and h == 0)

    zero = early(0) + [(None, local(h, ALONE)) for h in range(heads)]
    late = None
    for src in (1, 2, 3):
        for h in range(heads):
            zero.append((kv(src, h), late))
            late = mine(h, src)
    zero.append((None, late))

    one = early(1) + [
        (kv(2, 0), None), (kv(0, 0), mine(0, 2)), (kv(2, 1), mine(0, 0)), (kv(0, 3), mine(1, 2)),
        (kv(2, 2), mine(3, 0)), (kv(0, 1), mine(2, 2), 4), (kv(2, 3), mine(1, 0)), (kv(0, 2), mine(3, 2), 8),
        (kv(3, 0), mine(2, 0)), (kv(3, 1), mine(0, 3)), (slash, mine(1, 3)), (kv(3, 2), local(0)),
        (None, local(1)), (None, local(2)), (kv(3, 3), mine(2, 3)), (None, local(3)), (None, mine(3, 3))]

    two = early(2) + [
        (kv(3, 0), None), (kv(1, 0), mine(0, 3)), (kv(1, 3), mine(0, 1)), (quest, mine(3, 1)),
        (kv(1, 1), unit(4, 2, 3, False)), (kv(3, 1), unit(4, GUEST, 3, False)), (kv(0, 0), mine(1, 1)),
        (None, unit(4, 1, 3, False)), (kv(3, 2), mine(1, 3)), (kv(0, 3), mine(0, 0)), (kv(3, 3), mine(2, 3)),
        (None, unit(4, 0, 3)), (None, mine(3, 3), 2), (kv(0, 1), unit(3, 0, 3, False)), (kv(1, 2), mine(1, 0)),
        (kv(0, 2), mine(2, 1)), (None, mine(2, 0)), (slash, None), (None, local(0)),
        (None, local(1)), (None, local(2)), (None, local(3))]

    three = early(3) + [(None, local(3, ALONE)),
        (kv(2, 0), None), (slash, mine(0, 2)), (kv(2, 1), local(0)), (None, mine(1, 2)), (None, local(1)),
        (kv(2, 2), local(2)), (kv(1, 0), mine(2, 2)), (kv(1, 1), mine(0, 1)), (kv(0, 0), mine(1, 1)),
        (None, mine(0, 0)), (part, None), (kv(0, 1), None), (kv(1, 2), mine(1, 0)), (kv(0, 2), mine(2, 1)),
        (None, mine(2, 0))]
    return [build(role) for role in (zero, one, two, three)]


def chain(n, q_hbm, nk_hbm, nv_hbm, ck_hbm, cv_hbm, vp_ref, vl_ref, sl_ref, cnt_ref, o_ref,
          q_raw, nk_raw, nv_raw, ck_raw, cv_raw, q_ref, sort_kv, sort_q, ext,
          pool, acc, peak, total, mask, part_acc, part_stat, scores_a, scores_b, top_a, top_b,
          hop_send, hop_recv, sib_send, sib_recv, sl_sem, q_sem, part_sem, in_sem, ready):
    z = lax.axis_index("ctx")
    s = lax.axis_index("sub")
    heads = pool.shape[1]
    head_dim, rows = acc.shape[1:]
    groups = rows // BLK
    wide = heads * BLK
    last = n - 1
    stay = heads - GUESTS
    loads = [pltpu.make_async_copy(src, dst, in_sem.at[i]) for i, (src, dst) in enumerate(
        [(ck_hbm, ck_raw), (cv_hbm, cv_raw), (nk_hbm, nk_raw), (nv_hbm, nv_raw), (q_hbm, q_raw)])]
    for load in loads:
        load.start()
    c = math.log2(math.e) / math.sqrt(head_dim)
    has_left = z > 0
    has_right = z < last
    sib_id = {"sub": 1 - s}

    barrier = pltpu.get_barrier_semaphore()
    pl.semaphore_signal(barrier, inc=1, device_id=sib_id, device_id_type=MESH)

    @pl.when(has_right)
    def _():
        pl.semaphore_signal(barrier, inc=1, device_id={"ctx": z + 1}, device_id_type=MESH)

    ids = lax.broadcasted_iota(jnp.int32, (wide, wide), 0)
    at = lax.broadcasted_iota(jnp.int32, (wide, wide), 1)
    sort_kv[...] = jnp.where(at == (ids % BLK) * heads + ids // BLK, 1.0, 0.0).astype(jnp.bfloat16)

    pl.semaphore_wait(barrier, 1 + has_left.astype(jnp.int32))

    @pl.when(has_left)
    def _():
        pl.semaphore_signal(ready, inc=1, device_id={"ctx": z - 1}, device_id_type=MESH)

    def put_keys(raw, put):
        ordered = jnp.dot(sort_kv[...], raw, preferred_element_type=jnp.float32).astype(jnp.bfloat16)
        for h in range(heads):
            put(h, ordered[h * BLK:(h + 1) * BLK])

    def put_values(raw, put):
        ordered = lax.dot_general(raw, sort_kv[...], (((0,), (1,)), ((), ())),
                                  preferred_element_type=jnp.float32).astype(jnp.bfloat16)
        for h in range(heads):
            put(h, ordered[:, h * BLK:(h + 1) * BLK])

    def put_pool(b, kv):
        def put(h, block):
            pool[z, h, b, kv] = block
        return put

    def put_new(kv):
        def put(h, block):
            pool[OWN, h, 0, kv] = block
            pool[GUEST, h, 0, kv] = block
            pool[GUEST, h, 1, kv] = jnp.zeros_like(block)
        return put

    def hop(src, h, right):
        return pltpu.make_async_remote_copy(
            src_ref=pool.at[src, h, s], dst_ref=pool.at[src, h, s],
            send_sem=hop_send.at[src, h, int(right)], recv_sem=hop_recv.at[src, h],
            device_id={"ctx": z + 1 if right else z - 1}, device_id_type=MESH)

    def sib(src, h, part):
        return pltpu.make_async_remote_copy(
            src_ref=pool.at[src, h, part], dst_ref=pool.at[src, h, part],
            send_sem=sib_send.at[src, h], recv_sem=sib_recv.at[src, h],
            device_id=sib_id, device_id_type=MESH)

    def slash_hop(count):
        return pltpu.make_async_remote_copy(
            src_ref=pool.at[OWN, pl.ds(0, count), 0, s], dst_ref=pool.at[OWN, pl.ds(0, count), 1, s],
            send_sem=sl_sem.at[0], recv_sem=sl_sem.at[1],
            device_id={"ctx": z + 1}, device_id_type=MESH)

    def slash_sib(count, part):
        block = pool.at[OWN, pl.ds(0, count), 1, part]
        return pltpu.make_async_remote_copy(
            src_ref=block, dst_ref=block,
            send_sem=sl_sem.at[2], recv_sem=sl_sem.at[3],
            device_id=sib_id, device_id_type=MESH)

    def guest_q(g):
        return pltpu.make_async_remote_copy(
            src_ref=q_ref.at[stay + g, pl.ds(0, head_dim)], dst_ref=q_ref.at[heads + g, pl.ds(0, head_dim)],
            send_sem=q_sem.at[0, g], recv_sem=q_sem.at[1, g],
            device_id={"ctx": z - 1}, device_id_type=MESH)

    def guest_mask():
        return pltpu.make_async_remote_copy(
            src_ref=mask.at[0], dst_ref=mask.at[1],
            send_sem=q_sem.at[0, GUESTS], recv_sem=q_sem.at[1, GUESTS],
            device_id={"ctx": z - 1}, device_id_type=MESH)

    def guest_part(g):
        return [pltpu.make_async_remote_copy(
            src_ref=ref.at[g], dst_ref=ref.at[g],
            send_sem=part_sem.at[0, g, i], recv_sem=part_sem.at[1, g, i],
            device_id={"ctx": z + 1}, device_id_type=MESH)
            for i, ref in enumerate((part_acc, part_stat))]

    loads[0].wait()
    put_keys(ck_raw[vp_ref[s]], put_pool(s, 0))
    loads[1].wait()
    put_values(cv_raw[vp_ref[s]], put_pool(s, 1))

    @pl.when((z == 1) | (z == 2))
    def _():
        for h in range(heads):
            hop(z, h, False).start()

    @pl.when(z == last)
    def _():
        hop(z, 0, False).start()

    @pl.when(has_right)
    def _():
        pl.semaphore_wait(ready, 1)

    @pl.when(z == 0)
    def _():
        for h in (0, 3, 1, 2):
            hop(z, h, True).start()

    @pl.when(z == 1)
    def _():
        for h in (0, 3, 1):
            hop(z, h, True).start()

    @pl.when(z == 2)
    def _():
        hop(z, 0, True).start()

    loads[2].wait()
    loads[3].wait()
    put_keys(nk_raw[...], put_new(0))
    put_values(nv_raw[...], put_new(1))

    @pl.when(z == 0)
    def _():
        slash_hop(heads).start()

    @pl.when(z == 2)
    def _():
        slash_hop(stay).start()
        hop(z, 1, True).start()
        hop(z, 2, True).start()

    token = (ids % BLK) // groups
    sort_q[...] = jnp.where(at == (token * heads + ids // BLK) * groups + ids % groups,
                            1.0, 0.0).astype(jnp.bfloat16)
    loads[4].wait()
    for part in range(rows // BLK):
        ordered = lax.dot_general(q_raw[part * wide:(part + 1) * wide], sort_q[...], (((0,), (1,)), ((), ())),
                                  preferred_element_type=jnp.float32).astype(jnp.bfloat16)
        for h in range(heads):
            q_ref[h, 0:head_dim, part * BLK:(part + 1) * BLK] = ordered[:, h * BLK:(h + 1) * BLK]

    def unseen(hit):
        return jnp.full((1, BLK), jnp.where(hit > 0, 0.0, jnp.inf), jnp.float32)

    for slot in range(2 * n):
        hit = jnp.int32(0)
        for i in range(vl_ref.shape[1]):
            hit = hit | jnp.where((vl_ref[0, i] == slot) & (i < cnt_ref[0, 0]), 1, 0)
        mask[0, slot:slot + 1] = unseen(hit)
    hit = jnp.int32(0)
    for i in range(sl_ref.shape[1]):
        hit = hit | jnp.where((sl_ref[0, i] == 1) & (i < cnt_ref[0, 1]), 1, 0)
    mask[0, 2 * OWN:2 * OWN + 2] = jnp.concatenate([jnp.zeros((1, BLK), jnp.float32), unseen(hit)], 0)
    mask[0, 2 * GUEST:2 * GUEST + 2] = jnp.concatenate([unseen(hit), jnp.full((1, BLK), jnp.inf, jnp.float32)], 0)
    mask[0, 2 * ALONE:2 * ALONE + 2] = jnp.concatenate(
        [jnp.zeros((1, BLK), jnp.float32), jnp.full((1, BLK), jnp.inf, jnp.float32)], 0)

    @pl.when(z == last)
    def _():
        for g in range(GUESTS):
            guest_q(g).start()
        guest_mask().start()
        for h in range(1, heads):
            hop(z, h, False).start()

    put_keys(ck_raw[vp_ref[1 - s]], put_pool(1 - s, 0))
    put_values(cv_raw[vp_ref[1 - s]], put_pool(1 - s, 1))

    key_id = lax.broadcasted_iota(jnp.int32, (BLK, rows), 0)
    row_id = lax.broadcasted_iota(jnp.int32, (BLK, rows), 1) // groups
    later = jnp.where(key_id > row_id, -1e30, 0.0).astype(jnp.bfloat16)
    slots = acc.shape[0]
    for slot in range(slots):
        q_ref[slot, head_dim:] = later if slot < heads else jnp.zeros_like(later)
        acc[slot] = jnp.zeros_like(acc[slot])
        total[slot] = jnp.zeros_like(total[slot])
        peak[slot] = jnp.full_like(peak[slot], -1e30)
    q_ref[slots - 1, 0:head_dim] = jnp.zeros_like(later)
    one_at = lax.broadcasted_iota(jnp.int32, (BLK, BLK), 0) == lax.broadcasted_iota(jnp.int32, (BLK, BLK), 1)
    ext[0] = jnp.zeros((BLK, BLK), jnp.bfloat16)
    ext[1] = jnp.where(one_at, 1.0, 0.0).astype(jnp.bfloat16)
    scores_b[...] = jnp.zeros_like(scores_b)
    top_b[...] = jnp.zeros_like(top_b)

    def spread(row):
        return jnp.concatenate([row] * groups, 1)

    def place(src):
        return src - src // ALONE

    def hidden(slot, src, b):
        return spread(mask[(slot // heads) % 2 * (1 - slot // (slots - 1)), pl.ds(2 * src + b, 1)])

    def ahead(unit, scores, top):
        slot, src, h = unit
        q = q_ref[slot]
        high = None
        for b in range(2):
            causal = (src // OWN) * (1 - src % 2) if b == 0 else 0
            keys = jnp.concatenate([pool[place(src), h, b, 0], ext[causal]], 1)
            found = jnp.dot(keys, q, preferred_element_type=jnp.float32)
            scores[b * BLK:(b + 1) * BLK] = found
            part = jnp.max(found, axis=0, keepdims=True) - hidden(slot, src, b)
            high = part if high is None else jnp.maximum(high, part)
        top[...] = high

    def behind(unit, scores, top):
        slot, src, h = unit
        old = peak[slot]
        high = jnp.maximum(old, top[...])
        factor = jnp.exp2((old - high) * c)
        peak[slot] = high
        weights = [jnp.exp2((scores[b * BLK:(b + 1) * BLK] - (high + hidden(slot, src, b))) * c)
                   .astype(jnp.bfloat16) for b in range(2)]
        values = jnp.concatenate([pool[place(src), h, b, 1] for b in range(2)], 1)
        values = jnp.concatenate([values, jnp.ones((16, 2 * BLK), jnp.bfloat16)], 0)
        add = jnp.dot(values, jnp.concatenate(weights, 0), preferred_element_type=jnp.float32)
        acc[slot] = acc[slot] * factor + add[:head_dim]
        total[slot] = total[slot] * factor + add[head_dim:head_dim + 1]

    roles = plan(heads)
    steps = max(len(role) for role in roles)
    steps += steps % 2
    roles = [role + [(0, 0) + IDLE + (0,)] * (steps - len(role)) for role in roles]

    def by_role(values):
        out = jnp.int32(values[-1])
        for i in reversed(range(len(values) - 1)):
            out = jnp.where(z == i, jnp.int32(values[i]), out)
        return out

    words = [[by_role([sum(step[field] << (BITS * i) for i, step in enumerate(role[start:start + PACK]))
                       for role in roles]) for start in range(0, steps, PACK)] for field in range(5)]

    def step(t, before, bufs, old_bufs):
        def look(field):
            word = words[field][-1]
            for i in reversed(range(len(words[field]) - 1)):
                word = jnp.where(t // PACK == i, words[field][i], word)
            return lax.shift_right_logical(word, BITS * (t % PACK)) & (2 ** BITS - 1)

        kind, message, code, block, flags = [look(field) for field in range(5)]
        src, h = message // 4, message % 4

        @pl.when(kind == 1)
        def _():
            hop(src, h, True).wait_recv()

            @pl.when((src > z) & has_left)
            def _():
                hop(src, h, False).start()

            @pl.when((src < z) & ((z < last - 1) | ((z == last - 1) & (h < stay))))
            def _():
                hop(src, h, True).start()

            sib(src, h, s).start()

        @pl.when((flags // 4) % 2 == 1)
        def _():
            hop(z, 2, True).start()

        @pl.when(flags // 8 == 1)
        def _():
            slash_hop(heads).start()

        @pl.when(kind == 2)
        def _():
            guest_mask().wait_recv()
            for g in range(GUESTS):
                guest_q(g).wait_recv()

        @pl.when((kind == 3) & has_right)
        def _():
            slash_hop(heads).wait_recv()
            slash_sib(heads, s).start()

        @pl.when((kind == 3) & (z == last))
        def _():
            slash_hop(stay).wait_recv()
            slash_sib(stay, s).start()

        @pl.when(kind == 4)
        def _():
            for copy in guest_part(h):
                copy.wait_recv()
            slot = stay + h
            old, new = peak[slot], part_stat[h, 0:1]
            high = jnp.maximum(old, new)
            mine, theirs = jnp.exp2((old - high) * c), jnp.exp2((new - high) * c)
            acc[slot] = acc[slot] * mine + part_acc[h].astype(jnp.float32) * theirs
            total[slot] = total[slot] * mine + part_stat[h, 1:2] * theirs

        unit = (code % 8, block // 4, block % 4)

        @pl.when((code > 7) & (unit[1] < OWN))
        def _():
            sib(unit[1], unit[2], 1 - s).wait_recv()

        @pl.when((code > 7) & (unit[1] == OWN) & has_right)
        def _():
            slash_sib(heads, 1 - s).wait_recv()

        @pl.when((code > 7) & (unit[1] == OWN) & (z == last))
        def _():
            slash_sib(stay, 1 - s).wait_recv()

        @pl.when(flags % 2 == 1)
        def _():
            ahead(unit, *bufs)
            behind(before, *old_bufs)

        @pl.when((flags // 2) % 2 == 1)
        def _():
            g = 0
            part_acc[g] = acc[heads + g].astype(jnp.bfloat16)
            part_stat[g, 0:1] = peak[heads + g]
            part_stat[g, 1:2] = total[heads + g]
            for copy in guest_part(g):
                copy.start()

        return unit

    def two_steps(i, before):
        mid = step(2 * i, before, (scores_a, top_a), (scores_b, top_b))
        return step(2 * i + 1, mid, (scores_b, top_b), (scores_a, top_a))

    lengths = [max(t for t, step in enumerate(role) if step[0] or step[4]) + 1 for role in roles]
    idle = (jnp.int32(IDLE[0]), jnp.int32(GUEST), jnp.int32(0))
    lax.fori_loop(0, by_role([(length + 1) // 2 for length in lengths]), two_steps, idle)

    for part in range(rows // BLK):
        lanes = slice(part * BLK, (part + 1) * BLK)
        done = jnp.concatenate(
            [(acc[h, :, lanes] / total[h, :, lanes]).astype(jnp.bfloat16) for h in range(heads)], 1)
        o_ref[part * wide:(part + 1) * wide] = lax.dot_general(
            sort_q[...], done, (((0,), (1,)), ((), ())),
            preferred_element_type=jnp.float32).astype(o_ref.dtype)

    def drain(i, carry):
        src, h = i // heads, i % heads

        @pl.when((src <= z) & (z < last) & ((z < last - 1) | (h < stay)))
        def _():
            hop(src, h, True).wait_send()

        @pl.when((src >= z) & has_left)
        def _():
            hop(src, h, False).wait_send()

        @pl.when((src != z) & ((z < last) | (h < stay)))
        def _():
            sib(src, h, s).wait_send()
        return carry

    lax.fori_loop(0, n * heads, drain, 0)

    @pl.when(z < last - 1)
    def _():
        slash_hop(heads).wait_send()

    @pl.when(z == last - 1)
    def _():
        slash_hop(stay).wait_send()
        for g in range(GUESTS):
            for copy in guest_part(g):
                copy.wait_send()

    @pl.when(has_left & has_right)
    def _():
        slash_sib(heads, s).wait_send()

    @pl.when(z == last)
    def _():
        slash_sib(stay, s).wait_send()
        guest_mask().wait_send()
        for g in range(GUESTS):
            guest_q(g).wait_send()


def store(o_vmem, o_hbm, sem):
    copy = pltpu.make_async_copy(o_vmem, o_hbm, sem)
    copy.start()
    copy.wait()


def chain_call(n, q, nk, nv, ck, cv, tables, heads, rows, head_dim):
    def vmem(*shape):
        return pltpu.VMEM(shape, jnp.bfloat16)

    def wide_vmem(*shape):
        return pltpu.VMEM(shape, jnp.float32)

    hbm = pl.BlockSpec(memory_space=pltpu.HBM)
    smem = pl.BlockSpec(memory_space=pltpu.SMEM)
    in_vmem = pl.BlockSpec(memory_space=pltpu.VMEM)
    dma = pltpu.SemaphoreType.DMA
    cached, wide = ck.shape[:2]
    slots = 7
    out = pl.pallas_call(
        functools.partial(chain, n),
        out_shape=pltpu.VMEM((heads * rows, head_dim), jnp.bfloat16),
        in_specs=[hbm] * 5 + [smem] * 4,
        out_specs=in_vmem,
        scratch_shapes=[
            vmem(heads * rows, head_dim), vmem(wide, head_dim), vmem(wide, head_dim),
            vmem(cached, wide, head_dim), vmem(cached, wide, head_dim),
            vmem(slots, 2 * head_dim, rows), vmem(wide, wide), vmem(wide, wide), vmem(2, BLK, BLK),
            vmem(n + 2, heads, 2, 2, BLK, head_dim),
            wide_vmem(slots, head_dim, rows), wide_vmem(slots, 1, rows), wide_vmem(slots, 1, rows),
            wide_vmem(2, 16, BLK), vmem(GUESTS, head_dim, rows), wide_vmem(GUESTS, 8, rows),
            wide_vmem(2 * BLK, rows), wide_vmem(2 * BLK, rows), wide_vmem(1, rows), wide_vmem(1, rows),
            dma((n, heads, 2)), dma((n, heads)), dma((n, heads)), dma((n, heads)), dma((4,)),
            dma((2, GUESTS + 1)), dma((2, GUESTS, 2)), dma((5,)), pltpu.SemaphoreType.REGULAR,
        ],
        compiler_params=pltpu.CompilerParams(
            collective_id=0, has_side_effects=True, vmem_limit_bytes=60 * 2**20),
    )(*[pltpu.with_memory_space_constraint(x, pltpu.HBM) for x in (q, nk, nv, ck, cv)], *tables)
    return pl.pallas_call(
        store,
        out_shape=jax.ShapeDtypeStruct(out.shape, out.dtype),
        in_specs=[in_vmem],
        out_specs=hbm,
        scratch_shapes=[dma],
        compiler_params=pltpu.CompilerParams(vmem_limit_bytes=2**20),
    )(out)


def shards(n, queries, new_keys, new_values, cache_keys, cache_values,
           vertical_pool, vertical_lists, slash_lists, list_counts):
    tokens, heads, groups, head_dim = queries.shape
    rows = tokens * groups
    picked = vertical_pool.shape[0]

    def flat(x):
        return x.reshape(-1, head_dim)

    def vmem(*shape):
        return pltpu.VMEM(shape, jnp.bfloat16)

    hbm = pl.BlockSpec(memory_space=pltpu.HBM)
    smem = pl.BlockSpec(memory_space=pltpu.SMEM)
    dma = pltpu.SemaphoreType.DMA
    wide = heads * BLK
    cached = cache_keys.shape[0] // BLK
    if n == 4 and heads == 4 and picked == 2:
        out = chain_call(n, flat(queries), flat(new_keys), flat(new_values),
                         cache_keys.reshape(cached, wide, head_dim), cache_values.reshape(cached, wide, head_dim),
                         (vertical_pool, vertical_lists, slash_lists, list_counts), heads, rows, head_dim)
        return out.reshape(tokens, heads, groups, head_dim)
    out = pl.pallas_call(
        functools.partial(attend, n),
        out_shape=jax.ShapeDtypeStruct((tokens * heads * groups, head_dim), jnp.bfloat16),
        in_specs=[hbm] * 5 + [smem] * 4,
        out_specs=pl.BlockSpec(memory_space=pltpu.VMEM),
        scratch_shapes=[
            vmem(heads * rows, head_dim), vmem(wide, head_dim), vmem(wide, head_dim),
            vmem(cached, wide, head_dim), vmem(cached, wide, head_dim),
            vmem(heads, rows, head_dim), vmem(picked, 2, heads, BLK, head_dim),
            vmem(2, heads, BLK, head_dim), vmem(wide, wide), vmem(wide, wide),
            vmem(n, picked, 2, heads, BLK, head_dim),
            vmem(2, wide, head_dim), vmem(2, heads, BLK, head_dim),
            pltpu.VMEM((heads, head_dim, rows), jnp.float32),
            pltpu.VMEM((heads, 1, rows), jnp.float32),
            pltpu.VMEM((heads, 1, rows), jnp.float32),
            vmem(2, heads, 3 * BLK, rows), pltpu.VMEM((2, heads, 1, rows), jnp.float32),
            dma((n, 2, 2)), dma((n, 2)), dma((n, 2)), dma((n, 2)), dma((4,)), dma((5,)),
        ],
        compiler_params=pltpu.CompilerParams(
            collective_id=0, has_side_effects=True, vmem_limit_bytes=60 * 2**20),
    )(flat(queries), flat(new_keys), flat(new_values), cache_keys.reshape(cached, wide, head_dim),
      cache_values.reshape(cached, wide, head_dim),
      vertical_pool, vertical_lists, slash_lists, list_counts)
    return out.reshape(tokens, heads, groups, head_dim)


def solution(mesh):
    in_specs = (
        P(("grp", "ctx"), "kvh", "sub", None),
        P(("grp", "ctx"), "kvh", None),
        P(("grp", "ctx"), "kvh", None),
        P(("grp", "ctx"), "kvh", None),
        P(("grp", "ctx"), "kvh", None),
        P(("grp", "ctx")),
        P(("grp", "ctx"), None),
        P(("grp", "ctx"), None),
        P(("grp", "ctx"), None),
    )
    out_specs = P(("grp", "ctx"), "kvh", "sub", None)
    return jax.shard_map(functools.partial(shards, mesh.shape["ctx"]), mesh=mesh,
                         in_specs=in_specs, out_specs=out_specs, check_vma=False)
```

```python
import functools
import math

import jax
import jax.numpy as jnp
from jax import lax
from jax.experimental import pallas as pl
from jax.experimental.pallas import tpu as pltpu
from jax.sharding import PartitionSpec as P

BLK = 128
MESH = pl.DeviceIdType.MESH


def attend(n, q_hbm, nk_hbm, nv_hbm, ck_hbm, cv_hbm, vp_ref, vl_ref, sl_ref, cnt_ref, o_ref,
           q_raw, nk_raw, nv_raw, ck_raw, cv_raw, q_ref, own_ref, new_ref, sort_kv, sort_q,
           pool, slash_raw, slash, acc, peak, total, rounded, fade,
           hop_send, hop_recv, sib_send, sib_recv, sl_sem, in_sem):
    z = lax.axis_index("ctx")
    s = lax.axis_index("sub")
    heads, rows, head_dim = q_ref.shape
    groups = rows // BLK
    wide = heads * BLK
    loads = [pltpu.make_async_copy(src, dst, in_sem.at[i]) for i, (src, dst) in enumerate(
        [(ck_hbm, ck_raw), (cv_hbm, cv_raw), (nk_hbm, nk_raw), (nv_hbm, nv_raw), (q_hbm, q_raw)])]
    loads[0].start()
    c = math.log2(math.e) / math.sqrt(head_dim)
    has_left = z > 0
    has_right = z < n - 1
    sib_id = {"sub": 1 - s}

    barrier = pltpu.get_barrier_semaphore()
    pl.semaphore_signal(barrier, inc=1, device_id=sib_id, device_id_type=MESH)

    @pl.when(has_left)
    def _():
        pl.semaphore_signal(barrier, inc=1, device_id={"ctx": z - 1}, device_id_type=MESH)

    @pl.when(has_right)
    def _():
        pl.semaphore_signal(barrier, inc=1, device_id={"ctx": z + 1}, device_id_type=MESH)

    ids = lax.broadcasted_iota(jnp.int32, (wide, wide), 0)
    at = lax.broadcasted_iota(jnp.int32, (wide, wide), 1)
    sort_kv[...] = jnp.where(at == (ids % BLK) * heads + ids // BLK, 1.0, 0.0).astype(jnp.bfloat16)
    token = (ids % BLK) // groups
    sort_q[...] = jnp.where(at == (token * heads + ids // BLK) * groups + ids % groups,
                            1.0, 0.0).astype(jnp.bfloat16)

    def by_head(raw):
        return jnp.dot(sort_kv[...], raw, preferred_element_type=jnp.float32).astype(jnp.bfloat16)

    def put_keys(dst, raw):
        ordered = by_head(raw)
        for h in range(heads):
            dst[h] = ordered[h * BLK:(h + 1) * BLK]

    def put_values(dst, raw):
        ordered = lax.dot_general(raw, sort_kv[...], (((0,), (1,)), ((), ())),
                                  preferred_element_type=jnp.float32).astype(jnp.bfloat16)
        for h in range(heads):
            dst[h] = ordered[:, h * BLK:(h + 1) * BLK]

    def chosen(cache, b):
        return cache[vp_ref[b]]

    pl.semaphore_wait(barrier, 1 + has_left.astype(jnp.int32) + has_right.astype(jnp.int32))

    def hop(src_ref, src, kv, right):
        return pltpu.make_async_remote_copy(
            src_ref=src_ref, dst_ref=pool.at[src, s, kv],
            send_sem=hop_send.at[src, int(right), kv], recv_sem=hop_recv.at[src, kv],
            device_id={"ctx": z + 1 if right else z - 1}, device_id_type=MESH)

    def sib(src, kv):
        return pltpu.make_async_remote_copy(
            src_ref=pool.at[src, s, kv], dst_ref=pool.at[src, s, kv],
            send_sem=sib_send.at[src, kv], recv_sem=sib_recv.at[src, kv],
            device_id=sib_id, device_id_type=MESH)

    def sib_in(src, kv):
        return pltpu.make_async_remote_copy(
            src_ref=pool.at[src, 1 - s, kv], dst_ref=pool.at[src, 1 - s, kv],
            send_sem=sib_send.at[src, kv], recv_sem=sib_recv.at[src, kv],
            device_id=sib_id, device_id_type=MESH)

    def slash_hop(src_ref=nk_hbm):
        return pltpu.make_async_remote_copy(
            src_ref=src_ref, dst_ref=slash_raw.at[s],
            send_sem=sl_sem.at[0], recv_sem=sl_sem.at[1],
            device_id={"ctx": z + 1}, device_id_type=MESH)

    def slash_sib(part):
        return pltpu.make_async_remote_copy(
            src_ref=slash_raw.at[part], dst_ref=slash_raw.at[part],
            send_sem=sl_sem.at[2], recv_sem=sl_sem.at[3],
            device_id=sib_id, device_id_type=MESH)

    for part, src_ref in enumerate((nk_hbm, nv_hbm)):
        @pl.when(has_right & (s == part))
        def _():
            slash_hop(src_ref).start()

    def send_own(kv):
        @pl.when(has_right)
        def _():
            hop(own_ref.at[s, kv], z, kv, True).start()

        @pl.when(has_left)
        def _():
            hop(own_ref.at[s, kv], z, kv, False).start()

    loads[0].wait()
    loads[1].start()
    put_keys(own_ref.at[s, 0], chosen(ck_raw, s))
    for load in loads[2:]:
        load.start()
    send_own(0)
    loads[1].wait()
    put_values(own_ref.at[s, 1], chosen(cv_raw, s))
    send_own(1)
    loads[2].wait()
    loads[3].wait()
    put_keys(new_ref.at[0], nk_raw[...])
    put_values(new_ref.at[1], nv_raw[...])
    put_keys(own_ref.at[1 - s, 0], chosen(ck_raw, 1 - s))
    put_values(own_ref.at[1 - s, 1], chosen(cv_raw, 1 - s))
    loads[4].wait()
    for part in range(rows // BLK):
        ordered = jnp.dot(sort_q[...], q_raw[part * wide:(part + 1) * wide],
                          preferred_element_type=jnp.float32).astype(jnp.bfloat16)
        for h in range(heads):
            q_ref[h, part * BLK:(part + 1) * BLK] = ordered[h * BLK:(h + 1) * BLK]

    def listed(slot):
        count = cnt_ref[0, 0]
        width = vl_ref.shape[1]
        if width <= 8:
            hit = jnp.int32(0)
            for i in range(width):
                hit = hit | jnp.where((vl_ref[0, i] == slot) & (i < count), 1, 0)
            return hit

        def one(i, hit):
            return hit | jnp.where((vl_ref[0, i] == slot) & (i < count), 1, 0)

        return lax.fori_loop(0, width, one, jnp.int32(0))

    def score(keys, q):
        return lax.dot_general(keys, q, (((1,), (1,)), ((), ())),
                               preferred_element_type=jnp.float32)

    def take_keys(side, blocks, first=False):
        for h in range(heads):
            q = q_ref[h]
            raw = []
            tops = []
            for keys, seen in blocks:
                scores = score(keys[h], q)
                if seen is None:
                    key_id = lax.broadcasted_iota(jnp.int32, scores.shape, 0)
                    row_id = lax.broadcasted_iota(jnp.int32, scores.shape, 1) // groups
                    scores = jnp.where(key_id <= row_id, scores, -jnp.inf)
                top = jnp.max(scores, axis=0, keepdims=True)
                if seen is not None:
                    top = jnp.where(seen > 0, top, -jnp.inf)
                raw.append(scores)
                tops.append(top)
            high = functools.reduce(jnp.maximum, tops)
            if not first:
                old = peak[h]
                high = jnp.maximum(old, high)
                factor = jnp.exp2((old - high) * c)
                fade[side, h] = factor
            peak[h] = high
            sums = []
            for i, ((_, seen), scores) in enumerate(zip(blocks, raw)):
                base = high if seen is None else jnp.where(seen > 0, high, jnp.inf)
                weights = jnp.exp2((scores - base) * c)
                sums.append(jnp.sum(weights, axis=0, keepdims=True))
                rounded[side, h, i * BLK:(i + 1) * BLK] = weights.astype(jnp.bfloat16)
            add = sum(sums[1:], sums[0])
            total[h] = add if first else total[h] * fade[side, h] + add

    def take_values(side, blocks, first=False):
        depth = len(blocks) * BLK
        for h in range(heads):
            values = jnp.concatenate([values[h] for values in blocks], 1)
            add = jnp.dot(values, rounded[side, h, :depth], preferred_element_type=jnp.float32)
            acc[h] = add if first else acc[h] * fade[side, h] + add

    take_keys(0, [(new_ref.at[0], None)]
              + [(own_ref.at[b, 0], listed(2 * z + b)) for b in range(2)], first=True)
    take_values(0, [new_ref.at[1]] + [own_ref.at[b, 1] for b in range(2)], first=True)

    @pl.when(has_left)
    def _():
        slash_hop().wait_recv()
        slash_sib(s).start()

    def arrive(src, kv, right):
        hop(own_ref.at[s, kv], src, kv, right).wait_recv()

        @pl.when(has_right if right else has_left)
        def _():
            hop(pool.at[src, s, kv], src, kv, right).start()

        sib(src, kv).start()

    def step(d, carry):
        sides = ((z + d, z + d < n, False), (z - d, z - d >= 0, True))
        for kv in range(2):
            for src, there, right in sides:
                @pl.when(there)
                def _():
                    arrive(src, kv, right)

            for side, (src, there, right) in enumerate(sides):
                @pl.when(there)
                def _():
                    sib_in(src, kv).wait_recv()
                    if kv == 0:
                        take_keys(side, [(pool.at[src, b, 0], listed(2 * src + b))
                                         for b in range(2)])
                    else:
                        take_values(side, [pool.at[src, b, 1] for b in range(2)])

        @pl.when((d == 1) & has_left)
        def _():
            slash_sib(1 - s).wait_recv()
            put_keys(slash.at[0], slash_raw[0])
            put_values(slash.at[1], slash_raw[1])
            back = jnp.int32(0)
            for i in range(sl_ref.shape[1]):
                back = back | jnp.where((sl_ref[0, i] == 1) & (i < cnt_ref[0, 1]), 1, 0)
            take_keys(0, [(slash.at[0], back)])
            take_values(0, [slash.at[1]])

        return carry

    lax.fori_loop(1, n, step, 0)

    for part in range(rows // BLK):
        lanes = slice(part * BLK, (part + 1) * BLK)
        done = jnp.concatenate(
            [(acc[h, :, lanes] / total[h, :, lanes]).astype(jnp.bfloat16) for h in range(heads)], 1)
        o_ref[part * wide:(part + 1) * wide] = lax.dot_general(
            sort_q[...], done, (((0,), (1,)), ((), ())),
            preferred_element_type=jnp.float32).astype(o_ref.dtype)

    def drain(src, carry):
        for kv in range(2):
            @pl.when(has_right & (src <= z))
            def _():
                hop(own_ref.at[s, kv], src, kv, True).wait_send()

            @pl.when(has_left & (src >= z))
            def _():
                hop(own_ref.at[s, kv], src, kv, False).wait_send()

            @pl.when(src != z)
            def _():
                sib(src, kv).wait_send()
        return carry

    lax.fori_loop(0, n, drain, 0)

    @pl.when(has_right)
    def _():
        slash_hop().wait_send()

    @pl.when(has_left)
    def _():
        slash_sib(s).wait_send()

BITS = 5
PACK = 6
OWN, GUEST, ALONE = 4, 5, 6
IDLE = (6, 4 * GUEST)
GUESTS = 1


def plan(heads):
    def kv(src, h):
        return (1, src * 4 + h)

    def unit(slot, src, h, wait=True):
        return (slot + (8 if wait else 0), src * 4 + h)

    def mine(h, src):
        return unit(h, src, h)

    def early(z):
        return [(None, unit(h, z, h, False)) for h in range(heads)]

    def build(steps):
        out, before = [], None
        for recv, now, *more in steps + [(None, None)]:
            busy = now is not None or before is not None
            code = now if now is not None else IDLE
            out.append((recv or (0, 0)) + code + (int(busy) | sum(more),))
            before = now
        return out

    quest, slash = (2, 0), (3, 0)

    def local(h, src=OWN):
        return unit(h, src, h, src == OWN and h == 0)

    zero = early(0) + [(None, local(h, ALONE)) for h in range(heads)]
    late = None
    for src in (1, 2, 3):
        for h in range(heads - GUESTS):
            zero.append((kv(src, h), late))
            late = mine(h, src)
    zero.append((None, late))

    one = early(1) + [
        (kv(2, 0), None), (kv(0, 0), mine(0, 2)), (kv(2, 1), mine(0, 0)), (kv(0, 3), mine(1, 2)),
        (kv(2, 2), mine(3, 0)), (kv(0, 1), mine(2, 2), 4), (kv(2, 3), mine(1, 0)), (kv(0, 2), mine(3, 2), 8),
        (quest, unit(4, 2, 3, False)), (kv(3, 0), unit(4, 1, 3, False)), (kv(3, 3), mine(2, 0)),
        (kv(3, 1), mine(0, 3)), (None, unit(4, 3, 3)),
        (kv(3, 2), unit(3, 3, 3, False), 2), (slash, mine(1, 3)), (None, local(0)), (None, local(1)),
        (None, local(2)), (None, local(3)), (None, mine(2, 3))]

    two = early(2) + [
        (kv(3, 0), None), (kv(1, 0), mine(0, 3)), (kv(3, 3), mine(0, 1)), (kv(1, 3), mine(3, 3)),
        (kv(1, 1), mine(3, 1)), (kv(0, 0), mine(1, 1)), (quest, mine(0, 0)), (kv(3, 1), unit(4, 2, 3, False)),
        (kv(0, 3), unit(4, GUEST, 3, False)), (kv(3, 2), unit(4, 1, 3, False)), (None, mine(1, 3)),
        (kv(0, 1), unit(4, 0, 3)), (kv(1, 2), unit(3, 0, 3, False)), (None, mine(2, 3)), (None, mine(1, 0)),
        (kv(0, 2), mine(2, 1), 2), (None, mine(2, 0)), (slash, None), (None, local(0)), (None, local(1)),
        (None, local(2)), (None, local(3))]

    three = early(3) + [
        (None, local(3, ALONE)), (kv(2, 0), None), (slash, mine(0, 2)), (kv(2, 1), local(0)), (None, mine(1, 2)),
        (None, local(1)), (kv(2, 2), local(2)), (kv(1, 0), mine(2, 2)), (kv(1, 1), mine(0, 1)),
        (kv(0, 0), mine(1, 1)), (kv(0, 1), mine(0, 0)), (kv(1, 2), mine(1, 0)), (kv(0, 2), mine(2, 1)),
        (None, mine(2, 0))]
    return [build(role) for role in (zero, one, two, three)]


def chain(n, q_hbm, nk_hbm, nv_hbm, ck_hbm, cv_hbm, vp_ref, vl_ref, sl_ref, cnt_ref, o_ref,
          q_raw, nk_raw, nv_raw, ck_raw, cv_raw, q_ref, sort_kv, sort_q, ext,
          pool, acc, peak, total, mask, part_acc, part_stat, scores_a, scores_b, top_a, top_b, most,
          hop_send, hop_recv, sib_send, sib_recv, sl_sem, q_sem, part_sem, in_sem, ready):
    z = lax.axis_index("ctx")
    s = lax.axis_index("sub")
    heads = pool.shape[1]
    head_dim, rows = acc.shape[1:]
    groups = rows // BLK
    wide = heads * BLK
    last = n - 1
    stay = heads - GUESTS
    loads = [pltpu.make_async_copy(src, dst, in_sem.at[i]) for i, (src, dst) in enumerate(
        [(ck_hbm, ck_raw), (cv_hbm, cv_raw), (nk_hbm, nk_raw), (nv_hbm, nv_raw), (q_hbm, q_raw)])]
    loads[0].start()
    c = math.log2(math.e) / math.sqrt(head_dim)
    has_left = z > 0
    has_right = z < last
    sib_id = {"sub": 1 - s}
    inner = has_left & has_right
    host_id = {"ctx": jnp.where(z == 0, 1, last - 1)}
    guest_id = {"ctx": jnp.where(z == 1, 0, last)}

    barrier = pltpu.get_barrier_semaphore()
    pl.semaphore_signal(barrier, inc=1, device_id=sib_id, device_id_type=MESH)

    @pl.when(has_right)
    def _():
        pl.semaphore_signal(barrier, inc=1, device_id={"ctx": z + 1}, device_id_type=MESH)

    ids = lax.broadcasted_iota(jnp.int32, (wide, wide), 0)
    at = lax.broadcasted_iota(jnp.int32, (wide, wide), 1)
    sort_kv[...] = jnp.where(at == (ids % BLK) * heads + ids // BLK, 1.0, 0.0).astype(jnp.bfloat16)

    pl.semaphore_wait(barrier, 1 + has_left.astype(jnp.int32))

    @pl.when(has_left)
    def _():
        pl.semaphore_signal(ready, inc=1, device_id={"ctx": z - 1}, device_id_type=MESH)

    def put_keys(raw, put):
        ordered = jnp.dot(sort_kv[...], raw, preferred_element_type=jnp.float32).astype(jnp.bfloat16)
        for h in range(heads):
            put(h, ordered[h * BLK:(h + 1) * BLK])

    def put_values(raw, put):
        ordered = lax.dot_general(raw, sort_kv[...], (((0,), (1,)), ((), ())),
                                  preferred_element_type=jnp.float32).astype(jnp.bfloat16)
        for h in range(heads):
            put(h, ordered[:, h * BLK:(h + 1) * BLK])

    def put_pool(b, kv):
        def put(h, block):
            pool[z, h, b, kv] = block
        return put

    def put_new(kv):
        def put(h, block):
            pool[OWN, h, 0, kv] = block
            pool[GUEST, h, 0, kv] = block
            pool[GUEST, h, 1, kv] = jnp.zeros_like(block)
        return put

    def hop(src, h, right):
        return pltpu.make_async_remote_copy(
            src_ref=pool.at[src, h, s], dst_ref=pool.at[src, h, s],
            send_sem=hop_send.at[src, h, int(right)], recv_sem=hop_recv.at[src, h],
            device_id={"ctx": z + 1 if right else z - 1}, device_id_type=MESH)

    def first_hop(h, kv, right):
        return pltpu.make_async_remote_copy(
            src_ref=pool.at[z, h, s, kv], dst_ref=pool.at[z, h, s, kv],
            send_sem=hop_send.at[z, h, int(right)], recv_sem=hop_recv.at[z, h],
            device_id={"ctx": z + 1 if right else z - 1}, device_id_type=MESH)

    def sib(src, h, part):
        return pltpu.make_async_remote_copy(
            src_ref=pool.at[src, h, part], dst_ref=pool.at[src, h, part],
            send_sem=sib_send.at[src, h], recv_sem=sib_recv.at[src, h],
            device_id=sib_id, device_id_type=MESH)

    def slash_hop(count):
        return pltpu.make_async_remote_copy(
            src_ref=pool.at[OWN, pl.ds(0, count), 0, s], dst_ref=pool.at[OWN, pl.ds(0, count), 1, s],
            send_sem=sl_sem.at[0], recv_sem=sl_sem.at[1],
            device_id={"ctx": z + 1}, device_id_type=MESH)

    def slash_sib(count, part):
        block = pool.at[OWN, pl.ds(0, count), 1, part]
        return pltpu.make_async_remote_copy(
            src_ref=block, dst_ref=block,
            send_sem=sl_sem.at[2], recv_sem=sl_sem.at[3],
            device_id=sib_id, device_id_type=MESH)

    def guest_q(g):
        return pltpu.make_async_remote_copy(
            src_ref=q_ref.at[stay + g, pl.ds(0, head_dim)], dst_ref=q_ref.at[heads + g, pl.ds(0, head_dim)],
            send_sem=q_sem.at[0, g], recv_sem=q_sem.at[1, g],
            device_id=host_id, device_id_type=MESH)

    def guest_mask():
        return pltpu.make_async_remote_copy(
            src_ref=mask.at[0], dst_ref=mask.at[1],
            send_sem=q_sem.at[0, GUESTS], recv_sem=q_sem.at[1, GUESTS],
            device_id=host_id, device_id_type=MESH)

    def guest_part(g):
        return [pltpu.make_async_remote_copy(
            src_ref=ref.at[g], dst_ref=ref.at[g],
            send_sem=part_sem.at[0, g, i], recv_sem=part_sem.at[1, g, i],
            device_id=guest_id, device_id_type=MESH)
            for i, ref in enumerate((part_acc, part_stat))]

    def leftward(kv):
        @pl.when(inner)
        def _():
            for h in range(stay):
                first_hop(h, kv, False).start()

        @pl.when(z == 2)
        def _():
            for h in range(stay, heads):
                first_hop(h, kv, False).start()

        @pl.when(z == last)
        def _():
            for h in (0, 3):
                first_hop(h, kv, False).start()

    loads[0].wait()
    loads[1].start()
    put_keys(ck_raw[vp_ref[s]], put_pool(s, 0))
    leftward(0)
    for load in loads[2:]:
        load.start()
    loads[1].wait()
    put_values(cv_raw[vp_ref[s]], put_pool(s, 1))
    leftward(1)

    @pl.when(has_right)
    def _():
        pl.semaphore_wait(ready, 1)

    @pl.when(z == 0)
    def _():
        for h in (0, 3, 1, 2):
            for kv in range(2):
                first_hop(h, kv, True).start()

    @pl.when(z == 1)
    def _():
        for h in (0, 3, 1):
            for kv in range(2):
                first_hop(h, kv, True).start()

    @pl.when(z == 2)
    def _():
        for kv in range(2):
            first_hop(0, kv, True).start()

    loads[2].wait()
    loads[3].wait()
    put_keys(nk_raw[...], put_new(0))
    put_values(nv_raw[...], put_new(1))

    @pl.when(z == 2)
    def _():
        slash_hop(stay).start()
        for h in range(1, stay):
            for kv in range(2):
                first_hop(h, kv, True).start()

    token = (ids % BLK) // groups
    sort_q[...] = jnp.where(at == (token * heads + ids // BLK) * groups + ids % groups,
                            1.0, 0.0).astype(jnp.bfloat16)
    loads[4].wait()
    for part in range(rows // BLK):
        ordered = lax.dot_general(q_raw[part * wide:(part + 1) * wide], sort_q[...], (((0,), (1,)), ((), ())),
                                  preferred_element_type=jnp.float32).astype(jnp.bfloat16)
        for h in range(heads):
            q_ref[h, 0:head_dim, part * BLK:(part + 1) * BLK] = ordered[:, h * BLK:(h + 1) * BLK]

    def unseen(hit):
        return jnp.full((1, BLK), jnp.where(hit > 0, 0.0, jnp.inf), jnp.float32)

    for slot in range(2 * n):
        hit = jnp.int32(0)
        for i in range(vl_ref.shape[1]):
            hit = hit | jnp.where((vl_ref[0, i] == slot) & (i < cnt_ref[0, 0]), 1, 0)
        mask[0, slot:slot + 1] = unseen(hit)
    hit = jnp.int32(0)
    for i in range(sl_ref.shape[1]):
        hit = hit | jnp.where((sl_ref[0, i] == 1) & (i < cnt_ref[0, 1]), 1, 0)
    mask[0, 2 * OWN:2 * OWN + 2] = jnp.concatenate([jnp.zeros((1, BLK), jnp.float32), unseen(hit)], 0)
    mask[0, 2 * GUEST:2 * GUEST + 2] = jnp.concatenate([unseen(hit), jnp.full((1, BLK), jnp.inf, jnp.float32)], 0)
    mask[0, 2 * ALONE:2 * ALONE + 2] = jnp.concatenate(
        [jnp.zeros((1, BLK), jnp.float32), jnp.full((1, BLK), jnp.inf, jnp.float32)], 0)

    @pl.when((z == 0) | (z == last))
    def _():
        for g in range(GUESTS):
            guest_q(g).start()
        guest_mask().start()

    @pl.when(z == 0)
    def _():
        slash_hop(heads).start()

    @pl.when(z == last)
    def _():
        for h in (1, 2):
            for kv in range(2):
                first_hop(h, kv, False).start()

    put_keys(ck_raw[vp_ref[1 - s]], put_pool(1 - s, 0))
    put_values(cv_raw[vp_ref[1 - s]], put_pool(1 - s, 1))

    key_id = lax.broadcasted_iota(jnp.int32, (BLK, rows), 0)
    row_id = lax.broadcasted_iota(jnp.int32, (BLK, rows), 1) // groups
    later = jnp.where(key_id > row_id, -1e30, 0.0).astype(jnp.bfloat16)
    slots = acc.shape[0]
    for slot in range(slots):
        q_ref[slot, head_dim:] = later if slot < heads else jnp.zeros_like(later)
        acc[slot] = jnp.zeros_like(acc[slot])
        total[slot] = jnp.zeros_like(total[slot])
        peak[slot] = jnp.full_like(peak[slot], -1e30)
    q_ref[slots - 1, 0:head_dim] = jnp.zeros_like(later)
    one_at = lax.broadcasted_iota(jnp.int32, (BLK, BLK), 0) == lax.broadcasted_iota(jnp.int32, (BLK, BLK), 1)
    ext[0] = jnp.zeros((BLK, BLK), jnp.bfloat16)
    ext[1] = jnp.where(one_at, 1.0, 0.0).astype(jnp.bfloat16)
    scores_b[...] = jnp.zeros_like(scores_b)
    top_b[...] = jnp.zeros_like(top_b)

    def spread(row):
        return jnp.concatenate([row] * groups, 1)

    def place(src):
        return src - src // ALONE

    def hidden(slot, src, b):
        return spread(mask[(slot // heads) % 2 * (1 - slot // (slots - 1)), pl.ds(2 * src + b, 1)])

    def ahead(unit, scores, top):
        slot, src, h = unit
        q = q_ref[slot]
        high = None
        for b in range(2):
            causal = (src // OWN) * (1 - src % 2) if b == 0 else 0
            keys = jnp.concatenate([pool[place(src), h, b, 0], ext[causal]], 1)
            found = jnp.dot(keys, q, preferred_element_type=jnp.float32)
            scores[b * BLK:(b + 1) * BLK] = found
            part = jnp.max(found, axis=0, keepdims=True) - hidden(slot, src, b)
            high = part if high is None else jnp.maximum(high, part)
        top[...] = high

    def behind(unit, scores, top):
        slot, src, h = unit
        old = peak[slot]
        high = jnp.maximum(old, top[...])
        factor = jnp.exp2((old - high) * c)
        peak[slot] = high
        weights = [jnp.exp2((scores[b * BLK:(b + 1) * BLK] - (high + hidden(slot, src, b))) * c)
                   .astype(jnp.bfloat16) for b in range(2)]
        values = jnp.concatenate([pool[place(src), h, b, 1] for b in range(2)], 1)
        values = jnp.concatenate([values, jnp.ones((16, 2 * BLK), jnp.bfloat16)], 0)
        add = jnp.dot(values, jnp.concatenate(weights, 0), preferred_element_type=jnp.float32)
        acc[slot] = acc[slot] * factor + add[:head_dim]
        total[slot] = total[slot] * factor + add[head_dim:head_dim + 1]

    roles = plan(heads)
    steps = max(len(role) for role in roles)
    steps += steps % 2
    roles = [role + [(0, 0) + IDLE + (0,)] * (steps - len(role)) for role in roles]

    def by_role(values):
        out = jnp.int32(values[-1])
        for i in reversed(range(len(values) - 1)):
            out = jnp.where(z == i, jnp.int32(values[i]), out)
        return out

    words = [[by_role([sum(step[field] << (BITS * i) for i, step in enumerate(role[start:start + PACK]))
                       for role in roles]) for start in range(0, steps, PACK)] for field in range(5)]

    def step(t, before, bufs, old_bufs):
        def look(field):
            word = words[field][-1]
            for i in reversed(range(len(words[field]) - 1)):
                word = jnp.where(t // PACK == i, words[field][i], word)
            return lax.shift_right_logical(word, BITS * (t % PACK)) & (2 ** BITS - 1)

        kind, message, code, block, flags = [look(field) for field in range(5)]
        src, h = message // 4, message % 4

        @pl.when(kind == 1)
        def _():
            hop(src, h, True).wait_recv()

            @pl.when((src > z) & ((z > 1) | ((z == 1) & (h < stay))))
            def _():
                hop(src, h, False).start()

            @pl.when((src < z) & ((z < last - 1) | ((z == last - 1) & (h < stay))))
            def _():
                hop(src, h, True).start()

            sib(src, h, s).start()

        @pl.when((flags // 4) % 2 == 1)
        def _():
            for kv in range(2):
                first_hop(2, kv, True).start()

        @pl.when(flags // 8 == 1)
        def _():
            slash_hop(heads).start()

        @pl.when(kind == 2)
        def _():
            guest_mask().wait_recv()
            for g in range(GUESTS):
                guest_q(g).wait_recv()

        @pl.when((kind == 3) & has_right)
        def _():
            slash_hop(heads).wait_recv()
            slash_sib(heads, s).start()

        @pl.when((kind == 3) & (z == last))
        def _():
            slash_hop(stay).wait_recv()
            slash_sib(stay, s).start()

        unit = (code % 8, block // 4, block % 4)

        @pl.when((code > 7) & (unit[1] < OWN))
        def _():
            sib(unit[1], unit[2], 1 - s).wait_recv()

        @pl.when((code > 7) & (unit[1] == OWN) & has_right)
        def _():
            slash_sib(heads, 1 - s).wait_recv()

        @pl.when((code > 7) & (unit[1] == OWN) & (z == last))
        def _():
            slash_sib(stay, 1 - s).wait_recv()

        @pl.when(flags % 2 == 1)
        def _():
            ahead(unit, *bufs)
            behind(before, *old_bufs)

        @pl.when((flags // 2) % 2 == 1)
        def _():
            g = 0
            part_acc[g] = acc[heads + g].astype(jnp.bfloat16)
            part_stat[g, 0:1] = peak[heads + g]
            part_stat[g, 1:2] = total[heads + g]
            for copy in guest_part(g):
                copy.start()

        return unit

    def two_steps(i, before):
        mid = step(2 * i, before, (scores_a, top_a), (scores_b, top_b))
        return step(2 * i + 1, mid, (scores_b, top_b), (scores_a, top_a))

    lengths = [max(t for t, step in enumerate(role) if step[0] or step[4]) + 1 for role in roles]
    idle = (jnp.int32(IDLE[0]), jnp.int32(GUEST), jnp.int32(0))
    lax.fori_loop(0, by_role([(length + 1) // 2 for length in lengths]), two_steps, idle)

    def ordered(part, those):
        lanes = slice(part * BLK, (part + 1) * BLK)
        done = jnp.concatenate(
            [(acc[h, :, lanes] / total[h, :, lanes]).astype(jnp.bfloat16) for h in those], 1)
        return lax.dot_general(sort_q[those.start * BLK:those.stop * BLK], done, (((0,), (1,)), ((), ())),
                               preferred_element_type=jnp.float32)

    for part in range(rows // BLK):
        most[part * wide:(part + 1) * wide] = ordered(part, range(stay)).astype(o_ref.dtype)

    @pl.when((z == 0) | (z == last))
    def _():
        for g in range(GUESTS):
            for copy in guest_part(g):
                copy.wait_recv()
            slot = stay + g
            old, new = peak[slot], part_stat[g, 0:1]
            high = jnp.maximum(old, new)
            mine, theirs = jnp.exp2((old - high) * c), jnp.exp2((new - high) * c)
            acc[slot] = acc[slot] * mine + part_acc[g].astype(jnp.float32) * theirs
            total[slot] = total[slot] * mine + part_stat[g, 1:2] * theirs

    for part in range(rows // BLK):
        lines = slice(part * wide, (part + 1) * wide)
        o_ref[lines] = most[lines] + ordered(part, range(stay, heads)).astype(o_ref.dtype)

    def drain(i, carry):
        src, h = i // heads, i % heads

        @pl.when((src <= z) & (z < last) & ((z < last - 1) | (h < stay)))
        def _():
            hop(src, h, True).wait_send()

        @pl.when((src >= z) & ((z > 1) | ((z == 1) & (h < stay))))
        def _():
            hop(src, h, False).wait_send()

        @pl.when((src != z) & (inner | (h < stay)))
        def _():
            sib(src, h, s).wait_send()
        return carry

    lax.fori_loop(0, n * heads, drain, 0)

    @pl.when(z < last - 1)
    def _():
        slash_hop(heads).wait_send()

    @pl.when(z == last - 1)
    def _():
        slash_hop(stay).wait_send()

    @pl.when(inner)
    def _():
        slash_sib(heads, s).wait_send()
        for g in range(GUESTS):
            for copy in guest_part(g):
                copy.wait_send()

    @pl.when(z == last)
    def _():
        slash_sib(stay, s).wait_send()

    @pl.when((z == 0) | (z == last))
    def _():
        guest_mask().wait_send()
        for g in range(GUESTS):
            guest_q(g).wait_send()


def store(o_vmem, o_hbm, sem):
    copies = sem.shape[0]
    rows = o_vmem.shape[0] // copies
    for i in range(copies):
        lines = pl.ds(i * rows, rows)
        pltpu.make_async_copy(o_vmem.at[lines], o_hbm.at[lines], sem.at[i]).start()
    for i in range(copies):
        lines = pl.ds(i * rows, rows)
        pltpu.make_async_copy(o_vmem.at[lines], o_hbm.at[lines], sem.at[i]).wait()


def chain_call(n, q, nk, nv, ck, cv, tables, heads, rows, head_dim):
    def vmem(*shape):
        return pltpu.VMEM(shape, jnp.bfloat16)

    def wide_vmem(*shape):
        return pltpu.VMEM(shape, jnp.float32)

    hbm = pl.BlockSpec(memory_space=pltpu.HBM)
    smem = pl.BlockSpec(memory_space=pltpu.SMEM)
    in_vmem = pl.BlockSpec(memory_space=pltpu.VMEM)
    dma = pltpu.SemaphoreType.DMA
    cached, wide = ck.shape[:2]
    slots = 7
    out = pl.pallas_call(
        functools.partial(chain, n),
        out_shape=pltpu.VMEM((heads * rows, head_dim), jnp.bfloat16),
        in_specs=[hbm] * 5 + [smem] * 4,
        out_specs=in_vmem,
        scratch_shapes=[
            vmem(heads * rows, head_dim), vmem(wide, head_dim), vmem(wide, head_dim),
            vmem(cached, wide, head_dim), vmem(cached, wide, head_dim),
            vmem(slots, 2 * head_dim, rows), vmem(wide, wide), vmem(wide, wide), vmem(2, BLK, BLK),
            vmem(n + 2, heads, 2, 2, BLK, head_dim),
            wide_vmem(slots, head_dim, rows), wide_vmem(slots, 1, rows), wide_vmem(slots, 1, rows),
            wide_vmem(2, 16, BLK), vmem(GUESTS, head_dim, rows), wide_vmem(GUESTS, 8, rows),
            wide_vmem(2 * BLK, rows), wide_vmem(2 * BLK, rows), wide_vmem(1, rows), wide_vmem(1, rows),
            vmem(heads * rows, head_dim),
            dma((n, heads, 2)), dma((n, heads)), dma((n, heads)), dma((n, heads)), dma((4,)),
            dma((2, GUESTS + 1)), dma((2, GUESTS, 2)), dma((5,)), pltpu.SemaphoreType.REGULAR,
        ],
        compiler_params=pltpu.CompilerParams(
            collective_id=0, has_side_effects=True, vmem_limit_bytes=60 * 2**20),
    )(*[pltpu.with_memory_space_constraint(x, pltpu.HBM) for x in (q, nk, nv, ck, cv)], *tables)
    return pl.pallas_call(
        store,
        out_shape=jax.ShapeDtypeStruct(out.shape, out.dtype),
        in_specs=[in_vmem],
        out_specs=hbm,
        scratch_shapes=[dma((4,))],
        compiler_params=pltpu.CompilerParams(vmem_limit_bytes=2**20),
    )(out)


def shards(n, queries, new_keys, new_values, cache_keys, cache_values,
           vertical_pool, vertical_lists, slash_lists, list_counts):
    tokens, heads, groups, head_dim = queries.shape
    rows = tokens * groups
    picked = vertical_pool.shape[0]

    def flat(x):
        return x.reshape(-1, head_dim)

    def vmem(*shape):
        return pltpu.VMEM(shape, jnp.bfloat16)

    hbm = pl.BlockSpec(memory_space=pltpu.HBM)
    smem = pl.BlockSpec(memory_space=pltpu.SMEM)
    dma = pltpu.SemaphoreType.DMA
    wide = heads * BLK
    cached = cache_keys.shape[0] // BLK
    if n == 4 and heads == 4 and picked == 2:
        out = chain_call(n, flat(queries), flat(new_keys), flat(new_values),
                         cache_keys.reshape(cached, wide, head_dim), cache_values.reshape(cached, wide, head_dim),
                         (vertical_pool, vertical_lists, slash_lists, list_counts), heads, rows, head_dim)
        return out.reshape(tokens, heads, groups, head_dim)
    out = pl.pallas_call(
        functools.partial(attend, n),
        out_shape=jax.ShapeDtypeStruct((tokens * heads * groups, head_dim), jnp.bfloat16),
        in_specs=[hbm] * 5 + [smem] * 4,
        out_specs=pl.BlockSpec(memory_space=pltpu.VMEM),
        scratch_shapes=[
            vmem(heads * rows, head_dim), vmem(wide, head_dim), vmem(wide, head_dim),
            vmem(cached, wide, head_dim), vmem(cached, wide, head_dim),
            vmem(heads, rows, head_dim), vmem(picked, 2, heads, BLK, head_dim),
            vmem(2, heads, BLK, head_dim), vmem(wide, wide), vmem(wide, wide),
            vmem(n, picked, 2, heads, BLK, head_dim),
            vmem(2, wide, head_dim), vmem(2, heads, BLK, head_dim),
            pltpu.VMEM((heads, head_dim, rows), jnp.float32),
            pltpu.VMEM((heads, 1, rows), jnp.float32),
            pltpu.VMEM((heads, 1, rows), jnp.float32),
            vmem(2, heads, 3 * BLK, rows), pltpu.VMEM((2, heads, 1, rows), jnp.float32),
            dma((n, 2, 2)), dma((n, 2)), dma((n, 2)), dma((n, 2)), dma((4,)), dma((5,)),
        ],
        compiler_params=pltpu.CompilerParams(
            collective_id=0, has_side_effects=True, vmem_limit_bytes=60 * 2**20),
    )(flat(queries), flat(new_keys), flat(new_values), cache_keys.reshape(cached, wide, head_dim),
      cache_values.reshape(cached, wide, head_dim),
      vertical_pool, vertical_lists, slash_lists, list_counts)
    return out.reshape(tokens, heads, groups, head_dim)


def solution(mesh):
    in_specs = (
        P(("grp", "ctx"), "kvh", "sub", None),
        P(("grp", "ctx"), "kvh", None),
        P(("grp", "ctx"), "kvh", None),
        P(("grp", "ctx"), "kvh", None),
        P(("grp", "ctx"), "kvh", None),
        P(("grp", "ctx")),
        P(("grp", "ctx"), None),
        P(("grp", "ctx"), None),
        P(("grp", "ctx"), None),
    )
    out_specs = P(("grp", "ctx"), "kvh", "sub", None)
    return jax.shard_map(functools.partial(shards, mesh.shape["ctx"]), mesh=mesh,
                         in_specs=in_specs, out_specs=out_specs, check_vma=False)
```

```python
import functools
import math

import jax
import jax.numpy as jnp
from jax import lax
from jax.experimental import pallas as pl
from jax.experimental.pallas import tpu as pltpu
from jax.sharding import PartitionSpec as P

BLK = 128
MESH = pl.DeviceIdType.MESH


def attend(n, q_hbm, nk_hbm, nv_hbm, ck_hbm, cv_hbm, vp_ref, vl_ref, sl_ref, cnt_ref, o_ref,
           q_raw, nk_raw, nv_raw, ck_raw, cv_raw, q_ref, own_ref, new_ref, sort_kv, sort_q,
           pool, slash_raw, slash, acc, peak, total, rounded, fade,
           hop_send, hop_recv, sib_send, sib_recv, sl_sem, in_sem):
    z = lax.axis_index("ctx")
    s = lax.axis_index("sub")
    heads, rows, head_dim = q_ref.shape
    groups = rows // BLK
    wide = heads * BLK
    loads = [pltpu.make_async_copy(src, dst, in_sem.at[i]) for i, (src, dst) in enumerate(
        [(ck_hbm, ck_raw), (cv_hbm, cv_raw), (nk_hbm, nk_raw), (nv_hbm, nv_raw), (q_hbm, q_raw)])]
    loads[0].start()
    c = math.log2(math.e) / math.sqrt(head_dim)
    has_left = z > 0
    has_right = z < n - 1
    sib_id = {"sub": 1 - s}

    barrier = pltpu.get_barrier_semaphore()
    pl.semaphore_signal(barrier, inc=1, device_id=sib_id, device_id_type=MESH)

    @pl.when(has_left)
    def _():
        pl.semaphore_signal(barrier, inc=1, device_id={"ctx": z - 1}, device_id_type=MESH)

    @pl.when(has_right)
    def _():
        pl.semaphore_signal(barrier, inc=1, device_id={"ctx": z + 1}, device_id_type=MESH)

    ids = lax.broadcasted_iota(jnp.int32, (wide, wide), 0)
    at = lax.broadcasted_iota(jnp.int32, (wide, wide), 1)
    sort_kv[...] = jnp.where(at == (ids % BLK) * heads + ids // BLK, 1.0, 0.0).astype(jnp.bfloat16)
    token = (ids % BLK) // groups
    sort_q[...] = jnp.where(at == (token * heads + ids // BLK) * groups + ids % groups,
                            1.0, 0.0).astype(jnp.bfloat16)

    def by_head(raw):
        return jnp.dot(sort_kv[...], raw, preferred_element_type=jnp.float32).astype(jnp.bfloat16)

    def put_keys(dst, raw):
        ordered = by_head(raw)
        for h in range(heads):
            dst[h] = ordered[h * BLK:(h + 1) * BLK]

    def put_values(dst, raw):
        ordered = lax.dot_general(raw, sort_kv[...], (((0,), (1,)), ((), ())),
                                  preferred_element_type=jnp.float32).astype(jnp.bfloat16)
        for h in range(heads):
            dst[h] = ordered[:, h * BLK:(h + 1) * BLK]

    def chosen(cache, b):
        return cache[vp_ref[b]]

    pl.semaphore_wait(barrier, 1 + has_left.astype(jnp.int32) + has_right.astype(jnp.int32))

    def hop(src_ref, src, kv, right):
        return pltpu.make_async_remote_copy(
            src_ref=src_ref, dst_ref=pool.at[src, s, kv],
            send_sem=hop_send.at[src, int(right), kv], recv_sem=hop_recv.at[src, kv],
            device_id={"ctx": z + 1 if right else z - 1}, device_id_type=MESH)

    def sib(src, kv):
        return pltpu.make_async_remote_copy(
            src_ref=pool.at[src, s, kv], dst_ref=pool.at[src, s, kv],
            send_sem=sib_send.at[src, kv], recv_sem=sib_recv.at[src, kv],
            device_id=sib_id, device_id_type=MESH)

    def sib_in(src, kv):
        return pltpu.make_async_remote_copy(
            src_ref=pool.at[src, 1 - s, kv], dst_ref=pool.at[src, 1 - s, kv],
            send_sem=sib_send.at[src, kv], recv_sem=sib_recv.at[src, kv],
            device_id=sib_id, device_id_type=MESH)

    def slash_hop(src_ref=nk_hbm):
        return pltpu.make_async_remote_copy(
            src_ref=src_ref, dst_ref=slash_raw.at[s],
            send_sem=sl_sem.at[0], recv_sem=sl_sem.at[1],
            device_id={"ctx": z + 1}, device_id_type=MESH)

    def slash_sib(part):
        return pltpu.make_async_remote_copy(
            src_ref=slash_raw.at[part], dst_ref=slash_raw.at[part],
            send_sem=sl_sem.at[2], recv_sem=sl_sem.at[3],
            device_id=sib_id, device_id_type=MESH)

    for part, src_ref in enumerate((nk_hbm, nv_hbm)):
        @pl.when(has_right & (s == part))
        def _():
            slash_hop(src_ref).start()

    def send_own(kv):
        @pl.when(has_right)
        def _():
            hop(own_ref.at[s, kv], z, kv, True).start()

        @pl.when(has_left)
        def _():
            hop(own_ref.at[s, kv], z, kv, False).start()

    loads[0].wait()
    loads[1].start()
    put_keys(own_ref.at[s, 0], chosen(ck_raw, s))
    for load in loads[2:]:
        load.start()
    send_own(0)
    loads[1].wait()
    put_values(own_ref.at[s, 1], chosen(cv_raw, s))
    send_own(1)
    loads[2].wait()
    loads[3].wait()
    put_keys(new_ref.at[0], nk_raw[...])
    put_values(new_ref.at[1], nv_raw[...])
    put_keys(own_ref.at[1 - s, 0], chosen(ck_raw, 1 - s))
    put_values(own_ref.at[1 - s, 1], chosen(cv_raw, 1 - s))
    loads[4].wait()
    for part in range(rows // BLK):
        ordered = jnp.dot(sort_q[...], q_raw[part * wide:(part + 1) * wide],
                          preferred_element_type=jnp.float32).astype(jnp.bfloat16)
        for h in range(heads):
            q_ref[h, part * BLK:(part + 1) * BLK] = ordered[h * BLK:(h + 1) * BLK]

    def listed(slot):
        count = cnt_ref[0, 0]
        width = vl_ref.shape[1]
        if width <= 8:
            hit = jnp.int32(0)
            for i in range(width):
                hit = hit | jnp.where((vl_ref[0, i] == slot) & (i < count), 1, 0)
            return hit

        def one(i, hit):
            return hit | jnp.where((vl_ref[0, i] == slot) & (i < count), 1, 0)

        return lax.fori_loop(0, width, one, jnp.int32(0))

    def score(keys, q):
        return lax.dot_general(keys, q, (((1,), (1,)), ((), ())),
                               preferred_element_type=jnp.float32)

    def take_keys(side, blocks, first=False):
        for h in range(heads):
            q = q_ref[h]
            raw = []
            tops = []
            for keys, seen in blocks:
                scores = score(keys[h], q)
                if seen is None:
                    key_id = lax.broadcasted_iota(jnp.int32, scores.shape, 0)
                    row_id = lax.broadcasted_iota(jnp.int32, scores.shape, 1) // groups
                    scores = jnp.where(key_id <= row_id, scores, -jnp.inf)
                top = jnp.max(scores, axis=0, keepdims=True)
                if seen is not None:
                    top = jnp.where(seen > 0, top, -jnp.inf)
                raw.append(scores)
                tops.append(top)
            high = functools.reduce(jnp.maximum, tops)
            if not first:
                old = peak[h]
                high = jnp.maximum(old, high)
                factor = jnp.exp2((old - high) * c)
                fade[side, h] = factor
            peak[h] = high
            sums = []
            for i, ((_, seen), scores) in enumerate(zip(blocks, raw)):
                base = high if seen is None else jnp.where(seen > 0, high, jnp.inf)
                weights = jnp.exp2((scores - base) * c)
                sums.append(jnp.sum(weights, axis=0, keepdims=True))
                rounded[side, h, i * BLK:(i + 1) * BLK] = weights.astype(jnp.bfloat16)
            add = sum(sums[1:], sums[0])
            total[h] = add if first else total[h] * fade[side, h] + add

    def take_values(side, blocks, first=False):
        depth = len(blocks) * BLK
        for h in range(heads):
            values = jnp.concatenate([values[h] for values in blocks], 1)
            add = jnp.dot(values, rounded[side, h, :depth], preferred_element_type=jnp.float32)
            acc[h] = add if first else acc[h] * fade[side, h] + add

    take_keys(0, [(new_ref.at[0], None)]
              + [(own_ref.at[b, 0], listed(2 * z + b)) for b in range(2)], first=True)
    take_values(0, [new_ref.at[1]] + [own_ref.at[b, 1] for b in range(2)], first=True)

    @pl.when(has_left)
    def _():
        slash_hop().wait_recv()
        slash_sib(s).start()

    def arrive(src, kv, right):
        hop(own_ref.at[s, kv], src, kv, right).wait_recv()

        @pl.when(has_right if right else has_left)
        def _():
            hop(pool.at[src, s, kv], src, kv, right).start()

        sib(src, kv).start()

    def step(d, carry):
        sides = ((z + d, z + d < n, False), (z - d, z - d >= 0, True))
        for kv in range(2):
            for src, there, right in sides:
                @pl.when(there)
                def _():
                    arrive(src, kv, right)

            for side, (src, there, right) in enumerate(sides):
                @pl.when(there)
                def _():
                    sib_in(src, kv).wait_recv()
                    if kv == 0:
                        take_keys(side, [(pool.at[src, b, 0], listed(2 * src + b))
                                         for b in range(2)])
                    else:
                        take_values(side, [pool.at[src, b, 1] for b in range(2)])

        @pl.when((d == 1) & has_left)
        def _():
            slash_sib(1 - s).wait_recv()
            put_keys(slash.at[0], slash_raw[0])
            put_values(slash.at[1], slash_raw[1])
            back = jnp.int32(0)
            for i in range(sl_ref.shape[1]):
                back = back | jnp.where((sl_ref[0, i] == 1) & (i < cnt_ref[0, 1]), 1, 0)
            take_keys(0, [(slash.at[0], back)])
            take_values(0, [slash.at[1]])

        return carry

    lax.fori_loop(1, n, step, 0)

    for part in range(rows // BLK):
        lanes = slice(part * BLK, (part + 1) * BLK)
        done = jnp.concatenate(
            [(acc[h, :, lanes] / total[h, :, lanes]).astype(jnp.bfloat16) for h in range(heads)], 1)
        o_ref[part * wide:(part + 1) * wide] = lax.dot_general(
            sort_q[...], done, (((0,), (1,)), ((), ())),
            preferred_element_type=jnp.float32).astype(o_ref.dtype)

    def drain(src, carry):
        for kv in range(2):
            @pl.when(has_right & (src <= z))
            def _():
                hop(own_ref.at[s, kv], src, kv, True).wait_send()

            @pl.when(has_left & (src >= z))
            def _():
                hop(own_ref.at[s, kv], src, kv, False).wait_send()

            @pl.when(src != z)
            def _():
                sib(src, kv).wait_send()
        return carry

    lax.fori_loop(0, n, drain, 0)

    @pl.when(has_right)
    def _():
        slash_hop().wait_send()

    @pl.when(has_left)
    def _():
        slash_sib(s).wait_send()

BITS = 5
PACK = 6
OWN, GUEST, ALONE = 4, 5, 6
IDLE = (6, 4 * GUEST)
GUESTS = 1


NONE = (-1, -1)
QUEST = (-2, 0)
SLASH = (-3, 0)


def plan(heads):
    zero = [(NONE, (0, 0), 0), (NONE, (0, ALONE), 0), (NONE, (1, 0), 0), ((1, 0), (1, ALONE), 0), (NONE, (2, 0), 0),
        (NONE, (2, ALONE), 0), ((1, 1), (0, 1), 0), (NONE, (3, 0), 0), (NONE, (3, ALONE), 0), ((1, 2), (1, 1), 0),
        (NONE, NONE, 0), ((1, 3), NONE, 0), (NONE, (2, 1), 0), (NONE, NONE, 0), (NONE, (3, 1), 0), ((2, 0), NONE, 0),
        ((2, 1), NONE, 0), (NONE, (0, 2), 0), (NONE, NONE, 0), (NONE, (1, 2), 0), ((2, 2), NONE, 0),
        ((2, 3), NONE, 0), (NONE, (2, 2), 0), (NONE, NONE, 0), (NONE, (3, 2), 0), ((3, 0), NONE, 0),
        ((3, 1), NONE, 0), (NONE, (0, 3), 0), (NONE, NONE, 0), (NONE, (1, 3), 0), ((3, 2), NONE, 0),
        ((3, 3), NONE, 0), (NONE, (2, 3), 0), (NONE, NONE, 16), (NONE, (3, 3), 0), (NONE, NONE, 0)]
    one = [((0, 0), (0, 1), 0), ((2, 0), (1, 1), 0), ((0, 3), (2, 1), 0), (NONE, (0, 0), 0), ((2, 1), (0, 2), 0),
        ((0, 1), (3, 0), 4), (NONE, (3, 1), 0), (NONE, (1, 2), 0), ((2, 2), (1, 0), 0), ((0, 2), NONE, 8),
        ((2, 3), NONE, 0), (NONE, (2, 2), 0), (NONE, (2, 0), 0), (NONE, NONE, 0), ((3, 0), (3, 2), 0),
        (SLASH, NONE, 0), ((3, 1), NONE, 0), (NONE, (0, 3), 0), (NONE, NONE, 0), (NONE, (0, OWN), 0),
        ((3, 2), (1, 3), 0), (NONE, (1, OWN), 0), (NONE, (2, OWN), 0), ((3, 3), (2, 3), 0), (NONE, (3, OWN), 16),
        (NONE, NONE, 0), (NONE, (3, 3), 0), (NONE, NONE, 0)]
    two = [((1, 0), (0, 2), 0), ((3, 0), (1, 2), 0), (NONE, (2, 2), 0), ((1, 3), (0, 1), 0), ((3, 1), (0, 3), 0),
        (NONE, (3, 2), 0), ((1, 1), (3, 1), 0), ((3, 2), (1, 3), 0), (NONE, NONE, 0), ((0, 0), (1, 1), 0),
        ((3, 3), (2, 3), 0), (NONE, NONE, 0), ((0, 3), (0, 0), 0), (NONE, (3, 3), 0), (NONE, NONE, 0),
        (NONE, (3, 0), 0), ((0, 1), NONE, 0), (QUEST, NONE, 0), (NONE, (4, 2), 0), ((1, 2), (4, GUEST), 0),
        (NONE, (4, 1), 0), (NONE, (4, 0), 0), (NONE, (1, 0), 0), ((0, 2), (2, 1), 2), (NONE, NONE, 0),
        (NONE, (2, 0), 0), (NONE, NONE, 0), (SLASH, NONE, 0), (NONE, (0, OWN), 0), (NONE, (1, OWN), 0),
        (NONE, (2, OWN), 0), (NONE, (3, OWN), 16), (NONE, NONE, 0)]
    three = [(NONE, (0, 3), 0), ((2, 0), (1, 3), 0), (NONE, (2, 3), 0), (NONE, (3, 3), 0), (NONE, (0, 2), 0),
        (SLASH, (3, ALONE), 0), (NONE, NONE, 0), (NONE, (0, OWN), 0), ((2, 1), (1, OWN), 0), (NONE, (2, OWN), 0),
        (NONE, NONE, 0), ((2, 2), (1, 2), 0), (NONE, NONE, 0), ((1, 0), NONE, 0), (NONE, (2, 2), 0), (NONE, NONE, 0),
        (NONE, (0, 1), 0), ((1, 1), NONE, 0), ((0, 0), NONE, 0), (NONE, (1, 1), 0), (NONE, NONE, 0),
        (NONE, (0, 0), 0), ((0, 1), NONE, 0), ((1, 2), NONE, 0), (NONE, (1, 0), 0), (NONE, NONE, 0),
        (NONE, (2, 1), 0), ((0, 2), NONE, 0), (NONE, (2, 0), 0), (NONE, NONE, 16)]

    def build(z, table):
        out, before, used = [], NONE, set()
        for recv, now, flags in table + [(NONE, NONE, 0)]:
            kind, message = (1, recv[0] * 4 + recv[1]) if recv[0] >= 0 else (-recv[0] if recv != NONE else 0, 0)
            slot, src = now
            h = slot if slot < heads else slot - GUESTS
            key = OWN if src == OWN else (src, h)
            first = now != NONE and key not in used and src not in (z, GUEST, ALONE)
            used.add(key)
            code = (slot + (8 if first else 0), src * 4 + h) if now != NONE else IDLE
            busy = now != NONE or before != NONE
            out.append((kind, message) + code + (int(busy) | flags,))
            before = now
        return out

    return [build(z, table) for z, table in enumerate((zero, one, two, three))]


def chain(n, q_hbm, nk_hbm, nv_hbm, ck_hbm, cv_hbm, vp_ref, vl_ref, sl_ref, cnt_ref, o_ref,
          q_raw, nk_raw, nv_raw, ck_raw, cv_raw, q_ref, sort_kv, sort_q, ext,
          pool, acc, peak, total, mask, part_acc, part_stat, scores_a, scores_b, top_a, top_b, most,
          hop_send, hop_recv, sib_send, sib_recv, sl_sem, q_sem, part_sem, in_sem, ready):
    z = lax.axis_index("ctx")
    s = lax.axis_index("sub")
    heads = pool.shape[1]
    head_dim, rows = acc.shape[1:]
    groups = rows // BLK
    wide = heads * BLK
    last = n - 1
    stay = heads - GUESTS
    loads = [pltpu.make_async_copy(src, dst, in_sem.at[i]) for i, (src, dst) in enumerate(
        [(ck_hbm, ck_raw), (cv_hbm, cv_raw), (nk_hbm, nk_raw), (nv_hbm, nv_raw), (q_hbm, q_raw)])]
    loads[0].start()
    loads[1].start()
    c = math.log2(math.e) / math.sqrt(head_dim)
    has_left = z > 0
    has_right = z < last
    sib_id = {"sub": 1 - s}
    inner = has_left & has_right

    barrier = pltpu.get_barrier_semaphore()
    pl.semaphore_signal(barrier, inc=1, device_id=sib_id, device_id_type=MESH)

    @pl.when(has_right)
    def _():
        pl.semaphore_signal(barrier, inc=1, device_id={"ctx": z + 1}, device_id_type=MESH)

    ids = lax.broadcasted_iota(jnp.int32, (wide, wide), 0)
    at = lax.broadcasted_iota(jnp.int32, (wide, wide), 1)
    sort_kv[...] = jnp.where(at == (ids % BLK) * heads + ids // BLK, 1.0, 0.0).astype(jnp.bfloat16)

    pl.semaphore_wait(barrier, 1 + has_left.astype(jnp.int32))

    @pl.when(has_left)
    def _():
        pl.semaphore_signal(ready, inc=1, device_id={"ctx": z - 1}, device_id_type=MESH)

    def put_keys(raw, put):
        ordered = jnp.dot(sort_kv[...], raw, preferred_element_type=jnp.float32).astype(jnp.bfloat16)
        for h in range(heads):
            put(h, ordered[h * BLK:(h + 1) * BLK])

    def put_values(raw, put):
        ordered = lax.dot_general(raw, sort_kv[...], (((0,), (1,)), ((), ())),
                                  preferred_element_type=jnp.float32).astype(jnp.bfloat16)
        for h in range(heads):
            put(h, ordered[:, h * BLK:(h + 1) * BLK])

    def put_pool(b, kv):
        def put(h, block):
            pool[z, h, b, kv] = block
        return put

    def put_new(kv):
        def put(h, block):
            pool[OWN, h, 0, kv] = block
            pool[GUEST, h, 0, kv] = block
            pool[GUEST, h, 1, kv] = jnp.zeros_like(block)
        return put

    def hop(src, h, right):
        return pltpu.make_async_remote_copy(
            src_ref=pool.at[src, h, s], dst_ref=pool.at[src, h, s],
            send_sem=hop_send.at[src, h, int(right)], recv_sem=hop_recv.at[src, h],
            device_id={"ctx": z + 1 if right else z - 1}, device_id_type=MESH)

    def first_hop(h, kv, right):
        return pltpu.make_async_remote_copy(
            src_ref=pool.at[z, h, s, kv], dst_ref=pool.at[z, h, s, kv],
            send_sem=hop_send.at[z, h, int(right)], recv_sem=hop_recv.at[z, h],
            device_id={"ctx": z + 1 if right else z - 1}, device_id_type=MESH)

    def sib(src, h, part):
        return pltpu.make_async_remote_copy(
            src_ref=pool.at[src, h, part], dst_ref=pool.at[src, h, part],
            send_sem=sib_send.at[src, h], recv_sem=sib_recv.at[src, h],
            device_id=sib_id, device_id_type=MESH)

    def slash_hop(count):
        return pltpu.make_async_remote_copy(
            src_ref=pool.at[OWN, pl.ds(0, count), 0, s], dst_ref=pool.at[OWN, pl.ds(0, count), 1, s],
            send_sem=sl_sem.at[0], recv_sem=sl_sem.at[1],
            device_id={"ctx": z + 1}, device_id_type=MESH)

    def slash_sib(count, part):
        block = pool.at[OWN, pl.ds(0, count), 1, part]
        return pltpu.make_async_remote_copy(
            src_ref=block, dst_ref=block,
            send_sem=sl_sem.at[2], recv_sem=sl_sem.at[3],
            device_id=sib_id, device_id_type=MESH)

    def guest_q(g):
        return pltpu.make_async_remote_copy(
            src_ref=q_ref.at[stay + g, pl.ds(0, head_dim)], dst_ref=q_ref.at[heads + g, pl.ds(0, head_dim)],
            send_sem=q_sem.at[0, g], recv_sem=q_sem.at[1, g],
            device_id={"ctx": z - 1}, device_id_type=MESH)

    def guest_mask():
        return pltpu.make_async_remote_copy(
            src_ref=mask.at[0], dst_ref=mask.at[1],
            send_sem=q_sem.at[0, GUESTS], recv_sem=q_sem.at[1, GUESTS],
            device_id={"ctx": z - 1}, device_id_type=MESH)

    def guest_part(g):
        return [pltpu.make_async_remote_copy(
            src_ref=ref.at[g], dst_ref=ref.at[g],
            send_sem=part_sem.at[0, g, i], recv_sem=part_sem.at[1, g, i],
            device_id={"ctx": z + 1}, device_id_type=MESH)
            for i, ref in enumerate((part_acc, part_stat))]

    def leftward(*blocks):
        @pl.when(has_left)
        def _():
            for h, kv in blocks:
                first_hop(h, kv, False).start()

    loads[0].wait()
    put_keys(ck_raw[vp_ref[s]], put_pool(s, 0))
    leftward((0, 0), (1, 0))
    for load in loads[2:]:
        load.start()
    loads[1].wait()
    put_values(cv_raw[vp_ref[s]], put_pool(s, 1))
    leftward((0, 1), (1, 1), *[(h, kv) for h in range(2, heads) for kv in range(2)])

    @pl.when(has_right)
    def _():
        pl.semaphore_wait(ready, 1)

    @pl.when(z == 0)
    def _():
        for h in (0, 3, 1, 2):
            for kv in range(2):
                first_hop(h, kv, True).start()

    @pl.when(z == 1)
    def _():
        for h in (0, 3, 1):
            for kv in range(2):
                first_hop(h, kv, True).start()

    @pl.when(z == 2)
    def _():
        for kv in range(2):
            first_hop(0, kv, True).start()

    loads[2].wait()
    loads[3].wait()
    put_keys(nk_raw[...], put_new(0))
    put_values(nv_raw[...], put_new(1))

    @pl.when(z == 2)
    def _():
        slash_hop(stay).start()
        for h in range(1, stay):
            for kv in range(2):
                first_hop(h, kv, True).start()

    token = (ids % BLK) // groups
    sort_q[...] = jnp.where(at == (token * heads + ids // BLK) * groups + ids % groups,
                            1.0, 0.0).astype(jnp.bfloat16)
    loads[4].wait()
    for part in range(rows // BLK):
        ordered = lax.dot_general(q_raw[part * wide:(part + 1) * wide], sort_q[...], (((0,), (1,)), ((), ())),
                                  preferred_element_type=jnp.float32).astype(jnp.bfloat16)
        for h in range(heads):
            q_ref[h, 0:head_dim, part * BLK:(part + 1) * BLK] = ordered[:, h * BLK:(h + 1) * BLK]

    def unseen(hit):
        return jnp.full((1, BLK), jnp.where(hit > 0, 0.0, jnp.inf), jnp.float32)

    for slot in range(2 * n):
        hit = jnp.int32(0)
        for i in range(vl_ref.shape[1]):
            hit = hit | jnp.where((vl_ref[0, i] == slot) & (i < cnt_ref[0, 0]), 1, 0)
        mask[0, slot:slot + 1] = unseen(hit)
    hit = jnp.int32(0)
    for i in range(sl_ref.shape[1]):
        hit = hit | jnp.where((sl_ref[0, i] == 1) & (i < cnt_ref[0, 1]), 1, 0)
    mask[0, 2 * OWN:2 * OWN + 2] = jnp.concatenate([jnp.zeros((1, BLK), jnp.float32), unseen(hit)], 0)
    mask[0, 2 * GUEST:2 * GUEST + 2] = jnp.concatenate([unseen(hit), jnp.full((1, BLK), jnp.inf, jnp.float32)], 0)
    mask[0, 2 * ALONE:2 * ALONE + 2] = jnp.concatenate(
        [jnp.zeros((1, BLK), jnp.float32), jnp.full((1, BLK), jnp.inf, jnp.float32)], 0)

    @pl.when(z == 0)
    def _():
        slash_hop(heads).start()

    @pl.when(z == last)
    def _():
        for g in range(GUESTS):
            guest_q(g).start()
        guest_mask().start()

    put_keys(ck_raw[vp_ref[1 - s]], put_pool(1 - s, 0))
    put_values(cv_raw[vp_ref[1 - s]], put_pool(1 - s, 1))

    key_id = lax.broadcasted_iota(jnp.int32, (BLK, rows), 0)
    row_id = lax.broadcasted_iota(jnp.int32, (BLK, rows), 1) // groups
    later = jnp.where(key_id > row_id, -1e30, 0.0).astype(jnp.bfloat16)
    slots = acc.shape[0]
    for slot in range(slots):
        q_ref[slot, head_dim:] = later if slot < heads else jnp.zeros_like(later)
        acc[slot] = jnp.zeros_like(acc[slot])
        total[slot] = jnp.zeros_like(total[slot])
        peak[slot] = jnp.full_like(peak[slot], -1e30)
    q_ref[slots - 1, 0:head_dim] = jnp.zeros_like(later)
    one_at = lax.broadcasted_iota(jnp.int32, (BLK, BLK), 0) == lax.broadcasted_iota(jnp.int32, (BLK, BLK), 1)
    ext[0] = jnp.zeros((BLK, BLK), jnp.bfloat16)
    ext[1] = jnp.where(one_at, 1.0, 0.0).astype(jnp.bfloat16)
    scores_b[...] = jnp.zeros_like(scores_b)
    top_b[...] = jnp.zeros_like(top_b)

    def spread(row):
        return jnp.concatenate([row] * groups, 1)

    def place(src):
        return src - src // ALONE

    def hidden(slot, src, b):
        return spread(mask[(slot // heads) % 2 * (1 - slot // (slots - 1)), pl.ds(2 * src + b, 1)])

    def ahead(unit, scores, top):
        slot, src, h = unit
        q = q_ref[slot]
        high = None
        for b in range(2):
            causal = (src // OWN) * (1 - src % 2) if b == 0 else 0
            keys = jnp.concatenate([pool[place(src), h, b, 0], ext[causal]], 1)
            found = jnp.dot(keys, q, preferred_element_type=jnp.float32)
            scores[b * BLK:(b + 1) * BLK] = found
            part = jnp.max(found, axis=0, keepdims=True) - hidden(slot, src, b)
            high = part if high is None else jnp.maximum(high, part)
        top[...] = high

    def behind(unit, scores, top):
        slot, src, h = unit
        old = peak[slot]
        high = jnp.maximum(old, top[...])
        factor = jnp.exp2((old - high) * c)
        peak[slot] = high
        weights = [jnp.exp2((scores[b * BLK:(b + 1) * BLK] - (high + hidden(slot, src, b))) * c)
                   .astype(jnp.bfloat16) for b in range(2)]
        values = jnp.concatenate([pool[place(src), h, b, 1] for b in range(2)], 1)
        values = jnp.concatenate([values, jnp.ones((16, 2 * BLK), jnp.bfloat16)], 0)
        add = jnp.dot(values, jnp.concatenate(weights, 0), preferred_element_type=jnp.float32)
        acc[slot] = acc[slot] * factor + add[:head_dim]
        total[slot] = total[slot] * factor + add[head_dim:head_dim + 1]

    def ordered(part, those):
        lanes = slice(part * BLK, (part + 1) * BLK)
        done = jnp.concatenate(
            [(acc[h, :, lanes] / total[h, :, lanes]).astype(jnp.bfloat16) for h in those], 1)
        return lax.dot_general(sort_q[those.start * BLK:those.stop * BLK], done, (((0,), (1,)), ((), ())),
                               preferred_element_type=jnp.float32)

    def drain():
        for index in range(n):
            right = heads if index < last - 1 else stay if index < last else 0

            @pl.when(z == index)
            def _():
                for src in range(n):
                    for h in range(heads):
                        if src <= index and h < right:
                            hop(src, h, True).wait_send()
                        if src >= index and index > 0:
                            hop(src, h, False).wait_send()
                        if src != index and (index < last or h < stay):
                            sib(src, h, s).wait_send()
                if right:
                    slash_hop(right).wait_send()
                if index > 0:
                    slash_sib(heads if index < last else stay, s).wait_send()
                if index == last:
                    guest_mask().wait_send()
                    for g in range(GUESTS):
                        guest_q(g).wait_send()

    roles = plan(heads)
    steps = max(len(role) for role in roles)
    steps += steps % 2
    roles = [role + [(0, 0) + IDLE + (0,)] * (steps - len(role)) for role in roles]

    def by_role(values):
        out = jnp.int32(values[-1])
        for i in reversed(range(len(values) - 1)):
            out = jnp.where(z == i, jnp.int32(values[i]), out)
        return out

    words = [[by_role([sum(step[field] << (BITS * i) for i, step in enumerate(role[start:start + PACK]))
                       for role in roles]) for start in range(0, steps, PACK)] for field in range(5)]

    def step(t, before, bufs, old_bufs):
        def look(field):
            word = words[field][-1]
            for i in reversed(range(len(words[field]) - 1)):
                word = jnp.where(t // PACK == i, words[field][i], word)
            return lax.shift_right_logical(word, BITS * (t % PACK)) & (2 ** BITS - 1)

        kind, message, code, block, flags = [look(field) for field in range(5)]
        src, h = message // 4, message % 4

        @pl.when(kind == 1)
        def _():
            hop(src, h, True).wait_recv()

            @pl.when((src > z) & has_left)
            def _():
                hop(src, h, False).start()

            @pl.when((src < z) & ((z < last - 1) | ((z == last - 1) & (h < stay))))
            def _():
                hop(src, h, True).start()

            sib(src, h, s).start()

        @pl.when((flags // 4) % 2 == 1)
        def _():
            for kv in range(2):
                first_hop(2, kv, True).start()

        @pl.when((flags // 8) % 2 == 1)
        def _():
            slash_hop(heads).start()

        @pl.when(kind == 2)
        def _():
            guest_mask().wait_recv()
            for g in range(GUESTS):
                guest_q(g).wait_recv()

        @pl.when((kind == 3) & has_right)
        def _():
            slash_hop(heads).wait_recv()
            slash_sib(heads, s).start()

        @pl.when((kind == 3) & (z == last))
        def _():
            slash_hop(stay).wait_recv()
            slash_sib(stay, s).start()

        unit = (code % 8, block // 4, block % 4)

        @pl.when((code > 7) & (unit[1] < OWN))
        def _():
            sib(unit[1], unit[2], 1 - s).wait_recv()

        @pl.when((code > 7) & (unit[1] == OWN) & has_right)
        def _():
            slash_sib(heads, 1 - s).wait_recv()

        @pl.when((code > 7) & (unit[1] == OWN) & (z == last))
        def _():
            slash_sib(stay, 1 - s).wait_recv()

        @pl.when(flags % 2 == 1)
        def _():
            ahead(unit, *bufs)
            behind(before, *old_bufs)

        @pl.when(flags // 16 == 1)
        def _():
            for part in range(rows // BLK):
                most[part * wide:(part + 1) * wide] = ordered(part, range(stay)).astype(o_ref.dtype)

        @pl.when((flags // 2) % 2 == 1)
        def _():
            g = 0
            part_acc[g] = acc[heads + g].astype(jnp.bfloat16)
            part_stat[g, 0:1] = peak[heads + g]
            part_stat[g, 1:2] = total[heads + g]
            for copy in guest_part(g):
                copy.start()

        return unit

    def two_steps(i, before):
        mid = step(2 * i, before, (scores_a, top_a), (scores_b, top_b))
        return step(2 * i + 1, mid, (scores_b, top_b), (scores_a, top_a))

    lengths = [max(t for t, step in enumerate(role) if step[0] or step[4]) + 1 for role in roles]
    idle = (jnp.int32(IDLE[0]), jnp.int32(GUEST), jnp.int32(0))
    lax.fori_loop(0, by_role([(length + 1) // 2 for length in lengths]), two_steps, idle)

    drain()

    @pl.when(z == last)
    def _():
        for g in range(GUESTS):
            for copy in guest_part(g):
                copy.wait_recv()
            slot = stay + g
            old, new = peak[slot], part_stat[g, 0:1]
            high = jnp.maximum(old, new)
            mine, theirs = jnp.exp2((old - high) * c), jnp.exp2((new - high) * c)
            acc[slot] = acc[slot] * mine + part_acc[g].astype(jnp.float32) * theirs
            total[slot] = total[slot] * mine + part_stat[g, 1:2] * theirs

    for part in range(rows // BLK):
        lines = slice(part * wide, (part + 1) * wide)
        o_ref[lines] = most[lines] + ordered(part, range(stay, heads)).astype(o_ref.dtype)

    @pl.when(z == last - 1)
    def _():
        for g in range(GUESTS):
            for copy in guest_part(g):
                copy.wait_send()


def store(o_vmem, o_hbm, sem):
    copies = sem.shape[0]
    rows = o_vmem.shape[0] // copies
    for i in range(copies):
        lines = pl.ds(i * rows, rows)
        pltpu.make_async_copy(o_vmem.at[lines], o_hbm.at[lines], sem.at[i]).start()
    for i in range(copies):
        lines = pl.ds(i * rows, rows)
        pltpu.make_async_copy(o_vmem.at[lines], o_hbm.at[lines], sem.at[i]).wait()


def chain_call(n, q, nk, nv, ck, cv, tables, heads, rows, head_dim):
    def vmem(*shape):
        return pltpu.VMEM(shape, jnp.bfloat16)

    def wide_vmem(*shape):
        return pltpu.VMEM(shape, jnp.float32)

    hbm = pl.BlockSpec(memory_space=pltpu.HBM)
    smem = pl.BlockSpec(memory_space=pltpu.SMEM)
    in_vmem = pl.BlockSpec(memory_space=pltpu.VMEM)
    dma = pltpu.SemaphoreType.DMA
    cached, wide = ck.shape[:2]
    slots = 7
    out = pl.pallas_call(
        functools.partial(chain, n),
        out_shape=pltpu.VMEM((heads * rows, head_dim), jnp.bfloat16),
        in_specs=[hbm] * 5 + [smem] * 4,
        out_specs=in_vmem,
        scratch_shapes=[
            vmem(heads * rows, head_dim), vmem(wide, head_dim), vmem(wide, head_dim),
            vmem(cached, wide, head_dim), vmem(cached, wide, head_dim),
            vmem(slots, 2 * head_dim, rows), vmem(wide, wide), vmem(wide, wide), vmem(2, BLK, BLK),
            vmem(n + 2, heads, 2, 2, BLK, head_dim),
            wide_vmem(slots, head_dim, rows), wide_vmem(slots, 1, rows), wide_vmem(slots, 1, rows),
            wide_vmem(2, 16, BLK), vmem(GUESTS, head_dim, rows), wide_vmem(GUESTS, 8, rows),
            wide_vmem(2 * BLK, rows), wide_vmem(2 * BLK, rows), wide_vmem(1, rows), wide_vmem(1, rows),
            vmem(heads * rows, head_dim),
            dma((n, heads, 2)), dma((n, heads)), dma((n, heads)), dma((n, heads)), dma((4,)),
            dma((2, GUESTS + 1)), dma((2, GUESTS, 2)), dma((5,)), pltpu.SemaphoreType.REGULAR,
        ],
        compiler_params=pltpu.CompilerParams(
            collective_id=0, has_side_effects=True, vmem_limit_bytes=60 * 2**20),
    )(*[pltpu.with_memory_space_constraint(x, pltpu.HBM) for x in (q, nk, nv, ck, cv)], *tables)
    return pl.pallas_call(
        store,
        out_shape=jax.ShapeDtypeStruct(out.shape, out.dtype),
        in_specs=[in_vmem],
        out_specs=hbm,
        scratch_shapes=[dma((4,))],
        compiler_params=pltpu.CompilerParams(vmem_limit_bytes=2**20),
    )(out)


def shards(n, queries, new_keys, new_values, cache_keys, cache_values,
           vertical_pool, vertical_lists, slash_lists, list_counts):
    tokens, heads, groups, head_dim = queries.shape
    rows = tokens * groups
    picked = vertical_pool.shape[0]

    def flat(x):
        return x.reshape(-1, head_dim)

    def vmem(*shape):
        return pltpu.VMEM(shape, jnp.bfloat16)

    hbm = pl.BlockSpec(memory_space=pltpu.HBM)
    smem = pl.BlockSpec(memory_space=pltpu.SMEM)
    dma = pltpu.SemaphoreType.DMA
    wide = heads * BLK
    cached = cache_keys.shape[0] // BLK
    if n == 4 and heads == 4 and picked == 2:
        out = chain_call(n, flat(queries), flat(new_keys), flat(new_values),
                         cache_keys.reshape(cached, wide, head_dim), cache_values.reshape(cached, wide, head_dim),
                         (vertical_pool, vertical_lists, slash_lists, list_counts), heads, rows, head_dim)
        return out.reshape(tokens, heads, groups, head_dim)
    out = pl.pallas_call(
        functools.partial(attend, n),
        out_shape=jax.ShapeDtypeStruct((tokens * heads * groups, head_dim), jnp.bfloat16),
        in_specs=[hbm] * 5 + [smem] * 4,
        out_specs=pl.BlockSpec(memory_space=pltpu.VMEM),
        scratch_shapes=[
            vmem(heads * rows, head_dim), vmem(wide, head_dim), vmem(wide, head_dim),
            vmem(cached, wide, head_dim), vmem(cached, wide, head_dim),
            vmem(heads, rows, head_dim), vmem(picked, 2, heads, BLK, head_dim),
            vmem(2, heads, BLK, head_dim), vmem(wide, wide), vmem(wide, wide),
            vmem(n, picked, 2, heads, BLK, head_dim),
            vmem(2, wide, head_dim), vmem(2, heads, BLK, head_dim),
            pltpu.VMEM((heads, head_dim, rows), jnp.float32),
            pltpu.VMEM((heads, 1, rows), jnp.float32),
            pltpu.VMEM((heads, 1, rows), jnp.float32),
            vmem(2, heads, 3 * BLK, rows), pltpu.VMEM((2, heads, 1, rows), jnp.float32),
            dma((n, 2, 2)), dma((n, 2)), dma((n, 2)), dma((n, 2)), dma((4,)), dma((5,)),
        ],
        compiler_params=pltpu.CompilerParams(
            collective_id=0, has_side_effects=True, vmem_limit_bytes=60 * 2**20),
    )(flat(queries), flat(new_keys), flat(new_values), cache_keys.reshape(cached, wide, head_dim),
      cache_values.reshape(cached, wide, head_dim),
      vertical_pool, vertical_lists, slash_lists, list_counts)
    return out.reshape(tokens, heads, groups, head_dim)


def solution(mesh):
    in_specs = (
        P(("grp", "ctx"), "kvh", "sub", None),
        P(("grp", "ctx"), "kvh", None),
        P(("grp", "ctx"), "kvh", None),
        P(("grp", "ctx"), "kvh", None),
        P(("grp", "ctx"), "kvh", None),
        P(("grp", "ctx")),
        P(("grp", "ctx"), None),
        P(("grp", "ctx"), None),
        P(("grp", "ctx"), None),
    )
    out_specs = P(("grp", "ctx"), "kvh", "sub", None)
    return jax.shard_map(functools.partial(shards, mesh.shape["ctx"]), mesh=mesh,
                         in_specs=in_specs, out_specs=out_specs, check_vma=False)
```

```python
import functools
import math

import jax
import jax.numpy as jnp
from jax import lax
from jax.experimental import pallas as pl
from jax.experimental.pallas import tpu as pltpu
from jax.sharding import PartitionSpec as P

BLK = 128
MESH = pl.DeviceIdType.MESH


def attend(n, q_hbm, nk_hbm, nv_hbm, ck_hbm, cv_hbm, vp_ref, vl_ref, sl_ref, cnt_ref, o_ref,
           q_raw, nk_raw, nv_raw, ck_raw, cv_raw, q_ref, own_ref, new_ref, sort_kv, sort_q,
           pool, slash_raw, slash, acc, peak, total, rounded, fade,
           hop_send, hop_recv, sib_send, sib_recv, sl_sem, in_sem):
    z = lax.axis_index("ctx")
    s = lax.axis_index("sub")
    heads, rows, head_dim = q_ref.shape
    groups = rows // BLK
    wide = heads * BLK
    loads = [pltpu.make_async_copy(src, dst, in_sem.at[i]) for i, (src, dst) in enumerate(
        [(ck_hbm, ck_raw), (cv_hbm, cv_raw), (nk_hbm, nk_raw), (nv_hbm, nv_raw), (q_hbm, q_raw)])]
    loads[0].start()
    c = math.log2(math.e) / math.sqrt(head_dim)
    has_left = z > 0
    has_right = z < n - 1
    sib_id = {"sub": 1 - s}

    barrier = pltpu.get_barrier_semaphore()
    pl.semaphore_signal(barrier, inc=1, device_id=sib_id, device_id_type=MESH)

    @pl.when(has_left)
    def _():
        pl.semaphore_signal(barrier, inc=1, device_id={"ctx": z - 1}, device_id_type=MESH)

    @pl.when(has_right)
    def _():
        pl.semaphore_signal(barrier, inc=1, device_id={"ctx": z + 1}, device_id_type=MESH)

    ids = lax.broadcasted_iota(jnp.int32, (wide, wide), 0)
    at = lax.broadcasted_iota(jnp.int32, (wide, wide), 1)
    sort_kv[...] = jnp.where(at == (ids % BLK) * heads + ids // BLK, 1.0, 0.0).astype(jnp.bfloat16)
    token = (ids % BLK) // groups
    sort_q[...] = jnp.where(at == (token * heads + ids // BLK) * groups + ids % groups,
                            1.0, 0.0).astype(jnp.bfloat16)

    def by_head(raw):
        return jnp.dot(sort_kv[...], raw, preferred_element_type=jnp.float32).astype(jnp.bfloat16)

    def put_keys(dst, raw):
        ordered = by_head(raw)
        for h in range(heads):
            dst[h] = ordered[h * BLK:(h + 1) * BLK]

    def put_values(dst, raw):
        ordered = lax.dot_general(raw, sort_kv[...], (((0,), (1,)), ((), ())),
                                  preferred_element_type=jnp.float32).astype(jnp.bfloat16)
        for h in range(heads):
            dst[h] = ordered[:, h * BLK:(h + 1) * BLK]

    def chosen(cache, b):
        return cache[vp_ref[b]]

    pl.semaphore_wait(barrier, 1 + has_left.astype(jnp.int32) + has_right.astype(jnp.int32))

    def hop(src_ref, src, kv, right):
        return pltpu.make_async_remote_copy(
            src_ref=src_ref, dst_ref=pool.at[src, s, kv],
            send_sem=hop_send.at[src, int(right), kv], recv_sem=hop_recv.at[src, kv],
            device_id={"ctx": z + 1 if right else z - 1}, device_id_type=MESH)

    def sib(src, kv):
        return pltpu.make_async_remote_copy(
            src_ref=pool.at[src, s, kv], dst_ref=pool.at[src, s, kv],
            send_sem=sib_send.at[src, kv], recv_sem=sib_recv.at[src, kv],
            device_id=sib_id, device_id_type=MESH)

    def sib_in(src, kv):
        return pltpu.make_async_remote_copy(
            src_ref=pool.at[src, 1 - s, kv], dst_ref=pool.at[src, 1 - s, kv],
            send_sem=sib_send.at[src, kv], recv_sem=sib_recv.at[src, kv],
            device_id=sib_id, device_id_type=MESH)

    def slash_hop(src_ref=nk_hbm):
        return pltpu.make_async_remote_copy(
            src_ref=src_ref, dst_ref=slash_raw.at[s],
            send_sem=sl_sem.at[0], recv_sem=sl_sem.at[1],
            device_id={"ctx": z + 1}, device_id_type=MESH)

    def slash_sib(part):
        return pltpu.make_async_remote_copy(
            src_ref=slash_raw.at[part], dst_ref=slash_raw.at[part],
            send_sem=sl_sem.at[2], recv_sem=sl_sem.at[3],
            device_id=sib_id, device_id_type=MESH)

    for part, src_ref in enumerate((nk_hbm, nv_hbm)):
        @pl.when(has_right & (s == part))
        def _():
            slash_hop(src_ref).start()

    def send_own(kv):
        @pl.when(has_right)
        def _():
            hop(own_ref.at[s, kv], z, kv, True).start()

        @pl.when(has_left)
        def _():
            hop(own_ref.at[s, kv], z, kv, False).start()

    loads[0].wait()
    loads[1].start()
    put_keys(own_ref.at[s, 0], chosen(ck_raw, s))
    for load in loads[2:]:
        load.start()
    send_own(0)
    loads[1].wait()
    put_values(own_ref.at[s, 1], chosen(cv_raw, s))
    send_own(1)
    loads[2].wait()
    loads[3].wait()
    put_keys(new_ref.at[0], nk_raw[...])
    put_values(new_ref.at[1], nv_raw[...])
    put_keys(own_ref.at[1 - s, 0], chosen(ck_raw, 1 - s))
    put_values(own_ref.at[1 - s, 1], chosen(cv_raw, 1 - s))
    loads[4].wait()
    for part in range(rows // BLK):
        ordered = jnp.dot(sort_q[...], q_raw[part * wide:(part + 1) * wide],
                          preferred_element_type=jnp.float32).astype(jnp.bfloat16)
        for h in range(heads):
            q_ref[h, part * BLK:(part + 1) * BLK] = ordered[h * BLK:(h + 1) * BLK]

    def listed(slot):
        count = cnt_ref[0, 0]
        width = vl_ref.shape[1]
        if width <= 8:
            hit = jnp.int32(0)
            for i in range(width):
                hit = hit | jnp.where((vl_ref[0, i] == slot) & (i < count), 1, 0)
            return hit

        def one(i, hit):
            return hit | jnp.where((vl_ref[0, i] == slot) & (i < count), 1, 0)

        return lax.fori_loop(0, width, one, jnp.int32(0))

    def score(keys, q):
        return lax.dot_general(keys, q, (((1,), (1,)), ((), ())),
                               preferred_element_type=jnp.float32)

    def take_keys(side, blocks, first=False):
        for h in range(heads):
            q = q_ref[h]
            raw = []
            tops = []
            for keys, seen in blocks:
                scores = score(keys[h], q)
                if seen is None:
                    key_id = lax.broadcasted_iota(jnp.int32, scores.shape, 0)
                    row_id = lax.broadcasted_iota(jnp.int32, scores.shape, 1) // groups
                    scores = jnp.where(key_id <= row_id, scores, -jnp.inf)
                top = jnp.max(scores, axis=0, keepdims=True)
                if seen is not None:
                    top = jnp.where(seen > 0, top, -jnp.inf)
                raw.append(scores)
                tops.append(top)
            high = functools.reduce(jnp.maximum, tops)
            if not first:
                old = peak[h]
                high = jnp.maximum(old, high)
                factor = jnp.exp2((old - high) * c)
                fade[side, h] = factor
            peak[h] = high
            sums = []
            for i, ((_, seen), scores) in enumerate(zip(blocks, raw)):
                base = high if seen is None else jnp.where(seen > 0, high, jnp.inf)
                weights = jnp.exp2((scores - base) * c)
                sums.append(jnp.sum(weights, axis=0, keepdims=True))
                rounded[side, h, i * BLK:(i + 1) * BLK] = weights.astype(jnp.bfloat16)
            add = sum(sums[1:], sums[0])
            total[h] = add if first else total[h] * fade[side, h] + add

    def take_values(side, blocks, first=False):
        depth = len(blocks) * BLK
        for h in range(heads):
            values = jnp.concatenate([values[h] for values in blocks], 1)
            add = jnp.dot(values, rounded[side, h, :depth], preferred_element_type=jnp.float32)
            acc[h] = add if first else acc[h] * fade[side, h] + add

    take_keys(0, [(new_ref.at[0], None)]
              + [(own_ref.at[b, 0], listed(2 * z + b)) for b in range(2)], first=True)
    take_values(0, [new_ref.at[1]] + [own_ref.at[b, 1] for b in range(2)], first=True)

    @pl.when(has_left)
    def _():
        slash_hop().wait_recv()
        slash_sib(s).start()

    def arrive(src, kv, right):
        hop(own_ref.at[s, kv], src, kv, right).wait_recv()

        @pl.when(has_right if right else has_left)
        def _():
            hop(pool.at[src, s, kv], src, kv, right).start()

        sib(src, kv).start()

    def step(d, carry):
        sides = ((z + d, z + d < n, False), (z - d, z - d >= 0, True))
        for kv in range(2):
            for src, there, right in sides:
                @pl.when(there)
                def _():
                    arrive(src, kv, right)

            for side, (src, there, right) in enumerate(sides):
                @pl.when(there)
                def _():
                    sib_in(src, kv).wait_recv()
                    if kv == 0:
                        take_keys(side, [(pool.at[src, b, 0], listed(2 * src + b))
                                         for b in range(2)])
                    else:
                        take_values(side, [pool.at[src, b, 1] for b in range(2)])

        @pl.when((d == 1) & has_left)
        def _():
            slash_sib(1 - s).wait_recv()
            put_keys(slash.at[0], slash_raw[0])
            put_values(slash.at[1], slash_raw[1])
            back = jnp.int32(0)
            for i in range(sl_ref.shape[1]):
                back = back | jnp.where((sl_ref[0, i] == 1) & (i < cnt_ref[0, 1]), 1, 0)
            take_keys(0, [(slash.at[0], back)])
            take_values(0, [slash.at[1]])

        return carry

    lax.fori_loop(1, n, step, 0)

    for part in range(rows // BLK):
        lanes = slice(part * BLK, (part + 1) * BLK)
        done = jnp.concatenate(
            [(acc[h, :, lanes] / total[h, :, lanes]).astype(jnp.bfloat16) for h in range(heads)], 1)
        o_ref[part * wide:(part + 1) * wide] = lax.dot_general(
            sort_q[...], done, (((0,), (1,)), ((), ())),
            preferred_element_type=jnp.float32).astype(o_ref.dtype)

    def drain(src, carry):
        for kv in range(2):
            @pl.when(has_right & (src <= z))
            def _():
                hop(own_ref.at[s, kv], src, kv, True).wait_send()

            @pl.when(has_left & (src >= z))
            def _():
                hop(own_ref.at[s, kv], src, kv, False).wait_send()

            @pl.when(src != z)
            def _():
                sib(src, kv).wait_send()
        return carry

    lax.fori_loop(0, n, drain, 0)

    @pl.when(has_right)
    def _():
        slash_hop().wait_send()

    @pl.when(has_left)
    def _():
        slash_sib(s).wait_send()

BITS = 5
PACK = 6
OWN, GUEST, ALONE = 4, 5, 6
IDLE = (6, 4 * GUEST)
GUESTS = 1
EARLY = 2


NONE = (-1, -1)
QUEST = (-2, 0)
SLASH = (-3, 0)


def plan(heads):
    zero = [(NONE, (0, 0), 0), (NONE, (0, ALONE), 0), (NONE, (1, 0), 0), ((1, 0), (1, ALONE), 0), (NONE, (2, 0), 0),
        (NONE, (2, ALONE), 0), ((1, 1), (0, 1), 0), (NONE, (3, 0), 0), (NONE, (3, ALONE), 0), ((1, 2), (1, 1), 0),
        (NONE, NONE, 0), ((1, 3), NONE, 0), (NONE, (2, 1), 0), (NONE, NONE, 0), (NONE, (3, 1), 0), ((2, 0), NONE, 0),
        ((2, 1), NONE, 0), (NONE, (0, 2), 0), (NONE, NONE, 0), (NONE, (1, 2), 0), ((2, 2), NONE, 0),
        ((2, 3), NONE, 0), (NONE, (2, 2), 0), (NONE, NONE, 0), (NONE, (3, 2), 0), ((3, 0), NONE, 0),
        ((3, 1), NONE, 0), (NONE, (0, 3), 0), (NONE, NONE, 0), (NONE, (1, 3), 0), ((3, 2), NONE, 16),
        ((3, 3), NONE, 0), (NONE, (2, 3), 0), (NONE, NONE, 0), (NONE, (3, 3), 0), (NONE, NONE, 0)]
    one = [((0, 0), (0, 1), 0), ((2, 0), (1, 1), 0), ((0, 3), (2, 1), 0), (NONE, (0, 0), 0), ((2, 1), (0, 2), 0),
        ((0, 1), (3, 0), 4), (NONE, (3, 1), 0), (NONE, (1, 2), 0), ((2, 2), (1, 0), 0), ((0, 2), NONE, 8),
        ((2, 3), NONE, 0), (NONE, (2, 2), 0), (NONE, (2, 0), 0), (NONE, NONE, 0), ((3, 0), (3, 2), 0),
        (SLASH, NONE, 0), ((3, 1), NONE, 0), (NONE, (0, 3), 0), (NONE, NONE, 0), (NONE, (0, OWN), 0),
        ((3, 2), (1, 3), 0), (NONE, (1, OWN), 0), (NONE, (2, OWN), 16), ((3, 3), (2, 3), 0), (NONE, (3, OWN), 0),
        (NONE, NONE, 0), (NONE, (3, 3), 0), (NONE, NONE, 0)]
    two = [((1, 0), (0, 2), 0), ((3, 0), (1, 2), 0), (NONE, (2, 2), 0), ((1, 3), (0, 1), 0), ((3, 1), (0, 3), 0),
        (NONE, (3, 2), 0), ((1, 1), (3, 1), 0), ((3, 2), (1, 3), 0), (NONE, NONE, 0), ((0, 0), (1, 1), 0),
        ((3, 3), (2, 3), 0), (NONE, NONE, 0), ((0, 3), (0, 0), 0), (NONE, (3, 3), 0), (NONE, NONE, 0),
        (NONE, (3, 0), 0), ((0, 1), NONE, 0), (QUEST, NONE, 0), (NONE, (4, 2), 0), ((1, 2), (4, GUEST), 0),
        (NONE, (4, 1), 0), (NONE, (4, 0), 0), (NONE, (1, 0), 0), ((0, 2), (2, 1), 2), (NONE, NONE, 0),
        (NONE, (2, 0), 0), (NONE, NONE, 0), (SLASH, NONE, 0), (NONE, (0, OWN), 0), (NONE, (1, OWN), 0),
        (NONE, (2, OWN), 16), (NONE, (3, OWN), 0), (NONE, NONE, 0)]
    three = [(NONE, (0, 3), 0), ((2, 0), (1, 3), 0), (NONE, (2, 3), 0), (NONE, (3, 3), 0), (NONE, (0, 2), 0),
        (SLASH, (3, ALONE), 0), (NONE, NONE, 0), (NONE, (0, OWN), 0), ((2, 1), (1, OWN), 0), (NONE, (2, OWN), 0),
        (NONE, NONE, 0), ((2, 2), (1, 2), 0), (NONE, NONE, 0), ((1, 0), NONE, 0), (NONE, (2, 2), 0), (NONE, NONE, 0),
        (NONE, (0, 1), 0), ((1, 1), NONE, 0), ((0, 0), NONE, 0), (NONE, (1, 1), 0), (NONE, NONE, 0),
        (NONE, (0, 0), 0), ((0, 1), NONE, 0), ((1, 2), NONE, 0), (NONE, (1, 0), 0), (NONE, NONE, 16),
        (NONE, (2, 1), 0), ((0, 2), NONE, 0), (NONE, (2, 0), 0), (NONE, NONE, 0)]

    def build(z, table):
        out, before, used = [], NONE, set()
        for recv, now, flags in table + [(NONE, NONE, 0)]:
            kind, message = (1, recv[0] * 4 + recv[1]) if recv[0] >= 0 else (-recv[0] if recv != NONE else 0, 0)
            slot, src = now
            h = slot if slot < heads else slot - GUESTS
            key = OWN if src == OWN else (src, h)
            first = now != NONE and key not in used and src not in (z, GUEST, ALONE)
            used.add(key)
            code = (slot + (8 if first else 0), src * 4 + h) if now != NONE else IDLE
            busy = now != NONE or before != NONE
            out.append((kind, message) + code + (int(busy) | flags,))
            before = now
        return out

    return [build(z, table) for z, table in enumerate((zero, one, two, three))]


def chain(n, q_hbm, nk_hbm, nv_hbm, ck_hbm, cv_hbm, vp_hbm, vl_hbm, sl_hbm, cnt_hbm, o_ref,
          vp_ref, vl_ref, sl_ref, cnt_ref,
          q_raw, nk_raw, nv_raw, ck_raw, cv_raw, q_ref, sort_kv, sort_q, ext,
          pool, acc, peak, total, mask, part_acc, part_stat, scores_a, scores_b, top_a, top_b, most,
          send_sem, hop_recv, sib_recv, sl_sem, q_sem, part_sem, in_sem, table_sem, ready):
    z = lax.axis_index("ctx")
    s = lax.axis_index("sub")
    heads = pool.shape[1]
    head_dim, rows = acc.shape[1:]
    groups = rows // BLK
    wide = heads * BLK
    last = n - 1
    stay = heads - GUESTS
    loads = [pltpu.make_async_copy(src, dst, in_sem.at[i]) for i, (src, dst) in enumerate(
        [(ck_hbm, ck_raw), (cv_hbm, cv_raw), (nk_hbm, nk_raw), (nv_hbm, nv_raw), (q_hbm, q_raw)])]
    tables = [pltpu.make_async_copy(src, dst, table_sem.at[i]) for i, (src, dst) in enumerate(
        [(vp_hbm, vp_ref), (vl_hbm, vl_ref), (sl_hbm, sl_ref), (cnt_hbm, cnt_ref)])]
    loads[0].start()
    loads[1].start()
    for table in tables:
        table.start()
    c = math.log2(math.e) / math.sqrt(head_dim)
    has_left = z > 0
    has_right = z < last
    sib_id = {"sub": 1 - s}
    inner = has_left & has_right

    barrier = pltpu.get_barrier_semaphore()
    pl.semaphore_signal(barrier, inc=1, device_id=sib_id, device_id_type=MESH)

    @pl.when(has_right)
    def _():
        pl.semaphore_signal(barrier, inc=1, device_id={"ctx": z + 1}, device_id_type=MESH)

    ids = lax.broadcasted_iota(jnp.int32, (wide, wide), 0)
    at = lax.broadcasted_iota(jnp.int32, (wide, wide), 1)
    sort_kv[...] = jnp.where(at == (ids % BLK) * heads + ids // BLK, 1.0, 0.0).astype(jnp.bfloat16)

    pl.semaphore_wait(barrier, 1 + has_left.astype(jnp.int32))

    @pl.when(has_left)
    def _():
        pl.semaphore_signal(ready, inc=1, device_id={"ctx": z - 1}, device_id_type=MESH)

    def put_keys(raw, put):
        ordered = jnp.dot(sort_kv[...], raw, preferred_element_type=jnp.float32).astype(jnp.bfloat16)
        for h in range(heads):
            put(h, ordered[h * BLK:(h + 1) * BLK])

    def put_values(raw, put):
        ordered = lax.dot_general(raw, sort_kv[...], (((0,), (1,)), ((), ())),
                                  preferred_element_type=jnp.float32).astype(jnp.bfloat16)
        for h in range(heads):
            put(h, ordered[:, h * BLK:(h + 1) * BLK])

    def put_pool(b, kv):
        def put(h, block):
            pool[z, h, b, kv] = block
        return put

    def put_new(kv):
        def put(h, block):
            pool[OWN, h, 0, kv] = block
            pool[GUEST, h, 0, kv] = block
            pool[GUEST, h, 1, kv] = jnp.zeros_like(block)
        return put

    def hop(src, h, right):
        return pltpu.make_async_remote_copy(
            src_ref=pool.at[src, h, s], dst_ref=pool.at[src, h, s],
            send_sem=send_sem.at[int(right)], recv_sem=hop_recv.at[src if right else src - 1, h],
            device_id={"ctx": z + 1 if right else z - 1}, device_id_type=MESH)

    def first_hop(h, kv, right):
        return pltpu.make_async_remote_copy(
            src_ref=pool.at[z, h, s, kv], dst_ref=pool.at[z, h, s, kv],
            send_sem=send_sem.at[int(right)], recv_sem=hop_recv.at[z if right else z - 1, h],
            device_id={"ctx": z + 1 if right else z - 1}, device_id_type=MESH)

    def sib(src, h, part):
        return pltpu.make_async_remote_copy(
            src_ref=pool.at[src, h, part], dst_ref=pool.at[src, h, part],
            send_sem=send_sem.at[2], recv_sem=sib_recv.at[src - (src > z).astype(jnp.int32), h],
            device_id=sib_id, device_id_type=MESH)

    def slash_hop(count):
        return pltpu.make_async_remote_copy(
            src_ref=pool.at[OWN, pl.ds(0, count), 0, s], dst_ref=pool.at[OWN, pl.ds(0, count), 1, s],
            send_sem=sl_sem.at[0], recv_sem=sl_sem.at[1],
            device_id={"ctx": z + 1}, device_id_type=MESH)

    def slash_sib(count, part):
        block = pool.at[OWN, pl.ds(0, count), 1, part]
        return pltpu.make_async_remote_copy(
            src_ref=block, dst_ref=block,
            send_sem=sl_sem.at[2], recv_sem=sl_sem.at[3],
            device_id=sib_id, device_id_type=MESH)

    def guest_q(g):
        return pltpu.make_async_remote_copy(
            src_ref=q_ref.at[stay + g, pl.ds(0, head_dim)], dst_ref=q_ref.at[heads + g, pl.ds(0, head_dim)],
            send_sem=q_sem.at[0, g], recv_sem=q_sem.at[1, g],
            device_id={"ctx": z - 1}, device_id_type=MESH)

    def guest_mask():
        return pltpu.make_async_remote_copy(
            src_ref=mask.at[0], dst_ref=mask.at[1],
            send_sem=q_sem.at[0, GUESTS], recv_sem=q_sem.at[1, GUESTS],
            device_id={"ctx": z - 1}, device_id_type=MESH)

    def guest_part(g):
        return [pltpu.make_async_remote_copy(
            src_ref=ref.at[g], dst_ref=ref.at[g],
            send_sem=part_sem.at[0, g, i], recv_sem=part_sem.at[1, g, i],
            device_id={"ctx": z + 1}, device_id_type=MESH)
            for i, ref in enumerate((part_acc, part_stat))]

    def leftward(*blocks):
        @pl.when(has_left)
        def _():
            for h, kv in blocks:
                first_hop(h, kv, False).start()

    for table in tables:
        table.wait()
    loads[0].wait()
    put_keys(ck_raw[vp_ref[s]], put_pool(s, 0))
    leftward((0, 0), (1, 0))
    for load in loads[2:]:
        load.start()
    loads[1].wait()
    put_values(cv_raw[vp_ref[s]], put_pool(s, 1))
    leftward((0, 1), (1, 1), *[(h, kv) for h in range(2, heads) for kv in range(2)])

    @pl.when(has_right)
    def _():
        pl.semaphore_wait(ready, 1)

    @pl.when(z == 0)
    def _():
        for h in (0, 3, 1, 2):
            for kv in range(2):
                first_hop(h, kv, True).start()

    @pl.when(z == 1)
    def _():
        for h in (0, 3, 1):
            for kv in range(2):
                first_hop(h, kv, True).start()

    @pl.when(z == 2)
    def _():
        for kv in range(2):
            first_hop(0, kv, True).start()

    loads[2].wait()
    loads[3].wait()
    put_keys(nk_raw[...], put_new(0))
    put_values(nv_raw[...], put_new(1))

    @pl.when(z == 2)
    def _():
        slash_hop(stay).start()
        for h in range(1, stay):
            for kv in range(2):
                first_hop(h, kv, True).start()

    token = (ids % BLK) // groups
    sort_q[...] = jnp.where(at == (token * heads + ids // BLK) * groups + ids % groups,
                            1.0, 0.0).astype(jnp.bfloat16)
    loads[4].wait()
    for part in range(rows // BLK):
        ordered = lax.dot_general(q_raw[part * wide:(part + 1) * wide], sort_q[...], (((0,), (1,)), ((), ())),
                                  preferred_element_type=jnp.float32).astype(jnp.bfloat16)
        for h in range(heads):
            q_ref[h, 0:head_dim, part * BLK:(part + 1) * BLK] = ordered[:, h * BLK:(h + 1) * BLK]

    def unseen(hit):
        return jnp.full((1, BLK), jnp.where(hit > 0, 0.0, jnp.inf), jnp.float32)

    for slot in range(2 * n):
        hit = jnp.int32(0)
        for i in range(vl_ref.shape[1]):
            hit = hit | jnp.where((vl_ref[0, i] == slot) & (i < cnt_ref[0, 0]), 1, 0)
        mask[0, slot:slot + 1] = unseen(hit)
    hit = jnp.int32(0)
    for i in range(sl_ref.shape[1]):
        hit = hit | jnp.where((sl_ref[0, i] == 1) & (i < cnt_ref[0, 1]), 1, 0)
    mask[0, 2 * OWN:2 * OWN + 2] = jnp.concatenate([jnp.zeros((1, BLK), jnp.float32), unseen(hit)], 0)
    mask[0, 2 * GUEST:2 * GUEST + 2] = jnp.concatenate([unseen(hit), jnp.full((1, BLK), jnp.inf, jnp.float32)], 0)
    mask[0, 2 * ALONE:2 * ALONE + 2] = jnp.concatenate(
        [jnp.zeros((1, BLK), jnp.float32), jnp.full((1, BLK), jnp.inf, jnp.float32)], 0)

    @pl.when(z == 0)
    def _():
        slash_hop(heads).start()

    @pl.when(z == last)
    def _():
        for g in range(GUESTS):
            guest_q(g).start()
        guest_mask().start()

    put_keys(ck_raw[vp_ref[1 - s]], put_pool(1 - s, 0))
    put_values(cv_raw[vp_ref[1 - s]], put_pool(1 - s, 1))

    key_id = lax.broadcasted_iota(jnp.int32, (BLK, rows), 0)
    row_id = lax.broadcasted_iota(jnp.int32, (BLK, rows), 1) // groups
    later = jnp.where(key_id > row_id, -1e30, 0.0).astype(jnp.bfloat16)
    slots = acc.shape[0]
    for slot in range(slots):
        q_ref[slot, head_dim:] = later if slot < heads else jnp.zeros_like(later)
        acc[slot] = jnp.zeros_like(acc[slot])
        total[slot] = jnp.zeros_like(total[slot])
        peak[slot] = jnp.full_like(peak[slot], -1e30)
    q_ref[slots - 1, 0:head_dim] = jnp.zeros_like(later)
    one_at = lax.broadcasted_iota(jnp.int32, (BLK, BLK), 0) == lax.broadcasted_iota(jnp.int32, (BLK, BLK), 1)
    ext[0] = jnp.zeros((BLK, BLK), jnp.bfloat16)
    ext[1] = jnp.where(one_at, 1.0, 0.0).astype(jnp.bfloat16)
    scores_b[...] = jnp.zeros_like(scores_b)
    top_b[...] = jnp.zeros_like(top_b)

    def spread(row):
        return jnp.concatenate([row] * groups, 1)

    def place(src):
        return src - src // ALONE

    def hidden(slot, src, b):
        return spread(mask[(slot // heads) % 2 * (1 - slot // (slots - 1)), pl.ds(2 * src + b, 1)])

    def ahead(unit, scores, top):
        slot, src, h = unit
        q = q_ref[slot]
        high = None
        for b in range(2):
            causal = (src // OWN) * (1 - src % 2) if b == 0 else 0
            keys = jnp.concatenate([pool[place(src), h, b, 0], ext[causal]], 1)
            found = jnp.dot(keys, q, preferred_element_type=jnp.float32)
            scores[b * BLK:(b + 1) * BLK] = found
            part = jnp.max(found, axis=0, keepdims=True) - hidden(slot, src, b)
            high = part if high is None else jnp.maximum(high, part)
        top[...] = high

    def behind(unit, scores, top):
        slot, src, h = unit
        old = peak[slot]
        high = jnp.maximum(old, top[...])
        factor = jnp.exp2((old - high) * c)
        peak[slot] = high
        weights = [jnp.exp2((scores[b * BLK:(b + 1) * BLK] - (high + hidden(slot, src, b))) * c)
                   .astype(jnp.bfloat16) for b in range(2)]
        values = jnp.concatenate([pool[place(src), h, b, 1] for b in range(2)], 1)
        values = jnp.concatenate([values, jnp.ones((16, 2 * BLK), jnp.bfloat16)], 0)
        add = jnp.dot(values, jnp.concatenate(weights, 0), preferred_element_type=jnp.float32)
        acc[slot] = acc[slot] * factor + add[:head_dim]
        total[slot] = total[slot] * factor + add[head_dim:head_dim + 1]

    def ordered(part, those):
        lanes = slice(part * BLK, (part + 1) * BLK)
        done = jnp.concatenate(
            [(acc[h, :, lanes] * (1.0 / total[h, :, lanes])).astype(jnp.bfloat16) for h in those], 1)
        return lax.dot_general(sort_q[those.start * BLK:those.stop * BLK], done, (((0,), (1,)), ((), ())),
                               preferred_element_type=jnp.float32)

    def drain():
        def sent(kind, sources, count):
            blocks = pool.at[pl.ds(0, sources), pl.ds(0, count), s]
            pltpu.make_async_copy(blocks, blocks, send_sem.at[kind]).wait()

        for index in range(n):
            right = heads if index < last - 1 else stay if index < last else 0

            @pl.when(z == index)
            def _():
                if right:
                    sent(1, index + 1, right)
                    slash_hop(right).wait_send()
                if index > 0:
                    sent(0, n - index, heads)
                    slash_sib(heads if index < last else stay, s).wait_send()
                sent(2, n - 1, heads if index < last else stay)
                if index == last:
                    guest_mask().wait_send()
                    for g in range(GUESTS):
                        guest_q(g).wait_send()

    roles = plan(heads)
    steps = max(len(role) for role in roles)
    steps += steps % 2
    roles = [role + [(0, 0) + IDLE + (0,)] * (steps - len(role)) for role in roles]

    def by_role(values):
        out = jnp.int32(values[-1])
        for i in reversed(range(len(values) - 1)):
            out = jnp.where(z == i, jnp.int32(values[i]), out)
        return out

    words = [[by_role([sum(step[field] << (BITS * i) for i, step in enumerate(role[start:start + PACK]))
                       for role in roles]) for start in range(0, steps, PACK)] for field in range(5)]

    def step(t, before, bufs, old_bufs):
        def look(field):
            word = words[field][-1]
            for i in reversed(range(len(words[field]) - 1)):
                word = jnp.where(t // PACK == i, words[field][i], word)
            return lax.shift_right_logical(word, BITS * (t % PACK)) & (2 ** BITS - 1)

        kind, message, code, block, flags = [look(field) for field in range(5)]
        src, h = message // 4, message % 4

        @pl.when(kind == 1)
        def _():
            block = pool.at[src, h, s]
            pltpu.make_async_copy(block, block, hop_recv.at[src - (src > z).astype(jnp.int32), h]).wait()

            @pl.when((src > z) & has_left)
            def _():
                hop(src, h, False).start()

            @pl.when((src < z) & ((z < last - 1) | ((z == last - 1) & (h < stay))))
            def _():
                hop(src, h, True).start()

            sib(src, h, s).start()

        @pl.when((flags // 4) % 2 == 1)
        def _():
            for kv in range(2):
                first_hop(2, kv, True).start()

        @pl.when((flags // 8) % 2 == 1)
        def _():
            slash_hop(heads).start()

        @pl.when(kind == 2)
        def _():
            guest_mask().wait_recv()
            for g in range(GUESTS):
                guest_q(g).wait_recv()

        @pl.when((kind == 3) & has_right)
        def _():
            slash_hop(heads).wait_recv()
            slash_sib(heads, s).start()

        @pl.when((kind == 3) & (z == last))
        def _():
            slash_hop(stay).wait_recv()
            slash_sib(stay, s).start()

        unit = (code % 8, block // 4, block % 4)

        @pl.when((code > 7) & (unit[1] < OWN))
        def _():
            sib(unit[1], unit[2], 1 - s).wait_recv()

        @pl.when((code > 7) & (unit[1] == OWN) & has_right)
        def _():
            slash_sib(heads, 1 - s).wait_recv()

        @pl.when((code > 7) & (unit[1] == OWN) & (z == last))
        def _():
            slash_sib(stay, 1 - s).wait_recv()

        @pl.when(flags % 2 == 1)
        def _():
            ahead(unit, *bufs)
            behind(before, *old_bufs)

        @pl.when(flags // 16 == 1)
        def _():
            for part in range(rows // BLK):
                most[part * wide:(part + 1) * wide] = ordered(part, range(EARLY)).astype(o_ref.dtype)

        @pl.when((flags // 2) % 2 == 1)
        def _():
            g = 0
            part_acc[g] = acc[heads + g].astype(jnp.bfloat16)
            part_stat[g, 0:1] = peak[heads + g]
            part_stat[g, 1:2] = total[heads + g]
            for copy in guest_part(g):
                copy.start()

        return unit

    def two_steps(i, before):
        mid = step(2 * i, before, (scores_a, top_a), (scores_b, top_b))
        return step(2 * i + 1, mid, (scores_b, top_b), (scores_a, top_a))

    lengths = [max(t for t, step in enumerate(role) if step[0] or step[4]) + 1 for role in roles]
    idle = (jnp.int32(IDLE[0]), jnp.int32(GUEST), jnp.int32(0))
    lax.fori_loop(0, by_role([(length + 1) // 2 for length in lengths]), two_steps, idle)

    drain()

    @pl.when(z == last)
    def _():
        for g in range(GUESTS):
            for copy in guest_part(g):
                copy.wait_recv()
            slot = stay + g
            old, new = peak[slot], part_stat[g, 0:1]
            high = jnp.maximum(old, new)
            mine, theirs = jnp.exp2((old - high) * c), jnp.exp2((new - high) * c)
            acc[slot] = acc[slot] * mine + part_acc[g].astype(jnp.float32) * theirs
            total[slot] = total[slot] * mine + part_stat[g, 1:2] * theirs

    for part in range(rows // BLK):
        lines = slice(part * wide, (part + 1) * wide)
        o_ref[lines] = most[lines] + ordered(part, range(EARLY, heads)).astype(o_ref.dtype)

    @pl.when(z == last - 1)
    def _():
        for g in range(GUESTS):
            for copy in guest_part(g):
                copy.wait_send()


def store(o_vmem, o_hbm, sem):
    copies = sem.shape[0]
    rows = o_vmem.shape[0] // copies
    for i in range(copies):
        lines = pl.ds(i * rows, rows)
        pltpu.make_async_copy(o_vmem.at[lines], o_hbm.at[lines], sem.at[i]).start()
    for i in range(copies):
        lines = pl.ds(i * rows, rows)
        pltpu.make_async_copy(o_vmem.at[lines], o_hbm.at[lines], sem.at[i]).wait()


def chain_call(n, q, nk, nv, ck, cv, tables, heads, rows, head_dim):
    def vmem(*shape):
        return pltpu.VMEM(shape, jnp.bfloat16)

    def wide_vmem(*shape):
        return pltpu.VMEM(shape, jnp.float32)

    hbm = pl.BlockSpec(memory_space=pltpu.HBM)
    in_vmem = pl.BlockSpec(memory_space=pltpu.VMEM)
    dma = pltpu.SemaphoreType.DMA
    cached, wide = ck.shape[:2]
    slots = 7
    out = pl.pallas_call(
        functools.partial(chain, n),
        out_shape=pltpu.VMEM((heads * rows, head_dim), jnp.bfloat16),
        in_specs=[hbm] * 9,
        out_specs=in_vmem,
        scratch_shapes=[
            *[pltpu.SMEM(table.shape, table.dtype) for table in tables],
            vmem(heads * rows, head_dim), vmem(wide, head_dim), vmem(wide, head_dim),
            vmem(cached, wide, head_dim), vmem(cached, wide, head_dim),
            vmem(slots, 2 * head_dim, rows), vmem(wide, wide), vmem(wide, wide), vmem(2, BLK, BLK),
            vmem(n + 2, heads, 2, 2, BLK, head_dim),
            wide_vmem(slots, head_dim, rows), wide_vmem(slots, 1, rows), wide_vmem(slots, 1, rows),
            wide_vmem(2, 16, BLK), vmem(GUESTS, head_dim, rows), wide_vmem(GUESTS, 8, rows),
            wide_vmem(2 * BLK, rows), wide_vmem(2 * BLK, rows), wide_vmem(1, rows), wide_vmem(1, rows),
            vmem(heads * rows, head_dim),
            dma((3,)), dma((n - 1, heads)), dma((n - 1, heads)), dma((4,)),
            dma((2, GUESTS + 1)), dma((2, GUESTS, 2)), dma((5,)), dma((4,)), pltpu.SemaphoreType.REGULAR,
        ],
        compiler_params=pltpu.CompilerParams(
            collective_id=0, has_side_effects=True, vmem_limit_bytes=60 * 2**20),
    )(*[pltpu.with_memory_space_constraint(x, pltpu.HBM) for x in (q, nk, nv, ck, cv, *tables)])
    return pl.pallas_call(
        store,
        out_shape=jax.ShapeDtypeStruct(out.shape, out.dtype),
        in_specs=[in_vmem],
        out_specs=hbm,
        scratch_shapes=[dma((4,))],
        compiler_params=pltpu.CompilerParams(vmem_limit_bytes=2**20),
    )(out)


def shards(n, queries, new_keys, new_values, cache_keys, cache_values,
           vertical_pool, vertical_lists, slash_lists, list_counts):
    tokens, heads, groups, head_dim = queries.shape
    rows = tokens * groups
    picked = vertical_pool.shape[0]

    def flat(x):
        return x.reshape(-1, head_dim)

    def vmem(*shape):
        return pltpu.VMEM(shape, jnp.bfloat16)

    hbm = pl.BlockSpec(memory_space=pltpu.HBM)
    smem = pl.BlockSpec(memory_space=pltpu.SMEM)
    dma = pltpu.SemaphoreType.DMA
    wide = heads * BLK
    cached = cache_keys.shape[0] // BLK
    if n == 4 and heads == 4 and picked == 2:
        out = chain_call(n, flat(queries), flat(new_keys), flat(new_values),
                         cache_keys.reshape(cached, wide, head_dim), cache_values.reshape(cached, wide, head_dim),
                         (vertical_pool, vertical_lists, slash_lists, list_counts), heads, rows, head_dim)
        return out.reshape(tokens, heads, groups, head_dim)
    out = pl.pallas_call(
        functools.partial(attend, n),
        out_shape=jax.ShapeDtypeStruct((tokens * heads * groups, head_dim), jnp.bfloat16),
        in_specs=[hbm] * 5 + [smem] * 4,
        out_specs=pl.BlockSpec(memory_space=pltpu.VMEM),
        scratch_shapes=[
            vmem(heads * rows, head_dim), vmem(wide, head_dim), vmem(wide, head_dim),
            vmem(cached, wide, head_dim), vmem(cached, wide, head_dim),
            vmem(heads, rows, head_dim), vmem(picked, 2, heads, BLK, head_dim),
            vmem(2, heads, BLK, head_dim), vmem(wide, wide), vmem(wide, wide),
            vmem(n, picked, 2, heads, BLK, head_dim),
            vmem(2, wide, head_dim), vmem(2, heads, BLK, head_dim),
            pltpu.VMEM((heads, head_dim, rows), jnp.float32),
            pltpu.VMEM((heads, 1, rows), jnp.float32),
            pltpu.VMEM((heads, 1, rows), jnp.float32),
            vmem(2, heads, 3 * BLK, rows), pltpu.VMEM((2, heads, 1, rows), jnp.float32),
            dma((n, 2, 2)), dma((n, 2)), dma((n, 2)), dma((n, 2)), dma((4,)), dma((5,)),
        ],
        compiler_params=pltpu.CompilerParams(
            collective_id=0, has_side_effects=True, vmem_limit_bytes=60 * 2**20),
    )(flat(queries), flat(new_keys), flat(new_values), cache_keys.reshape(cached, wide, head_dim),
      cache_values.reshape(cached, wide, head_dim),
      vertical_pool, vertical_lists, slash_lists, list_counts)
    return out.reshape(tokens, heads, groups, head_dim)


def solution(mesh):
    in_specs = (
        P(("grp", "ctx"), "kvh", "sub", None),
        P(("grp", "ctx"), "kvh", None),
        P(("grp", "ctx"), "kvh", None),
        P(("grp", "ctx"), "kvh", None),
        P(("grp", "ctx"), "kvh", None),
        P(("grp", "ctx")),
        P(("grp", "ctx"), None),
        P(("grp", "ctx"), None),
        P(("grp", "ctx"), None),
    )
    out_specs = P(("grp", "ctx"), "kvh", "sub", None)
    return jax.shard_map(functools.partial(shards, mesh.shape["ctx"]), mesh=mesh,
                         in_specs=in_specs, out_specs=out_specs, check_vma=False)
```

```python
import functools
import math

import jax
import jax.numpy as jnp
from jax import lax
from jax.experimental import pallas as pl
from jax.experimental.pallas import tpu as pltpu
from jax.sharding import PartitionSpec as P

BLK = 128
MESH = pl.DeviceIdType.MESH


def attend(n, q_hbm, nk_hbm, nv_hbm, ck_hbm, cv_hbm, vp_ref, vl_ref, sl_ref, cnt_ref, o_ref,
           q_raw, nk_raw, nv_raw, ck_raw, cv_raw, q_ref, own_ref, new_ref, sort_kv, sort_q,
           pool, slash_raw, slash, acc, peak, total, rounded, fade,
           hop_send, hop_recv, sib_send, sib_recv, sl_sem, in_sem):
    z = lax.axis_index("ctx")
    s = lax.axis_index("sub")
    heads, rows, head_dim = q_ref.shape
    groups = rows // BLK
    wide = heads * BLK
    loads = [pltpu.make_async_copy(src, dst, in_sem.at[i]) for i, (src, dst) in enumerate(
        [(ck_hbm, ck_raw), (cv_hbm, cv_raw), (nk_hbm, nk_raw), (nv_hbm, nv_raw), (q_hbm, q_raw)])]
    loads[0].start()
    c = math.log2(math.e) / math.sqrt(head_dim)
    has_left = z > 0
    has_right = z < n - 1
    sib_id = {"sub": 1 - s}

    barrier = pltpu.get_barrier_semaphore()
    pl.semaphore_signal(barrier, inc=1, device_id=sib_id, device_id_type=MESH)

    @pl.when(has_left)
    def _():
        pl.semaphore_signal(barrier, inc=1, device_id={"ctx": z - 1}, device_id_type=MESH)

    @pl.when(has_right)
    def _():
        pl.semaphore_signal(barrier, inc=1, device_id={"ctx": z + 1}, device_id_type=MESH)

    ids = lax.broadcasted_iota(jnp.int32, (wide, wide), 0)
    at = lax.broadcasted_iota(jnp.int32, (wide, wide), 1)
    sort_kv[...] = jnp.where(at == (ids % BLK) * heads + ids // BLK, 1.0, 0.0).astype(jnp.bfloat16)
    token = (ids % BLK) // groups
    sort_q[...] = jnp.where(at == (token * heads + ids // BLK) * groups + ids % groups,
                            1.0, 0.0).astype(jnp.bfloat16)

    def by_head(raw):
        return jnp.dot(sort_kv[...], raw, preferred_element_type=jnp.float32).astype(jnp.bfloat16)

    def put_keys(dst, raw):
        ordered = by_head(raw)
        for h in range(heads):
            dst[h] = ordered[h * BLK:(h + 1) * BLK]

    def put_values(dst, raw):
        ordered = lax.dot_general(raw, sort_kv[...], (((0,), (1,)), ((), ())),
                                  preferred_element_type=jnp.float32).astype(jnp.bfloat16)
        for h in range(heads):
            dst[h] = ordered[:, h * BLK:(h + 1) * BLK]

    def chosen(cache, b):
        return cache[vp_ref[b]]

    pl.semaphore_wait(barrier, 1 + has_left.astype(jnp.int32) + has_right.astype(jnp.int32))

    def hop(src_ref, src, kv, right):
        return pltpu.make_async_remote_copy(
            src_ref=src_ref, dst_ref=pool.at[src, s, kv],
            send_sem=hop_send.at[src, int(right), kv], recv_sem=hop_recv.at[src, kv],
            device_id={"ctx": z + 1 if right else z - 1}, device_id_type=MESH)

    def sib(src, kv):
        return pltpu.make_async_remote_copy(
            src_ref=pool.at[src, s, kv], dst_ref=pool.at[src, s, kv],
            send_sem=sib_send.at[src, kv], recv_sem=sib_recv.at[src, kv],
            device_id=sib_id, device_id_type=MESH)

    def sib_in(src, kv):
        return pltpu.make_async_remote_copy(
            src_ref=pool.at[src, 1 - s, kv], dst_ref=pool.at[src, 1 - s, kv],
            send_sem=sib_send.at[src, kv], recv_sem=sib_recv.at[src, kv],
            device_id=sib_id, device_id_type=MESH)

    def slash_hop(src_ref=nk_hbm):
        return pltpu.make_async_remote_copy(
            src_ref=src_ref, dst_ref=slash_raw.at[s],
            send_sem=sl_sem.at[0], recv_sem=sl_sem.at[1],
            device_id={"ctx": z + 1}, device_id_type=MESH)

    def slash_sib(part):
        return pltpu.make_async_remote_copy(
            src_ref=slash_raw.at[part], dst_ref=slash_raw.at[part],
            send_sem=sl_sem.at[2], recv_sem=sl_sem.at[3],
            device_id=sib_id, device_id_type=MESH)

    for part, src_ref in enumerate((nk_hbm, nv_hbm)):
        @pl.when(has_right & (s == part))
        def _():
            slash_hop(src_ref).start()

    def send_own(kv):
        @pl.when(has_right)
        def _():
            hop(own_ref.at[s, kv], z, kv, True).start()

        @pl.when(has_left)
        def _():
            hop(own_ref.at[s, kv], z, kv, False).start()

    loads[0].wait()
    loads[1].start()
    put_keys(own_ref.at[s, 0], chosen(ck_raw, s))
    for load in loads[2:]:
        load.start()
    send_own(0)
    loads[1].wait()
    put_values(own_ref.at[s, 1], chosen(cv_raw, s))
    send_own(1)
    loads[2].wait()
    loads[3].wait()
    put_keys(new_ref.at[0], nk_raw[...])
    put_values(new_ref.at[1], nv_raw[...])
    put_keys(own_ref.at[1 - s, 0], chosen(ck_raw, 1 - s))
    put_values(own_ref.at[1 - s, 1], chosen(cv_raw, 1 - s))
    loads[4].wait()
    for part in range(rows // BLK):
        ordered = jnp.dot(sort_q[...], q_raw[part * wide:(part + 1) * wide],
                          preferred_element_type=jnp.float32).astype(jnp.bfloat16)
        for h in range(heads):
            q_ref[h, part * BLK:(part + 1) * BLK] = ordered[h * BLK:(h + 1) * BLK]

    def listed(slot):
        count = cnt_ref[0, 0]
        width = vl_ref.shape[1]
        if width <= 8:
            hit = jnp.int32(0)
            for i in range(width):
                hit = hit | jnp.where((vl_ref[0, i] == slot) & (i < count), 1, 0)
            return hit

        def one(i, hit):
            return hit | jnp.where((vl_ref[0, i] == slot) & (i < count), 1, 0)

        return lax.fori_loop(0, width, one, jnp.int32(0))

    def score(keys, q):
        return lax.dot_general(keys, q, (((1,), (1,)), ((), ())),
                               preferred_element_type=jnp.float32)

    def take_keys(side, blocks, first=False):
        for h in range(heads):
            q = q_ref[h]
            raw = []
            tops = []
            for keys, seen in blocks:
                scores = score(keys[h], q)
                if seen is None:
                    key_id = lax.broadcasted_iota(jnp.int32, scores.shape, 0)
                    row_id = lax.broadcasted_iota(jnp.int32, scores.shape, 1) // groups
                    scores = jnp.where(key_id <= row_id, scores, -jnp.inf)
                top = jnp.max(scores, axis=0, keepdims=True)
                if seen is not None:
                    top = jnp.where(seen > 0, top, -jnp.inf)
                raw.append(scores)
                tops.append(top)
            high = functools.reduce(jnp.maximum, tops)
            if not first:
                old = peak[h]
                high = jnp.maximum(old, high)
                factor = jnp.exp2((old - high) * c)
                fade[side, h] = factor
            peak[h] = high
            sums = []
            for i, ((_, seen), scores) in enumerate(zip(blocks, raw)):
                base = high if seen is None else jnp.where(seen > 0, high, jnp.inf)
                weights = jnp.exp2((scores - base) * c)
                sums.append(jnp.sum(weights, axis=0, keepdims=True))
                rounded[side, h, i * BLK:(i + 1) * BLK] = weights.astype(jnp.bfloat16)
            add = sum(sums[1:], sums[0])
            total[h] = add if first else total[h] * fade[side, h] + add

    def take_values(side, blocks, first=False):
        depth = len(blocks) * BLK
        for h in range(heads):
            values = jnp.concatenate([values[h] for values in blocks], 1)
            add = jnp.dot(values, rounded[side, h, :depth], preferred_element_type=jnp.float32)
            acc[h] = add if first else acc[h] * fade[side, h] + add

    take_keys(0, [(new_ref.at[0], None)]
              + [(own_ref.at[b, 0], listed(2 * z + b)) for b in range(2)], first=True)
    take_values(0, [new_ref.at[1]] + [own_ref.at[b, 1] for b in range(2)], first=True)

    @pl.when(has_left)
    def _():
        slash_hop().wait_recv()
        slash_sib(s).start()

    def arrive(src, kv, right):
        hop(own_ref.at[s, kv], src, kv, right).wait_recv()

        @pl.when(has_right if right else has_left)
        def _():
            hop(pool.at[src, s, kv], src, kv, right).start()

        sib(src, kv).start()

    def step(d, carry):
        sides = ((z + d, z + d < n, False), (z - d, z - d >= 0, True))
        for kv in range(2):
            for src, there, right in sides:
                @pl.when(there)
                def _():
                    arrive(src, kv, right)

            for side, (src, there, right) in enumerate(sides):
                @pl.when(there)
                def _():
                    sib_in(src, kv).wait_recv()
                    if kv == 0:
                        take_keys(side, [(pool.at[src, b, 0], listed(2 * src + b))
                                         for b in range(2)])
                    else:
                        take_values(side, [pool.at[src, b, 1] for b in range(2)])

        @pl.when((d == 1) & has_left)
        def _():
            slash_sib(1 - s).wait_recv()
            put_keys(slash.at[0], slash_raw[0])
            put_values(slash.at[1], slash_raw[1])
            back = jnp.int32(0)
            for i in range(sl_ref.shape[1]):
                back = back | jnp.where((sl_ref[0, i] == 1) & (i < cnt_ref[0, 1]), 1, 0)
            take_keys(0, [(slash.at[0], back)])
            take_values(0, [slash.at[1]])

        return carry

    lax.fori_loop(1, n, step, 0)

    for part in range(rows // BLK):
        lanes = slice(part * BLK, (part + 1) * BLK)
        done = jnp.concatenate(
            [(acc[h, :, lanes] / total[h, :, lanes]).astype(jnp.bfloat16) for h in range(heads)], 1)
        o_ref[part * wide:(part + 1) * wide] = lax.dot_general(
            sort_q[...], done, (((0,), (1,)), ((), ())),
            preferred_element_type=jnp.float32).astype(o_ref.dtype)

    def drain(src, carry):
        for kv in range(2):
            @pl.when(has_right & (src <= z))
            def _():
                hop(own_ref.at[s, kv], src, kv, True).wait_send()

            @pl.when(has_left & (src >= z))
            def _():
                hop(own_ref.at[s, kv], src, kv, False).wait_send()

            @pl.when(src != z)
            def _():
                sib(src, kv).wait_send()
        return carry

    lax.fori_loop(0, n, drain, 0)

    @pl.when(has_right)
    def _():
        slash_hop().wait_send()

    @pl.when(has_left)
    def _():
        slash_sib(s).wait_send()

BITS = 5
PACK = 6
OWN, GUEST, ALONE = 4, 5, 6
IDLE = (6, 4 * GUEST)
GUESTS = 1
EARLY = 2


NONE = (-1, -1)
QUEST = (-2, 0)
SLASH = (-3, 0)
VALUES = (-4, 0)
READY = (-5, 0)


def plan(heads):
    zero = [(NONE, (0, 0), 0), (NONE, (0, ALONE), 0), (NONE, (1, 0), 0), ((1, 0), (1, ALONE), 0), (NONE, (2, 0), 0),
        (NONE, (2, ALONE), 0), ((1, 1), (0, 1), 0), (NONE, (3, 0), 0), (NONE, (3, ALONE), 0), ((1, 2), (1, 1), 0),
        (NONE, NONE, 0), ((1, 3), NONE, 0), (NONE, (2, 1), 0), (NONE, NONE, 0), (NONE, (3, 1), 0), ((2, 0), NONE, 0),
        ((2, 1), NONE, 0), (NONE, (0, 2), 0), (NONE, NONE, 0), (NONE, (1, 2), 0), ((2, 2), NONE, 0),
        ((2, 3), NONE, 0), (NONE, (2, 2), 0), (NONE, NONE, 0), (NONE, (3, 2), 0), ((3, 0), NONE, 0),
        ((3, 1), NONE, 0), (NONE, (0, 3), 0), (NONE, NONE, 0), (NONE, (1, 3), 0), ((3, 2), NONE, 16),
        ((3, 3), NONE, 0), (NONE, (2, 3), 0), (VALUES, (3, 3), 0), (READY, NONE, 0)]
    one = [((0, 0), (0, 1), 0), ((2, 0), (1, 1), 0), ((0, 3), (2, 1), 0), (NONE, (0, 0), 0), ((2, 1), (0, 2), 0),
        ((0, 1), (3, 0), 4), (NONE, (3, 1), 0), (NONE, (1, 2), 0), ((2, 2), (1, 0), 0), ((0, 2), NONE, 8),
        ((2, 3), NONE, 0), (NONE, (2, 2), 0), (NONE, (2, 0), 0), (NONE, NONE, 0), ((3, 0), (3, 2), 0),
        (SLASH, NONE, 0), ((3, 1), NONE, 0), (NONE, (0, 3), 0), (NONE, NONE, 0), (NONE, (0, OWN), 0),
        ((3, 2), (1, 3), 0), (NONE, (1, OWN), 0), (NONE, (2, OWN), 16), ((3, 3), (2, 3), 0), (NONE, (3, OWN), 0),
        (NONE, NONE, 0), (NONE, (3, 3), 0), (NONE, NONE, 0)]
    two = [((1, 0), (0, 2), 0), ((3, 0), (1, 2), 0), (NONE, (2, 2), 0), ((1, 3), (0, 1), 0), ((3, 1), (0, 3), 0),
        (NONE, (3, 2), 0), ((1, 1), (3, 1), 0), ((3, 2), (1, 3), 0), (NONE, NONE, 0), ((0, 0), (1, 1), 0),
        ((3, 3), (2, 3), 0), (NONE, NONE, 0), ((0, 3), (0, 0), 0), (NONE, (3, 3), 0), (NONE, NONE, 0),
        (NONE, (3, 0), 0), ((0, 1), NONE, 0), (QUEST, NONE, 0), (NONE, (4, 2), 0), ((1, 2), (4, GUEST), 0),
        (NONE, (4, 1), 0), (NONE, (4, 0), 0), (NONE, (1, 0), 0), ((0, 2), (2, 1), 2), (NONE, NONE, 0),
        (NONE, (2, 0), 0), (NONE, NONE, 0), (SLASH, NONE, 0), (NONE, (0, OWN), 0), (NONE, (1, OWN), 0),
        (NONE, (2, OWN), 16), (NONE, (3, OWN), 0), (NONE, NONE, 0)]
    three = [(NONE, (0, 3), 0), ((2, 0), (1, 3), 0), (NONE, (2, 3), 0), (NONE, (3, 3), 0), (NONE, (0, 2), 0),
        (SLASH, (3, ALONE), 0), (NONE, NONE, 0), (NONE, (0, OWN), 0), ((2, 1), (1, OWN), 0), (NONE, (2, OWN), 0),
        (NONE, NONE, 0), ((2, 2), (1, 2), 0), (NONE, NONE, 0), ((1, 0), NONE, 0), (NONE, (2, 2), 0), (NONE, NONE, 0),
        (NONE, (0, 1), 0), ((1, 1), NONE, 0), ((0, 0), NONE, 0), (NONE, (1, 1), 0), (NONE, NONE, 0),
        (NONE, (0, 0), 0), ((0, 1), NONE, 0), ((1, 2), NONE, 0), (NONE, (1, 0), 0), (NONE, NONE, 16),
        (NONE, (2, 1), 0), ((0, 2), NONE, 0), (NONE, (2, 0), 0), (NONE, NONE, 0)]

    def build(z, table):
        out, before, used = [], NONE, set()
        for recv, now, flags in table + [(NONE, NONE, 0)]:
            kind, message = (1, recv[0] * 4 + recv[1]) if recv[0] >= 0 else (-recv[0] if recv != NONE else 0, 0)
            slot, src = now
            h = slot if slot < heads else slot - GUESTS
            key = OWN if src == OWN else (src, h)
            first = now != NONE and key not in used and src not in (z, GUEST, ALONE)
            used.add(key)
            code = (slot + (8 if first else 0), src * 4 + h) if now != NONE else IDLE
            busy = now != NONE or before != NONE
            out.append((kind, message) + code + (int(busy) | flags,))
            before = now
        return out

    return [build(z, table) for z, table in enumerate((zero, one, two, three))]


def chain(n, q_hbm, nk_hbm, nv_hbm, ck_hbm, cv_hbm, vp_hbm, vl_hbm, sl_hbm, cnt_hbm, o_ref,
          vp_ref, vl_ref, sl_ref, cnt_ref,
          q_raw, nk_raw, nv_raw, ck_raw, cv_raw, q_ref, sort_kv, sort_q, ext,
          pool, acc, peak, total, mask, part_acc, part_stat, scores_a, scores_b, top_a, top_b, most,
          send_sem, hop_recv, sib_recv, sl_sem, q_sem, part_sem, in_sem, table_sem, end_sem, ready):
    z = lax.axis_index("ctx")
    s = lax.axis_index("sub")
    heads = pool.shape[1]
    head_dim, rows = acc.shape[1:]
    groups = rows // BLK
    wide = heads * BLK
    last = n - 1
    stay = heads - GUESTS
    loads = [pltpu.make_async_copy(src, dst, in_sem.at[i]) for i, (src, dst) in enumerate(
        [(ck_hbm, ck_raw), (cv_hbm, cv_raw), (nk_hbm, nk_raw), (nv_hbm, nv_raw), (q_hbm, q_raw)])]
    tables = [pltpu.make_async_copy(src, dst, table_sem.at[i]) for i, (src, dst) in enumerate(
        [(vp_hbm, vp_ref), (vl_hbm, vl_ref), (sl_hbm, sl_ref), (cnt_hbm, cnt_ref)])]
    loads[0].start()
    loads[1].start()
    for table in tables:
        table.start()
    c = math.log2(math.e) / math.sqrt(head_dim)
    has_left = z > 0
    has_right = z < last
    sib_id = {"sub": 1 - s}
    inner = has_left & has_right

    barrier = pltpu.get_barrier_semaphore()
    pl.semaphore_signal(barrier, inc=1, device_id=sib_id, device_id_type=MESH)

    @pl.when(has_right)
    def _():
        pl.semaphore_signal(barrier, inc=1, device_id={"ctx": z + 1}, device_id_type=MESH)

    ids = lax.broadcasted_iota(jnp.int32, (wide, wide), 0)
    at = lax.broadcasted_iota(jnp.int32, (wide, wide), 1)
    sort_kv[...] = jnp.where(at == (ids % BLK) * heads + ids // BLK, 1.0, 0.0).astype(jnp.bfloat16)

    pl.semaphore_wait(barrier, 1 + has_left.astype(jnp.int32))

    @pl.when(has_left)
    def _():
        pl.semaphore_signal(ready, inc=1, device_id={"ctx": z - 1}, device_id_type=MESH)

    def put_keys(raw, put, those=range(heads)):
        ordered = jnp.dot(sort_kv[those.start * BLK:those.stop * BLK], raw,
                          preferred_element_type=jnp.float32).astype(jnp.bfloat16)
        for i, h in enumerate(those):
            put(h, ordered[i * BLK:(i + 1) * BLK])

    def put_values(raw, put):
        ordered = lax.dot_general(raw, sort_kv[...], (((0,), (1,)), ((), ())),
                                  preferred_element_type=jnp.float32).astype(jnp.bfloat16)
        for h in range(heads):
            put(h, ordered[:, h * BLK:(h + 1) * BLK])

    def put_pool(b, kv):
        def put(h, block):
            pool[z, h, b, kv] = block
        return put

    def put_new(kv):
        def put(h, block):
            pool[OWN, h, 0, kv] = block
            pool[GUEST, h, 0, kv] = block
            pool[GUEST, h, 1, kv] = jnp.zeros_like(block)
        return put

    def hop(src, h, right):
        return pltpu.make_async_remote_copy(
            src_ref=pool.at[src, h, s], dst_ref=pool.at[src, h, s],
            send_sem=send_sem.at[int(right)], recv_sem=hop_recv.at[src if right else src - 1, h],
            device_id={"ctx": z + 1 if right else z - 1}, device_id_type=MESH)

    def first_hop(h, kv, right):
        return pltpu.make_async_remote_copy(
            src_ref=pool.at[z, h, s, kv], dst_ref=pool.at[z, h, s, kv],
            send_sem=send_sem.at[int(right)], recv_sem=hop_recv.at[z if right else z - 1, h],
            device_id={"ctx": z + 1 if right else z - 1}, device_id_type=MESH)

    def sib(src, h, part):
        return pltpu.make_async_remote_copy(
            src_ref=pool.at[src, h, part], dst_ref=pool.at[src, h, part],
            send_sem=send_sem.at[2], recv_sem=sib_recv.at[src - (src > z).astype(jnp.int32), h],
            device_id=sib_id, device_id_type=MESH)

    def end_hop(kv):
        return pltpu.make_async_remote_copy(
            src_ref=pool.at[last, heads - 1, s, kv], dst_ref=pool.at[last, heads - 1, s, kv],
            send_sem=send_sem.at[0], recv_sem=end_sem.at[0] if kv else hop_recv.at[last - 1, heads - 1],
            device_id={"ctx": z - 1}, device_id_type=MESH)

    def end_sib(kv, part):
        block = pool.at[last, heads - 1, part, kv]
        return pltpu.make_async_remote_copy(
            src_ref=block, dst_ref=block,
            send_sem=send_sem.at[2], recv_sem=end_sem.at[1] if kv else sib_recv.at[last - 1, heads - 1],
            device_id=sib_id, device_id_type=MESH)

    def slash_hop(count):
        return pltpu.make_async_remote_copy(
            src_ref=pool.at[OWN, pl.ds(0, count), 0, s], dst_ref=pool.at[OWN, pl.ds(0, count), 1, s],
            send_sem=sl_sem.at[0], recv_sem=sl_sem.at[1],
            device_id={"ctx": z + 1}, device_id_type=MESH)

    def slash_sib(count, part):
        block = pool.at[OWN, pl.ds(0, count), 1, part]
        return pltpu.make_async_remote_copy(
            src_ref=block, dst_ref=block,
            send_sem=sl_sem.at[2], recv_sem=sl_sem.at[3],
            device_id=sib_id, device_id_type=MESH)

    def guest_q(g):
        return pltpu.make_async_remote_copy(
            src_ref=q_ref.at[stay + g, pl.ds(0, head_dim)], dst_ref=q_ref.at[heads + g, pl.ds(0, head_dim)],
            send_sem=q_sem.at[0, g], recv_sem=q_sem.at[1, g],
            device_id={"ctx": z - 1}, device_id_type=MESH)

    def guest_mask():
        return pltpu.make_async_remote_copy(
            src_ref=mask.at[0], dst_ref=mask.at[1],
            send_sem=q_sem.at[0, GUESTS], recv_sem=q_sem.at[1, GUESTS],
            device_id={"ctx": z - 1}, device_id_type=MESH)

    def guest_part(g):
        return [pltpu.make_async_remote_copy(
            src_ref=ref.at[g], dst_ref=ref.at[g],
            send_sem=part_sem.at[0, g, i], recv_sem=part_sem.at[1, g, i],
            device_id={"ctx": z + 1}, device_id_type=MESH)
            for i, ref in enumerate((part_acc, part_stat))]

    def leftward(*blocks):
        @pl.when(has_left)
        def _():
            for h, kv in blocks:
                first_hop(h, kv, False).start()

    for table in tables:
        table.wait()
    loads[0].wait()
    put_keys(ck_raw[vp_ref[s]], put_pool(s, 0), range(EARLY))
    leftward(*[(h, 0) for h in range(EARLY)])
    put_keys(ck_raw[vp_ref[s]], put_pool(s, 0), range(EARLY, heads))
    for load in loads[2:]:
        load.start()
    loads[1].wait()
    put_values(cv_raw[vp_ref[s]], put_pool(s, 1))
    leftward((0, 1), (1, 1), *[(h, kv) for h in range(2, heads) for kv in range(2)])

    @pl.when(has_right)
    def _():
        pl.semaphore_wait(ready, 1)

    @pl.when(z == 0)
    def _():
        for h in (0, 3, 1, 2):
            for kv in range(2):
                first_hop(h, kv, True).start()

    @pl.when(z == 1)
    def _():
        for h in (0, 3, 1):
            for kv in range(2):
                first_hop(h, kv, True).start()

    @pl.when(z == 2)
    def _():
        for kv in range(2):
            first_hop(0, kv, True).start()

    loads[2].wait()
    loads[3].wait()
    put_keys(nk_raw[...], put_new(0))
    put_values(nv_raw[...], put_new(1))

    @pl.when(z == 2)
    def _():
        slash_hop(stay).start()
        for h in range(1, stay):
            for kv in range(2):
                first_hop(h, kv, True).start()

    token = (ids % BLK) // groups
    sort_q[...] = jnp.where(at == (token * heads + ids // BLK) * groups + ids % groups,
                            1.0, 0.0).astype(jnp.bfloat16)
    loads[4].wait()
    for part in range(rows // BLK):
        ordered = lax.dot_general(q_raw[part * wide:(part + 1) * wide], sort_q[...], (((0,), (1,)), ((), ())),
                                  preferred_element_type=jnp.float32).astype(jnp.bfloat16)
        for h in range(heads):
            q_ref[h, 0:head_dim, part * BLK:(part + 1) * BLK] = ordered[:, h * BLK:(h + 1) * BLK]

    def unseen(hit):
        return jnp.full((1, BLK), jnp.where(hit > 0, 0.0, jnp.inf), jnp.float32)

    for slot in range(2 * n):
        hit = jnp.int32(0)
        for i in range(vl_ref.shape[1]):
            hit = hit | jnp.where((vl_ref[0, i] == slot) & (i < cnt_ref[0, 0]), 1, 0)
        mask[0, slot:slot + 1] = unseen(hit)
    hit = jnp.int32(0)
    for i in range(sl_ref.shape[1]):
        hit = hit | jnp.where((sl_ref[0, i] == 1) & (i < cnt_ref[0, 1]), 1, 0)
    mask[0, 2 * OWN:2 * OWN + 2] = jnp.concatenate([jnp.zeros((1, BLK), jnp.float32), unseen(hit)], 0)
    mask[0, 2 * GUEST:2 * GUEST + 2] = jnp.concatenate([unseen(hit), jnp.full((1, BLK), jnp.inf, jnp.float32)], 0)
    mask[0, 2 * ALONE:2 * ALONE + 2] = jnp.concatenate(
        [jnp.zeros((1, BLK), jnp.float32), jnp.full((1, BLK), jnp.inf, jnp.float32)], 0)

    @pl.when(z == 0)
    def _():
        slash_hop(heads).start()

    @pl.when(z == last)
    def _():
        for g in range(GUESTS):
            guest_q(g).start()
        guest_mask().start()

    put_keys(ck_raw[vp_ref[1 - s]], put_pool(1 - s, 0))
    put_values(cv_raw[vp_ref[1 - s]], put_pool(1 - s, 1))

    key_id = lax.broadcasted_iota(jnp.int32, (BLK, rows), 0)
    row_id = lax.broadcasted_iota(jnp.int32, (BLK, rows), 1) // groups
    later = jnp.where(key_id > row_id, -1e30, 0.0).astype(jnp.bfloat16)
    slots = acc.shape[0]
    for slot in range(slots):
        q_ref[slot, head_dim:] = later if slot < heads else jnp.zeros_like(later)
        acc[slot] = jnp.zeros_like(acc[slot])
        total[slot] = jnp.zeros_like(total[slot])
        peak[slot] = jnp.full_like(peak[slot], -1e30)
    q_ref[slots - 1, 0:head_dim] = jnp.zeros_like(later)
    one_at = lax.broadcasted_iota(jnp.int32, (BLK, BLK), 0) == lax.broadcasted_iota(jnp.int32, (BLK, BLK), 1)
    ext[0] = jnp.zeros((BLK, BLK), jnp.bfloat16)
    ext[1] = jnp.where(one_at, 1.0, 0.0).astype(jnp.bfloat16)
    scores_b[...] = jnp.zeros_like(scores_b)
    top_b[...] = jnp.zeros_like(top_b)

    def spread(row):
        return jnp.concatenate([row] * groups, 1)

    def place(src):
        return src - src // ALONE

    def hidden(slot, src, b):
        return spread(mask[(slot // heads) % 2 * (1 - slot // (slots - 1)), pl.ds(2 * src + b, 1)])

    def ahead(unit, scores, top):
        slot, src, h = unit
        q = q_ref[slot]
        high = None
        for b in range(2):
            causal = (src // OWN) * (1 - src % 2) if b == 0 else 0
            keys = jnp.concatenate([pool[place(src), h, b, 0], ext[causal]], 1)
            found = jnp.dot(keys, q, preferred_element_type=jnp.float32)
            scores[b * BLK:(b + 1) * BLK] = found
            part = jnp.max(found, axis=0, keepdims=True) - hidden(slot, src, b)
            high = part if high is None else jnp.maximum(high, part)
        top[...] = high

    def behind(unit, scores, top):
        slot, src, h = unit
        old = peak[slot]
        high = jnp.maximum(old, top[...])
        factor = jnp.exp2((old - high) * c)
        peak[slot] = high
        weights = [jnp.exp2((scores[b * BLK:(b + 1) * BLK] - (high + hidden(slot, src, b))) * c)
                   .astype(jnp.bfloat16) for b in range(2)]
        values = jnp.concatenate([pool[place(src), h, b, 1] for b in range(2)], 1)
        values = jnp.concatenate([values, jnp.ones((16, 2 * BLK), jnp.bfloat16)], 0)
        add = jnp.dot(values, jnp.concatenate(weights, 0), preferred_element_type=jnp.float32)
        acc[slot] = acc[slot] * factor + add[:head_dim]
        total[slot] = total[slot] * factor + add[head_dim:head_dim + 1]

    def ordered(part, those):
        lanes = slice(part * BLK, (part + 1) * BLK)
        done = jnp.concatenate(
            [(acc[h, :, lanes] * (1.0 / total[h, :, lanes])).astype(jnp.bfloat16) for h in those], 1)
        return lax.dot_general(sort_q[those.start * BLK:those.stop * BLK], done, (((0,), (1,)), ((), ())),
                               preferred_element_type=jnp.float32)

    def drain():
        def sent(kind, sources, count):
            blocks = pool.at[pl.ds(0, sources), pl.ds(0, count), s]
            pltpu.make_async_copy(blocks, blocks, send_sem.at[kind]).wait()

        for index in range(n):
            right = heads if index < last - 1 else stay if index < last else 0

            @pl.when(z == index)
            def _():
                if right:
                    sent(1, index + 1, right)
                    slash_hop(right).wait_send()
                if index > 0:
                    sent(0, n - index, heads)
                    slash_sib(heads if index < last else stay, s).wait_send()
                sent(2, n - 1, heads if index < last else stay)
                if index == last:
                    guest_mask().wait_send()
                    for g in range(GUESTS):
                        guest_q(g).wait_send()

    roles = plan(heads)
    steps = max(len(role) for role in roles)
    steps += steps % 2
    roles = [role + [(0, 0) + IDLE + (0,)] * (steps - len(role)) for role in roles]

    def by_role(values):
        out = jnp.int32(values[-1])
        for i in reversed(range(len(values) - 1)):
            out = jnp.where(z == i, jnp.int32(values[i]), out)
        return out

    words = [[by_role([sum(step[field] << (BITS * i) for i, step in enumerate(role[start:start + PACK]))
                       for role in roles]) for start in range(0, steps, PACK)] for field in range(5)]

    def step(t, before, bufs, old_bufs):
        def look(field):
            word = words[field][-1]
            for i in reversed(range(len(words[field]) - 1)):
                word = jnp.where(t // PACK == i, words[field][i], word)
            return lax.shift_right_logical(word, BITS * (t % PACK)) & (2 ** BITS - 1)

        kind, message, code, block, flags = [look(field) for field in range(5)]
        src, h = message // 4, message % 4

        end = (src == last) & (h == heads - 1)

        @pl.when((kind == 1) & end & (z == 0))
        def _():
            end_hop(0).wait_recv()
            end_sib(0, s).start()

        @pl.when(kind == 4)
        def _():
            end_hop(1).wait_recv()
            end_sib(1, s).start()

        @pl.when(kind == 5)
        def _():
            end_sib(1, 1 - s).wait_recv()

        @pl.when((kind == 1) & jnp.logical_not(end & (z == 0)))
        def _():
            block = pool.at[src, h, s]
            pltpu.make_async_copy(block, block, hop_recv.at[src - (src > z).astype(jnp.int32), h]).wait()

            @pl.when((src > z) & ((z > 1) | ((z == 1) & jnp.logical_not(end))))
            def _():
                hop(src, h, False).start()

            @pl.when((z == 1) & end)
            def _():
                end_hop(0).start()
                end_hop(1).start()

            @pl.when((src < z) & ((z < last - 1) | ((z == last - 1) & (h < stay))))
            def _():
                hop(src, h, True).start()

            sib(src, h, s).start()

        @pl.when((flags // 4) % 2 == 1)
        def _():
            for kv in range(2):
                first_hop(2, kv, True).start()

        @pl.when((flags // 8) % 2 == 1)
        def _():
            slash_hop(heads).start()

        @pl.when(kind == 2)
        def _():
            guest_mask().wait_recv()
            for g in range(GUESTS):
                guest_q(g).wait_recv()

        @pl.when((kind == 3) & has_right)
        def _():
            slash_hop(heads).wait_recv()
            slash_sib(heads, s).start()

        @pl.when((kind == 3) & (z == last))
        def _():
            slash_hop(stay).wait_recv()
            slash_sib(stay, s).start()

        unit = (code % 8, block // 4, block % 4)

        late = (unit[1] == last) & (unit[2] == heads - 1) & (z == 0)

        @pl.when((code > 7) & late)
        def _():
            end_sib(0, 1 - s).wait_recv()

        @pl.when((code > 7) & (unit[1] < OWN) & jnp.logical_not(late))
        def _():
            sib(unit[1], unit[2], 1 - s).wait_recv()

        @pl.when((code > 7) & (unit[1] == OWN) & has_right)
        def _():
            slash_sib(heads, 1 - s).wait_recv()

        @pl.when((code > 7) & (unit[1] == OWN) & (z == last))
        def _():
            slash_sib(stay, 1 - s).wait_recv()

        @pl.when(flags % 2 == 1)
        def _():
            ahead(unit, *bufs)
            behind(before, *old_bufs)

        @pl.when(flags // 16 == 1)
        def _():
            for part in range(rows // BLK):
                most[part * wide:(part + 1) * wide] = ordered(part, range(EARLY)).astype(o_ref.dtype)

        @pl.when((flags // 2) % 2 == 1)
        def _():
            g = 0
            part_acc[g] = acc[heads + g].astype(jnp.bfloat16)
            part_stat[g, 0:1] = peak[heads + g]
            part_stat[g, 1:2] = total[heads + g]
            for copy in guest_part(g):
                copy.start()

        return unit

    def two_steps(i, before):
        mid = step(2 * i, before, (scores_a, top_a), (scores_b, top_b))
        return step(2 * i + 1, mid, (scores_b, top_b), (scores_a, top_a))

    lengths = [max(t for t, step in enumerate(role) if step[0] or step[4]) + 1 for role in roles]
    idle = (jnp.int32(IDLE[0]), jnp.int32(GUEST), jnp.int32(0))
    lax.fori_loop(0, by_role([(length + 1) // 2 for length in lengths]), two_steps, idle)

    drain()

    @pl.when(z == last)
    def _():
        for g in range(GUESTS):
            for copy in guest_part(g):
                copy.wait_recv()
            slot = stay + g
            old, new = peak[slot], part_stat[g, 0:1]
            high = jnp.maximum(old, new)
            mine, theirs = jnp.exp2((old - high) * c), jnp.exp2((new - high) * c)
            acc[slot] = acc[slot] * mine + part_acc[g].astype(jnp.float32) * theirs
            total[slot] = total[slot] * mine + part_stat[g, 1:2] * theirs

    for part in range(rows // BLK):
        lines = slice(part * wide, (part + 1) * wide)
        o_ref[lines] = most[lines] + ordered(part, range(EARLY, heads)).astype(o_ref.dtype)

    @pl.when(z == last - 1)
    def _():
        for g in range(GUESTS):
            for copy in guest_part(g):
                copy.wait_send()


def store(o_vmem, o_hbm, sem):
    copies = sem.shape[0]
    rows = o_vmem.shape[0] // copies
    for i in range(copies):
        lines = pl.ds(i * rows, rows)
        pltpu.make_async_copy(o_vmem.at[lines], o_hbm.at[lines], sem.at[i]).start()
    for i in range(copies):
        lines = pl.ds(i * rows, rows)
        pltpu.make_async_copy(o_vmem.at[lines], o_hbm.at[lines], sem.at[i]).wait()


def chain_call(n, q, nk, nv, ck, cv, tables, heads, rows, head_dim):
    def vmem(*shape):
        return pltpu.VMEM(shape, jnp.bfloat16)

    def wide_vmem(*shape):
        return pltpu.VMEM(shape, jnp.float32)

    hbm = pl.BlockSpec(memory_space=pltpu.HBM)
    in_vmem = pl.BlockSpec(memory_space=pltpu.VMEM)
    dma = pltpu.SemaphoreType.DMA
    cached, wide = ck.shape[:2]
    slots = 7
    out = pl.pallas_call(
        functools.partial(chain, n),
        out_shape=pltpu.VMEM((heads * rows, head_dim), jnp.bfloat16),
        in_specs=[hbm] * 9,
        out_specs=in_vmem,
        scratch_shapes=[
            *[pltpu.SMEM(table.shape, table.dtype) for table in tables],
            vmem(heads * rows, head_dim), vmem(wide, head_dim), vmem(wide, head_dim),
            vmem(cached, wide, head_dim), vmem(cached, wide, head_dim),
            vmem(slots, 2 * head_dim, rows), vmem(wide, wide), vmem(wide, wide), vmem(2, BLK, BLK),
            vmem(n + 2, heads, 2, 2, BLK, head_dim),
            wide_vmem(slots, head_dim, rows), wide_vmem(slots, 1, rows), wide_vmem(slots, 1, rows),
            wide_vmem(2, 16, BLK), vmem(GUESTS, head_dim, rows), wide_vmem(GUESTS, 8, rows),
            wide_vmem(2 * BLK, rows), wide_vmem(2 * BLK, rows), wide_vmem(1, rows), wide_vmem(1, rows),
            vmem(heads * rows, head_dim),
            dma((3,)), dma((n - 1, heads)), dma((n - 1, heads)), dma((4,)),
            dma((2, GUESTS + 1)), dma((2, GUESTS, 2)), dma((5,)), dma((4,)), dma((2,)), pltpu.SemaphoreType.REGULAR,
        ],
        compiler_params=pltpu.CompilerParams(
            collective_id=0, has_side_effects=True, vmem_limit_bytes=60 * 2**20),
    )(*[pltpu.with_memory_space_constraint(x, pltpu.HBM) for x in (q, nk, nv, ck, cv, *tables)])
    return pl.pallas_call(
        store,
        out_shape=jax.ShapeDtypeStruct(out.shape, out.dtype),
        in_specs=[in_vmem],
        out_specs=hbm,
        scratch_shapes=[dma((4,))],
        compiler_params=pltpu.CompilerParams(vmem_limit_bytes=2**20),
    )(out)


def shards(n, queries, new_keys, new_values, cache_keys, cache_values,
           vertical_pool, vertical_lists, slash_lists, list_counts):
    tokens, heads, groups, head_dim = queries.shape
    rows = tokens * groups
    picked = vertical_pool.shape[0]

    def flat(x):
        return x.reshape(-1, head_dim)

    def vmem(*shape):
        return pltpu.VMEM(shape, jnp.bfloat16)

    hbm = pl.BlockSpec(memory_space=pltpu.HBM)
    smem = pl.BlockSpec(memory_space=pltpu.SMEM)
    dma = pltpu.SemaphoreType.DMA
    wide = heads * BLK
    cached = cache_keys.shape[0] // BLK
    if n == 4 and heads == 4 and picked == 2:
        out = chain_call(n, flat(queries), flat(new_keys), flat(new_values),
                         cache_keys.reshape(cached, wide, head_dim), cache_values.reshape(cached, wide, head_dim),
                         (vertical_pool, vertical_lists, slash_lists, list_counts), heads, rows, head_dim)
        return out.reshape(tokens, heads, groups, head_dim)
    out = pl.pallas_call(
        functools.partial(attend, n),
        out_shape=jax.ShapeDtypeStruct((tokens * heads * groups, head_dim), jnp.bfloat16),
        in_specs=[hbm] * 5 + [smem] * 4,
        out_specs=pl.BlockSpec(memory_space=pltpu.VMEM),
        scratch_shapes=[
            vmem(heads * rows, head_dim), vmem(wide, head_dim), vmem(wide, head_dim),
            vmem(cached, wide, head_dim), vmem(cached, wide, head_dim),
            vmem(heads, rows, head_dim), vmem(picked, 2, heads, BLK, head_dim),
            vmem(2, heads, BLK, head_dim), vmem(wide, wide), vmem(wide, wide),
            vmem(n, picked, 2, heads, BLK, head_dim),
            vmem(2, wide, head_dim), vmem(2, heads, BLK, head_dim),
            pltpu.VMEM((heads, head_dim, rows), jnp.float32),
            pltpu.VMEM((heads, 1, rows), jnp.float32),
            pltpu.VMEM((heads, 1, rows), jnp.float32),
            vmem(2, heads, 3 * BLK, rows), pltpu.VMEM((2, heads, 1, rows), jnp.float32),
            dma((n, 2, 2)), dma((n, 2)), dma((n, 2)), dma((n, 2)), dma((4,)), dma((5,)),
        ],
        compiler_params=pltpu.CompilerParams(
            collective_id=0, has_side_effects=True, vmem_limit_bytes=60 * 2**20),
    )(flat(queries), flat(new_keys), flat(new_values), cache_keys.reshape(cached, wide, head_dim),
      cache_values.reshape(cached, wide, head_dim),
      vertical_pool, vertical_lists, slash_lists, list_counts)
    return out.reshape(tokens, heads, groups, head_dim)


def solution(mesh):
    in_specs = (
        P(("grp", "ctx"), "kvh", "sub", None),
        P(("grp", "ctx"), "kvh", None),
        P(("grp", "ctx"), "kvh", None),
        P(("grp", "ctx"), "kvh", None),
        P(("grp", "ctx"), "kvh", None),
        P(("grp", "ctx")),
        P(("grp", "ctx"), None),
        P(("grp", "ctx"), None),
        P(("grp", "ctx"), None),
    )
    out_specs = P(("grp", "ctx"), "kvh", "sub", None)
    return jax.shard_map(functools.partial(shards, mesh.shape["ctx"]), mesh=mesh,
                         in_specs=in_specs, out_specs=out_specs, check_vma=False)
```

```python
import functools
import math

import jax
import jax.numpy as jnp
from jax import lax
from jax.experimental import pallas as pl
from jax.experimental.pallas import tpu as pltpu
from jax.sharding import PartitionSpec as P

BLK = 128
MESH = pl.DeviceIdType.MESH


def attend(n, q_hbm, nk_hbm, nv_hbm, ck_hbm, cv_hbm, vp_ref, vl_ref, sl_ref, cnt_ref, o_ref,
           q_raw, nk_raw, nv_raw, ck_raw, cv_raw, q_ref, own_ref, new_ref, sort_kv, sort_q,
           pool, slash_raw, slash, acc, peak, total, rounded, fade,
           hop_send, hop_recv, sib_send, sib_recv, sl_sem, in_sem):
    z = lax.axis_index("ctx")
    s = lax.axis_index("sub")
    heads, rows, head_dim = q_ref.shape
    groups = rows // BLK
    wide = heads * BLK
    loads = [pltpu.make_async_copy(src, dst, in_sem.at[i]) for i, (src, dst) in enumerate(
        [(ck_hbm, ck_raw), (cv_hbm, cv_raw), (nk_hbm, nk_raw), (nv_hbm, nv_raw), (q_hbm, q_raw)])]
    loads[0].start()
    c = math.log2(math.e) / math.sqrt(head_dim)
    has_left = z > 0
    has_right = z < n - 1
    sib_id = {"sub": 1 - s}

    barrier = pltpu.get_barrier_semaphore()
    pl.semaphore_signal(barrier, inc=1, device_id=sib_id, device_id_type=MESH)

    @pl.when(has_left)
    def _():
        pl.semaphore_signal(barrier, inc=1, device_id={"ctx": z - 1}, device_id_type=MESH)

    @pl.when(has_right)
    def _():
        pl.semaphore_signal(barrier, inc=1, device_id={"ctx": z + 1}, device_id_type=MESH)

    ids = lax.broadcasted_iota(jnp.int32, (wide, wide), 0)
    at = lax.broadcasted_iota(jnp.int32, (wide, wide), 1)
    sort_kv[...] = jnp.where(at == (ids % BLK) * heads + ids // BLK, 1.0, 0.0).astype(jnp.bfloat16)
    token = (ids % BLK) // groups
    sort_q[...] = jnp.where(at == (token * heads + ids // BLK) * groups + ids % groups,
                            1.0, 0.0).astype(jnp.bfloat16)

    def by_head(raw):
        return jnp.dot(sort_kv[...], raw, preferred_element_type=jnp.float32).astype(jnp.bfloat16)

    def put_keys(dst, raw):
        ordered = by_head(raw)
        for h in range(heads):
            dst[h] = ordered[h * BLK:(h + 1) * BLK]

    def put_values(dst, raw):
        ordered = lax.dot_general(raw, sort_kv[...], (((0,), (1,)), ((), ())),
                                  preferred_element_type=jnp.float32).astype(jnp.bfloat16)
        for h in range(heads):
            dst[h] = ordered[:, h * BLK:(h + 1) * BLK]

    def chosen(cache, b):
        return cache[vp_ref[b]]

    pl.semaphore_wait(barrier, 1 + has_left.astype(jnp.int32) + has_right.astype(jnp.int32))

    def hop(src_ref, src, kv, right):
        return pltpu.make_async_remote_copy(
            src_ref=src_ref, dst_ref=pool.at[src, s, kv],
            send_sem=hop_send.at[src, int(right), kv], recv_sem=hop_recv.at[src, kv],
            device_id={"ctx": z + 1 if right else z - 1}, device_id_type=MESH)

    def sib(src, kv):
        return pltpu.make_async_remote_copy(
            src_ref=pool.at[src, s, kv], dst_ref=pool.at[src, s, kv],
            send_sem=sib_send.at[src, kv], recv_sem=sib_recv.at[src, kv],
            device_id=sib_id, device_id_type=MESH)

    def sib_in(src, kv):
        return pltpu.make_async_remote_copy(
            src_ref=pool.at[src, 1 - s, kv], dst_ref=pool.at[src, 1 - s, kv],
            send_sem=sib_send.at[src, kv], recv_sem=sib_recv.at[src, kv],
            device_id=sib_id, device_id_type=MESH)

    def slash_hop(src_ref=nk_hbm):
        return pltpu.make_async_remote_copy(
            src_ref=src_ref, dst_ref=slash_raw.at[s],
            send_sem=sl_sem.at[0], recv_sem=sl_sem.at[1],
            device_id={"ctx": z + 1}, device_id_type=MESH)

    def slash_sib(part):
        return pltpu.make_async_remote_copy(
            src_ref=slash_raw.at[part], dst_ref=slash_raw.at[part],
            send_sem=sl_sem.at[2], recv_sem=sl_sem.at[3],
            device_id=sib_id, device_id_type=MESH)

    for part, src_ref in enumerate((nk_hbm, nv_hbm)):
        @pl.when(has_right & (s == part))
        def _():
            slash_hop(src_ref).start()

    def send_own(kv):
        @pl.when(has_right)
        def _():
            hop(own_ref.at[s, kv], z, kv, True).start()

        @pl.when(has_left)
        def _():
            hop(own_ref.at[s, kv], z, kv, False).start()

    loads[0].wait()
    loads[1].start()
    put_keys(own_ref.at[s, 0], chosen(ck_raw, s))
    for load in loads[2:]:
        load.start()
    send_own(0)
    loads[1].wait()
    put_values(own_ref.at[s, 1], chosen(cv_raw, s))
    send_own(1)
    loads[2].wait()
    loads[3].wait()
    put_keys(new_ref.at[0], nk_raw[...])
    put_values(new_ref.at[1], nv_raw[...])
    put_keys(own_ref.at[1 - s, 0], chosen(ck_raw, 1 - s))
    put_values(own_ref.at[1 - s, 1], chosen(cv_raw, 1 - s))
    loads[4].wait()
    for part in range(rows // BLK):
        ordered = jnp.dot(sort_q[...], q_raw[part * wide:(part + 1) * wide],
                          preferred_element_type=jnp.float32).astype(jnp.bfloat16)
        for h in range(heads):
            q_ref[h, part * BLK:(part + 1) * BLK] = ordered[h * BLK:(h + 1) * BLK]

    def listed(slot):
        count = cnt_ref[0, 0]
        width = vl_ref.shape[1]
        if width <= 8:
            hit = jnp.int32(0)
            for i in range(width):
                hit = hit | jnp.where((vl_ref[0, i] == slot) & (i < count), 1, 0)
            return hit

        def one(i, hit):
            return hit | jnp.where((vl_ref[0, i] == slot) & (i < count), 1, 0)

        return lax.fori_loop(0, width, one, jnp.int32(0))

    def score(keys, q):
        return lax.dot_general(keys, q, (((1,), (1,)), ((), ())),
                               preferred_element_type=jnp.float32)

    def take_keys(side, blocks, first=False):
        for h in range(heads):
            q = q_ref[h]
            raw = []
            tops = []
            for keys, seen in blocks:
                scores = score(keys[h], q)
                if seen is None:
                    key_id = lax.broadcasted_iota(jnp.int32, scores.shape, 0)
                    row_id = lax.broadcasted_iota(jnp.int32, scores.shape, 1) // groups
                    scores = jnp.where(key_id <= row_id, scores, -jnp.inf)
                top = jnp.max(scores, axis=0, keepdims=True)
                if seen is not None:
                    top = jnp.where(seen > 0, top, -jnp.inf)
                raw.append(scores)
                tops.append(top)
            high = functools.reduce(jnp.maximum, tops)
            if not first:
                old = peak[h]
                high = jnp.maximum(old, high)
                factor = jnp.exp2((old - high) * c)
                fade[side, h] = factor
            peak[h] = high
            sums = []
            for i, ((_, seen), scores) in enumerate(zip(blocks, raw)):
                base = high if seen is None else jnp.where(seen > 0, high, jnp.inf)
                weights = jnp.exp2((scores - base) * c)
                sums.append(jnp.sum(weights, axis=0, keepdims=True))
                rounded[side, h, i * BLK:(i + 1) * BLK] = weights.astype(jnp.bfloat16)
            add = sum(sums[1:], sums[0])
            total[h] = add if first else total[h] * fade[side, h] + add

    def take_values(side, blocks, first=False):
        depth = len(blocks) * BLK
        for h in range(heads):
            values = jnp.concatenate([values[h] for values in blocks], 1)
            add = jnp.dot(values, rounded[side, h, :depth], preferred_element_type=jnp.float32)
            acc[h] = add if first else acc[h] * fade[side, h] + add

    take_keys(0, [(new_ref.at[0], None)]
              + [(own_ref.at[b, 0], listed(2 * z + b)) for b in range(2)], first=True)
    take_values(0, [new_ref.at[1]] + [own_ref.at[b, 1] for b in range(2)], first=True)

    @pl.when(has_left)
    def _():
        slash_hop().wait_recv()
        slash_sib(s).start()

    def arrive(src, kv, right):
        hop(own_ref.at[s, kv], src, kv, right).wait_recv()

        @pl.when(has_right if right else has_left)
        def _():
            hop(pool.at[src, s, kv], src, kv, right).start()

        sib(src, kv).start()

    def step(d, carry):
        sides = ((z + d, z + d < n, False), (z - d, z - d >= 0, True))
        for kv in range(2):
            for src, there, right in sides:
                @pl.when(there)
                def _():
                    arrive(src, kv, right)

            for side, (src, there, right) in enumerate(sides):
                @pl.when(there)
                def _():
                    sib_in(src, kv).wait_recv()
                    if kv == 0:
                        take_keys(side, [(pool.at[src, b, 0], listed(2 * src + b))
                                         for b in range(2)])
                    else:
                        take_values(side, [pool.at[src, b, 1] for b in range(2)])

        @pl.when((d == 1) & has_left)
        def _():
            slash_sib(1 - s).wait_recv()
            put_keys(slash.at[0], slash_raw[0])
            put_values(slash.at[1], slash_raw[1])
            back = jnp.int32(0)
            for i in range(sl_ref.shape[1]):
                back = back | jnp.where((sl_ref[0, i] == 1) & (i < cnt_ref[0, 1]), 1, 0)
            take_keys(0, [(slash.at[0], back)])
            take_values(0, [slash.at[1]])

        return carry

    lax.fori_loop(1, n, step, 0)

    for part in range(rows // BLK):
        lanes = slice(part * BLK, (part + 1) * BLK)
        done = jnp.concatenate(
            [(acc[h, :, lanes] / total[h, :, lanes]).astype(jnp.bfloat16) for h in range(heads)], 1)
        o_ref[part * wide:(part + 1) * wide] = lax.dot_general(
            sort_q[...], done, (((0,), (1,)), ((), ())),
            preferred_element_type=jnp.float32).astype(o_ref.dtype)

    def drain(src, carry):
        for kv in range(2):
            @pl.when(has_right & (src <= z))
            def _():
                hop(own_ref.at[s, kv], src, kv, True).wait_send()

            @pl.when(has_left & (src >= z))
            def _():
                hop(own_ref.at[s, kv], src, kv, False).wait_send()

            @pl.when(src != z)
            def _():
                sib(src, kv).wait_send()
        return carry

    lax.fori_loop(0, n, drain, 0)

    @pl.when(has_right)
    def _():
        slash_hop().wait_send()

    @pl.when(has_left)
    def _():
        slash_sib(s).wait_send()

BITS = 5
OWN, GUEST, ALONE = 4, 5, 6
IDLE = (6, 4 * GUEST)
GUESTS = 1
EARLY = 2
PACK = 6


NONE = (-1, -1)
QUEST = (-2, 0)
SLASH = (-3, 0)


def plan(heads):
    zero = [(NONE, (0, 0), 0), (NONE, (0, ALONE), 0), (NONE, (1, 0), 0), ((1, 0), (1, ALONE), 0), (NONE, (2, 0), 0),
        (NONE, (2, ALONE), 0), ((1, 1), (0, 1), 0), (NONE, (3, 0), 0), (NONE, (3, ALONE), 0), ((1, 2), (1, 1), 0),
        (NONE, NONE, 0), ((1, 3), NONE, 0), (NONE, (2, 1), 0), (NONE, NONE, 0), (NONE, (3, 1), 0), ((2, 0), NONE, 0),
        ((2, 1), NONE, 0), (NONE, (0, 2), 0), (NONE, NONE, 0), (NONE, (1, 2), 0), ((2, 2), NONE, 0),
        ((2, 3), NONE, 0), (NONE, (2, 2), 0), (NONE, NONE, 0), (NONE, (3, 2), 0), ((3, 0), NONE, 0),
        ((3, 1), NONE, 0), (NONE, (0, 3), 0), (NONE, NONE, 0), (NONE, (1, 3), 0), ((3, 2), NONE, 16),
        ((3, 3), NONE, 0), (NONE, (2, 3), 0), (NONE, NONE, 0), (NONE, (3, 3), 0), (NONE, NONE, 0)]
    one = [((0, 0), (0, 1), 0), ((2, 0), (1, 1), 0), ((0, 3), (2, 1), 0), (NONE, (0, 0), 0), ((2, 1), (0, 2), 0),
        ((0, 1), (3, 0), 4), (NONE, (3, 1), 0), (NONE, (1, 2), 0), ((2, 2), (1, 0), 0), ((0, 2), NONE, 8),
        ((2, 3), NONE, 0), (NONE, (2, 2), 0), (NONE, (2, 0), 0), (NONE, NONE, 0), ((3, 0), (3, 2), 0),
        (SLASH, NONE, 0), ((3, 1), NONE, 0), (NONE, (0, 3), 0), (NONE, NONE, 0), (NONE, (0, OWN), 0),
        ((3, 2), (1, 3), 0), (NONE, (1, OWN), 0), (NONE, (2, OWN), 16), ((3, 3), (2, 3), 0), (NONE, (3, OWN), 0),
        (NONE, NONE, 0), (NONE, (3, 3), 0), (NONE, NONE, 0)]
    two = [((1, 0), (0, 2), 0), ((3, 0), (1, 2), 0), (NONE, (2, 2), 0), ((1, 3), (0, 1), 0), ((3, 1), (0, 3), 0),
        (NONE, (3, 2), 0), ((1, 1), (3, 1), 0), ((3, 2), (1, 3), 0), (NONE, NONE, 0), ((0, 0), (1, 1), 0),
        ((3, 3), (2, 3), 0), (NONE, NONE, 0), ((0, 3), (0, 0), 0), (NONE, (3, 3), 0), (NONE, NONE, 0),
        (NONE, (3, 0), 0), ((0, 1), NONE, 0), (QUEST, NONE, 0), (NONE, (4, 2), 0), ((1, 2), (4, GUEST), 0),
        (NONE, (4, 1), 0), (NONE, (4, 0), 0), (NONE, (1, 0), 0), ((0, 2), (2, 1), 2), (NONE, NONE, 0),
        (NONE, (2, 0), 0), (NONE, NONE, 0), (SLASH, NONE, 0), (NONE, (0, OWN), 0), (NONE, (1, OWN), 0),
        (NONE, (2, OWN), 16), (NONE, (3, OWN), 0), (NONE, NONE, 0)]
    three = [(NONE, (0, 3), 0), ((2, 0), (1, 3), 0), (NONE, (2, 3), 0), (NONE, (3, 3), 0), (NONE, (0, 2), 0),
        (SLASH, (3, ALONE), 0), (NONE, NONE, 0), (NONE, (0, OWN), 0), ((2, 1), (1, OWN), 0), (NONE, (2, OWN), 0),
        (NONE, NONE, 0), ((2, 2), (1, 2), 0), (NONE, NONE, 0), ((1, 0), NONE, 0), (NONE, (2, 2), 0), (NONE, NONE, 0),
        (NONE, (0, 1), 0), ((1, 1), NONE, 0), ((0, 0), NONE, 0), (NONE, (1, 1), 0), (NONE, NONE, 0),
        (NONE, (0, 0), 0), ((0, 1), NONE, 0), ((1, 2), NONE, 0), (NONE, (1, 0), 0), (NONE, NONE, 16),
        (NONE, (2, 1), 0), ((0, 2), NONE, 0), (NONE, (2, 0), 0), (NONE, NONE, 0)]

    def build(z, table):
        out, before, used = [], NONE, set()
        for recv, now, flags in table + [(NONE, NONE, 0)]:
            kind, message = (1, recv[0] * 4 + recv[1]) if recv[0] >= 0 else (-recv[0] if recv != NONE else 0, 0)
            slot, src = now
            h = slot if slot < heads else slot - GUESTS
            key = OWN if src == OWN else (src, h)
            first = now != NONE and key not in used and src not in (z, GUEST, ALONE)
            used.add(key)
            code = (slot + (8 if first else 0), src * 4 + h) if now != NONE else IDLE
            busy = now != NONE or before != NONE
            out.append((kind, message) + code + (int(busy) | flags,))
            before = now
        return out

    return [build(z, table) for z, table in enumerate((zero, one, two, three))]


def chain(n, q_hbm, nk_hbm, nv_hbm, ck_hbm, cv_hbm, vp_hbm, vl_hbm, sl_hbm, cnt_hbm, o_ref,
          vp_ref, vl_ref, sl_ref, cnt_ref,
          q_raw, nk_raw, nv_raw, ck_raw, cv_raw, q_ref, sort_kv, sort_q, ext,
          pool, acc, peak, total, mask, part_acc, part_stat, scores_a, scores_b, top_a, top_b, most, sort_o,
          send_sem, hop_recv, sib_recv, sl_sem, q_sem, part_sem, in_sem, table_sem, ready):
    z = lax.axis_index("ctx")
    s = lax.axis_index("sub")
    heads = pool.shape[1]
    head_dim, rows = acc.shape[1:]
    groups = rows // BLK
    wide = heads * BLK
    last = n - 1
    stay = heads - GUESTS
    loads = [pltpu.make_async_copy(src, dst, in_sem.at[i]) for i, (src, dst) in enumerate(
        [(ck_hbm, ck_raw), (cv_hbm, cv_raw), (nk_hbm, nk_raw), (nv_hbm, nv_raw), (q_hbm, q_raw)])]
    tables = [pltpu.make_async_copy(src, dst, table_sem.at[i]) for i, (src, dst) in enumerate(
        [(vp_hbm, vp_ref), (vl_hbm, vl_ref), (sl_hbm, sl_ref), (cnt_hbm, cnt_ref)])]
    loads[0].start()
    loads[1].start()
    for table in tables:
        table.start()
    c = math.log2(math.e) / math.sqrt(head_dim)
    has_left = z > 0
    has_right = z < last
    sib_id = {"sub": 1 - s}
    inner = has_left & has_right

    barrier = pltpu.get_barrier_semaphore()
    pl.semaphore_signal(barrier, inc=1, device_id=sib_id, device_id_type=MESH)

    @pl.when(has_right)
    def _():
        pl.semaphore_signal(barrier, inc=1, device_id={"ctx": z + 1}, device_id_type=MESH)

    def by_role(values):
        out = jnp.int32(values[-1])
        for i in reversed(range(len(values) - 1)):
            out = jnp.where(z == i, jnp.int32(values[i]), out)
        return out

    roles = plan(heads)
    lengths = [max(t for t, step in enumerate(role) if step[0] or step[4]) + 1 for role in roles]
    steps = -(-max(lengths) // PACK) * PACK
    roles = [(role + [(0, 0) + IDLE + (0,)] * steps)[:steps] for role in roles]
    ids = lax.broadcasted_iota(jnp.int32, (wide, wide), 0)
    at = lax.broadcasted_iota(jnp.int32, (wide, wide), 1)
    sort_kv[...] = jnp.where(at == (ids % BLK) * heads + ids // BLK, 1.0, 0.0).astype(jnp.bfloat16)

    pl.semaphore_wait(barrier, 1 + has_left.astype(jnp.int32))

    @pl.when(has_left)
    def _():
        pl.semaphore_signal(ready, inc=1, device_id={"ctx": z - 1}, device_id_type=MESH)

    def put_keys(raw, put, those=range(heads)):
        ordered = jnp.dot(sort_kv[those.start * BLK:those.stop * BLK], raw,
                          preferred_element_type=jnp.float32).astype(jnp.bfloat16)
        for i, h in enumerate(those):
            put(h, ordered[i * BLK:(i + 1) * BLK])

    def put_values(raw, put):
        ordered = lax.dot_general(raw, sort_kv[...], (((0,), (1,)), ((), ())),
                                  preferred_element_type=jnp.float32).astype(jnp.bfloat16)
        for h in range(heads):
            put(h, ordered[:, h * BLK:(h + 1) * BLK])

    def put_pool(b, kv):
        def put(h, block):
            pool[z, h, b, kv] = block
        return put

    def put_new(kv):
        def put(h, block):
            pool[OWN, h, 0, kv] = block
            pool[GUEST, h, 0, kv] = block
            pool[GUEST, h, 1, kv] = jnp.zeros_like(block)
        return put

    def hop(src, h, right):
        return pltpu.make_async_remote_copy(
            src_ref=pool.at[src, h, s], dst_ref=pool.at[src, h, s],
            send_sem=send_sem.at[int(right)], recv_sem=hop_recv.at[src if right else src - 1, h],
            device_id={"ctx": z + 1 if right else z - 1}, device_id_type=MESH)

    def first_hop(h, kv, right):
        return pltpu.make_async_remote_copy(
            src_ref=pool.at[z, h, s, kv], dst_ref=pool.at[z, h, s, kv],
            send_sem=send_sem.at[int(right)], recv_sem=hop_recv.at[z if right else z - 1, h],
            device_id={"ctx": z + 1 if right else z - 1}, device_id_type=MESH)

    def sib(src, h, part):
        return pltpu.make_async_remote_copy(
            src_ref=pool.at[src, h, part], dst_ref=pool.at[src, h, part],
            send_sem=send_sem.at[2], recv_sem=sib_recv.at[src - (src > z).astype(jnp.int32), h],
            device_id=sib_id, device_id_type=MESH)

    def slash_hop(count):
        return pltpu.make_async_remote_copy(
            src_ref=pool.at[OWN, pl.ds(0, count), 0, s], dst_ref=pool.at[OWN, pl.ds(0, count), 1, s],
            send_sem=sl_sem.at[0], recv_sem=sl_sem.at[1],
            device_id={"ctx": z + 1}, device_id_type=MESH)

    def slash_sib(count, part):
        block = pool.at[OWN, pl.ds(0, count), 1, part]
        return pltpu.make_async_remote_copy(
            src_ref=block, dst_ref=block,
            send_sem=sl_sem.at[2], recv_sem=sl_sem.at[3],
            device_id=sib_id, device_id_type=MESH)

    def guest_q(g):
        return pltpu.make_async_remote_copy(
            src_ref=q_ref.at[stay + g, pl.ds(0, head_dim)], dst_ref=q_ref.at[heads + g, pl.ds(0, head_dim)],
            send_sem=q_sem.at[0, g], recv_sem=q_sem.at[1, g],
            device_id={"ctx": z - 1}, device_id_type=MESH)

    def guest_mask():
        return pltpu.make_async_remote_copy(
            src_ref=mask.at[0], dst_ref=mask.at[1],
            send_sem=q_sem.at[0, GUESTS], recv_sem=q_sem.at[1, GUESTS],
            device_id={"ctx": z - 1}, device_id_type=MESH)

    def guest_part(g):
        return [pltpu.make_async_remote_copy(
            src_ref=ref.at[g], dst_ref=ref.at[g],
            send_sem=part_sem.at[0, g, i], recv_sem=part_sem.at[1, g, i],
            device_id={"ctx": z + 1}, device_id_type=MESH)
            for i, ref in enumerate((part_acc, part_stat))]

    def leftward(*blocks):
        @pl.when(has_left)
        def _():
            for h, kv in blocks:
                first_hop(h, kv, False).start()

    for table in tables:
        table.wait()
    loads[0].wait()
    put_keys(ck_raw[vp_ref[s]], put_pool(s, 0), range(EARLY))
    leftward(*[(h, 0) for h in range(EARLY)])
    put_keys(ck_raw[vp_ref[s]], put_pool(s, 0), range(EARLY, heads))
    for load in loads[2:]:
        load.start()
    loads[1].wait()
    put_values(cv_raw[vp_ref[s]], put_pool(s, 1))
    leftward((0, 1), (1, 1), *[(h, kv) for h in range(2, heads) for kv in range(2)])

    @pl.when(has_right)
    def _():
        pl.semaphore_wait(ready, 1)

    @pl.when(z == 0)
    def _():
        for h in (0, 3, 1, 2):
            for kv in range(2):
                first_hop(h, kv, True).start()

    @pl.when(z == 1)
    def _():
        for h in (0, 3, 1):
            for kv in range(2):
                first_hop(h, kv, True).start()

    @pl.when(z == 2)
    def _():
        for kv in range(2):
            first_hop(0, kv, True).start()

    loads[2].wait()
    loads[3].wait()
    put_keys(nk_raw[...], put_new(0))
    put_values(nv_raw[...], put_new(1))

    @pl.when(z == 2)
    def _():
        slash_hop(stay).start()
        for h in range(1, stay):
            for kv in range(2):
                first_hop(h, kv, True).start()

    token = (ids % BLK) // groups
    sort_q[...] = jnp.where(at == (token * heads + ids // BLK) * groups + ids % groups,
                            1.0, 0.0).astype(jnp.bfloat16)
    half = EARLY * BLK
    ids = lax.broadcasted_iota(jnp.int32, (half, half), 0)
    at = lax.broadcasted_iota(jnp.int32, (half, half), 1)
    sort_o[...] = jnp.where(at == ((ids % BLK) // groups * EARLY + ids // BLK) * groups + ids % groups,
                            1.0, 0.0).astype(jnp.bfloat16)
    loads[4].wait()
    for part in range(rows // BLK):
        ordered = lax.dot_general(q_raw[part * wide:(part + 1) * wide], sort_q[...], (((0,), (1,)), ((), ())),
                                  preferred_element_type=jnp.float32).astype(jnp.bfloat16)
        for h in range(heads):
            q_ref[h, 0:head_dim, part * BLK:(part + 1) * BLK] = ordered[:, h * BLK:(h + 1) * BLK]

    def unseen(hit):
        return jnp.full((1, BLK), jnp.where(hit > 0, 0.0, jnp.inf), jnp.float32)

    for slot in range(2 * n):
        hit = jnp.int32(0)
        for i in range(vl_ref.shape[1]):
            hit = hit | jnp.where((vl_ref[0, i] == slot) & (i < cnt_ref[0, 0]), 1, 0)
        mask[0, slot:slot + 1] = unseen(hit)
    hit = jnp.int32(0)
    for i in range(sl_ref.shape[1]):
        hit = hit | jnp.where((sl_ref[0, i] == 1) & (i < cnt_ref[0, 1]), 1, 0)
    mask[0, 2 * OWN:2 * OWN + 2] = jnp.concatenate([jnp.zeros((1, BLK), jnp.float32), unseen(hit)], 0)
    mask[0, 2 * GUEST:2 * GUEST + 2] = jnp.concatenate([unseen(hit), jnp.full((1, BLK), jnp.inf, jnp.float32)], 0)
    mask[0, 2 * ALONE:2 * ALONE + 2] = jnp.concatenate(
        [jnp.zeros((1, BLK), jnp.float32), jnp.full((1, BLK), jnp.inf, jnp.float32)], 0)

    @pl.when(z == 0)
    def _():
        slash_hop(heads).start()

    @pl.when(z == last)
    def _():
        for g in range(GUESTS):
            guest_q(g).start()
        guest_mask().start()

    put_keys(ck_raw[vp_ref[1 - s]], put_pool(1 - s, 0))
    put_values(cv_raw[vp_ref[1 - s]], put_pool(1 - s, 1))

    key_id = lax.broadcasted_iota(jnp.int32, (BLK, rows), 0)
    row_id = lax.broadcasted_iota(jnp.int32, (BLK, rows), 1) // groups
    later = jnp.where(key_id > row_id, -1e30, 0.0).astype(jnp.bfloat16)
    slots = acc.shape[0]
    for slot in range(slots):
        q_ref[slot, head_dim:] = later if slot < heads else jnp.zeros_like(later)
        acc[slot] = jnp.zeros_like(acc[slot])
        total[slot] = jnp.zeros_like(total[slot])
        peak[slot] = jnp.full_like(peak[slot], -1e30)
    q_ref[slots - 1, 0:head_dim] = jnp.zeros_like(later)
    one_at = lax.broadcasted_iota(jnp.int32, (BLK, BLK), 0) == lax.broadcasted_iota(jnp.int32, (BLK, BLK), 1)
    ext[0] = jnp.zeros((BLK, BLK), jnp.bfloat16)
    ext[1] = jnp.where(one_at, 1.0, 0.0).astype(jnp.bfloat16)
    scores_b[...] = jnp.zeros_like(scores_b)
    top_b[...] = jnp.zeros_like(top_b)

    def spread(row):
        return jnp.concatenate([row] * groups, 1)

    def place(src):
        return src - src // ALONE

    def hidden(slot, src, b):
        return spread(mask[(slot // heads) % 2 * (1 - slot // (slots - 1)), pl.ds(2 * src + b, 1)])

    def ahead(unit, scores, top):
        slot, src, h = unit
        q = q_ref[slot]
        high = None
        for b in range(2):
            causal = (src // OWN) * (1 - src % 2) if b == 0 else 0
            keys = jnp.concatenate([pool[place(src), h, b, 0], ext[causal]], 1)
            found = jnp.dot(keys, q, preferred_element_type=jnp.float32)
            scores[b * BLK:(b + 1) * BLK] = found
            part = jnp.max(found, axis=0, keepdims=True) - hidden(slot, src, b)
            high = part if high is None else jnp.maximum(high, part)
        top[...] = high

    def behind(unit, scores, top):
        slot, src, h = unit
        old = peak[slot]
        high = jnp.maximum(old, top[...])
        factor = jnp.exp2((old - high) * c)
        peak[slot] = high
        weights = [jnp.exp2((scores[b * BLK:(b + 1) * BLK] - (high + hidden(slot, src, b))) * c)
                   .astype(jnp.bfloat16) for b in range(2)]
        values = jnp.concatenate([pool[place(src), h, b, 1] for b in range(2)], 1)
        values = jnp.concatenate([values, jnp.ones((16, 2 * BLK), jnp.bfloat16)], 0)
        add = jnp.dot(values, jnp.concatenate(weights, 0), preferred_element_type=jnp.float32)
        acc[slot] = acc[slot] * factor + add[:head_dim]
        total[slot] = total[slot] * factor + add[head_dim:head_dim + 1]

    def ordered(part, those):
        lanes = slice(part * BLK, (part + 1) * BLK)
        done = jnp.concatenate(
            [(acc[h, :, lanes] * (1.0 / total[h, :, lanes])).astype(jnp.bfloat16) for h in those], 1)
        return lax.dot_general(sort_o[...], done, (((0,), (1,)), ((), ())), preferred_element_type=jnp.float32)

    def drain():
        def sent(kind, sources, count):
            blocks = pool.at[pl.ds(0, sources), pl.ds(0, count), s]
            pltpu.make_async_copy(blocks, blocks, send_sem.at[kind]).wait()

        for index in range(n):
            right = heads if index < last - 1 else stay if index < last else 0

            @pl.when(z == index)
            def _():
                if right:
                    sent(1, index + 1, right)
                    slash_hop(right).wait_send()
                if index > 0:
                    sent(0, n - index, heads)
                    slash_sib(heads if index < last else stay, s).wait_send()
                sent(2, n - 1, heads if index < last else stay)
                if index == last:
                    guest_mask().wait_send()
                    for g in range(GUESTS):
                        guest_q(g).wait_send()

    words = [[by_role([sum(step[field] << (BITS * i) for i, step in enumerate(role[start:start + PACK]))
                       for role in roles]) for start in range(0, steps, PACK)] for field in range(5)]

    def step(here, t, before, bufs, old_bufs):
        kind, message, code, block, flags = [(word >> (BITS * t)) & (2 ** BITS - 1) for word in here]
        src, h = message // 4, message % 4

        @pl.when(kind == 1)
        def _():
            block = pool.at[src, h, s]
            pltpu.make_async_copy(block, block, hop_recv.at[src - (src > z).astype(jnp.int32), h]).wait()

            @pl.when((src > z) & has_left)
            def _():
                hop(src, h, False).start()

            @pl.when((src < z) & ((z < last - 1) | ((z == last - 1) & (h < stay))))
            def _():
                hop(src, h, True).start()

            sib(src, h, s).start()

        @pl.when(kind > 1)
        def _():
            @pl.when(kind == 2)
            def _():
                guest_mask().wait_recv()
                for g in range(GUESTS):
                    guest_q(g).wait_recv()

            @pl.when((kind == 3) & has_right)
            def _():
                slash_hop(heads).wait_recv()
                slash_sib(heads, s).start()

            @pl.when((kind == 3) & (z == last))
            def _():
                slash_hop(stay).wait_recv()
                slash_sib(stay, s).start()

        unit = (code % 8, block // 4, block % 4)

        @pl.when(code > 7)
        def _():
            @pl.when(unit[1] < OWN)
            def _():
                sib(unit[1], unit[2], 1 - s).wait_recv()

            @pl.when((unit[1] == OWN) & has_right)
            def _():
                slash_sib(heads, 1 - s).wait_recv()

            @pl.when((unit[1] == OWN) & (z == last))
            def _():
                slash_sib(stay, 1 - s).wait_recv()

        @pl.when(flags % 2 == 1)
        def _():
            ahead(unit, *bufs)
            behind(before, *old_bufs)

        @pl.when(flags > 1)
        def _():
            @pl.when((flags // 4) % 2 == 1)
            def _():
                for kv in range(2):
                    first_hop(2, kv, True).start()

            @pl.when((flags // 8) % 2 == 1)
            def _():
                slash_hop(heads).start()

            @pl.when((flags // 2) % 2 == 1)
            def _():
                g = 0
                part_acc[g] = acc[heads + g].astype(jnp.bfloat16)
                part_stat[g, 0:1] = peak[heads + g]
                part_stat[g, 1:2] = total[heads + g]
                for copy in guest_part(g):
                    copy.start()

            @pl.when(flags // 16 == 1)
            def _():
                for part in range(rows // BLK):
                    most[part] = ordered(part, range(EARLY))

        return unit

    pairs = by_role([(length + 1) // 2 for length in lengths])

    def some_steps(group, before):
        here = []
        for chunks in words:
            word = chunks[-1]
            for i in reversed(range(len(chunks) - 1)):
                word = jnp.where(group == i, chunks[i], word)
            here.append(word)

        def two_steps(i, before):
            mid = step(here, 2 * i, before, (scores_a, top_a), (scores_b, top_b))
            return step(here, 2 * i + 1, mid, (scores_b, top_b), (scores_a, top_a))

        return lax.fori_loop(0, jnp.minimum(PACK // 2, pairs - group * (PACK // 2)), two_steps, before)

    idle = (jnp.int32(IDLE[0]), jnp.int32(GUEST), jnp.int32(0))
    lax.fori_loop(0, by_role([-(-length // PACK) for length in lengths]), some_steps, idle)

    drain()

    @pl.when(z == last)
    def _():
        for g in range(GUESTS):
            for copy in guest_part(g):
                copy.wait_recv()
            slot = stay + g
            old, new = peak[slot], part_stat[g, 0:1]
            high = jnp.maximum(old, new)
            mine, theirs = jnp.exp2((old - high) * c), jnp.exp2((new - high) * c)
            acc[slot] = acc[slot] * mine + part_acc[g].astype(jnp.float32) * theirs
            total[slot] = total[slot] * mine + part_stat[g, 1:2] * theirs

    tile = EARLY * groups
    for part in range(rows // BLK):
        pair = [half.reshape(-1, tile, head_dim) for half in (most[part], ordered(part, range(EARLY, heads)))]
        o_ref[part * wide:(part + 1) * wide] = jnp.concatenate(pair, 1).reshape(wide, head_dim).astype(o_ref.dtype)

    @pl.when(z == last - 1)
    def _():
        for g in range(GUESTS):
            for copy in guest_part(g):
                copy.wait_send()


def store(o_vmem, o_hbm, sem):
    copies = sem.shape[0]
    rows = o_vmem.shape[0] // copies
    for i in range(copies):
        lines = pl.ds(i * rows, rows)
        pltpu.make_async_copy(o_vmem.at[lines], o_hbm.at[lines], sem.at[i]).start()
    for i in range(copies):
        lines = pl.ds(i * rows, rows)
        pltpu.make_async_copy(o_vmem.at[lines], o_hbm.at[lines], sem.at[i]).wait()


def chain_call(n, q, nk, nv, ck, cv, tables, heads, rows, head_dim):
    def vmem(*shape):
        return pltpu.VMEM(shape, jnp.bfloat16)

    def wide_vmem(*shape):
        return pltpu.VMEM(shape, jnp.float32)

    hbm = pl.BlockSpec(memory_space=pltpu.HBM)
    in_vmem = pl.BlockSpec(memory_space=pltpu.VMEM)
    dma = pltpu.SemaphoreType.DMA
    cached, wide = ck.shape[:2]
    slots = 7
    out = pl.pallas_call(
        functools.partial(chain, n),
        out_shape=pltpu.VMEM((heads * rows, head_dim), jnp.bfloat16),
        in_specs=[hbm] * 9,
        out_specs=in_vmem,
        scratch_shapes=[
            *[pltpu.SMEM(table.shape, table.dtype) for table in tables],
            vmem(heads * rows, head_dim), vmem(wide, head_dim), vmem(wide, head_dim),
            vmem(cached, wide, head_dim), vmem(cached, wide, head_dim),
            vmem(slots, 2 * head_dim, rows), vmem(wide, wide), vmem(wide, wide), vmem(2, BLK, BLK),
            vmem(n + 2, heads, 2, 2, BLK, head_dim),
            wide_vmem(slots, head_dim, rows), wide_vmem(slots, 1, rows), wide_vmem(slots, 1, rows),
            wide_vmem(2, 16, BLK), vmem(GUESTS, head_dim, rows), wide_vmem(GUESTS, 8, rows),
            wide_vmem(2 * BLK, rows), wide_vmem(2 * BLK, rows), wide_vmem(1, rows), wide_vmem(1, rows),
            wide_vmem(rows // BLK, EARLY * BLK, head_dim), vmem(EARLY * BLK, EARLY * BLK),
            dma((3,)), dma((n - 1, heads)), dma((n - 1, heads)), dma((4,)),
            dma((2, GUESTS + 1)), dma((2, GUESTS, 2)), dma((5,)), dma((4,)), pltpu.SemaphoreType.REGULAR,
        ],
        compiler_params=pltpu.CompilerParams(
            collective_id=0, has_side_effects=True, vmem_limit_bytes=60 * 2**20),
    )(*[pltpu.with_memory_space_constraint(x, pltpu.HBM) for x in (q, nk, nv, ck, cv, *tables)])
    return pl.pallas_call(
        store,
        out_shape=jax.ShapeDtypeStruct(out.shape, out.dtype),
        in_specs=[in_vmem],
        out_specs=hbm,
        scratch_shapes=[dma((4,))],
        compiler_params=pltpu.CompilerParams(vmem_limit_bytes=2**20),
    )(out)


def shards(n, queries, new_keys, new_values, cache_keys, cache_values,
           vertical_pool, vertical_lists, slash_lists, list_counts):
    tokens, heads, groups, head_dim = queries.shape
    rows = tokens * groups
    picked = vertical_pool.shape[0]

    def flat(x):
        return x.reshape(-1, head_dim)

    def vmem(*shape):
        return pltpu.VMEM(shape, jnp.bfloat16)

    hbm = pl.BlockSpec(memory_space=pltpu.HBM)
    smem = pl.BlockSpec(memory_space=pltpu.SMEM)
    dma = pltpu.SemaphoreType.DMA
    wide = heads * BLK
    cached = cache_keys.shape[0] // BLK
    if n == 4 and heads == 4 and picked == 2:
        out = chain_call(n, flat(queries), flat(new_keys), flat(new_values),
                         cache_keys.reshape(cached, wide, head_dim), cache_values.reshape(cached, wide, head_dim),
                         (vertical_pool, vertical_lists, slash_lists, list_counts), heads, rows, head_dim)
        return out.reshape(tokens, heads, groups, head_dim)
    out = pl.pallas_call(
        functools.partial(attend, n),
        out_shape=jax.ShapeDtypeStruct((tokens * heads * groups, head_dim), jnp.bfloat16),
        in_specs=[hbm] * 5 + [smem] * 4,
        out_specs=pl.BlockSpec(memory_space=pltpu.VMEM),
        scratch_shapes=[
            vmem(heads * rows, head_dim), vmem(wide, head_dim), vmem(wide, head_dim),
            vmem(cached, wide, head_dim), vmem(cached, wide, head_dim),
            vmem(heads, rows, head_dim), vmem(picked, 2, heads, BLK, head_dim),
            vmem(2, heads, BLK, head_dim), vmem(wide, wide), vmem(wide, wide),
            vmem(n, picked, 2, heads, BLK, head_dim),
            vmem(2, wide, head_dim), vmem(2, heads, BLK, head_dim),
            pltpu.VMEM((heads, head_dim, rows), jnp.float32),
            pltpu.VMEM((heads, 1, rows), jnp.float32),
            pltpu.VMEM((heads, 1, rows), jnp.float32),
            vmem(2, heads, 3 * BLK, rows), pltpu.VMEM((2, heads, 1, rows), jnp.float32),
            dma((n, 2, 2)), dma((n, 2)), dma((n, 2)), dma((n, 2)), dma((4,)), dma((5,)),
        ],
        compiler_params=pltpu.CompilerParams(
            collective_id=0, has_side_effects=True, vmem_limit_bytes=60 * 2**20),
    )(flat(queries), flat(new_keys), flat(new_values), cache_keys.reshape(cached, wide, head_dim),
      cache_values.reshape(cached, wide, head_dim),
      vertical_pool, vertical_lists, slash_lists, list_counts)
    return out.reshape(tokens, heads, groups, head_dim)


def solution(mesh):
    in_specs = (
        P(("grp", "ctx"), "kvh", "sub", None),
        P(("grp", "ctx"), "kvh", None),
        P(("grp", "ctx"), "kvh", None),
        P(("grp", "ctx"), "kvh", None),
        P(("grp", "ctx"), "kvh", None),
        P(("grp", "ctx")),
        P(("grp", "ctx"), None),
        P(("grp", "ctx"), None),
        P(("grp", "ctx"), None),
    )
    out_specs = P(("grp", "ctx"), "kvh", "sub", None)
    return jax.shard_map(functools.partial(shards, mesh.shape["ctx"]), mesh=mesh,
                         in_specs=in_specs, out_specs=out_specs, check_vma=False)
```

```python
import functools
import math

import jax
import jax.numpy as jnp
from jax import lax
from jax.experimental import pallas as pl
from jax.experimental.pallas import tpu as pltpu
from jax.sharding import PartitionSpec as P

BLK = 128
MESH = pl.DeviceIdType.MESH


def attend(n, q_hbm, nk_hbm, nv_hbm, ck_hbm, cv_hbm, vp_ref, vl_ref, sl_ref, cnt_ref, o_ref,
           q_raw, nk_raw, nv_raw, ck_raw, cv_raw, q_ref, own_ref, new_ref, sort_kv, sort_q,
           pool, slash_raw, slash, acc, peak, total, rounded, fade,
           hop_send, hop_recv, sib_send, sib_recv, sl_sem, in_sem):
    z = lax.axis_index("ctx")
    s = lax.axis_index("sub")
    heads, rows, head_dim = q_ref.shape
    groups = rows // BLK
    wide = heads * BLK
    loads = [pltpu.make_async_copy(src, dst, in_sem.at[i]) for i, (src, dst) in enumerate(
        [(ck_hbm, ck_raw), (cv_hbm, cv_raw), (nk_hbm, nk_raw), (nv_hbm, nv_raw), (q_hbm, q_raw)])]
    loads[0].start()
    c = math.log2(math.e) / math.sqrt(head_dim)
    has_left = z > 0
    has_right = z < n - 1
    sib_id = {"sub": 1 - s}

    barrier = pltpu.get_barrier_semaphore()
    pl.semaphore_signal(barrier, inc=1, device_id=sib_id, device_id_type=MESH)

    @pl.when(has_left)
    def _():
        pl.semaphore_signal(barrier, inc=1, device_id={"ctx": z - 1}, device_id_type=MESH)

    @pl.when(has_right)
    def _():
        pl.semaphore_signal(barrier, inc=1, device_id={"ctx": z + 1}, device_id_type=MESH)

    ids = lax.broadcasted_iota(jnp.int32, (wide, wide), 0)
    at = lax.broadcasted_iota(jnp.int32, (wide, wide), 1)
    sort_kv[...] = jnp.where(at == (ids % BLK) * heads + ids // BLK, 1.0, 0.0).astype(jnp.bfloat16)
    token = (ids % BLK) // groups
    sort_q[...] = jnp.where(at == (token * heads + ids // BLK) * groups + ids % groups,
                            1.0, 0.0).astype(jnp.bfloat16)

    def by_head(raw):
        return jnp.dot(sort_kv[...], raw, preferred_element_type=jnp.float32).astype(jnp.bfloat16)

    def put_keys(dst, raw):
        ordered = by_head(raw)
        for h in range(heads):
            dst[h] = ordered[h * BLK:(h + 1) * BLK]

    def put_values(dst, raw):
        ordered = lax.dot_general(raw, sort_kv[...], (((0,), (1,)), ((), ())),
                                  preferred_element_type=jnp.float32).astype(jnp.bfloat16)
        for h in range(heads):
            dst[h] = ordered[:, h * BLK:(h + 1) * BLK]

    def chosen(cache, b):
        return cache[vp_ref[b]]

    pl.semaphore_wait(barrier, 1 + has_left.astype(jnp.int32) + has_right.astype(jnp.int32))

    def hop(src_ref, src, kv, right):
        return pltpu.make_async_remote_copy(
            src_ref=src_ref, dst_ref=pool.at[src, s, kv],
            send_sem=hop_send.at[src, int(right), kv], recv_sem=hop_recv.at[src, kv],
            device_id={"ctx": z + 1 if right else z - 1}, device_id_type=MESH)

    def sib(src, kv):
        return pltpu.make_async_remote_copy(
            src_ref=pool.at[src, s, kv], dst_ref=pool.at[src, s, kv],
            send_sem=sib_send.at[src, kv], recv_sem=sib_recv.at[src, kv],
            device_id=sib_id, device_id_type=MESH)

    def sib_in(src, kv):
        return pltpu.make_async_remote_copy(
            src_ref=pool.at[src, 1 - s, kv], dst_ref=pool.at[src, 1 - s, kv],
            send_sem=sib_send.at[src, kv], recv_sem=sib_recv.at[src, kv],
            device_id=sib_id, device_id_type=MESH)

    def slash_hop(src_ref=nk_hbm):
        return pltpu.make_async_remote_copy(
            src_ref=src_ref, dst_ref=slash_raw.at[s],
            send_sem=sl_sem.at[0], recv_sem=sl_sem.at[1],
            device_id={"ctx": z + 1}, device_id_type=MESH)

    def slash_sib(part):
        return pltpu.make_async_remote_copy(
            src_ref=slash_raw.at[part], dst_ref=slash_raw.at[part],
            send_sem=sl_sem.at[2], recv_sem=sl_sem.at[3],
            device_id=sib_id, device_id_type=MESH)

    for part, src_ref in enumerate((nk_hbm, nv_hbm)):
        @pl.when(has_right & (s == part))
        def _():
            slash_hop(src_ref).start()

    def send_own(kv):
        @pl.when(has_right)
        def _():
            hop(own_ref.at[s, kv], z, kv, True).start()

        @pl.when(has_left)
        def _():
            hop(own_ref.at[s, kv], z, kv, False).start()

    loads[0].wait()
    loads[1].start()
    put_keys(own_ref.at[s, 0], chosen(ck_raw, s))
    for load in loads[2:]:
        load.start()
    send_own(0)
    loads[1].wait()
    put_values(own_ref.at[s, 1], chosen(cv_raw, s))
    send_own(1)
    loads[2].wait()
    loads[3].wait()
    put_keys(new_ref.at[0], nk_raw[...])
    put_values(new_ref.at[1], nv_raw[...])
    put_keys(own_ref.at[1 - s, 0], chosen(ck_raw, 1 - s))
    put_values(own_ref.at[1 - s, 1], chosen(cv_raw, 1 - s))
    loads[4].wait()
    for part in range(rows // BLK):
        ordered = jnp.dot(sort_q[...], q_raw[part * wide:(part + 1) * wide],
                          preferred_element_type=jnp.float32).astype(jnp.bfloat16)
        for h in range(heads):
            q_ref[h, part * BLK:(part + 1) * BLK] = ordered[h * BLK:(h + 1) * BLK]

    def listed(slot):
        count = cnt_ref[0, 0]
        width = vl_ref.shape[1]
        if width <= 8:
            hit = jnp.int32(0)
            for i in range(width):
                hit = hit | jnp.where((vl_ref[0, i] == slot) & (i < count), 1, 0)
            return hit

        def one(i, hit):
            return hit | jnp.where((vl_ref[0, i] == slot) & (i < count), 1, 0)

        return lax.fori_loop(0, width, one, jnp.int32(0))

    def score(keys, q):
        return lax.dot_general(keys, q, (((1,), (1,)), ((), ())),
                               preferred_element_type=jnp.float32)

    def take_keys(side, blocks, first=False):
        for h in range(heads):
            q = q_ref[h]
            raw = []
            tops = []
            for keys, seen in blocks:
                scores = score(keys[h], q)
                if seen is None:
                    key_id = lax.broadcasted_iota(jnp.int32, scores.shape, 0)
                    row_id = lax.broadcasted_iota(jnp.int32, scores.shape, 1) // groups
                    scores = jnp.where(key_id <= row_id, scores, -jnp.inf)
                top = jnp.max(scores, axis=0, keepdims=True)
                if seen is not None:
                    top = jnp.where(seen > 0, top, -jnp.inf)
                raw.append(scores)
                tops.append(top)
            high = functools.reduce(jnp.maximum, tops)
            if not first:
                old = peak[h]
                high = jnp.maximum(old, high)
                factor = jnp.exp2((old - high) * c)
                fade[side, h] = factor
            peak[h] = high
            sums = []
            for i, ((_, seen), scores) in enumerate(zip(blocks, raw)):
                base = high if seen is None else jnp.where(seen > 0, high, jnp.inf)
                weights = jnp.exp2((scores - base) * c)
                sums.append(jnp.sum(weights, axis=0, keepdims=True))
                rounded[side, h, i * BLK:(i + 1) * BLK] = weights.astype(jnp.bfloat16)
            add = sum(sums[1:], sums[0])
            total[h] = add if first else total[h] * fade[side, h] + add

    def take_values(side, blocks, first=False):
        depth = len(blocks) * BLK
        for h in range(heads):
            values = jnp.concatenate([values[h] for values in blocks], 1)
            add = jnp.dot(values, rounded[side, h, :depth], preferred_element_type=jnp.float32)
            acc[h] = add if first else acc[h] * fade[side, h] + add

    take_keys(0, [(new_ref.at[0], None)]
              + [(own_ref.at[b, 0], listed(2 * z + b)) for b in range(2)], first=True)
    take_values(0, [new_ref.at[1]] + [own_ref.at[b, 1] for b in range(2)], first=True)

    @pl.when(has_left)
    def _():
        slash_hop().wait_recv()
        slash_sib(s).start()

    def arrive(src, kv, right):
        hop(own_ref.at[s, kv], src, kv, right).wait_recv()

        @pl.when(has_right if right else has_left)
        def _():
            hop(pool.at[src, s, kv], src, kv, right).start()

        sib(src, kv).start()

    def step(d, carry):
        sides = ((z + d, z + d < n, False), (z - d, z - d >= 0, True))
        for kv in range(2):
            for src, there, right in sides:
                @pl.when(there)
                def _():
                    arrive(src, kv, right)

            for side, (src, there, right) in enumerate(sides):
                @pl.when(there)
                def _():
                    sib_in(src, kv).wait_recv()
                    if kv == 0:
                        take_keys(side, [(pool.at[src, b, 0], listed(2 * src + b))
                                         for b in range(2)])
                    else:
                        take_values(side, [pool.at[src, b, 1] for b in range(2)])

        @pl.when((d == 1) & has_left)
        def _():
            slash_sib(1 - s).wait_recv()
            put_keys(slash.at[0], slash_raw[0])
            put_values(slash.at[1], slash_raw[1])
            back = jnp.int32(0)
            for i in range(sl_ref.shape[1]):
                back = back | jnp.where((sl_ref[0, i] == 1) & (i < cnt_ref[0, 1]), 1, 0)
            take_keys(0, [(slash.at[0], back)])
            take_values(0, [slash.at[1]])

        return carry

    lax.fori_loop(1, n, step, 0)

    for part in range(rows // BLK):
        lanes = slice(part * BLK, (part + 1) * BLK)
        done = jnp.concatenate(
            [(acc[h, :, lanes] / total[h, :, lanes]).astype(jnp.bfloat16) for h in range(heads)], 1)
        o_ref[part * wide:(part + 1) * wide] = lax.dot_general(
            sort_q[...], done, (((0,), (1,)), ((), ())),
            preferred_element_type=jnp.float32).astype(o_ref.dtype)

    def drain(src, carry):
        for kv in range(2):
            @pl.when(has_right & (src <= z))
            def _():
                hop(own_ref.at[s, kv], src, kv, True).wait_send()

            @pl.when(has_left & (src >= z))
            def _():
                hop(own_ref.at[s, kv], src, kv, False).wait_send()

            @pl.when(src != z)
            def _():
                sib(src, kv).wait_send()
        return carry

    lax.fori_loop(0, n, drain, 0)

    @pl.when(has_right)
    def _():
        slash_hop().wait_send()

    @pl.when(has_left)
    def _():
        slash_sib(s).wait_send()

BITS = 5
OWN, GUEST, ALONE = 4, 5, 6
IDLE = (6, 4 * GUEST)
GUESTS = 1
EARLY = 2
PACK = 6


NONE = (-1, -1)
QUEST = (-2, 0)
SLASH = (-3, 0)


def plan(heads):
    zero = [(NONE, (0, 0), 0), (NONE, (0, ALONE), 0), (NONE, (1, 0), 0), ((1, 0), (1, ALONE), 0), (NONE, (2, 0), 0),
        (NONE, (2, ALONE), 0), ((1, 1), (0, 1), 0), (NONE, (3, 0), 0), (NONE, (3, ALONE), 0), ((1, 2), (1, 1), 0),
        (NONE, NONE, 0), ((1, 3), NONE, 0), (NONE, (2, 1), 0), (NONE, NONE, 0), (NONE, (3, 1), 0), ((2, 0), NONE, 0),
        ((2, 1), NONE, 0), (NONE, (0, 2), 0), (NONE, NONE, 0), (NONE, (1, 2), 0), ((2, 2), NONE, 0),
        ((2, 3), NONE, 0), (NONE, (2, 2), 0), (NONE, NONE, 0), (NONE, (3, 2), 0), ((3, 0), NONE, 0),
        ((3, 1), NONE, 0), (NONE, (0, 3), 0), (NONE, NONE, 0), (NONE, (1, 3), 0), ((3, 2), NONE, 16),
        ((3, 3), NONE, 0), (NONE, (2, 3), 0)]
    one = [((0, 0), (0, 1), 0), ((2, 0), (1, 1), 0), ((0, 3), (2, 1), 0), (NONE, (0, 0), 0), ((2, 1), (0, 2), 0),
        ((0, 1), (3, 0), 4), (NONE, (3, 1), 0), (NONE, (1, 2), 0), ((2, 2), (1, 0), 0), ((0, 2), NONE, 8),
        ((2, 3), NONE, 0), (NONE, (2, 2), 0), (NONE, (2, 0), 0), (NONE, NONE, 0), ((3, 0), (3, 2), 0),
        (SLASH, NONE, 0), ((3, 1), NONE, 0), (NONE, (0, 3), 0), (NONE, NONE, 0), (NONE, (0, OWN), 0),
        ((3, 2), (1, 3), 0), (NONE, (1, OWN), 0), (NONE, (2, OWN), 16), ((3, 3), (2, 3), 0), (NONE, (3, OWN), 0),
        (NONE, NONE, 0), (NONE, (3, 3), 0), (NONE, NONE, 0)]
    two = [((1, 0), (0, 2), 0), ((3, 0), (1, 2), 0), (NONE, (2, 2), 0), ((1, 3), (0, 1), 0), ((3, 1), (0, 3), 0),
        (NONE, (3, 2), 0), ((1, 1), (3, 1), 0), ((3, 2), (1, 3), 0), (NONE, NONE, 0), ((0, 0), (1, 1), 0),
        ((3, 3), (2, 3), 0), (NONE, NONE, 0), ((0, 3), (0, 0), 0), (NONE, (3, 3), 0), (NONE, NONE, 0),
        (NONE, (3, 0), 0), ((0, 1), NONE, 0), (QUEST, NONE, 0), (NONE, (4, 2), 0), ((1, 2), (4, GUEST), 0),
        (NONE, (4, 1), 0), (NONE, (4, 0), 0), (NONE, (1, 0), 0), ((0, 2), (2, 1), 2), (NONE, NONE, 0),
        (NONE, (2, 0), 0), (NONE, NONE, 0), (SLASH, NONE, 0), (NONE, (0, OWN), 0), (NONE, (1, OWN), 0),
        (NONE, (2, OWN), 16), (NONE, (3, OWN), 0), (NONE, NONE, 0)]
    three = [(NONE, (0, 3), 0), ((2, 0), (1, 3), 0), (NONE, (2, 3), 0), (NONE, (3, 3), 0), (NONE, (0, 2), 0),
        (SLASH, (3, ALONE), 0), (NONE, NONE, 0), (NONE, (0, OWN), 0), ((2, 1), (1, OWN), 0), (NONE, (2, OWN), 0),
        (NONE, NONE, 0), ((2, 2), (1, 2), 0), (NONE, NONE, 0), ((1, 0), NONE, 0), (NONE, (2, 2), 0), (NONE, NONE, 0),
        (NONE, (0, 1), 0), ((1, 1), NONE, 0), ((0, 0), NONE, 0), (NONE, (1, 1), 0), (NONE, NONE, 0),
        (NONE, (0, 0), 0), ((0, 1), NONE, 0), ((1, 2), NONE, 0), (NONE, (1, 0), 0), (NONE, NONE, 16),
        (NONE, (2, 1), 0), ((0, 2), NONE, 0), (NONE, (2, 0), 0), (NONE, NONE, 0)]

    def build(z, table):
        out, before, used = [], NONE, set()
        for recv, now, flags in table + [(NONE, NONE, 0)]:
            kind, message = (1, recv[0] * 4 + recv[1]) if recv[0] >= 0 else (-recv[0] if recv != NONE else 0, 0)
            slot, src = now
            h = slot if slot < heads else slot - GUESTS
            key = OWN if src == OWN else (src, h)
            first = now != NONE and key not in used and src not in (z, GUEST, ALONE)
            used.add(key)
            code = (slot + (8 if first else 0), src * 4 + h) if now != NONE else IDLE
            busy = now != NONE or before != NONE
            out.append((kind, message) + code + (int(busy) | flags,))
            before = now
        return out

    return [build(z, table) for z, table in enumerate((zero, one, two, three))]


def chain(n, q_hbm, nk_hbm, nv_hbm, ck_hbm, cv_hbm, vp_hbm, vl_hbm, sl_hbm, cnt_hbm, o_ref,
          vp_ref, vl_ref, sl_ref, cnt_ref,
          q_raw, nk_raw, nv_raw, ck_raw, cv_raw, q_ref, sort_kv, sort_q, ext,
          pool, acc, peak, total, mask, part_acc, part_stat, scores_a, scores_b, top_a, top_b, most, sort_o,
          send_sem, hop_recv, sib_recv, sl_sem, q_sem, part_sem, in_sem, table_sem, ready):
    z = lax.axis_index("ctx")
    s = lax.axis_index("sub")
    heads = pool.shape[1]
    head_dim, rows = acc.shape[1:]
    groups = rows // BLK
    wide = heads * BLK
    last = n - 1
    stay = heads - GUESTS
    loads = [pltpu.make_async_copy(src, dst, in_sem.at[i]) for i, (src, dst) in enumerate(
        [(ck_hbm, ck_raw), (cv_hbm, cv_raw), (nk_hbm, nk_raw), (nv_hbm, nv_raw), (q_hbm, q_raw)])]
    tables = [pltpu.make_async_copy(src, dst, table_sem.at[i]) for i, (src, dst) in enumerate(
        [(vp_hbm, vp_ref), (vl_hbm, vl_ref), (sl_hbm, sl_ref), (cnt_hbm, cnt_ref)])]
    loads[0].start()
    loads[1].start()
    for table in tables:
        table.start()
    c = math.log2(math.e) / math.sqrt(head_dim)
    has_left = z > 0
    has_right = z < last
    sib_id = {"sub": 1 - s}
    inner = has_left & has_right

    barrier = pltpu.get_barrier_semaphore()
    pl.semaphore_signal(barrier, inc=1, device_id=sib_id, device_id_type=MESH)

    @pl.when(has_right)
    def _():
        pl.semaphore_signal(barrier, inc=1, device_id={"ctx": z + 1}, device_id_type=MESH)

    def by_role(values):
        out = jnp.int32(values[-1])
        for i in reversed(range(len(values) - 1)):
            out = jnp.where(z == i, jnp.int32(values[i]), out)
        return out

    roles = plan(heads)
    lengths = [max(t for t, step in enumerate(role) if step[0] or step[4]) + 1 for role in roles]
    steps = -(-max(lengths) // PACK) * PACK
    roles = [(role + [(0, 0) + IDLE + (0,)] * steps)[:steps] for role in roles]
    ids = lax.broadcasted_iota(jnp.int32, (wide, wide), 0)
    at = lax.broadcasted_iota(jnp.int32, (wide, wide), 1)
    sort_kv[...] = jnp.where(at == (ids % BLK) * heads + ids // BLK, 1.0, 0.0).astype(jnp.bfloat16)

    pl.semaphore_wait(barrier, 1 + has_left.astype(jnp.int32))

    @pl.when(has_left)
    def _():
        pl.semaphore_signal(ready, inc=1, device_id={"ctx": z - 1}, device_id_type=MESH)

    def put_keys(raw, put, those=range(heads)):
        ordered = jnp.dot(sort_kv[those.start * BLK:those.stop * BLK], raw,
                          preferred_element_type=jnp.float32).astype(jnp.bfloat16)
        for i, h in enumerate(those):
            put(h, ordered[i * BLK:(i + 1) * BLK])

    def put_values(raw, put):
        ordered = lax.dot_general(raw, sort_kv[...], (((0,), (1,)), ((), ())),
                                  preferred_element_type=jnp.float32).astype(jnp.bfloat16)
        for h in range(heads):
            put(h, ordered[:, h * BLK:(h + 1) * BLK])

    def put_pool(b, kv):
        def put(h, block):
            pool[z, h, b, kv] = block
        return put

    def put_new(kv):
        def put(h, block):
            pool[OWN, h, 0, kv] = block
            pool[GUEST, h, 0, kv] = block
            pool[GUEST, h, 1, kv] = jnp.zeros_like(block)
        return put

    def hop(src, h, right):
        return pltpu.make_async_remote_copy(
            src_ref=pool.at[src, h, s], dst_ref=pool.at[src, h, s],
            send_sem=send_sem.at[int(right)], recv_sem=hop_recv.at[src if right else src - 1, h],
            device_id={"ctx": z + 1 if right else z - 1}, device_id_type=MESH)

    def first_hop(h, kv, right):
        return pltpu.make_async_remote_copy(
            src_ref=pool.at[z, h, s, kv], dst_ref=pool.at[z, h, s, kv],
            send_sem=send_sem.at[int(right)], recv_sem=hop_recv.at[z if right else z - 1, h],
            device_id={"ctx": z + 1 if right else z - 1}, device_id_type=MESH)

    def sib(src, h, part):
        return pltpu.make_async_remote_copy(
            src_ref=pool.at[src, h, part], dst_ref=pool.at[src, h, part],
            send_sem=send_sem.at[2], recv_sem=sib_recv.at[src - (src > z).astype(jnp.int32), h],
            device_id=sib_id, device_id_type=MESH)

    def slash_hop(count):
        return pltpu.make_async_remote_copy(
            src_ref=pool.at[OWN, pl.ds(0, count), 0, s], dst_ref=pool.at[OWN, pl.ds(0, count), 1, s],
            send_sem=sl_sem.at[0], recv_sem=sl_sem.at[1],
            device_id={"ctx": z + 1}, device_id_type=MESH)

    def slash_sib(count, part):
        block = pool.at[OWN, pl.ds(0, count), 1, part]
        return pltpu.make_async_remote_copy(
            src_ref=block, dst_ref=block,
            send_sem=sl_sem.at[2], recv_sem=sl_sem.at[3],
            device_id=sib_id, device_id_type=MESH)

    def guest_q(g):
        return pltpu.make_async_remote_copy(
            src_ref=q_ref.at[stay + g, pl.ds(0, head_dim)], dst_ref=q_ref.at[heads + g, pl.ds(0, head_dim)],
            send_sem=q_sem.at[0, g], recv_sem=q_sem.at[1, g],
            device_id={"ctx": z - 1}, device_id_type=MESH)

    def guest_mask():
        return pltpu.make_async_remote_copy(
            src_ref=mask.at[0], dst_ref=mask.at[1],
            send_sem=q_sem.at[0, GUESTS], recv_sem=q_sem.at[1, GUESTS],
            device_id={"ctx": z - 1}, device_id_type=MESH)

    def guest_part(g):
        return [pltpu.make_async_remote_copy(
            src_ref=ref.at[g], dst_ref=ref.at[g],
            send_sem=part_sem.at[0, g, i], recv_sem=part_sem.at[1, g, i],
            device_id={"ctx": z + 1}, device_id_type=MESH)
            for i, ref in enumerate((part_acc, part_stat))]

    def leftward(*blocks):
        @pl.when(has_left)
        def _():
            for h, kv in blocks:
                first_hop(h, kv, False).start()

    for table in tables:
        table.wait()
    loads[0].wait()
    put_keys(ck_raw[vp_ref[s]], put_pool(s, 0), range(EARLY))
    leftward(*[(h, 0) for h in range(EARLY)])
    put_keys(ck_raw[vp_ref[s]], put_pool(s, 0), range(EARLY, heads))
    for load in loads[2:]:
        load.start()
    loads[1].wait()
    put_values(cv_raw[vp_ref[s]], put_pool(s, 1))
    leftward((0, 1), (1, 1), *[(h, kv) for h in range(2, heads) for kv in range(2)])

    @pl.when(has_right)
    def _():
        pl.semaphore_wait(ready, 1)

    @pl.when(z == 0)
    def _():
        for h in (0, 3, 1, 2):
            for kv in range(2):
                first_hop(h, kv, True).start()

    @pl.when(z == 1)
    def _():
        for h in (0, 3, 1):
            for kv in range(2):
                first_hop(h, kv, True).start()

    @pl.when(z == 2)
    def _():
        for kv in range(2):
            first_hop(0, kv, True).start()

    loads[2].wait()
    loads[3].wait()
    put_keys(nk_raw[...], put_new(0))
    put_values(nv_raw[...], put_new(1))

    @pl.when(z == 2)
    def _():
        slash_hop(stay).start()
        for h in range(1, stay):
            for kv in range(2):
                first_hop(h, kv, True).start()

    token = (ids % BLK) // groups
    sort_q[...] = jnp.where(at == (token * heads + ids // BLK) * groups + ids % groups,
                            1.0, 0.0).astype(jnp.bfloat16)
    half = EARLY * BLK
    ids = lax.broadcasted_iota(jnp.int32, (half, half), 0)
    at = lax.broadcasted_iota(jnp.int32, (half, half), 1)
    sort_o[...] = jnp.where(at == ((ids % BLK) // groups * EARLY + ids // BLK) * groups + ids % groups,
                            1.0, 0.0).astype(jnp.bfloat16)
    loads[4].wait()
    for part in range(rows // BLK):
        ordered = lax.dot_general(q_raw[part * wide:(part + 1) * wide], sort_q[...], (((0,), (1,)), ((), ())),
                                  preferred_element_type=jnp.float32).astype(jnp.bfloat16)
        for h in range(heads):
            q_ref[h, 0:head_dim, part * BLK:(part + 1) * BLK] = ordered[:, h * BLK:(h + 1) * BLK]

    def unseen(hit):
        return jnp.full((1, BLK), jnp.where(hit > 0, 0.0, jnp.inf), jnp.float32)

    for slot in range(2 * n):
        hit = jnp.int32(0)
        for i in range(vl_ref.shape[1]):
            hit = hit | jnp.where((vl_ref[0, i] == slot) & (i < cnt_ref[0, 0]), 1, 0)
        mask[0, slot:slot + 1] = unseen(hit)
    hit = jnp.int32(0)
    for i in range(sl_ref.shape[1]):
        hit = hit | jnp.where((sl_ref[0, i] == 1) & (i < cnt_ref[0, 1]), 1, 0)
    mask[0, 2 * OWN:2 * OWN + 2] = jnp.concatenate([jnp.zeros((1, BLK), jnp.float32), unseen(hit)], 0)
    mask[0, 2 * GUEST:2 * GUEST + 2] = jnp.concatenate([unseen(hit), jnp.full((1, BLK), jnp.inf, jnp.float32)], 0)
    mask[0, 2 * ALONE:2 * ALONE + 2] = jnp.concatenate(
        [jnp.zeros((1, BLK), jnp.float32), jnp.full((1, BLK), jnp.inf, jnp.float32)], 0)

    @pl.when(z == 0)
    def _():
        slash_hop(heads).start()

    @pl.when(z == last)
    def _():
        for g in range(GUESTS):
            guest_q(g).start()
        guest_mask().start()

    put_keys(ck_raw[vp_ref[1 - s]], put_pool(1 - s, 0))
    put_values(cv_raw[vp_ref[1 - s]], put_pool(1 - s, 1))

    key_id = lax.broadcasted_iota(jnp.int32, (BLK, rows), 0)
    row_id = lax.broadcasted_iota(jnp.int32, (BLK, rows), 1) // groups
    later = jnp.where(key_id > row_id, -1e30, 0.0).astype(jnp.bfloat16)
    slots = acc.shape[0]
    for slot in range(slots):
        q_ref[slot, head_dim:] = later if slot < heads else jnp.zeros_like(later)
        acc[slot] = jnp.zeros_like(acc[slot])
        total[slot] = jnp.zeros_like(total[slot])
        peak[slot] = jnp.full_like(peak[slot], -1e30)
    q_ref[slots - 1, 0:head_dim] = jnp.zeros_like(later)
    one_at = lax.broadcasted_iota(jnp.int32, (BLK, BLK), 0) == lax.broadcasted_iota(jnp.int32, (BLK, BLK), 1)
    ext[0] = jnp.zeros((BLK, BLK), jnp.bfloat16)
    ext[1] = jnp.where(one_at, 1.0, 0.0).astype(jnp.bfloat16)
    scores_b[...] = jnp.zeros_like(scores_b)
    top_b[...] = jnp.zeros_like(top_b)

    def spread(row):
        return jnp.concatenate([row] * groups, 1)

    def place(src):
        return src - src // ALONE

    def hidden(slot, src, b):
        return spread(mask[(slot // heads) % 2 * (1 - slot // (slots - 1)), pl.ds(2 * src + b, 1)])

    def ahead(unit, scores, top):
        slot, src, h = unit
        q = q_ref[slot]
        high = None
        for b in range(2):
            causal = (src // OWN) * (1 - src % 2) if b == 0 else 0
            keys = jnp.concatenate([pool[place(src), h, b, 0], ext[causal]], 1)
            found = jnp.dot(keys, q, preferred_element_type=jnp.float32)
            scores[b * BLK:(b + 1) * BLK] = found
            part = jnp.max(found, axis=0, keepdims=True) - hidden(slot, src, b)
            high = part if high is None else jnp.maximum(high, part)
        top[...] = high

    def behind(unit, scores, top):
        slot, src, h = unit
        old = peak[slot]
        high = jnp.maximum(old, top[...])
        factor = jnp.exp2((old - high) * c)
        peak[slot] = high
        weights = [jnp.exp2((scores[b * BLK:(b + 1) * BLK] - (high + hidden(slot, src, b))) * c)
                   .astype(jnp.bfloat16) for b in range(2)]
        values = jnp.concatenate([pool[place(src), h, b, 1] for b in range(2)], 1)
        values = jnp.concatenate([values, jnp.ones((16, 2 * BLK), jnp.bfloat16)], 0)
        add = jnp.dot(values, jnp.concatenate(weights, 0), preferred_element_type=jnp.float32)
        acc[slot] = acc[slot] * factor + add[:head_dim]
        total[slot] = total[slot] * factor + add[head_dim:head_dim + 1]

    def ordered(part, those):
        lanes = slice(part * BLK, (part + 1) * BLK)
        done = jnp.concatenate(
            [(acc[h, :, lanes] * (1.0 / total[h, :, lanes])).astype(jnp.bfloat16) for h in those], 1)
        return lax.dot_general(sort_o[...], done, (((0,), (1,)), ((), ())), preferred_element_type=jnp.float32)

    def drain():
        def sent(kind, sources, count):
            blocks = pool.at[pl.ds(0, sources), pl.ds(0, count), s]
            pltpu.make_async_copy(blocks, blocks, send_sem.at[kind]).wait()

        for index in range(n):
            right = heads if index < last - 1 else stay if index < last else 0

            @pl.when(z == index)
            def _():
                if right:
                    sent(1, index + 1, right)
                    slash_hop(right).wait_send()
                if index > 0:
                    sent(0, n - index, heads)
                    slash_sib(heads if index < last else stay, s).wait_send()
                sent(2, n - 1, heads if index < last else stay)
                if index == last:
                    guest_mask().wait_send()
                    for g in range(GUESTS):
                        guest_q(g).wait_send()

    words = [[by_role([sum(step[field] << (BITS * i) for i, step in enumerate(role[start:start + PACK]))
                       for role in roles]) for start in range(0, steps, PACK)] for field in range(5)]

    def step(here, t, before, bufs, old_bufs):
        kind, message, code, block, flags = [(word >> (BITS * t)) & (2 ** BITS - 1) for word in here]
        src, h = message // 4, message % 4

        @pl.when(kind == 1)
        def _():
            block = pool.at[src, h, s]
            pltpu.make_async_copy(block, block, hop_recv.at[src - (src > z).astype(jnp.int32), h]).wait()

            @pl.when((src > z) & has_left)
            def _():
                hop(src, h, False).start()

            @pl.when((src < z) & ((z < last - 1) | ((z == last - 1) & (h < stay))))
            def _():
                hop(src, h, True).start()

            sib(src, h, s).start()

        @pl.when(kind > 1)
        def _():
            @pl.when(kind == 2)
            def _():
                guest_mask().wait_recv()
                for g in range(GUESTS):
                    guest_q(g).wait_recv()

            @pl.when((kind == 3) & has_right)
            def _():
                slash_hop(heads).wait_recv()
                slash_sib(heads, s).start()

            @pl.when((kind == 3) & (z == last))
            def _():
                slash_hop(stay).wait_recv()
                slash_sib(stay, s).start()

        unit = (code % 8, block // 4, block % 4)

        @pl.when(code > 7)
        def _():
            @pl.when(unit[1] < OWN)
            def _():
                sib(unit[1], unit[2], 1 - s).wait_recv()

            @pl.when((unit[1] == OWN) & has_right)
            def _():
                slash_sib(heads, 1 - s).wait_recv()

            @pl.when((unit[1] == OWN) & (z == last))
            def _():
                slash_sib(stay, 1 - s).wait_recv()

        @pl.when(flags % 2 == 1)
        def _():
            ahead(unit, *bufs)
            behind(before, *old_bufs)

        @pl.when(flags > 1)
        def _():
            @pl.when((flags // 4) % 2 == 1)
            def _():
                for kv in range(2):
                    first_hop(2, kv, True).start()

            @pl.when((flags // 8) % 2 == 1)
            def _():
                slash_hop(heads).start()

            @pl.when((flags // 2) % 2 == 1)
            def _():
                g = 0
                part_acc[g] = acc[heads + g].astype(jnp.bfloat16)
                part_stat[g, 0:1] = peak[heads + g]
                part_stat[g, 1:2] = total[heads + g]
                for copy in guest_part(g):
                    copy.start()

            @pl.when(flags // 16 == 1)
            def _():
                for part in range(rows // BLK):
                    most[part] = ordered(part, range(EARLY))

        return unit

    pairs = by_role([(length + 1) // 2 for length in lengths])

    def some_steps(group, before):
        here = []
        for chunks in words:
            word = chunks[-1]
            for i in reversed(range(len(chunks) - 1)):
                word = jnp.where(group == i, chunks[i], word)
            here.append(word)

        def two_steps(i, before):
            mid = step(here, 2 * i, before, (scores_a, top_a), (scores_b, top_b))
            return step(here, 2 * i + 1, mid, (scores_b, top_b), (scores_a, top_a))

        return lax.fori_loop(0, jnp.minimum(PACK // 2, pairs - group * (PACK // 2)), two_steps, before)

    idle = (jnp.int32(IDLE[0]), jnp.int32(GUEST), jnp.int32(0))
    lax.fori_loop(0, by_role([-(-length // PACK) for length in lengths]), some_steps, idle)

    drain()

    @pl.when(z == 0)
    def _():
        unit = (heads - 1, last, heads - 1)
        sib(*unit[1:], 1 - s).wait_recv()
        ahead(unit, scores_a, top_a)
        behind(unit, scores_a, top_a)

    @pl.when(z == last)
    def _():
        for g in range(GUESTS):
            for copy in guest_part(g):
                copy.wait_recv()
            slot = stay + g
            old, new = peak[slot], part_stat[g, 0:1]
            high = jnp.maximum(old, new)
            mine, theirs = jnp.exp2((old - high) * c), jnp.exp2((new - high) * c)
            acc[slot] = acc[slot] * mine + part_acc[g].astype(jnp.float32) * theirs
            total[slot] = total[slot] * mine + part_stat[g, 1:2] * theirs

    tile = EARLY * groups
    for part in range(rows // BLK):
        pair = [half.reshape(-1, tile, head_dim) for half in (most[part], ordered(part, range(EARLY, heads)))]
        o_ref[part * wide:(part + 1) * wide] = jnp.concatenate(pair, 1).reshape(wide, head_dim).astype(o_ref.dtype)

    @pl.when(z == last - 1)
    def _():
        for g in range(GUESTS):
            for copy in guest_part(g):
                copy.wait_send()


def store(o_vmem, o_hbm, sem):
    copies = sem.shape[0]
    rows = o_vmem.shape[0] // copies
    for i in range(copies):
        lines = pl.ds(i * rows, rows)
        pltpu.make_async_copy(o_vmem.at[lines], o_hbm.at[lines], sem.at[i]).start()
    for i in range(copies):
        lines = pl.ds(i * rows, rows)
        pltpu.make_async_copy(o_vmem.at[lines], o_hbm.at[lines], sem.at[i]).wait()


def chain_call(n, q, nk, nv, ck, cv, tables, heads, rows, head_dim):
    def vmem(*shape):
        return pltpu.VMEM(shape, jnp.bfloat16)

    def wide_vmem(*shape):
        return pltpu.VMEM(shape, jnp.float32)

    hbm = pl.BlockSpec(memory_space=pltpu.HBM)
    in_vmem = pl.BlockSpec(memory_space=pltpu.VMEM)
    dma = pltpu.SemaphoreType.DMA
    cached, wide = ck.shape[:2]
    slots = 7
    out = pl.pallas_call(
        functools.partial(chain, n),
        out_shape=pltpu.VMEM((heads * rows, head_dim), jnp.bfloat16),
        in_specs=[hbm] * 9,
        out_specs=in_vmem,
        scratch_shapes=[
            *[pltpu.SMEM(table.shape, table.dtype) for table in tables],
            vmem(heads * rows, head_dim), vmem(wide, head_dim), vmem(wide, head_dim),
            vmem(cached, wide, head_dim), vmem(cached, wide, head_dim),
            vmem(slots, 2 * head_dim, rows), vmem(wide, wide), vmem(wide, wide), vmem(2, BLK, BLK),
            vmem(n + 2, heads, 2, 2, BLK, head_dim),
            wide_vmem(slots, head_dim, rows), wide_vmem(slots, 1, rows), wide_vmem(slots, 1, rows),
            wide_vmem(2, 16, BLK), vmem(GUESTS, head_dim, rows), wide_vmem(GUESTS, 8, rows),
            wide_vmem(2 * BLK, rows), wide_vmem(2 * BLK, rows), wide_vmem(1, rows), wide_vmem(1, rows),
            wide_vmem(rows // BLK, EARLY * BLK, head_dim), vmem(EARLY * BLK, EARLY * BLK),
            dma((3,)), dma((n - 1, heads)), dma((n - 1, heads)), dma((4,)),
            dma((2, GUESTS + 1)), dma((2, GUESTS, 2)), dma((5,)), dma((4,)), pltpu.SemaphoreType.REGULAR,
        ],
        compiler_params=pltpu.CompilerParams(
            collective_id=0, has_side_effects=True, vmem_limit_bytes=60 * 2**20),
    )(*[pltpu.with_memory_space_constraint(x, pltpu.HBM) for x in (q, nk, nv, ck, cv, *tables)])
    return pl.pallas_call(
        store,
        out_shape=jax.ShapeDtypeStruct(out.shape, out.dtype),
        in_specs=[in_vmem],
        out_specs=hbm,
        scratch_shapes=[dma((4,))],
        compiler_params=pltpu.CompilerParams(vmem_limit_bytes=2**20),
    )(out)


def shards(n, queries, new_keys, new_values, cache_keys, cache_values,
           vertical_pool, vertical_lists, slash_lists, list_counts):
    tokens, heads, groups, head_dim = queries.shape
    rows = tokens * groups
    picked = vertical_pool.shape[0]

    def flat(x):
        return x.reshape(-1, head_dim)

    def vmem(*shape):
        return pltpu.VMEM(shape, jnp.bfloat16)

    hbm = pl.BlockSpec(memory_space=pltpu.HBM)
    smem = pl.BlockSpec(memory_space=pltpu.SMEM)
    dma = pltpu.SemaphoreType.DMA
    wide = heads * BLK
    cached = cache_keys.shape[0] // BLK
    if n == 4 and heads == 4 and picked == 2:
        out = chain_call(n, flat(queries), flat(new_keys), flat(new_values),
                         cache_keys.reshape(cached, wide, head_dim), cache_values.reshape(cached, wide, head_dim),
                         (vertical_pool, vertical_lists, slash_lists, list_counts), heads, rows, head_dim)
        return out.reshape(tokens, heads, groups, head_dim)
    out = pl.pallas_call(
        functools.partial(attend, n),
        out_shape=jax.ShapeDtypeStruct((tokens * heads * groups, head_dim), jnp.bfloat16),
        in_specs=[hbm] * 5 + [smem] * 4,
        out_specs=pl.BlockSpec(memory_space=pltpu.VMEM),
        scratch_shapes=[
            vmem(heads * rows, head_dim), vmem(wide, head_dim), vmem(wide, head_dim),
            vmem(cached, wide, head_dim), vmem(cached, wide, head_dim),
            vmem(heads, rows, head_dim), vmem(picked, 2, heads, BLK, head_dim),
            vmem(2, heads, BLK, head_dim), vmem(wide, wide), vmem(wide, wide),
            vmem(n, picked, 2, heads, BLK, head_dim),
            vmem(2, wide, head_dim), vmem(2, heads, BLK, head_dim),
            pltpu.VMEM((heads, head_dim, rows), jnp.float32),
            pltpu.VMEM((heads, 1, rows), jnp.float32),
            pltpu.VMEM((heads, 1, rows), jnp.float32),
            vmem(2, heads, 3 * BLK, rows), pltpu.VMEM((2, heads, 1, rows), jnp.float32),
            dma((n, 2, 2)), dma((n, 2)), dma((n, 2)), dma((n, 2)), dma((4,)), dma((5,)),
        ],
        compiler_params=pltpu.CompilerParams(
            collective_id=0, has_side_effects=True, vmem_limit_bytes=60 * 2**20),
    )(flat(queries), flat(new_keys), flat(new_values), cache_keys.reshape(cached, wide, head_dim),
      cache_values.reshape(cached, wide, head_dim),
      vertical_pool, vertical_lists, slash_lists, list_counts)
    return out.reshape(tokens, heads, groups, head_dim)


def solution(mesh):
    in_specs = (
        P(("grp", "ctx"), "kvh", "sub", None),
        P(("grp", "ctx"), "kvh", None),
        P(("grp", "ctx"), "kvh", None),
        P(("grp", "ctx"), "kvh", None),
        P(("grp", "ctx"), "kvh", None),
        P(("grp", "ctx")),
        P(("grp", "ctx"), None),
        P(("grp", "ctx"), None),
        P(("grp", "ctx"), None),
    )
    out_specs = P(("grp", "ctx"), "kvh", "sub", None)
    return jax.shard_map(functools.partial(shards, mesh.shape["ctx"]), mesh=mesh,
                         in_specs=in_specs, out_specs=out_specs, check_vma=False)
```

```python
import functools
import math

import jax
import jax.numpy as jnp
from jax import lax
from jax.experimental import pallas as pl
from jax.experimental.pallas import tpu as pltpu
from jax.sharding import PartitionSpec as P

BLK = 128
MESH = pl.DeviceIdType.MESH


def attend(n, q_hbm, nk_hbm, nv_hbm, ck_hbm, cv_hbm, vp_ref, vl_ref, sl_ref, cnt_ref, o_ref,
           q_raw, nk_raw, nv_raw, ck_raw, cv_raw, q_ref, own_ref, new_ref, sort_kv, sort_q,
           pool, slash_raw, slash, acc, peak, total, rounded, fade,
           hop_send, hop_recv, sib_send, sib_recv, sl_sem, in_sem):
    z = lax.axis_index("ctx")
    s = lax.axis_index("sub")
    heads, rows, head_dim = q_ref.shape
    groups = rows // BLK
    wide = heads * BLK
    loads = [pltpu.make_async_copy(src, dst, in_sem.at[i]) for i, (src, dst) in enumerate(
        [(ck_hbm, ck_raw), (cv_hbm, cv_raw), (nk_hbm, nk_raw), (nv_hbm, nv_raw), (q_hbm, q_raw)])]
    loads[0].start()
    c = math.log2(math.e) / math.sqrt(head_dim)
    has_left = z > 0
    has_right = z < n - 1
    sib_id = {"sub": 1 - s}

    barrier = pltpu.get_barrier_semaphore()
    pl.semaphore_signal(barrier, inc=1, device_id=sib_id, device_id_type=MESH)

    @pl.when(has_left)
    def _():
        pl.semaphore_signal(barrier, inc=1, device_id={"ctx": z - 1}, device_id_type=MESH)

    @pl.when(has_right)
    def _():
        pl.semaphore_signal(barrier, inc=1, device_id={"ctx": z + 1}, device_id_type=MESH)

    ids = lax.broadcasted_iota(jnp.int32, (wide, wide), 0)
    at = lax.broadcasted_iota(jnp.int32, (wide, wide), 1)
    sort_kv[...] = jnp.where(at == (ids % BLK) * heads + ids // BLK, 1.0, 0.0).astype(jnp.bfloat16)
    token = (ids % BLK) // groups
    sort_q[...] = jnp.where(at == (token * heads + ids // BLK) * groups + ids % groups,
                            1.0, 0.0).astype(jnp.bfloat16)

    def by_head(raw):
        return jnp.dot(sort_kv[...], raw, preferred_element_type=jnp.float32).astype(jnp.bfloat16)

    def put_keys(dst, raw):
        ordered = by_head(raw)
        for h in range(heads):
            dst[h] = ordered[h * BLK:(h + 1) * BLK]

    def put_values(dst, raw):
        ordered = lax.dot_general(raw, sort_kv[...], (((0,), (1,)), ((), ())),
                                  preferred_element_type=jnp.float32).astype(jnp.bfloat16)
        for h in range(heads):
            dst[h] = ordered[:, h * BLK:(h + 1) * BLK]

    def chosen(cache, b):
        return cache[vp_ref[b]]

    pl.semaphore_wait(barrier, 1 + has_left.astype(jnp.int32) + has_right.astype(jnp.int32))

    def hop(src_ref, src, kv, right):
        return pltpu.make_async_remote_copy(
            src_ref=src_ref, dst_ref=pool.at[src, s, kv],
            send_sem=hop_send.at[src, int(right), kv], recv_sem=hop_recv.at[src, kv],
            device_id={"ctx": z + 1 if right else z - 1}, device_id_type=MESH)

    def sib(src, kv):
        return pltpu.make_async_remote_copy(
            src_ref=pool.at[src, s, kv], dst_ref=pool.at[src, s, kv],
            send_sem=sib_send.at[src, kv], recv_sem=sib_recv.at[src, kv],
            device_id=sib_id, device_id_type=MESH)

    def sib_in(src, kv):
        return pltpu.make_async_remote_copy(
            src_ref=pool.at[src, 1 - s, kv], dst_ref=pool.at[src, 1 - s, kv],
            send_sem=sib_send.at[src, kv], recv_sem=sib_recv.at[src, kv],
            device_id=sib_id, device_id_type=MESH)

    def slash_hop(src_ref=nk_hbm):
        return pltpu.make_async_remote_copy(
            src_ref=src_ref, dst_ref=slash_raw.at[s],
            send_sem=sl_sem.at[0], recv_sem=sl_sem.at[1],
            device_id={"ctx": z + 1}, device_id_type=MESH)

    def slash_sib(part):
        return pltpu.make_async_remote_copy(
            src_ref=slash_raw.at[part], dst_ref=slash_raw.at[part],
            send_sem=sl_sem.at[2], recv_sem=sl_sem.at[3],
            device_id=sib_id, device_id_type=MESH)

    for part, src_ref in enumerate((nk_hbm, nv_hbm)):
        @pl.when(has_right & (s == part))
        def _():
            slash_hop(src_ref).start()

    def send_own(kv):
        @pl.when(has_right)
        def _():
            hop(own_ref.at[s, kv], z, kv, True).start()

        @pl.when(has_left)
        def _():
            hop(own_ref.at[s, kv], z, kv, False).start()

    loads[0].wait()
    loads[1].start()
    put_keys(own_ref.at[s, 0], chosen(ck_raw, s))
    for load in loads[2:]:
        load.start()
    send_own(0)
    loads[1].wait()
    put_values(own_ref.at[s, 1], chosen(cv_raw, s))
    send_own(1)
    loads[2].wait()
    loads[3].wait()
    put_keys(new_ref.at[0], nk_raw[...])
    put_values(new_ref.at[1], nv_raw[...])
    put_keys(own_ref.at[1 - s, 0], chosen(ck_raw, 1 - s))
    put_values(own_ref.at[1 - s, 1], chosen(cv_raw, 1 - s))
    loads[4].wait()
    for part in range(rows // BLK):
        ordered = jnp.dot(sort_q[...], q_raw[part * wide:(part + 1) * wide],
                          preferred_element_type=jnp.float32).astype(jnp.bfloat16)
        for h in range(heads):
            q_ref[h, part * BLK:(part + 1) * BLK] = ordered[h * BLK:(h + 1) * BLK]

    def listed(slot):
        count = cnt_ref[0, 0]
        width = vl_ref.shape[1]
        if width <= 8:
            hit = jnp.int32(0)
            for i in range(width):
                hit = hit | jnp.where((vl_ref[0, i] == slot) & (i < count), 1, 0)
            return hit

        def one(i, hit):
            return hit | jnp.where((vl_ref[0, i] == slot) & (i < count), 1, 0)

        return lax.fori_loop(0, width, one, jnp.int32(0))

    def score(keys, q):
        return lax.dot_general(keys, q, (((1,), (1,)), ((), ())),
                               preferred_element_type=jnp.float32)

    def take_keys(side, blocks, first=False):
        for h in range(heads):
            q = q_ref[h]
            raw = []
            tops = []
            for keys, seen in blocks:
                scores = score(keys[h], q)
                if seen is None:
                    key_id = lax.broadcasted_iota(jnp.int32, scores.shape, 0)
                    row_id = lax.broadcasted_iota(jnp.int32, scores.shape, 1) // groups
                    scores = jnp.where(key_id <= row_id, scores, -jnp.inf)
                top = jnp.max(scores, axis=0, keepdims=True)
                if seen is not None:
                    top = jnp.where(seen > 0, top, -jnp.inf)
                raw.append(scores)
                tops.append(top)
            high = functools.reduce(jnp.maximum, tops)
            if not first:
                old = peak[h]
                high = jnp.maximum(old, high)
                factor = jnp.exp2((old - high) * c)
                fade[side, h] = factor
            peak[h] = high
            sums = []
            for i, ((_, seen), scores) in enumerate(zip(blocks, raw)):
                base = high if seen is None else jnp.where(seen > 0, high, jnp.inf)
                weights = jnp.exp2((scores - base) * c)
                sums.append(jnp.sum(weights, axis=0, keepdims=True))
                rounded[side, h, i * BLK:(i + 1) * BLK] = weights.astype(jnp.bfloat16)
            add = sum(sums[1:], sums[0])
            total[h] = add if first else total[h] * fade[side, h] + add

    def take_values(side, blocks, first=False):
        depth = len(blocks) * BLK
        for h in range(heads):
            values = jnp.concatenate([values[h] for values in blocks], 1)
            add = jnp.dot(values, rounded[side, h, :depth], preferred_element_type=jnp.float32)
            acc[h] = add if first else acc[h] * fade[side, h] + add

    take_keys(0, [(new_ref.at[0], None)]
              + [(own_ref.at[b, 0], listed(2 * z + b)) for b in range(2)], first=True)
    take_values(0, [new_ref.at[1]] + [own_ref.at[b, 1] for b in range(2)], first=True)

    @pl.when(has_left)
    def _():
        slash_hop().wait_recv()
        slash_sib(s).start()

    def arrive(src, kv, right):
        hop(own_ref.at[s, kv], src, kv, right).wait_recv()

        @pl.when(has_right if right else has_left)
        def _():
            hop(pool.at[src, s, kv], src, kv, right).start()

        sib(src, kv).start()

    def step(d, carry):
        sides = ((z + d, z + d < n, False), (z - d, z - d >= 0, True))
        for kv in range(2):
            for src, there, right in sides:
                @pl.when(there)
                def _():
                    arrive(src, kv, right)

            for side, (src, there, right) in enumerate(sides):
                @pl.when(there)
                def _():
                    sib_in(src, kv).wait_recv()
                    if kv == 0:
                        take_keys(side, [(pool.at[src, b, 0], listed(2 * src + b))
                                         for b in range(2)])
                    else:
                        take_values(side, [pool.at[src, b, 1] for b in range(2)])

        @pl.when((d == 1) & has_left)
        def _():
            slash_sib(1 - s).wait_recv()
            put_keys(slash.at[0], slash_raw[0])
            put_values(slash.at[1], slash_raw[1])
            back = jnp.int32(0)
            for i in range(sl_ref.shape[1]):
                back = back | jnp.where((sl_ref[0, i] == 1) & (i < cnt_ref[0, 1]), 1, 0)
            take_keys(0, [(slash.at[0], back)])
            take_values(0, [slash.at[1]])

        return carry

    lax.fori_loop(1, n, step, 0)

    for part in range(rows // BLK):
        lanes = slice(part * BLK, (part + 1) * BLK)
        done = jnp.concatenate(
            [(acc[h, :, lanes] / total[h, :, lanes]).astype(jnp.bfloat16) for h in range(heads)], 1)
        o_ref[part * wide:(part + 1) * wide] = lax.dot_general(
            sort_q[...], done, (((0,), (1,)), ((), ())),
            preferred_element_type=jnp.float32).astype(o_ref.dtype)

    def drain(src, carry):
        for kv in range(2):
            @pl.when(has_right & (src <= z))
            def _():
                hop(own_ref.at[s, kv], src, kv, True).wait_send()

            @pl.when(has_left & (src >= z))
            def _():
                hop(own_ref.at[s, kv], src, kv, False).wait_send()

            @pl.when(src != z)
            def _():
                sib(src, kv).wait_send()
        return carry

    lax.fori_loop(0, n, drain, 0)

    @pl.when(has_right)
    def _():
        slash_hop().wait_send()

    @pl.when(has_left)
    def _():
        slash_sib(s).wait_send()

BITS = 5
OWN, GUEST, ALONE = 4, 5, 6
IDLE = (6, 4 * GUEST)
GUESTS = 1
EARLY = 2
PACK = 6


NONE = (-1, -1)
QUEST = (-2, 0)
SLASH = (-3, 0)


def plan(heads):
    zero = [(NONE, (0, 0), 0), (NONE, (0, ALONE), 0), (NONE, (1, 0), 0), ((1, 0), (1, ALONE), 0), (NONE, (2, 0), 0),
        (NONE, (2, ALONE), 0), ((1, 1), (0, 1), 0), (NONE, (3, 0), 0), (NONE, (3, ALONE), 0), ((1, 2), (1, 1), 0),
        (NONE, NONE, 0), ((1, 3), NONE, 0), (NONE, (2, 1), 0), (NONE, NONE, 0), (NONE, (3, 1), 0), ((2, 0), NONE, 0),
        ((2, 1), NONE, 0), (NONE, (0, 2), 0), (NONE, NONE, 0), (NONE, (1, 2), 0), ((2, 2), NONE, 0),
        ((2, 3), NONE, 0), (NONE, (2, 2), 0), (NONE, NONE, 0), (NONE, (3, 2), 0), ((3, 0), NONE, 0),
        ((3, 1), NONE, 0), (NONE, (0, 3), 0), (NONE, NONE, 0), (NONE, (1, 3), 0), ((3, 2), NONE, 16)]
    one = [((0, 0), (0, 1), 0), ((2, 0), (1, 1), 0), ((0, 3), (2, 1), 0), (NONE, (0, 0), 0), ((2, 1), (0, 2), 0),
        ((0, 1), (3, 0), 4), (NONE, (3, 1), 0), (NONE, (1, 2), 0), ((2, 2), (1, 0), 0), ((0, 2), NONE, 8),
        ((2, 3), NONE, 0), (NONE, (2, 2), 0), (NONE, (2, 0), 0), (NONE, NONE, 0), ((3, 0), (3, 2), 0),
        (SLASH, NONE, 0), ((3, 1), NONE, 0), (NONE, (0, 3), 0), (NONE, NONE, 0), (NONE, (0, OWN), 0),
        ((3, 2), (1, 3), 0), (NONE, (1, OWN), 0), (NONE, (2, OWN), 16), ((3, 3), (2, 3), 0), (NONE, (3, OWN), 0),
        (NONE, NONE, 0), (NONE, (3, 3), 0), (NONE, NONE, 0)]
    two = [((1, 0), (0, 2), 0), ((3, 0), (1, 2), 0), (NONE, (2, 2), 0), ((1, 3), (0, 1), 0), ((3, 1), (0, 3), 0),
        (NONE, (3, 2), 0), ((1, 1), (3, 1), 0), ((3, 2), (1, 3), 0), (NONE, NONE, 0), ((0, 0), (1, 1), 0),
        ((3, 3), (2, 3), 0), (NONE, NONE, 0), ((0, 3), (0, 0), 0), (NONE, (3, 3), 0), (NONE, NONE, 0),
        (NONE, (3, 0), 0), ((0, 1), NONE, 0), (QUEST, NONE, 0), (NONE, (4, 2), 0), ((1, 2), (4, GUEST), 0),
        (NONE, (4, 1), 0), (NONE, (4, 0), 0), (NONE, (1, 0), 0), ((0, 2), (2, 1), 2), (NONE, NONE, 0),
        (NONE, (2, 0), 0), (NONE, NONE, 0), (SLASH, NONE, 0), (NONE, (0, OWN), 0), (NONE, (1, OWN), 0),
        (NONE, (2, OWN), 16), (NONE, (3, OWN), 0), (NONE, NONE, 0)]
    three = [(NONE, (0, 3), 0), ((2, 0), (1, 3), 0), (NONE, (2, 3), 0), (NONE, (3, 3), 0), (NONE, (0, 2), 0),
        (SLASH, (3, ALONE), 0), (NONE, NONE, 0), (NONE, (0, OWN), 0), ((2, 1), (1, OWN), 0), (NONE, (2, OWN), 0),
        (NONE, NONE, 0), ((2, 2), (1, 2), 0), (NONE, NONE, 0), ((1, 0), NONE, 0), (NONE, (2, 2), 0), (NONE, NONE, 0),
        (NONE, (0, 1), 0), ((1, 1), NONE, 0), ((0, 0), NONE, 0), (NONE, (1, 1), 0), (NONE, NONE, 0),
        (NONE, (0, 0), 0), ((0, 1), NONE, 0), ((1, 2), NONE, 0), (NONE, (1, 0), 0), (NONE, NONE, 16),
        (NONE, (2, 1), 0), ((0, 2), NONE, 0), (NONE, (2, 0), 0), (NONE, NONE, 0)]

    def build(z, table):
        out, before, used = [], NONE, set()
        for recv, now, flags in table + [(NONE, NONE, 0)]:
            kind, message = (1, recv[0] * 4 + recv[1]) if recv[0] >= 0 else (-recv[0] if recv != NONE else 0, 0)
            slot, src = now
            h = slot if slot < heads else slot - GUESTS
            key = OWN if src == OWN else (src, h)
            first = now != NONE and key not in used and src not in (z, GUEST, ALONE)
            used.add(key)
            code = (slot + (8 if first else 0), src * 4 + h) if now != NONE else IDLE
            busy = now != NONE or before != NONE
            out.append((kind, message) + code + (int(busy) | flags,))
            before = now
        return out

    return [build(z, table) for z, table in enumerate((zero, one, two, three))]


def chain(n, q_hbm, nk_hbm, nv_hbm, ck_hbm, cv_hbm, vp_hbm, vl_hbm, sl_hbm, cnt_hbm, o_ref,
          vp_ref, vl_ref, sl_ref, cnt_ref,
          q_raw, nk_raw, nv_raw, ck_raw, cv_raw, q_ref, sort_kv, sort_q, ext,
          pool, acc, peak, total, mask, part_acc, part_stat, scores_a, scores_b, top_a, top_b, most, sort_o,
          send_sem, hop_recv, sib_recv, sl_sem, q_sem, part_sem, in_sem, table_sem, end_sem, ready):
    z = lax.axis_index("ctx")
    s = lax.axis_index("sub")
    heads = pool.shape[1]
    head_dim, rows = acc.shape[1:]
    groups = rows // BLK
    wide = heads * BLK
    last = n - 1
    stay = heads - GUESTS
    loads = [pltpu.make_async_copy(src, dst, in_sem.at[i]) for i, (src, dst) in enumerate(
        [(ck_hbm, ck_raw), (cv_hbm, cv_raw), (nk_hbm, nk_raw), (nv_hbm, nv_raw), (q_hbm, q_raw)])]
    tables = [pltpu.make_async_copy(src, dst, table_sem.at[i]) for i, (src, dst) in enumerate(
        [(vp_hbm, vp_ref), (vl_hbm, vl_ref), (sl_hbm, sl_ref), (cnt_hbm, cnt_ref)])]
    loads[0].start()
    loads[1].start()
    for table in tables:
        table.start()
    c = math.log2(math.e) / math.sqrt(head_dim)
    has_left = z > 0
    has_right = z < last
    sib_id = {"sub": 1 - s}
    inner = has_left & has_right

    barrier = pltpu.get_barrier_semaphore()
    pl.semaphore_signal(barrier, inc=1, device_id=sib_id, device_id_type=MESH)

    @pl.when(has_right)
    def _():
        pl.semaphore_signal(barrier, inc=1, device_id={"ctx": z + 1}, device_id_type=MESH)

    def by_role(values):
        out = jnp.int32(values[-1])
        for i in reversed(range(len(values) - 1)):
            out = jnp.where(z == i, jnp.int32(values[i]), out)
        return out

    roles = plan(heads)
    lengths = [max(t for t, step in enumerate(role) if step[0] or step[4]) + 1 for role in roles]
    steps = -(-max(lengths) // PACK) * PACK
    roles = [(role + [(0, 0) + IDLE + (0,)] * steps)[:steps] for role in roles]
    ids = lax.broadcasted_iota(jnp.int32, (wide, wide), 0)
    at = lax.broadcasted_iota(jnp.int32, (wide, wide), 1)
    sort_kv[...] = jnp.where(at == (ids % BLK) * heads + ids // BLK, 1.0, 0.0).astype(jnp.bfloat16)

    pl.semaphore_wait(barrier, 1 + has_left.astype(jnp.int32))

    @pl.when(has_left)
    def _():
        pl.semaphore_signal(ready, inc=1, device_id={"ctx": z - 1}, device_id_type=MESH)

    def put_keys(raw, put, those=range(heads)):
        ordered = jnp.dot(sort_kv[those.start * BLK:those.stop * BLK], raw,
                          preferred_element_type=jnp.float32).astype(jnp.bfloat16)
        for i, h in enumerate(those):
            put(h, ordered[i * BLK:(i + 1) * BLK])

    def put_values(raw, put):
        ordered = lax.dot_general(raw, sort_kv[...], (((0,), (1,)), ((), ())),
                                  preferred_element_type=jnp.float32).astype(jnp.bfloat16)
        for h in range(heads):
            put(h, ordered[:, h * BLK:(h + 1) * BLK])

    def put_pool(b, kv):
        def put(h, block):
            pool[z, h, b, kv] = block
        return put

    def put_new(kv):
        def put(h, block):
            pool[OWN, h, 0, kv] = block
            pool[GUEST, h, 0, kv] = block
            pool[GUEST, h, 1, kv] = jnp.zeros_like(block)
        return put

    def hop(src, h, right):
        return pltpu.make_async_remote_copy(
            src_ref=pool.at[src, h, s], dst_ref=pool.at[src, h, s],
            send_sem=send_sem.at[int(right)], recv_sem=hop_recv.at[src if right else src - 1, h],
            device_id={"ctx": z + 1 if right else z - 1}, device_id_type=MESH)

    def first_hop(h, kv, right):
        return pltpu.make_async_remote_copy(
            src_ref=pool.at[z, h, s, kv], dst_ref=pool.at[z, h, s, kv],
            send_sem=send_sem.at[int(right)], recv_sem=hop_recv.at[z if right else z - 1, h],
            device_id={"ctx": z + 1 if right else z - 1}, device_id_type=MESH)

    def sib(src, h, part):
        return pltpu.make_async_remote_copy(
            src_ref=pool.at[src, h, part], dst_ref=pool.at[src, h, part],
            send_sem=send_sem.at[2], recv_sem=sib_recv.at[src - (src > z).astype(jnp.int32), h],
            device_id=sib_id, device_id_type=MESH)

    end = heads - 1

    def end_hop(kv):
        block = pool.at[last, end, s, kv]
        return pltpu.make_async_remote_copy(
            src_ref=block, dst_ref=block,
            send_sem=send_sem.at[0], recv_sem=end_sem.at[0] if kv else hop_recv.at[last - 1, end],
            device_id={"ctx": z - 1}, device_id_type=MESH)

    def end_across():
        block = pool.at[last, end, s, 1]
        return pltpu.make_async_remote_copy(
            src_ref=block, dst_ref=block, send_sem=end_sem.at[2], recv_sem=end_sem.at[1],
            device_id={"ctx": z - 1, "sub": 1 - s}, device_id_type=MESH)

    def end_sib(part):
        block = pool.at[last, end, part, 0]
        return pltpu.make_async_remote_copy(
            src_ref=block, dst_ref=block, send_sem=end_sem.at[3], recv_sem=sib_recv.at[last - 1, end],
            device_id=sib_id, device_id_type=MESH)

    def slash_hop(count):
        return pltpu.make_async_remote_copy(
            src_ref=pool.at[OWN, pl.ds(0, count), 0, s], dst_ref=pool.at[OWN, pl.ds(0, count), 1, s],
            send_sem=sl_sem.at[0], recv_sem=sl_sem.at[1],
            device_id={"ctx": z + 1}, device_id_type=MESH)

    def slash_sib(count, part):
        block = pool.at[OWN, pl.ds(0, count), 1, part]
        return pltpu.make_async_remote_copy(
            src_ref=block, dst_ref=block,
            send_sem=sl_sem.at[2], recv_sem=sl_sem.at[3],
            device_id=sib_id, device_id_type=MESH)

    def guest_q(g):
        return pltpu.make_async_remote_copy(
            src_ref=q_ref.at[stay + g, pl.ds(0, head_dim)], dst_ref=q_ref.at[heads + g, pl.ds(0, head_dim)],
            send_sem=q_sem.at[0, g], recv_sem=q_sem.at[1, g],
            device_id={"ctx": z - 1}, device_id_type=MESH)

    def guest_mask():
        return pltpu.make_async_remote_copy(
            src_ref=mask.at[0], dst_ref=mask.at[1],
            send_sem=q_sem.at[0, GUESTS], recv_sem=q_sem.at[1, GUESTS],
            device_id={"ctx": z - 1}, device_id_type=MESH)

    def guest_part(g):
        return [pltpu.make_async_remote_copy(
            src_ref=ref.at[g], dst_ref=ref.at[g],
            send_sem=part_sem.at[0, g, i], recv_sem=part_sem.at[1, g, i],
            device_id={"ctx": z + 1}, device_id_type=MESH)
            for i, ref in enumerate((part_acc, part_stat))]

    def leftward(*blocks):
        @pl.when(has_left)
        def _():
            for h, kv in blocks:
                first_hop(h, kv, False).start()

    for table in tables:
        table.wait()
    loads[0].wait()
    put_keys(ck_raw[vp_ref[s]], put_pool(s, 0), range(EARLY))
    leftward(*[(h, 0) for h in range(EARLY)])
    put_keys(ck_raw[vp_ref[s]], put_pool(s, 0), range(EARLY, heads))
    for load in loads[2:]:
        load.start()
    loads[1].wait()
    put_values(cv_raw[vp_ref[s]], put_pool(s, 1))
    leftward((0, 1), (1, 1), *[(h, kv) for h in range(2, heads) for kv in range(2)])

    @pl.when(has_right)
    def _():
        pl.semaphore_wait(ready, 1)

    @pl.when(z == 0)
    def _():
        for h in (0, 3, 1, 2):
            for kv in range(2):
                first_hop(h, kv, True).start()

    @pl.when(z == 1)
    def _():
        for h in (0, 3, 1):
            for kv in range(2):
                first_hop(h, kv, True).start()

    @pl.when(z == 2)
    def _():
        for kv in range(2):
            first_hop(0, kv, True).start()

    loads[2].wait()
    loads[3].wait()
    put_keys(nk_raw[...], put_new(0))
    put_values(nv_raw[...], put_new(1))

    @pl.when(z == 2)
    def _():
        slash_hop(stay).start()
        for h in range(1, stay):
            for kv in range(2):
                first_hop(h, kv, True).start()

    token = (ids % BLK) // groups
    sort_q[...] = jnp.where(at == (token * heads + ids // BLK) * groups + ids % groups,
                            1.0, 0.0).astype(jnp.bfloat16)
    half = EARLY * BLK
    ids = lax.broadcasted_iota(jnp.int32, (half, half), 0)
    at = lax.broadcasted_iota(jnp.int32, (half, half), 1)
    sort_o[...] = jnp.where(at == ((ids % BLK) // groups * EARLY + ids // BLK) * groups + ids % groups,
                            1.0, 0.0).astype(jnp.bfloat16)
    loads[4].wait()
    for part in range(rows // BLK):
        ordered = lax.dot_general(q_raw[part * wide:(part + 1) * wide], sort_q[...], (((0,), (1,)), ((), ())),
                                  preferred_element_type=jnp.float32).astype(jnp.bfloat16)
        for h in range(heads):
            q_ref[h, 0:head_dim, part * BLK:(part + 1) * BLK] = ordered[:, h * BLK:(h + 1) * BLK]

    def unseen(hit):
        return jnp.full((1, BLK), jnp.where(hit > 0, 0.0, jnp.inf), jnp.float32)

    for slot in range(2 * n):
        hit = jnp.int32(0)
        for i in range(vl_ref.shape[1]):
            hit = hit | jnp.where((vl_ref[0, i] == slot) & (i < cnt_ref[0, 0]), 1, 0)
        mask[0, slot:slot + 1] = unseen(hit)
    hit = jnp.int32(0)
    for i in range(sl_ref.shape[1]):
        hit = hit | jnp.where((sl_ref[0, i] == 1) & (i < cnt_ref[0, 1]), 1, 0)
    mask[0, 2 * OWN:2 * OWN + 2] = jnp.concatenate([jnp.zeros((1, BLK), jnp.float32), unseen(hit)], 0)
    mask[0, 2 * GUEST:2 * GUEST + 2] = jnp.concatenate([unseen(hit), jnp.full((1, BLK), jnp.inf, jnp.float32)], 0)
    mask[0, 2 * ALONE:2 * ALONE + 2] = jnp.concatenate(
        [jnp.zeros((1, BLK), jnp.float32), jnp.full((1, BLK), jnp.inf, jnp.float32)], 0)

    @pl.when(z == 0)
    def _():
        slash_hop(heads).start()

    @pl.when(z == last)
    def _():
        for g in range(GUESTS):
            guest_q(g).start()
        guest_mask().start()

    put_keys(ck_raw[vp_ref[1 - s]], put_pool(1 - s, 0))
    put_values(cv_raw[vp_ref[1 - s]], put_pool(1 - s, 1))

    key_id = lax.broadcasted_iota(jnp.int32, (BLK, rows), 0)
    row_id = lax.broadcasted_iota(jnp.int32, (BLK, rows), 1) // groups
    later = jnp.where(key_id > row_id, -1e30, 0.0).astype(jnp.bfloat16)
    slots = acc.shape[0]
    for slot in range(slots):
        q_ref[slot, head_dim:] = later if slot < heads else jnp.zeros_like(later)
        acc[slot] = jnp.zeros_like(acc[slot])
        total[slot] = jnp.zeros_like(total[slot])
        peak[slot] = jnp.full_like(peak[slot], -1e30)
    q_ref[slots - 1, 0:head_dim] = jnp.zeros_like(later)
    one_at = lax.broadcasted_iota(jnp.int32, (BLK, BLK), 0) == lax.broadcasted_iota(jnp.int32, (BLK, BLK), 1)
    ext[0] = jnp.zeros((BLK, BLK), jnp.bfloat16)
    ext[1] = jnp.where(one_at, 1.0, 0.0).astype(jnp.bfloat16)
    scores_b[...] = jnp.zeros_like(scores_b)
    top_b[...] = jnp.zeros_like(top_b)

    def spread(row):
        return jnp.concatenate([row] * groups, 1)

    def place(src):
        return src - src // ALONE

    def hidden(slot, src, b):
        return spread(mask[(slot // heads) % 2 * (1 - slot // (slots - 1)), pl.ds(2 * src + b, 1)])

    def ahead(unit, scores, top):
        slot, src, h = unit
        q = q_ref[slot]
        high = None
        for b in range(2):
            causal = (src // OWN) * (1 - src % 2) if b == 0 else 0
            keys = jnp.concatenate([pool[place(src), h, b, 0], ext[causal]], 1)
            found = jnp.dot(keys, q, preferred_element_type=jnp.float32)
            scores[b * BLK:(b + 1) * BLK] = found
            part = jnp.max(found, axis=0, keepdims=True) - hidden(slot, src, b)
            high = part if high is None else jnp.maximum(high, part)
        top[...] = high

    def behind(unit, scores, top):
        slot, src, h = unit
        old = peak[slot]
        high = jnp.maximum(old, top[...])
        factor = jnp.exp2((old - high) * c)
        peak[slot] = high
        weights = [jnp.exp2((scores[b * BLK:(b + 1) * BLK] - (high + hidden(slot, src, b))) * c)
                   .astype(jnp.bfloat16) for b in range(2)]
        values = jnp.concatenate([pool[place(src), h, b, 1] for b in range(2)], 1)
        values = jnp.concatenate([values, jnp.ones((16, 2 * BLK), jnp.bfloat16)], 0)
        add = jnp.dot(values, jnp.concatenate(weights, 0), preferred_element_type=jnp.float32)
        acc[slot] = acc[slot] * factor + add[:head_dim]
        total[slot] = total[slot] * factor + add[head_dim:head_dim + 1]

    def ordered(part, those):
        lanes = slice(part * BLK, (part + 1) * BLK)
        done = jnp.concatenate(
            [(acc[h, :, lanes] * (1.0 / total[h, :, lanes])).astype(jnp.bfloat16) for h in those], 1)
        return lax.dot_general(sort_o[...], done, (((0,), (1,)), ((), ())), preferred_element_type=jnp.float32)

    def drain():
        def sent(kind, sources, count):
            blocks = pool.at[pl.ds(0, sources), pl.ds(0, count), s]
            pltpu.make_async_copy(blocks, blocks, send_sem.at[kind]).wait()

        for index in range(n):
            right = heads if index < last - 1 else stay if index < last else 0

            @pl.when(z == index)
            def _():
                if right:
                    sent(1, index + 1, right)
                    slash_hop(right).wait_send()
                if index > 0:
                    sent(0, n - index, heads)
                    slash_sib(heads if index < last else stay, s).wait_send()
                if index > 0:
                    sent(2, n - 1, heads if index < last else stay)
                else:
                    copied = q_ref.at[pl.ds(0, heads), pl.ds(0, ((n - 1) * heads - 1) * (2 * BLK * head_dim // rows) // heads)]
                    pltpu.make_async_copy(copied, copied, send_sem.at[2]).wait()
                if index == 1:
                    end_across().wait_send()
                if index == last:
                    guest_mask().wait_send()
                    for g in range(GUESTS):
                        guest_q(g).wait_send()

    words = [[by_role([sum(step[field] << (BITS * i) for i, step in enumerate(role[start:start + PACK]))
                       for role in roles]) for start in range(0, steps, PACK)] for field in range(5)]

    def step(here, t, before, bufs, old_bufs):
        kind, message, code, block, flags = [(word >> (BITS * t)) & (2 ** BITS - 1) for word in here]
        src, h = message // 4, message % 4

        @pl.when(kind == 1)
        def _():
            block = pool.at[src, h, s]
            pltpu.make_async_copy(block, block, hop_recv.at[src - (src > z).astype(jnp.int32), h]).wait()

            split = (z == 1) & (message == last * 4 + end)

            @pl.when((src > z) & has_left & jnp.logical_not(split))
            def _():
                hop(src, h, False).start()

            @pl.when(split)
            def _():
                end_hop(0).start()
                end_hop(1).start()
                end_across().start()

            @pl.when((src < z) & ((z < last - 1) | ((z == last - 1) & (h < stay))))
            def _():
                hop(src, h, True).start()

            sib(src, h, s).start()

        @pl.when(kind > 1)
        def _():
            @pl.when(kind == 2)
            def _():
                guest_mask().wait_recv()
                for g in range(GUESTS):
                    guest_q(g).wait_recv()

            @pl.when((kind == 3) & has_right)
            def _():
                slash_hop(heads).wait_recv()
                slash_sib(heads, s).start()

            @pl.when((kind == 3) & (z == last))
            def _():
                slash_hop(stay).wait_recv()
                slash_sib(stay, s).start()

        unit = (code % 8, block // 4, block % 4)

        @pl.when(code > 7)
        def _():
            @pl.when(unit[1] < OWN)
            def _():
                sib(unit[1], unit[2], 1 - s).wait_recv()

            @pl.when((unit[1] == OWN) & has_right)
            def _():
                slash_sib(heads, 1 - s).wait_recv()

            @pl.when((unit[1] == OWN) & (z == last))
            def _():
                slash_sib(stay, 1 - s).wait_recv()

        @pl.when(flags % 2 == 1)
        def _():
            ahead(unit, *bufs)
            behind(before, *old_bufs)

        @pl.when(flags > 1)
        def _():
            @pl.when((flags // 4) % 2 == 1)
            def _():
                for kv in range(2):
                    first_hop(2, kv, True).start()

            @pl.when((flags // 8) % 2 == 1)
            def _():
                slash_hop(heads).start()

            @pl.when((flags // 2) % 2 == 1)
            def _():
                g = 0
                part_acc[g] = acc[heads + g].astype(jnp.bfloat16)
                part_stat[g, 0:1] = peak[heads + g]
                part_stat[g, 1:2] = total[heads + g]
                for copy in guest_part(g):
                    copy.start()

            @pl.when(flags // 16 == 1)
            def _():
                for part in range(rows // BLK):
                    most[part] = ordered(part, range(EARLY))

        return unit

    pairs = by_role([(length + 1) // 2 for length in lengths])

    def some_steps(group, before):
        here = []
        for chunks in words:
            word = chunks[-1]
            for i in reversed(range(len(chunks) - 1)):
                word = jnp.where(group == i, chunks[i], word)
            here.append(word)

        def two_steps(i, before):
            mid = step(here, 2 * i, before, (scores_a, top_a), (scores_b, top_b))
            return step(here, 2 * i + 1, mid, (scores_b, top_b), (scores_a, top_a))

        return lax.fori_loop(0, jnp.minimum(PACK // 2, pairs - group * (PACK // 2)), two_steps, before)

    idle = (jnp.int32(IDLE[0]), jnp.int32(GUEST), jnp.int32(0))
    lax.fori_loop(0, by_role([-(-length // PACK) for length in lengths]), some_steps, idle)

    drain()

    @pl.when(z == 0)
    def _():
        end_hop(0).wait_recv()
        end_sib(s).start()
        sib(last, end - 1, 1 - s).wait_recv()
        unit = (end - 1, last, end - 1)
        ahead(unit, scores_a, top_a)
        behind(unit, scores_a, top_a)
        end_sib(1 - s).wait_recv()
        unit = (end, last, end)
        ahead(unit, scores_b, top_b)
        end_hop(1).wait_recv()
        block = pool.at[last, end, 1 - s, 1]
        pltpu.make_async_copy(block, block, end_sem.at[1]).wait()
        behind(unit, scores_b, top_b)

    @pl.when(z == last)
    def _():
        for g in range(GUESTS):
            for copy in guest_part(g):
                copy.wait_recv()
            slot = stay + g
            old, new = peak[slot], part_stat[g, 0:1]
            high = jnp.maximum(old, new)
            mine, theirs = jnp.exp2((old - high) * c), jnp.exp2((new - high) * c)
            acc[slot] = acc[slot] * mine + part_acc[g].astype(jnp.float32) * theirs
            total[slot] = total[slot] * mine + part_stat[g, 1:2] * theirs

    tile = EARLY * groups
    for part in range(rows // BLK):
        pair = [half.reshape(-1, tile, head_dim) for half in (most[part], ordered(part, range(EARLY, heads)))]
        o_ref[part * wide:(part + 1) * wide] = jnp.concatenate(pair, 1).reshape(wide, head_dim).astype(o_ref.dtype)

    @pl.when(z == 0)
    def _():
        end_sib(s).wait_send()

    @pl.when(z == last - 1)
    def _():
        for g in range(GUESTS):
            for copy in guest_part(g):
                copy.wait_send()


def store(o_vmem, o_hbm, sem):
    copies = sem.shape[0]
    rows = o_vmem.shape[0] // copies
    for i in range(copies):
        lines = pl.ds(i * rows, rows)
        pltpu.make_async_copy(o_vmem.at[lines], o_hbm.at[lines], sem.at[i]).start()
    for i in range(copies):
        lines = pl.ds(i * rows, rows)
        pltpu.make_async_copy(o_vmem.at[lines], o_hbm.at[lines], sem.at[i]).wait()


def chain_call(n, q, nk, nv, ck, cv, tables, heads, rows, head_dim):
    def vmem(*shape):
        return pltpu.VMEM(shape, jnp.bfloat16)

    def wide_vmem(*shape):
        return pltpu.VMEM(shape, jnp.float32)

    hbm = pl.BlockSpec(memory_space=pltpu.HBM)
    in_vmem = pl.BlockSpec(memory_space=pltpu.VMEM)
    dma = pltpu.SemaphoreType.DMA
    cached, wide = ck.shape[:2]
    slots = 7
    out = pl.pallas_call(
        functools.partial(chain, n),
        out_shape=pltpu.VMEM((heads * rows, head_dim), jnp.bfloat16),
        in_specs=[hbm] * 9,
        out_specs=in_vmem,
        scratch_shapes=[
            *[pltpu.SMEM(table.shape, table.dtype) for table in tables],
            vmem(heads * rows, head_dim), vmem(wide, head_dim), vmem(wide, head_dim),
            vmem(cached, wide, head_dim), vmem(cached, wide, head_dim),
            vmem(slots, 2 * head_dim, rows), vmem(wide, wide), vmem(wide, wide), vmem(2, BLK, BLK),
            vmem(n + 2, heads, 2, 2, BLK, head_dim),
            wide_vmem(slots, head_dim, rows), wide_vmem(slots, 1, rows), wide_vmem(slots, 1, rows),
            wide_vmem(2, 16, BLK), vmem(GUESTS, head_dim, rows), wide_vmem(GUESTS, 8, rows),
            wide_vmem(2 * BLK, rows), wide_vmem(2 * BLK, rows), wide_vmem(1, rows), wide_vmem(1, rows),
            wide_vmem(rows // BLK, EARLY * BLK, head_dim), vmem(EARLY * BLK, EARLY * BLK),
            dma((3,)), dma((n - 1, heads)), dma((n - 1, heads)), dma((4,)),
            dma((2, GUESTS + 1)), dma((2, GUESTS, 2)), dma((5,)), dma((4,)), dma((4,)), pltpu.SemaphoreType.REGULAR,
        ],
        compiler_params=pltpu.CompilerParams(
            collective_id=0, has_side_effects=True, vmem_limit_bytes=60 * 2**20),
    )(*[pltpu.with_memory_space_constraint(x, pltpu.HBM) for x in (q, nk, nv, ck, cv, *tables)])
    return pl.pallas_call(
        store,
        out_shape=jax.ShapeDtypeStruct(out.shape, out.dtype),
        in_specs=[in_vmem],
        out_specs=hbm,
        scratch_shapes=[dma((4,))],
        compiler_params=pltpu.CompilerParams(vmem_limit_bytes=2**20),
    )(out)


def shards(n, queries, new_keys, new_values, cache_keys, cache_values,
           vertical_pool, vertical_lists, slash_lists, list_counts):
    tokens, heads, groups, head_dim = queries.shape
    rows = tokens * groups
    picked = vertical_pool.shape[0]

    def flat(x):
        return x.reshape(-1, head_dim)

    def vmem(*shape):
        return pltpu.VMEM(shape, jnp.bfloat16)

    hbm = pl.BlockSpec(memory_space=pltpu.HBM)
    smem = pl.BlockSpec(memory_space=pltpu.SMEM)
    dma = pltpu.SemaphoreType.DMA
    wide = heads * BLK
    cached = cache_keys.shape[0] // BLK
    if n == 4 and heads == 4 and picked == 2:
        out = chain_call(n, flat(queries), flat(new_keys), flat(new_values),
                         cache_keys.reshape(cached, wide, head_dim), cache_values.reshape(cached, wide, head_dim),
                         (vertical_pool, vertical_lists, slash_lists, list_counts), heads, rows, head_dim)
        return out.reshape(tokens, heads, groups, head_dim)
    out = pl.pallas_call(
        functools.partial(attend, n),
        out_shape=jax.ShapeDtypeStruct((tokens * heads * groups, head_dim), jnp.bfloat16),
        in_specs=[hbm] * 5 + [smem] * 4,
        out_specs=pl.BlockSpec(memory_space=pltpu.VMEM),
        scratch_shapes=[
            vmem(heads * rows, head_dim), vmem(wide, head_dim), vmem(wide, head_dim),
            vmem(cached, wide, head_dim), vmem(cached, wide, head_dim),
            vmem(heads, rows, head_dim), vmem(picked, 2, heads, BLK, head_dim),
            vmem(2, heads, BLK, head_dim), vmem(wide, wide), vmem(wide, wide),
            vmem(n, picked, 2, heads, BLK, head_dim),
            vmem(2, wide, head_dim), vmem(2, heads, BLK, head_dim),
            pltpu.VMEM((heads, head_dim, rows), jnp.float32),
            pltpu.VMEM((heads, 1, rows), jnp.float32),
            pltpu.VMEM((heads, 1, rows), jnp.float32),
            vmem(2, heads, 3 * BLK, rows), pltpu.VMEM((2, heads, 1, rows), jnp.float32),
            dma((n, 2, 2)), dma((n, 2)), dma((n, 2)), dma((n, 2)), dma((4,)), dma((5,)),
        ],
        compiler_params=pltpu.CompilerParams(
            collective_id=0, has_side_effects=True, vmem_limit_bytes=60 * 2**20),
    )(flat(queries), flat(new_keys), flat(new_values), cache_keys.reshape(cached, wide, head_dim),
      cache_values.reshape(cached, wide, head_dim),
      vertical_pool, vertical_lists, slash_lists, list_counts)
    return out.reshape(tokens, heads, groups, head_dim)


def solution(mesh):
    in_specs = (
        P(("grp", "ctx"), "kvh", "sub", None),
        P(("grp", "ctx"), "kvh", None),
        P(("grp", "ctx"), "kvh", None),
        P(("grp", "ctx"), "kvh", None),
        P(("grp", "ctx"), "kvh", None),
        P(("grp", "ctx")),
        P(("grp", "ctx"), None),
        P(("grp", "ctx"), None),
        P(("grp", "ctx"), None),
    )
    out_specs = P(("grp", "ctx"), "kvh", "sub", None)
    return jax.shard_map(functools.partial(shards, mesh.shape["ctx"]), mesh=mesh,
                         in_specs=in_specs, out_specs=out_specs, check_vma=False)
```

```python
import functools
import math

import jax
import jax.numpy as jnp
from jax import lax
from jax.experimental import pallas as pl
from jax.experimental.pallas import tpu as pltpu
from jax.sharding import PartitionSpec as P

BLK = 128
MESH = pl.DeviceIdType.MESH


def attend(n, q_hbm, nk_hbm, nv_hbm, ck_hbm, cv_hbm, vp_ref, vl_ref, sl_ref, cnt_ref, o_ref,
           q_raw, nk_raw, nv_raw, ck_raw, cv_raw, q_ref, own_ref, new_ref, sort_kv, sort_q,
           pool, slash_raw, slash, acc, peak, total, rounded, fade,
           hop_send, hop_recv, sib_send, sib_recv, sl_sem, in_sem):
    z = lax.axis_index("ctx")
    s = lax.axis_index("sub")
    heads, rows, head_dim = q_ref.shape
    groups = rows // BLK
    wide = heads * BLK
    loads = [pltpu.make_async_copy(src, dst, in_sem.at[i]) for i, (src, dst) in enumerate(
        [(ck_hbm, ck_raw), (cv_hbm, cv_raw), (nk_hbm, nk_raw), (nv_hbm, nv_raw), (q_hbm, q_raw)])]
    loads[0].start()
    c = math.log2(math.e) / math.sqrt(head_dim)
    has_left = z > 0
    has_right = z < n - 1
    sib_id = {"sub": 1 - s}

    barrier = pltpu.get_barrier_semaphore()
    pl.semaphore_signal(barrier, inc=1, device_id=sib_id, device_id_type=MESH)

    @pl.when(has_left)
    def _():
        pl.semaphore_signal(barrier, inc=1, device_id={"ctx": z - 1}, device_id_type=MESH)

    @pl.when(has_right)
    def _():
        pl.semaphore_signal(barrier, inc=1, device_id={"ctx": z + 1}, device_id_type=MESH)

    ids = lax.broadcasted_iota(jnp.int32, (wide, wide), 0)
    at = lax.broadcasted_iota(jnp.int32, (wide, wide), 1)
    sort_kv[...] = jnp.where(at == (ids % BLK) * heads + ids // BLK, 1.0, 0.0).astype(jnp.bfloat16)
    token = (ids % BLK) // groups
    sort_q[...] = jnp.where(at == (token * heads + ids // BLK) * groups + ids % groups,
                            1.0, 0.0).astype(jnp.bfloat16)

    def by_head(raw):
        return jnp.dot(sort_kv[...], raw, preferred_element_type=jnp.float32).astype(jnp.bfloat16)

    def put_keys(dst, raw):
        ordered = by_head(raw)
        for h in range(heads):
            dst[h] = ordered[h * BLK:(h + 1) * BLK]

    def put_values(dst, raw):
        ordered = lax.dot_general(raw, sort_kv[...], (((0,), (1,)), ((), ())),
                                  preferred_element_type=jnp.float32).astype(jnp.bfloat16)
        for h in range(heads):
            dst[h] = ordered[:, h * BLK:(h + 1) * BLK]

    def chosen(cache, b):
        return cache[vp_ref[b]]

    pl.semaphore_wait(barrier, 1 + has_left.astype(jnp.int32) + has_right.astype(jnp.int32))

    def hop(src_ref, src, kv, right):
        return pltpu.make_async_remote_copy(
            src_ref=src_ref, dst_ref=pool.at[src, s, kv],
            send_sem=hop_send.at[src, int(right), kv], recv_sem=hop_recv.at[src, kv],
            device_id={"ctx": z + 1 if right else z - 1}, device_id_type=MESH)

    def sib(src, kv):
        return pltpu.make_async_remote_copy(
            src_ref=pool.at[src, s, kv], dst_ref=pool.at[src, s, kv],
            send_sem=sib_send.at[src, kv], recv_sem=sib_recv.at[src, kv],
            device_id=sib_id, device_id_type=MESH)

    def sib_in(src, kv):
        return pltpu.make_async_remote_copy(
            src_ref=pool.at[src, 1 - s, kv], dst_ref=pool.at[src, 1 - s, kv],
            send_sem=sib_send.at[src, kv], recv_sem=sib_recv.at[src, kv],
            device_id=sib_id, device_id_type=MESH)

    def slash_hop(src_ref=nk_hbm):
        return pltpu.make_async_remote_copy(
            src_ref=src_ref, dst_ref=slash_raw.at[s],
            send_sem=sl_sem.at[0], recv_sem=sl_sem.at[1],
            device_id={"ctx": z + 1}, device_id_type=MESH)

    def slash_sib(part):
        return pltpu.make_async_remote_copy(
            src_ref=slash_raw.at[part], dst_ref=slash_raw.at[part],
            send_sem=sl_sem.at[2], recv_sem=sl_sem.at[3],
            device_id=sib_id, device_id_type=MESH)

    for part, src_ref in enumerate((nk_hbm, nv_hbm)):
        @pl.when(has_right & (s == part))
        def _():
            slash_hop(src_ref).start()

    def send_own(kv):
        @pl.when(has_right)
        def _():
            hop(own_ref.at[s, kv], z, kv, True).start()

        @pl.when(has_left)
        def _():
            hop(own_ref.at[s, kv], z, kv, False).start()

    loads[0].wait()
    loads[1].start()
    put_keys(own_ref.at[s, 0], chosen(ck_raw, s))
    for load in loads[2:]:
        load.start()
    send_own(0)
    loads[1].wait()
    put_values(own_ref.at[s, 1], chosen(cv_raw, s))
    send_own(1)
    loads[2].wait()
    loads[3].wait()
    put_keys(new_ref.at[0], nk_raw[...])
    put_values(new_ref.at[1], nv_raw[...])
    put_keys(own_ref.at[1 - s, 0], chosen(ck_raw, 1 - s))
    put_values(own_ref.at[1 - s, 1], chosen(cv_raw, 1 - s))
    loads[4].wait()
    for part in range(rows // BLK):
        ordered = jnp.dot(sort_q[...], q_raw[part * wide:(part + 1) * wide],
                          preferred_element_type=jnp.float32).astype(jnp.bfloat16)
        for h in range(heads):
            q_ref[h, part * BLK:(part + 1) * BLK] = ordered[h * BLK:(h + 1) * BLK]

    def listed(slot):
        count = cnt_ref[0, 0]
        width = vl_ref.shape[1]
        if width <= 8:
            hit = jnp.int32(0)
            for i in range(width):
                hit = hit | jnp.where((vl_ref[0, i] == slot) & (i < count), 1, 0)
            return hit

        def one(i, hit):
            return hit | jnp.where((vl_ref[0, i] == slot) & (i < count), 1, 0)

        return lax.fori_loop(0, width, one, jnp.int32(0))

    def score(keys, q):
        return lax.dot_general(keys, q, (((1,), (1,)), ((), ())),
                               preferred_element_type=jnp.float32)

    def take_keys(side, blocks, first=False):
        for h in range(heads):
            q = q_ref[h]
            raw = []
            tops = []
            for keys, seen in blocks:
                scores = score(keys[h], q)
                if seen is None:
                    key_id = lax.broadcasted_iota(jnp.int32, scores.shape, 0)
                    row_id = lax.broadcasted_iota(jnp.int32, scores.shape, 1) // groups
                    scores = jnp.where(key_id <= row_id, scores, -jnp.inf)
                top = jnp.max(scores, axis=0, keepdims=True)
                if seen is not None:
                    top = jnp.where(seen > 0, top, -jnp.inf)
                raw.append(scores)
                tops.append(top)
            high = functools.reduce(jnp.maximum, tops)
            if not first:
                old = peak[h]
                high = jnp.maximum(old, high)
                factor = jnp.exp2((old - high) * c)
                fade[side, h] = factor
            peak[h] = high
            sums = []
            for i, ((_, seen), scores) in enumerate(zip(blocks, raw)):
                base = high if seen is None else jnp.where(seen > 0, high, jnp.inf)
                weights = jnp.exp2((scores - base) * c)
                sums.append(jnp.sum(weights, axis=0, keepdims=True))
                rounded[side, h, i * BLK:(i + 1) * BLK] = weights.astype(jnp.bfloat16)
            add = sum(sums[1:], sums[0])
            total[h] = add if first else total[h] * fade[side, h] + add

    def take_values(side, blocks, first=False):
        depth = len(blocks) * BLK
        for h in range(heads):
            values = jnp.concatenate([values[h] for values in blocks], 1)
            add = jnp.dot(values, rounded[side, h, :depth], preferred_element_type=jnp.float32)
            acc[h] = add if first else acc[h] * fade[side, h] + add

    take_keys(0, [(new_ref.at[0], None)]
              + [(own_ref.at[b, 0], listed(2 * z + b)) for b in range(2)], first=True)
    take_values(0, [new_ref.at[1]] + [own_ref.at[b, 1] for b in range(2)], first=True)

    @pl.when(has_left)
    def _():
        slash_hop().wait_recv()
        slash_sib(s).start()

    def arrive(src, kv, right):
        hop(own_ref.at[s, kv], src, kv, right).wait_recv()

        @pl.when(has_right if right else has_left)
        def _():
            hop(pool.at[src, s, kv], src, kv, right).start()

        sib(src, kv).start()

    def step(d, carry):
        sides = ((z + d, z + d < n, False), (z - d, z - d >= 0, True))
        for kv in range(2):
            for src, there, right in sides:
                @pl.when(there)
                def _():
                    arrive(src, kv, right)

            for side, (src, there, right) in enumerate(sides):
                @pl.when(there)
                def _():
                    sib_in(src, kv).wait_recv()
                    if kv == 0:
                        take_keys(side, [(pool.at[src, b, 0], listed(2 * src + b))
                                         for b in range(2)])
                    else:
                        take_values(side, [pool.at[src, b, 1] for b in range(2)])

        @pl.when((d == 1) & has_left)
        def _():
            slash_sib(1 - s).wait_recv()
            put_keys(slash.at[0], slash_raw[0])
            put_values(slash.at[1], slash_raw[1])
            back = jnp.int32(0)
            for i in range(sl_ref.shape[1]):
                back = back | jnp.where((sl_ref[0, i] == 1) & (i < cnt_ref[0, 1]), 1, 0)
            take_keys(0, [(slash.at[0], back)])
            take_values(0, [slash.at[1]])

        return carry

    lax.fori_loop(1, n, step, 0)

    for part in range(rows // BLK):
        lanes = slice(part * BLK, (part + 1) * BLK)
        done = jnp.concatenate(
            [(acc[h, :, lanes] / total[h, :, lanes]).astype(jnp.bfloat16) for h in range(heads)], 1)
        o_ref[part * wide:(part + 1) * wide] = lax.dot_general(
            sort_q[...], done, (((0,), (1,)), ((), ())),
            preferred_element_type=jnp.float32).astype(o_ref.dtype)

    def drain(src, carry):
        for kv in range(2):
            @pl.when(has_right & (src <= z))
            def _():
                hop(own_ref.at[s, kv], src, kv, True).wait_send()

            @pl.when(has_left & (src >= z))
            def _():
                hop(own_ref.at[s, kv], src, kv, False).wait_send()

            @pl.when(src != z)
            def _():
                sib(src, kv).wait_send()
        return carry

    lax.fori_loop(0, n, drain, 0)

    @pl.when(has_right)
    def _():
        slash_hop().wait_send()

    @pl.when(has_left)
    def _():
        slash_sib(s).wait_send()

BITS = 5
OWN, GUEST, ALONE = 4, 5, 6
IDLE = (6, 4 * GUEST)
GUESTS = 1
EARLY = 2
PACK = 6


NONE = (-1, -1)
QUEST = (-2, 0)
SLASH = (-3, 0)


def plan(heads):
    zero = [(NONE, (0, 0), 0), (NONE, (0, ALONE), 0), (NONE, (1, 0), 0), ((1, 0), (1, ALONE), 0), (NONE, (2, 0), 0),
        (NONE, (2, ALONE), 0), ((1, 1), (0, 1), 0), (NONE, (3, 0), 0), (NONE, (3, ALONE), 0), ((1, 2), (1, 1), 0),
        (NONE, NONE, 0), ((1, 3), NONE, 0), (NONE, (2, 1), 0), (NONE, NONE, 0), (NONE, (3, 1), 0), ((2, 0), NONE, 0),
        ((2, 1), NONE, 0), (NONE, (0, 2), 0), (NONE, NONE, 0), (NONE, (1, 2), 0), ((2, 2), NONE, 0),
        ((2, 3), NONE, 0), (NONE, (2, 2), 0), (NONE, NONE, 0), (NONE, (3, 2), 0), ((3, 0), NONE, 0),
        ((3, 1), NONE, 0), (NONE, (0, 3), 0), (NONE, NONE, 0), (NONE, (1, 3), 0), ((3, 2), NONE, 16)]
    one = [((0, 0), (0, 1), 0), ((2, 0), (1, 1), 0), ((0, 3), (2, 1), 0), (NONE, (0, 0), 0), ((2, 1), (0, 2), 0),
        ((0, 1), (3, 0), 4), (NONE, (3, 1), 0), (NONE, (1, 2), 0), ((2, 2), (1, 0), 0), ((0, 2), NONE, 8),
        ((2, 3), NONE, 0), (NONE, (2, 2), 0), (NONE, (2, 0), 0), (NONE, NONE, 0), ((3, 0), (3, 2), 0),
        (SLASH, NONE, 0), ((3, 1), NONE, 0), (NONE, (0, 3), 0), (NONE, NONE, 0), (NONE, (0, OWN), 0),
        ((3, 2), (1, 3), 0), (NONE, (1, OWN), 0), (NONE, (2, OWN), 16), ((3, 3), (2, 3), 0), (NONE, (3, OWN), 0),
        (NONE, NONE, 0), (NONE, (3, 3), 0), (NONE, NONE, 0)]
    two = [((1, 0), (0, 2), 0), ((3, 0), (1, 2), 0), (NONE, (2, 2), 0), ((1, 3), (0, 1), 0), ((3, 1), (0, 3), 0),
        (NONE, (3, 2), 0), ((1, 1), (3, 1), 0), ((3, 2), (1, 3), 0), (NONE, NONE, 0), ((0, 0), (1, 1), 0),
        ((3, 3), (2, 3), 0), (NONE, NONE, 0), ((0, 3), (0, 0), 0), (NONE, (3, 3), 0), (NONE, NONE, 0),
        (NONE, (3, 0), 0), ((0, 1), NONE, 0), (QUEST, NONE, 0), (NONE, (4, 2), 0), ((1, 2), (4, GUEST), 0),
        (NONE, (4, 1), 0), (NONE, (4, 0), 0), (NONE, (1, 0), 0), ((0, 2), (2, 1), 2), (NONE, NONE, 0),
        (NONE, (2, 0), 0), (NONE, NONE, 0), (SLASH, NONE, 0), (NONE, (0, OWN), 0), (NONE, (1, OWN), 0),
        (NONE, (2, OWN), 16), (NONE, (3, OWN), 0), (NONE, NONE, 0)]
    three = [(NONE, (0, 3), 0), ((2, 0), (1, 3), 0), (NONE, (2, 3), 0), (NONE, (3, 3), 0), (NONE, (0, 2), 0),
        (SLASH, (3, ALONE), 0), (NONE, NONE, 0), (NONE, (0, OWN), 0), ((2, 1), (1, OWN), 0), (NONE, (2, OWN), 0),
        (NONE, NONE, 0), ((2, 2), (1, 2), 0), (NONE, NONE, 0), ((1, 0), NONE, 0), (NONE, (2, 2), 0), (NONE, NONE, 0),
        (NONE, (0, 1), 0), ((1, 1), NONE, 0), ((0, 0), NONE, 0), (NONE, (1, 1), 0), (NONE, NONE, 0),
        (NONE, (0, 0), 0), ((0, 1), NONE, 0), ((1, 2), NONE, 0), (NONE, (1, 0), 0), (NONE, NONE, 16),
        (NONE, (2, 1), 0), ((0, 2), NONE, 0), (NONE, (2, 0), 0), (NONE, NONE, 0)]

    def build(z, table):
        out, before, used = [], NONE, set()
        for recv, now, flags in table + [(NONE, NONE, 0)]:
            kind, message = (1, recv[0] * 4 + recv[1]) if recv[0] >= 0 else (-recv[0] if recv != NONE else 0, 0)
            slot, src = now
            h = slot if slot < heads else slot - GUESTS
            key = OWN if src == OWN else (src, h)
            first = now != NONE and key not in used and src not in (z, GUEST, ALONE)
            used.add(key)
            code = (slot + (8 if first else 0), src * 4 + h) if now != NONE else IDLE
            busy = now != NONE or before != NONE
            out.append((kind, message) + code + (int(busy) | flags,))
            before = now
        return out

    return [build(z, table) for z, table in enumerate((zero, one, two, three))]


def chain(n, q_hbm, nk_hbm, nv_hbm, ck_hbm, cv_hbm, vp_hbm, vl_hbm, sl_hbm, cnt_hbm, o_ref,
          vp_ref, vl_ref, sl_ref, cnt_ref,
          q_raw, nk_raw, nv_raw, ck_raw, cv_raw, q_ref, sort_kv, sort_q, ext,
          pool, acc, peak, total, mask, part_acc, part_stat, scores_a, scores_b, top_a, top_b, most, sort_o,
          send_sem, hop_recv, sib_recv, sl_sem, ends_sem, in_sem, ready):
    z = lax.axis_index("ctx")
    s = lax.axis_index("sub")
    heads = pool.shape[1]
    head_dim, rows = acc.shape[1:]
    groups = rows // BLK
    wide = heads * BLK
    last = n - 1
    stay = heads - GUESTS
    loads = [pltpu.make_async_copy(src, dst, in_sem.at[i]) for i, (src, dst) in enumerate(
        [(ck_hbm, ck_raw), (cv_hbm, cv_raw), (nk_hbm, nk_raw), (nv_hbm, nv_raw), (q_hbm, q_raw)])]
    tables = [pltpu.make_async_copy(src, dst, in_sem.at[2 + i]) for i, (src, dst) in enumerate(
        [(vp_hbm, vp_ref), (vl_hbm, vl_ref), (sl_hbm, sl_ref), (cnt_hbm, cnt_ref)])]
    loads[0].start()
    loads[1].start()
    for table in tables:
        table.start()
    c = math.log2(math.e) / math.sqrt(head_dim)
    has_left = z > 0
    has_right = z < last
    sib_id = {"sub": 1 - s}
    inner = has_left & has_right

    barrier = pltpu.get_barrier_semaphore()
    pl.semaphore_signal(barrier, inc=1, device_id=sib_id, device_id_type=MESH)

    @pl.when(has_right)
    def _():
        pl.semaphore_signal(barrier, inc=1, device_id={"ctx": z + 1}, device_id_type=MESH)

    def by_role(values):
        out = jnp.int32(values[-1])
        for i in reversed(range(len(values) - 1)):
            out = jnp.where(z == i, jnp.int32(values[i]), out)
        return out

    roles = plan(heads)
    lengths = [max(t for t, step in enumerate(role) if step[0] or step[4]) + 1 for role in roles]
    steps = -(-max(lengths) // PACK) * PACK
    roles = [(role + [(0, 0) + IDLE + (0,)] * steps)[:steps] for role in roles]
    ids = lax.broadcasted_iota(jnp.int32, (wide, wide), 0)
    at = lax.broadcasted_iota(jnp.int32, (wide, wide), 1)
    sort_kv[...] = jnp.where(at == (ids % BLK) * heads + ids // BLK, 1.0, 0.0).astype(jnp.bfloat16)

    pl.semaphore_wait(barrier, 1 + has_left.astype(jnp.int32))

    @pl.when(has_left)
    def _():
        pl.semaphore_signal(ready, inc=1, device_id={"ctx": z - 1}, device_id_type=MESH)

    def put_keys(raw, put, those=range(heads)):
        ordered = jnp.dot(sort_kv[those.start * BLK:those.stop * BLK], raw,
                          preferred_element_type=jnp.float32).astype(jnp.bfloat16)
        for i, h in enumerate(those):
            put(h, ordered[i * BLK:(i + 1) * BLK])

    def put_values(raw, put):
        ordered = lax.dot_general(raw, sort_kv[...], (((0,), (1,)), ((), ())),
                                  preferred_element_type=jnp.float32).astype(jnp.bfloat16)
        for h in range(heads):
            put(h, ordered[:, h * BLK:(h + 1) * BLK])

    def put_pool(b, kv):
        def put(h, block):
            pool[z, h, b, kv] = block
        return put

    def put_new(kv):
        def put(h, block):
            pool[OWN, h, 0, kv] = block
            pool[GUEST, h, 0, kv] = block
            pool[GUEST, h, 1, kv] = jnp.zeros_like(block)
        return put

    def hop(src, h, right):
        return pltpu.make_async_remote_copy(
            src_ref=pool.at[src, h, s], dst_ref=pool.at[src, h, s],
            send_sem=send_sem.at[int(right)], recv_sem=hop_recv.at[src if right else src - 1, h],
            device_id={"ctx": z + 1 if right else z - 1}, device_id_type=MESH)

    def first_hop(h, kv, right):
        return pltpu.make_async_remote_copy(
            src_ref=pool.at[z, h, s, kv], dst_ref=pool.at[z, h, s, kv],
            send_sem=send_sem.at[int(right)], recv_sem=hop_recv.at[z if right else z - 1, h],
            device_id={"ctx": z + 1 if right else z - 1}, device_id_type=MESH)

    def sib(src, h, part):
        return pltpu.make_async_remote_copy(
            src_ref=pool.at[src, h, part], dst_ref=pool.at[src, h, part],
            send_sem=send_sem.at[2], recv_sem=sib_recv.at[src - (src > z).astype(jnp.int32), h],
            device_id=sib_id, device_id_type=MESH)

    end = heads - 1

    def end_hop(kv):
        block = pool.at[last, end, s, kv]
        return pltpu.make_async_remote_copy(
            src_ref=block, dst_ref=block,
            send_sem=send_sem.at[0], recv_sem=ends_sem.at[1, 0] if kv else hop_recv.at[last - 1, end],
            device_id={"ctx": z - 1}, device_id_type=MESH)

    def end_across():
        block = pool.at[last, end, s, 1]
        return pltpu.make_async_remote_copy(
            src_ref=block, dst_ref=block, send_sem=ends_sem.at[0, 0], recv_sem=ends_sem.at[1, 1],
            device_id={"ctx": z - 1, "sub": 1 - s}, device_id_type=MESH)

    def end_sib(part):
        block = pool.at[last, end, part, 0]
        return pltpu.make_async_remote_copy(
            src_ref=block, dst_ref=block, send_sem=ends_sem.at[0, 1], recv_sem=sib_recv.at[last - 1, end],
            device_id=sib_id, device_id_type=MESH)

    def slash_hop(count):
        return pltpu.make_async_remote_copy(
            src_ref=pool.at[OWN, pl.ds(0, count), 0, s], dst_ref=pool.at[OWN, pl.ds(0, count), 1, s],
            send_sem=sl_sem.at[0], recv_sem=sl_sem.at[1],
            device_id={"ctx": z + 1}, device_id_type=MESH)

    def slash_sib(count, part):
        block = pool.at[OWN, pl.ds(0, count), 1, part]
        return pltpu.make_async_remote_copy(
            src_ref=block, dst_ref=block,
            send_sem=sl_sem.at[2], recv_sem=sl_sem.at[3],
            device_id=sib_id, device_id_type=MESH)

    def guest_q(g):
        return pltpu.make_async_remote_copy(
            src_ref=q_ref.at[stay + g, pl.ds(0, head_dim)], dst_ref=q_ref.at[heads + g, pl.ds(0, head_dim)],
            send_sem=ends_sem.at[0, g], recv_sem=ends_sem.at[1, g],
            device_id={"ctx": z - 1}, device_id_type=MESH)

    def guest_mask():
        return pltpu.make_async_remote_copy(
            src_ref=mask.at[0], dst_ref=mask.at[1],
            send_sem=ends_sem.at[0, GUESTS], recv_sem=ends_sem.at[1, GUESTS],
            device_id={"ctx": z - 1}, device_id_type=MESH)

    def guest_part(g):
        return [pltpu.make_async_remote_copy(
            src_ref=ref.at[g], dst_ref=ref.at[g],
            send_sem=ends_sem.at[0, 2 * g + i], recv_sem=ends_sem.at[1, 2 * g + i],
            device_id={"ctx": z + 1}, device_id_type=MESH)
            for i, ref in enumerate((part_acc, part_stat))]

    def leftward(*blocks):
        @pl.when(has_left)
        def _():
            for h, kv in blocks:
                first_hop(h, kv, False).start()

    for table in tables:
        table.wait()
    loads[0].wait()
    put_keys(ck_raw[vp_ref[s]], put_pool(s, 0), range(EARLY))
    leftward(*[(h, 0) for h in range(EARLY)])
    put_keys(ck_raw[vp_ref[s]], put_pool(s, 0), range(EARLY, heads))
    for load in loads[2:]:
        load.start()
    loads[1].wait()
    put_values(cv_raw[vp_ref[s]], put_pool(s, 1))
    leftward((0, 1), (1, 1), *[(h, kv) for h in range(2, heads) for kv in range(2)])

    @pl.when(has_right)
    def _():
        pl.semaphore_wait(ready, 1)

    @pl.when(z == 0)
    def _():
        for h in (0, 3, 1, 2):
            for kv in range(2):
                first_hop(h, kv, True).start()

    @pl.when(z == 1)
    def _():
        for h in (0, 3, 1):
            for kv in range(2):
                first_hop(h, kv, True).start()

    @pl.when(z == 2)
    def _():
        for kv in range(2):
            first_hop(0, kv, True).start()

    loads[2].wait()
    loads[3].wait()
    put_keys(nk_raw[...], put_new(0))
    put_values(nv_raw[...], put_new(1))

    @pl.when(z == 2)
    def _():
        slash_hop(stay).start()
        for h in range(1, stay):
            for kv in range(2):
                first_hop(h, kv, True).start()

    token = (ids % BLK) // groups
    sort_q[...] = jnp.where(at == (token * heads + ids // BLK) * groups + ids % groups,
                            1.0, 0.0).astype(jnp.bfloat16)
    half = EARLY * BLK
    ids = lax.broadcasted_iota(jnp.int32, (half, half), 0)
    at = lax.broadcasted_iota(jnp.int32, (half, half), 1)
    sort_o[...] = jnp.where(at == ((ids % BLK) // groups * EARLY + ids // BLK) * groups + ids % groups,
                            1.0, 0.0).astype(jnp.bfloat16)
    loads[4].wait()
    for part in range(rows // BLK):
        ordered = lax.dot_general(q_raw[part * wide:(part + 1) * wide], sort_q[...], (((0,), (1,)), ((), ())),
                                  preferred_element_type=jnp.float32).astype(jnp.bfloat16)
        for h in range(heads):
            q_ref[h, 0:head_dim, part * BLK:(part + 1) * BLK] = ordered[:, h * BLK:(h + 1) * BLK]

    def unseen(hit):
        return jnp.full((1, BLK), jnp.where(hit > 0, 0.0, jnp.inf), jnp.float32)

    for slot in range(2 * n):
        hit = jnp.int32(0)
        for i in range(vl_ref.shape[1]):
            hit = hit | jnp.where((vl_ref[0, i] == slot) & (i < cnt_ref[0, 0]), 1, 0)
        mask[0, slot:slot + 1] = unseen(hit)
    hit = jnp.int32(0)
    for i in range(sl_ref.shape[1]):
        hit = hit | jnp.where((sl_ref[0, i] == 1) & (i < cnt_ref[0, 1]), 1, 0)
    mask[0, 2 * OWN:2 * OWN + 2] = jnp.concatenate([jnp.zeros((1, BLK), jnp.float32), unseen(hit)], 0)
    mask[0, 2 * GUEST:2 * GUEST + 2] = jnp.concatenate([unseen(hit), jnp.full((1, BLK), jnp.inf, jnp.float32)], 0)
    mask[0, 2 * ALONE:2 * ALONE + 2] = jnp.concatenate(
        [jnp.zeros((1, BLK), jnp.float32), jnp.full((1, BLK), jnp.inf, jnp.float32)], 0)

    @pl.when(z == 0)
    def _():
        slash_hop(heads).start()

    @pl.when(z == last)
    def _():
        for g in range(GUESTS):
            guest_q(g).start()
        guest_mask().start()

    put_keys(ck_raw[vp_ref[1 - s]], put_pool(1 - s, 0))
    put_values(cv_raw[vp_ref[1 - s]], put_pool(1 - s, 1))

    key_id = lax.broadcasted_iota(jnp.int32, (BLK, rows), 0)
    row_id = lax.broadcasted_iota(jnp.int32, (BLK, rows), 1) // groups
    later = jnp.where(key_id > row_id, -1e30, 0.0).astype(jnp.bfloat16)
    slots = acc.shape[0]
    for slot in range(slots):
        q_ref[slot, head_dim:] = later if slot < heads else jnp.zeros_like(later)
        acc[slot] = jnp.zeros_like(acc[slot])
        total[slot] = jnp.zeros_like(total[slot])
        peak[slot] = jnp.full_like(peak[slot], -1e30)
    q_ref[slots - 1, 0:head_dim] = jnp.zeros_like(later)
    one_at = lax.broadcasted_iota(jnp.int32, (BLK, BLK), 0) == lax.broadcasted_iota(jnp.int32, (BLK, BLK), 1)
    ext[0] = jnp.zeros((BLK, BLK), jnp.bfloat16)
    ext[1] = jnp.where(one_at, 1.0, 0.0).astype(jnp.bfloat16)
    scores_b[...] = jnp.zeros_like(scores_b)
    top_b[...] = jnp.zeros_like(top_b)

    def spread(row):
        return jnp.concatenate([row] * groups, 1)

    def place(src):
        return src - src // ALONE

    def hidden(slot, src, b):
        return spread(mask[(slot // heads) % 2 * (1 - slot // (slots - 1)), pl.ds(2 * src + b, 1)])

    def ahead(unit, scores, top):
        slot, src, h = unit
        q = q_ref[slot]
        high = None
        for b in range(2):
            causal = (src // OWN) * (1 - src % 2) if b == 0 else 0
            keys = jnp.concatenate([pool[place(src), h, b, 0], ext[causal]], 1)
            found = jnp.dot(keys, q, preferred_element_type=jnp.float32)
            scores[b * BLK:(b + 1) * BLK] = found
            part = jnp.max(found, axis=0, keepdims=True) - hidden(slot, src, b)
            high = part if high is None else jnp.maximum(high, part)
        top[...] = high

    def behind(unit, scores, top):
        slot, src, h = unit
        old = peak[slot]
        high = jnp.maximum(old, top[...])
        factor = jnp.exp2((old - high) * c)
        peak[slot] = high
        weights = [jnp.exp2((scores[b * BLK:(b + 1) * BLK] - (high + hidden(slot, src, b))) * c)
                   .astype(jnp.bfloat16) for b in range(2)]
        values = jnp.concatenate([pool[place(src), h, b, 1] for b in range(2)], 1)
        values = jnp.concatenate([values, jnp.ones((16, 2 * BLK), jnp.bfloat16)], 0)
        add = jnp.dot(values, jnp.concatenate(weights, 0), preferred_element_type=jnp.float32)
        acc[slot] = acc[slot] * factor + add[:head_dim]
        total[slot] = total[slot] * factor + add[head_dim:head_dim + 1]

    def ordered(part, those):
        lanes = slice(part * BLK, (part + 1) * BLK)
        done = jnp.concatenate(
            [(acc[h, :, lanes] * (1.0 / total[h, :, lanes])).astype(jnp.bfloat16) for h in those], 1)
        return lax.dot_general(sort_o[...], done, (((0,), (1,)), ((), ())), preferred_element_type=jnp.float32)

    def drain():
        def sent(kind, sources, count):
            blocks = pool.at[pl.ds(0, sources), pl.ds(0, count), s]
            pltpu.make_async_copy(blocks, blocks, send_sem.at[kind]).wait()

        for index in range(n):
            right = heads if index < last - 1 else stay if index < last else 0

            @pl.when(z == index)
            def _():
                if right:
                    sent(1, index + 1, right)
                    slash_hop(right).wait_send()
                if index > 0:
                    sent(0, n - index, heads)
                    slash_sib(heads if index < last else stay, s).wait_send()
                if index > 0:
                    sent(2, n - 1, heads if index < last else stay)
                else:
                    copied = q_ref.at[pl.ds(0, heads), pl.ds(0, ((n - 1) * heads - 1) * (2 * BLK * head_dim // rows) // heads)]
                    pltpu.make_async_copy(copied, copied, send_sem.at[2]).wait()
                if index == 1:
                    end_across().wait_send()
                if index == last:
                    guest_mask().wait_send()
                    for g in range(GUESTS):
                        guest_q(g).wait_send()

    words = [[by_role([sum(step[field] << (BITS * i) for i, step in enumerate(role[start:start + PACK]))
                       for role in roles]) for start in range(0, steps, PACK)] for field in range(5)]

    def step(here, t, before, bufs, old_bufs):
        kind, message, code, block, flags = [(word >> (BITS * t)) & (2 ** BITS - 1) for word in here]
        src, h = message // 4, message % 4

        @pl.when(kind == 1)
        def _():
            block = pool.at[src, h, s]
            pltpu.make_async_copy(block, block, hop_recv.at[src - (src > z).astype(jnp.int32), h]).wait()

            split = (z == 1) & (message == last * 4 + end)

            @pl.when((src > z) & has_left & jnp.logical_not(split))
            def _():
                hop(src, h, False).start()

            @pl.when(split)
            def _():
                end_hop(0).start()
                end_hop(1).start()
                end_across().start()

            @pl.when((src < z) & ((z < last - 1) | ((z == last - 1) & (h < stay))))
            def _():
                hop(src, h, True).start()

            sib(src, h, s).start()

        @pl.when(kind > 1)
        def _():
            @pl.when(kind == 2)
            def _():
                guest_mask().wait_recv()
                for g in range(GUESTS):
                    guest_q(g).wait_recv()

            @pl.when((kind == 3) & has_right)
            def _():
                slash_hop(heads).wait_recv()
                slash_sib(heads, s).start()

            @pl.when((kind == 3) & (z == last))
            def _():
                slash_hop(stay).wait_recv()
                slash_sib(stay, s).start()

        unit = (code % 8, block // 4, block % 4)

        @pl.when(code > 7)
        def _():
            @pl.when(unit[1] < OWN)
            def _():
                sib(unit[1], unit[2], 1 - s).wait_recv()

            @pl.when((unit[1] == OWN) & has_right)
            def _():
                slash_sib(heads, 1 - s).wait_recv()

            @pl.when((unit[1] == OWN) & (z == last))
            def _():
                slash_sib(stay, 1 - s).wait_recv()

        @pl.when(flags % 2 == 1)
        def _():
            ahead(unit, *bufs)
            behind(before, *old_bufs)

        @pl.when(flags > 1)
        def _():
            @pl.when((flags // 4) % 2 == 1)
            def _():
                for kv in range(2):
                    first_hop(2, kv, True).start()

            @pl.when((flags // 8) % 2 == 1)
            def _():
                slash_hop(heads).start()

            @pl.when((flags // 2) % 2 == 1)
            def _():
                g = 0
                part_acc[g] = acc[heads + g].astype(jnp.bfloat16)
                part_stat[g, 0:1] = peak[heads + g]
                part_stat[g, 1:2] = total[heads + g]
                for copy in guest_part(g):
                    copy.start()

            @pl.when(flags // 16 == 1)
            def _():
                for part in range(rows // BLK):
                    most[part] = ordered(part, range(EARLY))

        return unit

    pairs = by_role([(length + 1) // 2 for length in lengths])

    def some_steps(group, before):
        here = []
        for chunks in words:
            word = chunks[-1]
            for i in reversed(range(len(chunks) - 1)):
                word = jnp.where(group == i, chunks[i], word)
            here.append(word)

        def two_steps(i, before):
            mid = step(here, 2 * i, before, (scores_a, top_a), (scores_b, top_b))
            return step(here, 2 * i + 1, mid, (scores_b, top_b), (scores_a, top_a))

        return lax.fori_loop(0, jnp.minimum(PACK // 2, pairs - group * (PACK // 2)), two_steps, before)

    idle = (jnp.int32(IDLE[0]), jnp.int32(GUEST), jnp.int32(0))
    lax.fori_loop(0, by_role([-(-length // PACK) for length in lengths]), some_steps, idle)

    drain()

    @pl.when(z == 0)
    def _():
        end_hop(0).wait_recv()
        end_sib(s).start()
        sib(last, end - 1, 1 - s).wait_recv()
        unit = (end - 1, last, end - 1)
        ahead(unit, scores_a, top_a)
        behind(unit, scores_a, top_a)
        end_sib(1 - s).wait_recv()
        unit = (end, last, end)
        ahead(unit, scores_b, top_b)
        end_hop(1).wait_recv()
        block = pool.at[last, end, 1 - s, 1]
        pltpu.make_async_copy(block, block, ends_sem.at[1, 1]).wait()
        behind(unit, scores_b, top_b)

    @pl.when(z == last)
    def _():
        for g in range(GUESTS):
            for copy in guest_part(g):
                copy.wait_recv()
            slot = stay + g
            old, new = peak[slot], part_stat[g, 0:1]
            high = jnp.maximum(old, new)
            mine, theirs = jnp.exp2((old - high) * c), jnp.exp2((new - high) * c)
            acc[slot] = acc[slot] * mine + part_acc[g].astype(jnp.float32) * theirs
            total[slot] = total[slot] * mine + part_stat[g, 1:2] * theirs

    tile = EARLY * groups
    for part in range(rows // BLK):
        pair = [half.reshape(-1, tile, head_dim) for half in (most[part], ordered(part, range(EARLY, heads)))]
        o_ref[part * wide:(part + 1) * wide] = jnp.concatenate(pair, 1).reshape(wide, head_dim).astype(o_ref.dtype)

    @pl.when(z == 0)
    def _():
        end_sib(s).wait_send()

    @pl.when(z == last - 1)
    def _():
        for g in range(GUESTS):
            for copy in guest_part(g):
                copy.wait_send()


def store(o_vmem, o_hbm, sem):
    copies = sem.shape[0]
    rows = o_vmem.shape[0] // copies
    for i in range(copies):
        lines = pl.ds(i * rows, rows)
        pltpu.make_async_copy(o_vmem.at[lines], o_hbm.at[lines], sem.at[i]).start()
    for i in range(copies):
        lines = pl.ds(i * rows, rows)
        pltpu.make_async_copy(o_vmem.at[lines], o_hbm.at[lines], sem.at[i]).wait()


def chain_call(n, q, nk, nv, ck, cv, tables, heads, rows, head_dim):
    def vmem(*shape):
        return pltpu.VMEM(shape, jnp.bfloat16)

    def wide_vmem(*shape):
        return pltpu.VMEM(shape, jnp.float32)

    hbm = pl.BlockSpec(memory_space=pltpu.HBM)
    in_vmem = pl.BlockSpec(memory_space=pltpu.VMEM)
    dma = pltpu.SemaphoreType.DMA
    cached, wide = ck.shape[:2]
    slots = 7
    out = pl.pallas_call(
        functools.partial(chain, n),
        out_shape=pltpu.VMEM((heads * rows, head_dim), jnp.bfloat16),
        in_specs=[hbm] * 9,
        out_specs=in_vmem,
        scratch_shapes=[
            *[pltpu.SMEM(table.shape, table.dtype) for table in tables],
            vmem(heads * rows, head_dim), vmem(wide, head_dim), vmem(wide, head_dim),
            vmem(cached, wide, head_dim), vmem(cached, wide, head_dim),
            vmem(slots, 2 * head_dim, rows), vmem(wide, wide), vmem(wide, wide), vmem(2, BLK, BLK),
            vmem(n + 2, heads, 2, 2, BLK, head_dim),
            wide_vmem(slots, head_dim, rows), wide_vmem(slots, 1, rows), wide_vmem(slots, 1, rows),
            wide_vmem(2, 16, BLK), vmem(GUESTS, head_dim, rows), wide_vmem(GUESTS, 8, rows),
            wide_vmem(2 * BLK, rows), wide_vmem(2 * BLK, rows), wide_vmem(1, rows), wide_vmem(1, rows),
            wide_vmem(rows // BLK, EARLY * BLK, head_dim), vmem(EARLY * BLK, EARLY * BLK),
            dma((3,)), dma((n - 1, heads)), dma((n - 1, heads)), dma((4,)),
            dma((2, 2 * GUESTS)), dma((6,)), pltpu.SemaphoreType.REGULAR,
        ],
        compiler_params=pltpu.CompilerParams(
            collective_id=0, has_side_effects=True, vmem_limit_bytes=60 * 2**20),
    )(*[pltpu.with_memory_space_constraint(x, pltpu.HBM) for x in (q, nk, nv, ck, cv, *tables)])
    return pl.pallas_call(
        store,
        out_shape=jax.ShapeDtypeStruct(out.shape, out.dtype),
        in_specs=[in_vmem],
        out_specs=hbm,
        scratch_shapes=[dma((4,))],
        compiler_params=pltpu.CompilerParams(vmem_limit_bytes=2**20),
    )(out)


def shards(n, queries, new_keys, new_values, cache_keys, cache_values,
           vertical_pool, vertical_lists, slash_lists, list_counts):
    tokens, heads, groups, head_dim = queries.shape
    rows = tokens * groups
    picked = vertical_pool.shape[0]

    def flat(x):
        return x.reshape(-1, head_dim)

    def vmem(*shape):
        return pltpu.VMEM(shape, jnp.bfloat16)

    hbm = pl.BlockSpec(memory_space=pltpu.HBM)
    smem = pl.BlockSpec(memory_space=pltpu.SMEM)
    dma = pltpu.SemaphoreType.DMA
    wide = heads * BLK
    cached = cache_keys.shape[0] // BLK
    if n == 4 and heads == 4 and picked == 2:
        out = chain_call(n, flat(queries), flat(new_keys), flat(new_values),
                         cache_keys.reshape(cached, wide, head_dim), cache_values.reshape(cached, wide, head_dim),
                         (vertical_pool, vertical_lists, slash_lists, list_counts), heads, rows, head_dim)
        return out.reshape(tokens, heads, groups, head_dim)
    out = pl.pallas_call(
        functools.partial(attend, n),
        out_shape=jax.ShapeDtypeStruct((tokens * heads * groups, head_dim), jnp.bfloat16),
        in_specs=[hbm] * 5 + [smem] * 4,
        out_specs=pl.BlockSpec(memory_space=pltpu.VMEM),
        scratch_shapes=[
            vmem(heads * rows, head_dim), vmem(wide, head_dim), vmem(wide, head_dim),
            vmem(cached, wide, head_dim), vmem(cached, wide, head_dim),
            vmem(heads, rows, head_dim), vmem(picked, 2, heads, BLK, head_dim),
            vmem(2, heads, BLK, head_dim), vmem(wide, wide), vmem(wide, wide),
            vmem(n, picked, 2, heads, BLK, head_dim),
            vmem(2, wide, head_dim), vmem(2, heads, BLK, head_dim),
            pltpu.VMEM((heads, head_dim, rows), jnp.float32),
            pltpu.VMEM((heads, 1, rows), jnp.float32),
            pltpu.VMEM((heads, 1, rows), jnp.float32),
            vmem(2, heads, 3 * BLK, rows), pltpu.VMEM((2, heads, 1, rows), jnp.float32),
            dma((n, 2, 2)), dma((n, 2)), dma((n, 2)), dma((n, 2)), dma((4,)), dma((5,)),
        ],
        compiler_params=pltpu.CompilerParams(
            collective_id=0, has_side_effects=True, vmem_limit_bytes=60 * 2**20),
    )(flat(queries), flat(new_keys), flat(new_values), cache_keys.reshape(cached, wide, head_dim),
      cache_values.reshape(cached, wide, head_dim),
      vertical_pool, vertical_lists, slash_lists, list_counts)
    return out.reshape(tokens, heads, groups, head_dim)


def solution(mesh):
    in_specs = (
        P(("grp", "ctx"), "kvh", "sub", None),
        P(("grp", "ctx"), "kvh", None),
        P(("grp", "ctx"), "kvh", None),
        P(("grp", "ctx"), "kvh", None),
        P(("grp", "ctx"), "kvh", None),
        P(("grp", "ctx")),
        P(("grp", "ctx"), None),
        P(("grp", "ctx"), None),
        P(("grp", "ctx"), None),
    )
    out_specs = P(("grp", "ctx"), "kvh", "sub", None)
    return jax.shard_map(functools.partial(shards, mesh.shape["ctx"]), mesh=mesh,
                         in_specs=in_specs, out_specs=out_specs, check_vma=False)
```

```python
import functools
import math

import jax
import jax.numpy as jnp
from jax import lax
from jax.experimental import pallas as pl
from jax.experimental.pallas import tpu as pltpu
from jax.sharding import PartitionSpec as P

BLK = 128
MESH = pl.DeviceIdType.MESH


def attend(n, q_hbm, nk_hbm, nv_hbm, ck_hbm, cv_hbm, vp_ref, vl_ref, sl_ref, cnt_ref, o_ref,
           q_raw, nk_raw, nv_raw, ck_raw, cv_raw, q_ref, own_ref, new_ref, sort_kv, sort_q,
           pool, slash_raw, slash, acc, peak, total, rounded, fade,
           hop_send, hop_recv, sib_send, sib_recv, sl_sem, in_sem):
    z = lax.axis_index("ctx")
    s = lax.axis_index("sub")
    heads, rows, head_dim = q_ref.shape
    groups = rows // BLK
    wide = heads * BLK
    loads = [pltpu.make_async_copy(src, dst, in_sem.at[i]) for i, (src, dst) in enumerate(
        [(ck_hbm, ck_raw), (cv_hbm, cv_raw), (nk_hbm, nk_raw), (nv_hbm, nv_raw), (q_hbm, q_raw)])]
    loads[0].start()
    c = math.log2(math.e) / math.sqrt(head_dim)
    has_left = z > 0
    has_right = z < n - 1
    sib_id = {"sub": 1 - s}

    barrier = pltpu.get_barrier_semaphore()
    pl.semaphore_signal(barrier, inc=1, device_id=sib_id, device_id_type=MESH)

    @pl.when(has_left)
    def _():
        pl.semaphore_signal(barrier, inc=1, device_id={"ctx": z - 1}, device_id_type=MESH)

    @pl.when(has_right)
    def _():
        pl.semaphore_signal(barrier, inc=1, device_id={"ctx": z + 1}, device_id_type=MESH)

    ids = lax.broadcasted_iota(jnp.int32, (wide, wide), 0)
    at = lax.broadcasted_iota(jnp.int32, (wide, wide), 1)
    sort_kv[...] = jnp.where(at == (ids % BLK) * heads + ids // BLK, 1.0, 0.0).astype(jnp.bfloat16)
    token = (ids % BLK) // groups
    sort_q[...] = jnp.where(at == (token * heads + ids // BLK) * groups + ids % groups,
                            1.0, 0.0).astype(jnp.bfloat16)

    def by_head(raw):
        return jnp.dot(sort_kv[...], raw, preferred_element_type=jnp.float32).astype(jnp.bfloat16)

    def put_keys(dst, raw):
        ordered = by_head(raw)
        for h in range(heads):
            dst[h] = ordered[h * BLK:(h + 1) * BLK]

    def put_values(dst, raw):
        ordered = lax.dot_general(raw, sort_kv[...], (((0,), (1,)), ((), ())),
                                  preferred_element_type=jnp.float32).astype(jnp.bfloat16)
        for h in range(heads):
            dst[h] = ordered[:, h * BLK:(h + 1) * BLK]

    def chosen(cache, b):
        return cache[vp_ref[b]]

    pl.semaphore_wait(barrier, 1 + has_left.astype(jnp.int32) + has_right.astype(jnp.int32))

    def hop(src_ref, src, kv, right):
        return pltpu.make_async_remote_copy(
            src_ref=src_ref, dst_ref=pool.at[src, s, kv],
            send_sem=hop_send.at[src, int(right), kv], recv_sem=hop_recv.at[src, kv],
            device_id={"ctx": z + 1 if right else z - 1}, device_id_type=MESH)

    def sib(src, kv):
        return pltpu.make_async_remote_copy(
            src_ref=pool.at[src, s, kv], dst_ref=pool.at[src, s, kv],
            send_sem=sib_send.at[src, kv], recv_sem=sib_recv.at[src, kv],
            device_id=sib_id, device_id_type=MESH)

    def sib_in(src, kv):
        return pltpu.make_async_remote_copy(
            src_ref=pool.at[src, 1 - s, kv], dst_ref=pool.at[src, 1 - s, kv],
            send_sem=sib_send.at[src, kv], recv_sem=sib_recv.at[src, kv],
            device_id=sib_id, device_id_type=MESH)

    def slash_hop(src_ref=nk_hbm):
        return pltpu.make_async_remote_copy(
            src_ref=src_ref, dst_ref=slash_raw.at[s],
            send_sem=sl_sem.at[0], recv_sem=sl_sem.at[1],
            device_id={"ctx": z + 1}, device_id_type=MESH)

    def slash_sib(part):
        return pltpu.make_async_remote_copy(
            src_ref=slash_raw.at[part], dst_ref=slash_raw.at[part],
            send_sem=sl_sem.at[2], recv_sem=sl_sem.at[3],
            device_id=sib_id, device_id_type=MESH)

    for part, src_ref in enumerate((nk_hbm, nv_hbm)):
        @pl.when(has_right & (s == part))
        def _():
            slash_hop(src_ref).start()

    def send_own(kv):
        @pl.when(has_right)
        def _():
            hop(own_ref.at[s, kv], z, kv, True).start()

        @pl.when(has_left)
        def _():
            hop(own_ref.at[s, kv], z, kv, False).start()

    loads[0].wait()
    loads[1].start()
    put_keys(own_ref.at[s, 0], chosen(ck_raw, s))
    for load in loads[2:]:
        load.start()
    send_own(0)
    loads[1].wait()
    put_values(own_ref.at[s, 1], chosen(cv_raw, s))
    send_own(1)
    loads[2].wait()
    loads[3].wait()
    put_keys(new_ref.at[0], nk_raw[...])
    put_values(new_ref.at[1], nv_raw[...])
    put_keys(own_ref.at[1 - s, 0], chosen(ck_raw, 1 - s))
    put_values(own_ref.at[1 - s, 1], chosen(cv_raw, 1 - s))
    loads[4].wait()
    for part in range(rows // BLK):
        ordered = jnp.dot(sort_q[...], q_raw[part * wide:(part + 1) * wide],
                          preferred_element_type=jnp.float32).astype(jnp.bfloat16)
        for h in range(heads):
            q_ref[h, part * BLK:(part + 1) * BLK] = ordered[h * BLK:(h + 1) * BLK]

    def listed(slot):
        count = cnt_ref[0, 0]
        width = vl_ref.shape[1]
        if width <= 8:
            hit = jnp.int32(0)
            for i in range(width):
                hit = hit | jnp.where((vl_ref[0, i] == slot) & (i < count), 1, 0)
            return hit

        def one(i, hit):
            return hit | jnp.where((vl_ref[0, i] == slot) & (i < count), 1, 0)

        return lax.fori_loop(0, width, one, jnp.int32(0))

    def score(keys, q):
        return lax.dot_general(keys, q, (((1,), (1,)), ((), ())),
                               preferred_element_type=jnp.float32)

    def take_keys(side, blocks, first=False):
        for h in range(heads):
            q = q_ref[h]
            raw = []
            tops = []
            for keys, seen in blocks:
                scores = score(keys[h], q)
                if seen is None:
                    key_id = lax.broadcasted_iota(jnp.int32, scores.shape, 0)
                    row_id = lax.broadcasted_iota(jnp.int32, scores.shape, 1) // groups
                    scores = jnp.where(key_id <= row_id, scores, -jnp.inf)
                top = jnp.max(scores, axis=0, keepdims=True)
                if seen is not None:
                    top = jnp.where(seen > 0, top, -jnp.inf)
                raw.append(scores)
                tops.append(top)
            high = functools.reduce(jnp.maximum, tops)
            if not first:
                old = peak[h]
                high = jnp.maximum(old, high)
                factor = jnp.exp2((old - high) * c)
                fade[side, h] = factor
            peak[h] = high
            sums = []
            for i, ((_, seen), scores) in enumerate(zip(blocks, raw)):
                base = high if seen is None else jnp.where(seen > 0, high, jnp.inf)
                weights = jnp.exp2((scores - base) * c)
                sums.append(jnp.sum(weights, axis=0, keepdims=True))
                rounded[side, h, i * BLK:(i + 1) * BLK] = weights.astype(jnp.bfloat16)
            add = sum(sums[1:], sums[0])
            total[h] = add if first else total[h] * fade[side, h] + add

    def take_values(side, blocks, first=False):
        depth = len(blocks) * BLK
        for h in range(heads):
            values = jnp.concatenate([values[h] for values in blocks], 1)
            add = jnp.dot(values, rounded[side, h, :depth], preferred_element_type=jnp.float32)
            acc[h] = add if first else acc[h] * fade[side, h] + add

    take_keys(0, [(new_ref.at[0], None)]
              + [(own_ref.at[b, 0], listed(2 * z + b)) for b in range(2)], first=True)
    take_values(0, [new_ref.at[1]] + [own_ref.at[b, 1] for b in range(2)], first=True)

    @pl.when(has_left)
    def _():
        slash_hop().wait_recv()
        slash_sib(s).start()

    def arrive(src, kv, right):
        hop(own_ref.at[s, kv], src, kv, right).wait_recv()

        @pl.when(has_right if right else has_left)
        def _():
            hop(pool.at[src, s, kv], src, kv, right).start()

        sib(src, kv).start()

    def step(d, carry):
        sides = ((z + d, z + d < n, False), (z - d, z - d >= 0, True))
        for kv in range(2):
            for src, there, right in sides:
                @pl.when(there)
                def _():
                    arrive(src, kv, right)

            for side, (src, there, right) in enumerate(sides):
                @pl.when(there)
                def _():
                    sib_in(src, kv).wait_recv()
                    if kv == 0:
                        take_keys(side, [(pool.at[src, b, 0], listed(2 * src + b))
                                         for b in range(2)])
                    else:
                        take_values(side, [pool.at[src, b, 1] for b in range(2)])

        @pl.when((d == 1) & has_left)
        def _():
            slash_sib(1 - s).wait_recv()
            put_keys(slash.at[0], slash_raw[0])
            put_values(slash.at[1], slash_raw[1])
            back = jnp.int32(0)
            for i in range(sl_ref.shape[1]):
                back = back | jnp.where((sl_ref[0, i] == 1) & (i < cnt_ref[0, 1]), 1, 0)
            take_keys(0, [(slash.at[0], back)])
            take_values(0, [slash.at[1]])

        return carry

    lax.fori_loop(1, n, step, 0)

    for part in range(rows // BLK):
        lanes = slice(part * BLK, (part + 1) * BLK)
        done = jnp.concatenate(
            [(acc[h, :, lanes] / total[h, :, lanes]).astype(jnp.bfloat16) for h in range(heads)], 1)
        o_ref[part * wide:(part + 1) * wide] = lax.dot_general(
            sort_q[...], done, (((0,), (1,)), ((), ())),
            preferred_element_type=jnp.float32).astype(o_ref.dtype)

    def drain(src, carry):
        for kv in range(2):
            @pl.when(has_right & (src <= z))
            def _():
                hop(own_ref.at[s, kv], src, kv, True).wait_send()

            @pl.when(has_left & (src >= z))
            def _():
                hop(own_ref.at[s, kv], src, kv, False).wait_send()

            @pl.when(src != z)
            def _():
                sib(src, kv).wait_send()
        return carry

    lax.fori_loop(0, n, drain, 0)

    @pl.when(has_right)
    def _():
        slash_hop().wait_send()

    @pl.when(has_left)
    def _():
        slash_sib(s).wait_send()

BITS = 5
OWN, GUEST, ALONE = 4, 5, 6
IDLE = (6, 4 * GUEST)
GUESTS = 1
EARLY = 2
PACK = 6


NONE = (-1, -1)
QUEST = (-2, 0)
SLASH = (-3, 0)


def plan(heads):
    zero = [(NONE, (0, 0), 0), (NONE, (0, ALONE), 0), (NONE, (1, 0), 0), ((1, 0), (1, ALONE), 0), (NONE, (2, 0), 0),
        (NONE, (2, ALONE), 0), ((1, 1), (0, 1), 0), (NONE, (3, 0), 0), (NONE, (3, ALONE), 0), ((1, 2), (1, 1), 0),
        (NONE, NONE, 0), ((1, 3), NONE, 0), (NONE, (2, 1), 0), (NONE, NONE, 0), (NONE, (3, 1), 0), ((2, 0), NONE, 0),
        ((2, 1), NONE, 0), (NONE, (0, 2), 0), (NONE, NONE, 0), (NONE, (1, 2), 0), ((2, 2), NONE, 0),
        ((2, 3), NONE, 0), (NONE, (2, 2), 0), (NONE, NONE, 0), (NONE, (3, 2), 0), ((3, 0), NONE, 0),
        ((3, 1), NONE, 0), (NONE, (0, 3), 0), (NONE, NONE, 0), (NONE, (1, 3), 0), ((3, 2), NONE, 0)]
    one = [((0, 0), (0, 1), 0), ((2, 0), (1, 1), 0), ((0, 3), (2, 1), 0), (NONE, (0, 0), 0), ((2, 1), (0, 2), 0),
        ((0, 1), (3, 0), 4), (NONE, (3, 1), 0), (NONE, (1, 2), 0), ((2, 2), (1, 0), 0), ((0, 2), NONE, 8),
        ((2, 3), NONE, 0), (NONE, (2, 2), 0), (NONE, (2, 0), 0), (NONE, NONE, 0), ((3, 0), (3, 2), 0),
        (SLASH, NONE, 0), ((3, 1), NONE, 0), (NONE, (0, 3), 0), (NONE, NONE, 0), (NONE, (0, OWN), 0),
        ((3, 2), (1, 3), 0), (NONE, (1, OWN), 0), (NONE, (2, OWN), 16), ((3, 3), (2, 3), 0), (NONE, (3, OWN), 0),
        (NONE, NONE, 0), (NONE, (3, 3), 0), (NONE, NONE, 0)]
    two = [((1, 0), (0, 2), 0), ((3, 0), (1, 2), 0), (NONE, (2, 2), 0), ((1, 3), (0, 1), 0), ((3, 1), (0, 3), 0),
        (NONE, (3, 2), 0), ((1, 1), (3, 1), 0), ((3, 2), (1, 3), 0), (NONE, NONE, 0), ((0, 0), (1, 1), 0),
        ((3, 3), (2, 3), 0), (NONE, NONE, 0), ((0, 3), (0, 0), 0), (NONE, (3, 3), 0), (NONE, NONE, 0),
        (NONE, (3, 0), 0), ((0, 1), NONE, 0), (QUEST, NONE, 0), (NONE, (4, 2), 0), ((1, 2), (4, GUEST), 0),
        (NONE, (4, 1), 0), (NONE, (4, 0), 0), (NONE, (1, 0), 0), ((0, 2), (2, 1), 2), (NONE, NONE, 0),
        (NONE, (2, 0), 0), (NONE, NONE, 0), (SLASH, NONE, 0), (NONE, (0, OWN), 0), (NONE, (1, OWN), 0),
        (NONE, (2, OWN), 16), (NONE, (3, OWN), 0), (NONE, NONE, 0)]
    three = [(NONE, (0, 3), 0), ((2, 0), (1, 3), 0), (NONE, (2, 3), 0), (NONE, (3, 3), 0), (NONE, (0, 2), 0),
        (SLASH, (3, ALONE), 0), (NONE, NONE, 0), (NONE, (0, OWN), 0), ((2, 1), (1, OWN), 0), (NONE, (2, OWN), 0),
        (NONE, NONE, 0), ((2, 2), (1, 2), 0), (NONE, NONE, 0), ((1, 0), NONE, 0), (NONE, (2, 2), 0), (NONE, NONE, 0),
        (NONE, (0, 1), 0), ((1, 1), NONE, 0), ((0, 0), NONE, 0), (NONE, (1, 1), 0), (NONE, NONE, 0),
        (NONE, (0, 0), 0), ((0, 1), NONE, 0), ((1, 2), NONE, 0), (NONE, (1, 0), 0), (NONE, NONE, 16),
        (NONE, (2, 1), 0), ((0, 2), NONE, 0), (NONE, (2, 0), 0), (NONE, NONE, 0)]

    def build(z, table):
        out, before, used = [], NONE, set()
        for recv, now, flags in table + [(NONE, NONE, 0)]:
            kind, message = (1, recv[0] * 4 + recv[1]) if recv[0] >= 0 else (-recv[0] if recv != NONE else 0, 0)
            slot, src = now
            h = slot if slot < heads else slot - GUESTS
            key = OWN if src == OWN else (src, h)
            first = now != NONE and key not in used and src not in (z, GUEST, ALONE)
            used.add(key)
            code = (slot + (8 if first else 0), src * 4 + h) if now != NONE else IDLE
            busy = now != NONE or before != NONE
            out.append((kind, message) + code + (int(busy) | flags,))
            before = now
        return out

    return [build(z, table) for z, table in enumerate((zero, one, two, three))]


def chain(n, q_hbm, nk_hbm, nv_hbm, ck_hbm, cv_hbm, vp_hbm, vl_hbm, sl_hbm, cnt_hbm, o_ref,
          vp_ref, vl_ref, sl_ref, cnt_ref,
          q_raw, nk_raw, nv_raw, ck_raw, cv_raw, q_ref, sort_kv, sort_q, ext,
          pool, acc, peak, total, mask, part_acc, part_stat, scores_a, scores_b, top_a, top_b, most, sort_o,
          send_sem, hop_recv, sib_recv, sl_sem, ends_sem, in_sem, ready):
    z = lax.axis_index("ctx")
    s = lax.axis_index("sub")
    heads = pool.shape[1]
    head_dim, rows = acc.shape[1:]
    groups = rows // BLK
    wide = heads * BLK
    last = n - 1
    stay = heads - GUESTS
    loads = [pltpu.make_async_copy(src, dst, in_sem.at[i]) for i, (src, dst) in enumerate(
        [(ck_hbm, ck_raw), (cv_hbm, cv_raw), (nk_hbm, nk_raw), (nv_hbm, nv_raw), (q_hbm, q_raw)])]
    tables = [pltpu.make_async_copy(src, dst, in_sem.at[2 + i]) for i, (src, dst) in enumerate(
        [(vp_hbm, vp_ref), (vl_hbm, vl_ref), (sl_hbm, sl_ref), (cnt_hbm, cnt_ref)])]
    loads[0].start()
    loads[1].start()
    for table in tables:
        table.start()
    c = math.log2(math.e) / math.sqrt(head_dim)
    has_left = z > 0
    has_right = z < last
    sib_id = {"sub": 1 - s}
    inner = has_left & has_right

    barrier = pltpu.get_barrier_semaphore()
    pl.semaphore_signal(barrier, inc=1, device_id=sib_id, device_id_type=MESH)

    @pl.when(has_right)
    def _():
        pl.semaphore_signal(barrier, inc=1, device_id={"ctx": z + 1}, device_id_type=MESH)

    def by_role(values):
        out = jnp.int32(values[-1])
        for i in reversed(range(len(values) - 1)):
            out = jnp.where(z == i, jnp.int32(values[i]), out)
        return out

    roles = plan(heads)
    lengths = [max(t for t, step in enumerate(role) if step[0] or step[4]) + 1 for role in roles]
    steps = -(-max(lengths) // PACK) * PACK
    roles = [(role + [(0, 0) + IDLE + (0,)] * steps)[:steps] for role in roles]
    ids = lax.broadcasted_iota(jnp.int32, (wide, wide), 0)
    at = lax.broadcasted_iota(jnp.int32, (wide, wide), 1)
    sort_kv[...] = jnp.where(at == (ids % BLK) * heads + ids // BLK, 1.0, 0.0).astype(jnp.bfloat16)

    pl.semaphore_wait(barrier, 1 + has_left.astype(jnp.int32))

    @pl.when(has_left)
    def _():
        pl.semaphore_signal(ready, inc=1, device_id={"ctx": z - 1}, device_id_type=MESH)

    def put_keys(raw, put, those=range(heads)):
        ordered = jnp.dot(sort_kv[those.start * BLK:those.stop * BLK], raw,
                          preferred_element_type=jnp.float32).astype(jnp.bfloat16)
        for i, h in enumerate(those):
            put(h, ordered[i * BLK:(i + 1) * BLK])

    def put_values(raw, put):
        ordered = lax.dot_general(raw, sort_kv[...], (((0,), (1,)), ((), ())),
                                  preferred_element_type=jnp.float32).astype(jnp.bfloat16)
        for h in range(heads):
            put(h, ordered[:, h * BLK:(h + 1) * BLK])

    def put_pool(b, kv):
        def put(h, block):
            pool[z, h, b, kv] = block
        return put

    def put_new(kv):
        def put(h, block):
            pool[OWN, h, 0, kv] = block
            pool[GUEST, h, 0, kv] = block
            pool[GUEST, h, 1, kv] = jnp.zeros_like(block)
        return put

    def hop(src, h, right):
        return pltpu.make_async_remote_copy(
            src_ref=pool.at[src, h, s], dst_ref=pool.at[src, h, s],
            send_sem=send_sem.at[int(right)], recv_sem=hop_recv.at[src if right else src - 1, h],
            device_id={"ctx": z + 1 if right else z - 1}, device_id_type=MESH)

    def first_hop(h, kv, right):
        return pltpu.make_async_remote_copy(
            src_ref=pool.at[z, h, s, kv], dst_ref=pool.at[z, h, s, kv],
            send_sem=send_sem.at[int(right)], recv_sem=hop_recv.at[z if right else z - 1, h],
            device_id={"ctx": z + 1 if right else z - 1}, device_id_type=MESH)

    def sib(src, h, part):
        return pltpu.make_async_remote_copy(
            src_ref=pool.at[src, h, part], dst_ref=pool.at[src, h, part],
            send_sem=send_sem.at[2], recv_sem=sib_recv.at[src - (src > z).astype(jnp.int32), h],
            device_id=sib_id, device_id_type=MESH)

    end = heads - 1

    def end_hop(kv):
        block = pool.at[last, end, s, kv]
        return pltpu.make_async_remote_copy(
            src_ref=block, dst_ref=block,
            send_sem=send_sem.at[0], recv_sem=ends_sem.at[1, 0] if kv else hop_recv.at[last - 1, end],
            device_id={"ctx": z - 1}, device_id_type=MESH)

    def end_across():
        block = pool.at[last, end, s, 1]
        return pltpu.make_async_remote_copy(
            src_ref=block, dst_ref=block, send_sem=ends_sem.at[0, 0], recv_sem=ends_sem.at[1, 1],
            device_id={"ctx": z - 1, "sub": 1 - s}, device_id_type=MESH)

    def end_sib(part):
        block = pool.at[last, end, part, 0]
        return pltpu.make_async_remote_copy(
            src_ref=block, dst_ref=block, send_sem=ends_sem.at[0, 1], recv_sem=sib_recv.at[last - 1, end],
            device_id=sib_id, device_id_type=MESH)

    def slash_hop(count):
        return pltpu.make_async_remote_copy(
            src_ref=pool.at[OWN, pl.ds(0, count), 0, s], dst_ref=pool.at[OWN, pl.ds(0, count), 1, s],
            send_sem=sl_sem.at[0], recv_sem=sl_sem.at[1],
            device_id={"ctx": z + 1}, device_id_type=MESH)

    def slash_sib(count, part):
        block = pool.at[OWN, pl.ds(0, count), 1, part]
        return pltpu.make_async_remote_copy(
            src_ref=block, dst_ref=block,
            send_sem=sl_sem.at[2], recv_sem=sl_sem.at[3],
            device_id=sib_id, device_id_type=MESH)

    def guest_q(g):
        return pltpu.make_async_remote_copy(
            src_ref=q_ref.at[stay + g, pl.ds(0, head_dim)], dst_ref=q_ref.at[heads + g, pl.ds(0, head_dim)],
            send_sem=ends_sem.at[0, g], recv_sem=ends_sem.at[1, g],
            device_id={"ctx": z - 1}, device_id_type=MESH)

    def guest_mask():
        return pltpu.make_async_remote_copy(
            src_ref=mask.at[0], dst_ref=mask.at[1],
            send_sem=ends_sem.at[0, GUESTS], recv_sem=ends_sem.at[1, GUESTS],
            device_id={"ctx": z - 1}, device_id_type=MESH)

    def guest_part(g):
        return [pltpu.make_async_remote_copy(
            src_ref=ref.at[g], dst_ref=ref.at[g],
            send_sem=ends_sem.at[0, 2 * g + i], recv_sem=ends_sem.at[1, 2 * g + i],
            device_id={"ctx": z + 1}, device_id_type=MESH)
            for i, ref in enumerate((part_acc, part_stat))]

    def leftward(*blocks):
        @pl.when(has_left)
        def _():
            for h, kv in blocks:
                first_hop(h, kv, False).start()

    for table in tables:
        table.wait()
    loads[0].wait()
    put_keys(ck_raw[vp_ref[s]], put_pool(s, 0), range(EARLY))
    leftward(*[(h, 0) for h in range(EARLY)])
    put_keys(ck_raw[vp_ref[s]], put_pool(s, 0), range(EARLY, heads))
    for load in loads[2:]:
        load.start()
    loads[1].wait()
    put_values(cv_raw[vp_ref[s]], put_pool(s, 1))
    leftward((0, 1), (1, 1), *[(h, kv) for h in range(2, heads) for kv in range(2)])

    @pl.when(has_right)
    def _():
        pl.semaphore_wait(ready, 1)

    @pl.when(z == 0)
    def _():
        for h in (0, 3, 1, 2):
            for kv in range(2):
                first_hop(h, kv, True).start()

    @pl.when(z == 1)
    def _():
        for h in (0, 3, 1):
            for kv in range(2):
                first_hop(h, kv, True).start()

    @pl.when(z == 2)
    def _():
        for kv in range(2):
            first_hop(0, kv, True).start()

    loads[2].wait()
    loads[3].wait()
    put_keys(nk_raw[...], put_new(0))
    put_values(nv_raw[...], put_new(1))

    @pl.when(z == 2)
    def _():
        slash_hop(stay).start()
        for h in range(1, stay):
            for kv in range(2):
                first_hop(h, kv, True).start()

    token = (ids % BLK) // groups
    sort_q[...] = jnp.where(at == (token * heads + ids // BLK) * groups + ids % groups,
                            1.0, 0.0).astype(jnp.bfloat16)
    half = EARLY * BLK
    ids = lax.broadcasted_iota(jnp.int32, (half, half), 0)
    at = lax.broadcasted_iota(jnp.int32, (half, half), 1)
    sort_o[...] = jnp.where(at == ((ids % BLK) // groups * EARLY + ids // BLK) * groups + ids % groups,
                            1.0, 0.0).astype(jnp.bfloat16)
    loads[4].wait()
    for part in range(rows // BLK):
        ordered = lax.dot_general(q_raw[part * wide:(part + 1) * wide], sort_q[...], (((0,), (1,)), ((), ())),
                                  preferred_element_type=jnp.float32).astype(jnp.bfloat16)
        for h in range(heads):
            q_ref[h, 0:head_dim, part * BLK:(part + 1) * BLK] = ordered[:, h * BLK:(h + 1) * BLK]

    def unseen(hit):
        return jnp.full((1, BLK), jnp.where(hit > 0, 0.0, jnp.inf), jnp.float32)

    for slot in range(2 * n):
        hit = jnp.int32(0)
        for i in range(vl_ref.shape[1]):
            hit = hit | jnp.where((vl_ref[0, i] == slot) & (i < cnt_ref[0, 0]), 1, 0)
        mask[0, slot:slot + 1] = unseen(hit)
    hit = jnp.int32(0)
    for i in range(sl_ref.shape[1]):
        hit = hit | jnp.where((sl_ref[0, i] == 1) & (i < cnt_ref[0, 1]), 1, 0)
    mask[0, 2 * OWN:2 * OWN + 2] = jnp.concatenate([jnp.zeros((1, BLK), jnp.float32), unseen(hit)], 0)
    mask[0, 2 * GUEST:2 * GUEST + 2] = jnp.concatenate([unseen(hit), jnp.full((1, BLK), jnp.inf, jnp.float32)], 0)
    mask[0, 2 * ALONE:2 * ALONE + 2] = jnp.concatenate(
        [jnp.zeros((1, BLK), jnp.float32), jnp.full((1, BLK), jnp.inf, jnp.float32)], 0)

    @pl.when(z == 0)
    def _():
        slash_hop(heads).start()

    @pl.when(z == last)
    def _():
        for g in range(GUESTS):
            guest_q(g).start()
        guest_mask().start()

    put_keys(ck_raw[vp_ref[1 - s]], put_pool(1 - s, 0))
    put_values(cv_raw[vp_ref[1 - s]], put_pool(1 - s, 1))

    key_id = lax.broadcasted_iota(jnp.int32, (BLK, rows), 0)
    row_id = lax.broadcasted_iota(jnp.int32, (BLK, rows), 1) // groups
    later = jnp.where(key_id > row_id, -1e30, 0.0).astype(jnp.bfloat16)
    slots = acc.shape[0]
    for slot in range(slots):
        q_ref[slot, head_dim:] = later if slot < heads else jnp.zeros_like(later)
        acc[slot] = jnp.zeros_like(acc[slot])
        total[slot] = jnp.zeros_like(total[slot])
        peak[slot] = jnp.full_like(peak[slot], -1e30)
    q_ref[slots - 1, 0:head_dim] = jnp.zeros_like(later)
    one_at = lax.broadcasted_iota(jnp.int32, (BLK, BLK), 0) == lax.broadcasted_iota(jnp.int32, (BLK, BLK), 1)
    ext[0] = jnp.zeros((BLK, BLK), jnp.bfloat16)
    ext[1] = jnp.where(one_at, 1.0, 0.0).astype(jnp.bfloat16)
    scores_b[...] = jnp.zeros_like(scores_b)
    top_b[...] = jnp.zeros_like(top_b)

    def spread(row):
        return jnp.concatenate([row] * groups, 1)

    def place(src):
        return src - src // ALONE

    def hidden(slot, src, b):
        return spread(mask[(slot // heads) % 2 * (1 - slot // (slots - 1)), pl.ds(2 * src + b, 1)])

    def ahead(unit, scores, top):
        slot, src, h = unit
        q = q_ref[slot]
        high = None
        for b in range(2):
            causal = (src // OWN) * (1 - src % 2) if b == 0 else 0
            keys = jnp.concatenate([pool[place(src), h, b, 0], ext[causal]], 1)
            found = jnp.dot(keys, q, preferred_element_type=jnp.float32)
            scores[b * BLK:(b + 1) * BLK] = found
            part = jnp.max(found, axis=0, keepdims=True) - hidden(slot, src, b)
            high = part if high is None else jnp.maximum(high, part)
        top[...] = high

    def behind(unit, scores, top):
        slot, src, h = unit
        old = peak[slot]
        high = jnp.maximum(old, top[...])
        factor = jnp.exp2((old - high) * c)
        peak[slot] = high
        weights = [jnp.exp2((scores[b * BLK:(b + 1) * BLK] - (high + hidden(slot, src, b))) * c)
                   .astype(jnp.bfloat16) for b in range(2)]
        values = jnp.concatenate([pool[place(src), h, b, 1] for b in range(2)], 1)
        values = jnp.concatenate([values, jnp.ones((16, 2 * BLK), jnp.bfloat16)], 0)
        add = jnp.dot(values, jnp.concatenate(weights, 0), preferred_element_type=jnp.float32)
        acc[slot] = acc[slot] * factor + add[:head_dim]
        total[slot] = total[slot] * factor + add[head_dim:head_dim + 1]

    def ordered(part, those):
        lanes = slice(part * BLK, (part + 1) * BLK)
        done = jnp.concatenate(
            [(acc[h, :, lanes] * (1.0 / total[h, :, lanes])).astype(jnp.bfloat16) for h in those], 1)
        return lax.dot_general(sort_o[...], done, (((0,), (1,)), ((), ())), preferred_element_type=jnp.float32)

    def early_output():
        for part in range(rows // BLK):
            most[part] = ordered(part, range(EARLY))

    def drain(index):
        def sent(kind, sources, count):
            blocks = pool.at[pl.ds(0, sources), pl.ds(0, count), s]
            pltpu.make_async_copy(blocks, blocks, send_sem.at[kind]).wait()

        right = heads if index < last - 1 else stay if index < last else 0
        if right:
            sent(1, index + 1, right)
            slash_hop(right).wait_send()
        if index > 0:
            sent(0, n - index, heads)
            slash_sib(heads if index < last else stay, s).wait_send()
            sent(2, n - 1, heads if index < last else stay)
        else:
            copied = q_ref.at[pl.ds(0, heads), pl.ds(0, ((n - 1) * heads - 1) * (2 * BLK * head_dim // rows) // heads)]
            pltpu.make_async_copy(copied, copied, send_sem.at[2]).wait()
        if index == 1:
            end_across().wait_send()
        if index == last:
            guest_mask().wait_send()
            for g in range(GUESTS):
                guest_q(g).wait_send()

    words = [[by_role([sum(step[field] << (BITS * i) for i, step in enumerate(role[start:start + PACK]))
                       for role in roles]) for start in range(0, steps, PACK)] for field in range(5)]

    def step(here, t, before, bufs, old_bufs):
        kind, message, code, block, flags = [(word >> (BITS * t)) & (2 ** BITS - 1) for word in here]
        src, h = message // 4, message % 4

        @pl.when(kind == 1)
        def _():
            block = pool.at[src, h, s]
            pltpu.make_async_copy(block, block, hop_recv.at[src - (src > z).astype(jnp.int32), h]).wait()

            split = (z == 1) & (message == last * 4 + end)

            @pl.when((src > z) & has_left & jnp.logical_not(split))
            def _():
                hop(src, h, False).start()

            @pl.when(split)
            def _():
                end_hop(0).start()
                end_hop(1).start()
                end_across().start()

            @pl.when((src < z) & ((z < last - 1) | ((z == last - 1) & (h < stay))))
            def _():
                hop(src, h, True).start()

            sib(src, h, s).start()

        @pl.when(kind > 1)
        def _():
            @pl.when(kind == 2)
            def _():
                guest_mask().wait_recv()
                for g in range(GUESTS):
                    guest_q(g).wait_recv()

            @pl.when((kind == 3) & has_right)
            def _():
                slash_hop(heads).wait_recv()
                slash_sib(heads, s).start()

            @pl.when((kind == 3) & (z == last))
            def _():
                slash_hop(stay).wait_recv()
                slash_sib(stay, s).start()

        unit = (code % 8, block // 4, block % 4)

        @pl.when(code > 7)
        def _():
            @pl.when(unit[1] < OWN)
            def _():
                sib(unit[1], unit[2], 1 - s).wait_recv()

            @pl.when((unit[1] == OWN) & has_right)
            def _():
                slash_sib(heads, 1 - s).wait_recv()

            @pl.when((unit[1] == OWN) & (z == last))
            def _():
                slash_sib(stay, 1 - s).wait_recv()

        @pl.when(flags % 2 == 1)
        def _():
            ahead(unit, *bufs)
            behind(before, *old_bufs)

        @pl.when(flags > 1)
        def _():
            @pl.when((flags // 4) % 2 == 1)
            def _():
                for kv in range(2):
                    first_hop(2, kv, True).start()

            @pl.when((flags // 8) % 2 == 1)
            def _():
                slash_hop(heads).start()

            @pl.when((flags // 2) % 2 == 1)
            def _():
                g = 0
                part_acc[g] = acc[heads + g].astype(jnp.bfloat16)
                part_stat[g, 0:1] = peak[heads + g]
                part_stat[g, 1:2] = total[heads + g]
                for copy in guest_part(g):
                    copy.start()

            @pl.when(flags // 16 == 1)
            def _():
                early_output()

        return unit

    pairs = by_role([(length + 1) // 2 for length in lengths])

    def some_steps(group, before):
        here = []
        for chunks in words:
            word = chunks[-1]
            for i in reversed(range(len(chunks) - 1)):
                word = jnp.where(group == i, chunks[i], word)
            here.append(word)

        def two_steps(i, before):
            mid = step(here, 2 * i, before, (scores_a, top_a), (scores_b, top_b))
            return step(here, 2 * i + 1, mid, (scores_b, top_b), (scores_a, top_a))

        return lax.fori_loop(0, jnp.minimum(PACK // 2, pairs - group * (PACK // 2)), two_steps, before)

    idle = (jnp.int32(IDLE[0]), jnp.int32(GUEST), jnp.int32(0))
    lax.fori_loop(0, by_role([-(-length // PACK) for length in lengths]), some_steps, idle)

    for index in range(1, n):
        @pl.when(z == index)
        def _():
            drain(index)

    @pl.when(z == 0)
    def _():
        end_hop(0).wait_recv()
        end_sib(s).start()
        sib(last, end - 1, 1 - s).wait_recv()
        unit = (end - 1, last, end - 1)
        ahead(unit, scores_a, top_a)
        behind(unit, scores_a, top_a)
        early_output()
        drain(0)
        end_sib(1 - s).wait_recv()
        unit = (end, last, end)
        ahead(unit, scores_b, top_b)
        end_hop(1).wait_recv()
        block = pool.at[last, end, 1 - s, 1]
        pltpu.make_async_copy(block, block, ends_sem.at[1, 1]).wait()
        behind(unit, scores_b, top_b)

    @pl.when(z == last)
    def _():
        for g in range(GUESTS):
            for copy in guest_part(g):
                copy.wait_recv()
            slot = stay + g
            old, new = peak[slot], part_stat[g, 0:1]
            high = jnp.maximum(old, new)
            mine, theirs = jnp.exp2((old - high) * c), jnp.exp2((new - high) * c)
            acc[slot] = acc[slot] * mine + part_acc[g].astype(jnp.float32) * theirs
            total[slot] = total[slot] * mine + part_stat[g, 1:2] * theirs

    tile = EARLY * groups
    for part in range(rows // BLK):
        pair = [half.reshape(-1, tile, head_dim) for half in (most[part], ordered(part, range(EARLY, heads)))]
        o_ref[part * wide:(part + 1) * wide] = jnp.concatenate(pair, 1).reshape(wide, head_dim).astype(o_ref.dtype)

    @pl.when(z == 0)
    def _():
        end_sib(s).wait_send()

    @pl.when(z == last - 1)
    def _():
        for g in range(GUESTS):
            for copy in guest_part(g):
                copy.wait_send()


def store(o_vmem, o_hbm, sem):
    copies = sem.shape[0]
    rows = o_vmem.shape[0] // copies
    for i in range(copies):
        lines = pl.ds(i * rows, rows)
        pltpu.make_async_copy(o_vmem.at[lines], o_hbm.at[lines], sem.at[i]).start()
    for i in range(copies):
        lines = pl.ds(i * rows, rows)
        pltpu.make_async_copy(o_vmem.at[lines], o_hbm.at[lines], sem.at[i]).wait()


def chain_call(n, q, nk, nv, ck, cv, tables, heads, rows, head_dim):
    def vmem(*shape):
        return pltpu.VMEM(shape, jnp.bfloat16)

    def wide_vmem(*shape):
        return pltpu.VMEM(shape, jnp.float32)

    hbm = pl.BlockSpec(memory_space=pltpu.HBM)
    in_vmem = pl.BlockSpec(memory_space=pltpu.VMEM)
    dma = pltpu.SemaphoreType.DMA
    cached, wide = ck.shape[:2]
    slots = 7
    out = pl.pallas_call(
        functools.partial(chain, n),
        out_shape=pltpu.VMEM((heads * rows, head_dim), jnp.bfloat16),
        in_specs=[hbm] * 9,
        out_specs=in_vmem,
        scratch_shapes=[
            *[pltpu.SMEM(table.shape, table.dtype) for table in tables],
            vmem(heads * rows, head_dim), vmem(wide, head_dim), vmem(wide, head_dim),
            vmem(cached, wide, head_dim), vmem(cached, wide, head_dim),
            vmem(slots, 2 * head_dim, rows), vmem(wide, wide), vmem(wide, wide), vmem(2, BLK, BLK),
            vmem(n + 2, heads, 2, 2, BLK, head_dim),
            wide_vmem(slots, head_dim, rows), wide_vmem(slots, 1, rows), wide_vmem(slots, 1, rows),
            wide_vmem(2, 16, BLK), vmem(GUESTS, head_dim, rows), wide_vmem(GUESTS, 8, rows),
            wide_vmem(2 * BLK, rows), wide_vmem(2 * BLK, rows), wide_vmem(1, rows), wide_vmem(1, rows),
            wide_vmem(rows // BLK, EARLY * BLK, head_dim), vmem(EARLY * BLK, EARLY * BLK),
            dma((3,)), dma((n - 1, heads)), dma((n - 1, heads)), dma((4,)),
            dma((2, 2 * GUESTS)), dma((6,)), pltpu.SemaphoreType.REGULAR,
        ],
        compiler_params=pltpu.CompilerParams(
            collective_id=0, has_side_effects=True, vmem_limit_bytes=60 * 2**20),
    )(*[pltpu.with_memory_space_constraint(x, pltpu.HBM) for x in (q, nk, nv, ck, cv, *tables)])
    return pl.pallas_call(
        store,
        out_shape=jax.ShapeDtypeStruct(out.shape, out.dtype),
        in_specs=[in_vmem],
        out_specs=hbm,
        scratch_shapes=[dma((4,))],
        compiler_params=pltpu.CompilerParams(vmem_limit_bytes=2**20),
    )(out)


def shards(n, queries, new_keys, new_values, cache_keys, cache_values,
           vertical_pool, vertical_lists, slash_lists, list_counts):
    tokens, heads, groups, head_dim = queries.shape
    rows = tokens * groups
    picked = vertical_pool.shape[0]

    def flat(x):
        return x.reshape(-1, head_dim)

    def vmem(*shape):
        return pltpu.VMEM(shape, jnp.bfloat16)

    hbm = pl.BlockSpec(memory_space=pltpu.HBM)
    smem = pl.BlockSpec(memory_space=pltpu.SMEM)
    dma = pltpu.SemaphoreType.DMA
    wide = heads * BLK
    cached = cache_keys.shape[0] // BLK
    if n == 4 and heads == 4 and picked == 2:
        out = chain_call(n, flat(queries), flat(new_keys), flat(new_values),
                         cache_keys.reshape(cached, wide, head_dim), cache_values.reshape(cached, wide, head_dim),
                         (vertical_pool, vertical_lists, slash_lists, list_counts), heads, rows, head_dim)
        return out.reshape(tokens, heads, groups, head_dim)
    out = pl.pallas_call(
        functools.partial(attend, n),
        out_shape=jax.ShapeDtypeStruct((tokens * heads * groups, head_dim), jnp.bfloat16),
        in_specs=[hbm] * 5 + [smem] * 4,
        out_specs=pl.BlockSpec(memory_space=pltpu.VMEM),
        scratch_shapes=[
            vmem(heads * rows, head_dim), vmem(wide, head_dim), vmem(wide, head_dim),
            vmem(cached, wide, head_dim), vmem(cached, wide, head_dim),
            vmem(heads, rows, head_dim), vmem(picked, 2, heads, BLK, head_dim),
            vmem(2, heads, BLK, head_dim), vmem(wide, wide), vmem(wide, wide),
            vmem(n, picked, 2, heads, BLK, head_dim),
            vmem(2, wide, head_dim), vmem(2, heads, BLK, head_dim),
            pltpu.VMEM((heads, head_dim, rows), jnp.float32),
            pltpu.VMEM((heads, 1, rows), jnp.float32),
            pltpu.VMEM((heads, 1, rows), jnp.float32),
            vmem(2, heads, 3 * BLK, rows), pltpu.VMEM((2, heads, 1, rows), jnp.float32),
            dma((n, 2, 2)), dma((n, 2)), dma((n, 2)), dma((n, 2)), dma((4,)), dma((5,)),
        ],
        compiler_params=pltpu.CompilerParams(
            collective_id=0, has_side_effects=True, vmem_limit_bytes=60 * 2**20),
    )(flat(queries), flat(new_keys), flat(new_values), cache_keys.reshape(cached, wide, head_dim),
      cache_values.reshape(cached, wide, head_dim),
      vertical_pool, vertical_lists, slash_lists, list_counts)
    return out.reshape(tokens, heads, groups, head_dim)


def solution(mesh):
    in_specs = (
        P(("grp", "ctx"), "kvh", "sub", None),
        P(("grp", "ctx"), "kvh", None),
        P(("grp", "ctx"), "kvh", None),
        P(("grp", "ctx"), "kvh", None),
        P(("grp", "ctx"), "kvh", None),
        P(("grp", "ctx")),
        P(("grp", "ctx"), None),
        P(("grp", "ctx"), None),
        P(("grp", "ctx"), None),
    )
    out_specs = P(("grp", "ctx"), "kvh", "sub", None)
    return jax.shard_map(functools.partial(shards, mesh.shape["ctx"]), mesh=mesh,
                         in_specs=in_specs, out_specs=out_specs, check_vma=False)
```

```python
import functools
import math

import jax
import jax.numpy as jnp
from jax import lax
from jax.experimental import pallas as pl
from jax.experimental.pallas import tpu as pltpu
from jax.sharding import PartitionSpec as P

BLK = 128
MESH = pl.DeviceIdType.MESH


def attend(n, q_hbm, nk_hbm, nv_hbm, ck_hbm, cv_hbm, vp_ref, vl_ref, sl_ref, cnt_ref, o_ref,
           q_raw, nk_raw, nv_raw, ck_raw, cv_raw, q_ref, own_ref, new_ref, sort_kv, sort_q,
           pool, slash_raw, slash, acc, peak, total, rounded, fade,
           hop_send, hop_recv, sib_send, sib_recv, sl_sem, in_sem):
    z = lax.axis_index("ctx")
    s = lax.axis_index("sub")
    heads, rows, head_dim = q_ref.shape
    groups = rows // BLK
    wide = heads * BLK
    loads = [pltpu.make_async_copy(src, dst, in_sem.at[i]) for i, (src, dst) in enumerate(
        [(ck_hbm, ck_raw), (cv_hbm, cv_raw), (nk_hbm, nk_raw), (nv_hbm, nv_raw), (q_hbm, q_raw)])]
    loads[0].start()
    c = math.log2(math.e) / math.sqrt(head_dim)
    has_left = z > 0
    has_right = z < n - 1
    sib_id = {"sub": 1 - s}

    barrier = pltpu.get_barrier_semaphore()
    pl.semaphore_signal(barrier, inc=1, device_id=sib_id, device_id_type=MESH)

    @pl.when(has_left)
    def _():
        pl.semaphore_signal(barrier, inc=1, device_id={"ctx": z - 1}, device_id_type=MESH)

    @pl.when(has_right)
    def _():
        pl.semaphore_signal(barrier, inc=1, device_id={"ctx": z + 1}, device_id_type=MESH)

    ids = lax.broadcasted_iota(jnp.int32, (wide, wide), 0)
    at = lax.broadcasted_iota(jnp.int32, (wide, wide), 1)
    sort_kv[...] = jnp.where(at == (ids % BLK) * heads + ids // BLK, 1.0, 0.0).astype(jnp.bfloat16)
    token = (ids % BLK) // groups
    sort_q[...] = jnp.where(at == (token * heads + ids // BLK) * groups + ids % groups,
                            1.0, 0.0).astype(jnp.bfloat16)

    def by_head(raw):
        return jnp.dot(sort_kv[...], raw, preferred_element_type=jnp.float32).astype(jnp.bfloat16)

    def put_keys(dst, raw):
        ordered = by_head(raw)
        for h in range(heads):
            dst[h] = ordered[h * BLK:(h + 1) * BLK]

    def put_values(dst, raw):
        ordered = lax.dot_general(raw, sort_kv[...], (((0,), (1,)), ((), ())),
                                  preferred_element_type=jnp.float32).astype(jnp.bfloat16)
        for h in range(heads):
            dst[h] = ordered[:, h * BLK:(h + 1) * BLK]

    def chosen(cache, b):
        return cache[vp_ref[b]]

    pl.semaphore_wait(barrier, 1 + has_left.astype(jnp.int32) + has_right.astype(jnp.int32))

    def hop(src_ref, src, kv, right):
        return pltpu.make_async_remote_copy(
            src_ref=src_ref, dst_ref=pool.at[src, s, kv],
            send_sem=hop_send.at[src, int(right), kv], recv_sem=hop_recv.at[src, kv],
            device_id={"ctx": z + 1 if right else z - 1}, device_id_type=MESH)

    def sib(src, kv):
        return pltpu.make_async_remote_copy(
            src_ref=pool.at[src, s, kv], dst_ref=pool.at[src, s, kv],
            send_sem=sib_send.at[src, kv], recv_sem=sib_recv.at[src, kv],
            device_id=sib_id, device_id_type=MESH)

    def sib_in(src, kv):
        return pltpu.make_async_remote_copy(
            src_ref=pool.at[src, 1 - s, kv], dst_ref=pool.at[src, 1 - s, kv],
            send_sem=sib_send.at[src, kv], recv_sem=sib_recv.at[src, kv],
            device_id=sib_id, device_id_type=MESH)

    def slash_hop(src_ref=nk_hbm):
        return pltpu.make_async_remote_copy(
            src_ref=src_ref, dst_ref=slash_raw.at[s],
            send_sem=sl_sem.at[0], recv_sem=sl_sem.at[1],
            device_id={"ctx": z + 1}, device_id_type=MESH)

    def slash_sib(part):
        return pltpu.make_async_remote_copy(
            src_ref=slash_raw.at[part], dst_ref=slash_raw.at[part],
            send_sem=sl_sem.at[2], recv_sem=sl_sem.at[3],
            device_id=sib_id, device_id_type=MESH)

    for part, src_ref in enumerate((nk_hbm, nv_hbm)):
        @pl.when(has_right & (s == part))
        def _():
            slash_hop(src_ref).start()

    def send_own(kv):
        @pl.when(has_right)
        def _():
            hop(own_ref.at[s, kv], z, kv, True).start()

        @pl.when(has_left)
        def _():
            hop(own_ref.at[s, kv], z, kv, False).start()

    loads[0].wait()
    loads[1].start()
    put_keys(own_ref.at[s, 0], chosen(ck_raw, s))
    for load in loads[2:]:
        load.start()
    send_own(0)
    loads[1].wait()
    put_values(own_ref.at[s, 1], chosen(cv_raw, s))
    send_own(1)
    loads[2].wait()
    loads[3].wait()
    put_keys(new_ref.at[0], nk_raw[...])
    put_values(new_ref.at[1], nv_raw[...])
    put_keys(own_ref.at[1 - s, 0], chosen(ck_raw, 1 - s))
    put_values(own_ref.at[1 - s, 1], chosen(cv_raw, 1 - s))
    loads[4].wait()
    for part in range(rows // BLK):
        ordered = jnp.dot(sort_q[...], q_raw[part * wide:(part + 1) * wide],
                          preferred_element_type=jnp.float32).astype(jnp.bfloat16)
        for h in range(heads):
            q_ref[h, part * BLK:(part + 1) * BLK] = ordered[h * BLK:(h + 1) * BLK]

    def listed(slot):
        count = cnt_ref[0, 0]
        width = vl_ref.shape[1]
        if width <= 8:
            hit = jnp.int32(0)
            for i in range(width):
                hit = hit | jnp.where((vl_ref[0, i] == slot) & (i < count), 1, 0)
            return hit

        def one(i, hit):
            return hit | jnp.where((vl_ref[0, i] == slot) & (i < count), 1, 0)

        return lax.fori_loop(0, width, one, jnp.int32(0))

    def score(keys, q):
        return lax.dot_general(keys, q, (((1,), (1,)), ((), ())),
                               preferred_element_type=jnp.float32)

    def take_keys(side, blocks, first=False):
        for h in range(heads):
            q = q_ref[h]
            raw = []
            tops = []
            for keys, seen in blocks:
                scores = score(keys[h], q)
                if seen is None:
                    key_id = lax.broadcasted_iota(jnp.int32, scores.shape, 0)
                    row_id = lax.broadcasted_iota(jnp.int32, scores.shape, 1) // groups
                    scores = jnp.where(key_id <= row_id, scores, -jnp.inf)
                top = jnp.max(scores, axis=0, keepdims=True)
                if seen is not None:
                    top = jnp.where(seen > 0, top, -jnp.inf)
                raw.append(scores)
                tops.append(top)
            high = functools.reduce(jnp.maximum, tops)
            if not first:
                old = peak[h]
                high = jnp.maximum(old, high)
                factor = jnp.exp2((old - high) * c)
                fade[side, h] = factor
            peak[h] = high
            sums = []
            for i, ((_, seen), scores) in enumerate(zip(blocks, raw)):
                base = high if seen is None else jnp.where(seen > 0, high, jnp.inf)
                weights = jnp.exp2((scores - base) * c)
                sums.append(jnp.sum(weights, axis=0, keepdims=True))
                rounded[side, h, i * BLK:(i + 1) * BLK] = weights.astype(jnp.bfloat16)
            add = sum(sums[1:], sums[0])
            total[h] = add if first else total[h] * fade[side, h] + add

    def take_values(side, blocks, first=False):
        depth = len(blocks) * BLK
        for h in range(heads):
            values = jnp.concatenate([values[h] for values in blocks], 1)
            add = jnp.dot(values, rounded[side, h, :depth], preferred_element_type=jnp.float32)
            acc[h] = add if first else acc[h] * fade[side, h] + add

    take_keys(0, [(new_ref.at[0], None)]
              + [(own_ref.at[b, 0], listed(2 * z + b)) for b in range(2)], first=True)
    take_values(0, [new_ref.at[1]] + [own_ref.at[b, 1] for b in range(2)], first=True)

    @pl.when(has_left)
    def _():
        slash_hop().wait_recv()
        slash_sib(s).start()

    def arrive(src, kv, right):
        hop(own_ref.at[s, kv], src, kv, right).wait_recv()

        @pl.when(has_right if right else has_left)
        def _():
            hop(pool.at[src, s, kv], src, kv, right).start()

        sib(src, kv).start()

    def step(d, carry):
        sides = ((z + d, z + d < n, False), (z - d, z - d >= 0, True))
        for kv in range(2):
            for src, there, right in sides:
                @pl.when(there)
                def _():
                    arrive(src, kv, right)

            for side, (src, there, right) in enumerate(sides):
                @pl.when(there)
                def _():
                    sib_in(src, kv).wait_recv()
                    if kv == 0:
                        take_keys(side, [(pool.at[src, b, 0], listed(2 * src + b))
                                         for b in range(2)])
                    else:
                        take_values(side, [pool.at[src, b, 1] for b in range(2)])

        @pl.when((d == 1) & has_left)
        def _():
            slash_sib(1 - s).wait_recv()
            put_keys(slash.at[0], slash_raw[0])
            put_values(slash.at[1], slash_raw[1])
            back = jnp.int32(0)
            for i in range(sl_ref.shape[1]):
                back = back | jnp.where((sl_ref[0, i] == 1) & (i < cnt_ref[0, 1]), 1, 0)
            take_keys(0, [(slash.at[0], back)])
            take_values(0, [slash.at[1]])

        return carry

    lax.fori_loop(1, n, step, 0)

    for part in range(rows // BLK):
        lanes = slice(part * BLK, (part + 1) * BLK)
        done = jnp.concatenate(
            [(acc[h, :, lanes] / total[h, :, lanes]).astype(jnp.bfloat16) for h in range(heads)], 1)
        o_ref[part * wide:(part + 1) * wide] = lax.dot_general(
            sort_q[...], done, (((0,), (1,)), ((), ())),
            preferred_element_type=jnp.float32).astype(o_ref.dtype)

    def drain(src, carry):
        for kv in range(2):
            @pl.when(has_right & (src <= z))
            def _():
                hop(own_ref.at[s, kv], src, kv, True).wait_send()

            @pl.when(has_left & (src >= z))
            def _():
                hop(own_ref.at[s, kv], src, kv, False).wait_send()

            @pl.when(src != z)
            def _():
                sib(src, kv).wait_send()
        return carry

    lax.fori_loop(0, n, drain, 0)

    @pl.when(has_right)
    def _():
        slash_hop().wait_send()

    @pl.when(has_left)
    def _():
        slash_sib(s).wait_send()

BITS = 5
OWN, GUEST, ALONE = 4, 5, 6
IDLE = (6, 4 * GUEST)
GUESTS = 1
EARLY = 2
PACK = 6


NONE = (-1, -1)
QUEST = (-2, 0)
SLASH = (-3, 0)


def plan(heads):
    zero = [(NONE, (0, 0), 0), (NONE, (0, ALONE), 0), (NONE, (1, 0), 0), ((1, 0), (1, ALONE), 0), (NONE, (2, 0), 0),
        (NONE, (2, ALONE), 0), ((1, 1), (0, 1), 0), (NONE, (3, 0), 0), (NONE, (3, ALONE), 0), ((1, 2), (1, 1), 0),
        (NONE, NONE, 0), ((1, 3), NONE, 0), (NONE, (2, 1), 0), (NONE, NONE, 0), (NONE, (3, 1), 0), ((2, 0), NONE, 0),
        ((2, 1), NONE, 0), (NONE, (0, 2), 0), (NONE, NONE, 0), (NONE, (1, 2), 0), ((2, 2), NONE, 0),
        ((2, 3), NONE, 0), (NONE, (2, 2), 0), (NONE, NONE, 0), (NONE, (3, 2), 0), ((3, 0), NONE, 0),
        ((3, 1), NONE, 0), (NONE, (0, 3), 0), (NONE, NONE, 0), (NONE, (1, 3), 0), ((3, 2), NONE, 0)]
    one = [((0, 0), (0, 1), 0), ((2, 0), (1, 1), 0), ((0, 3), (2, 1), 0), (NONE, (0, 0), 0), ((2, 1), (0, 2), 0),
        ((0, 1), (3, 0), 4), (NONE, (3, 1), 0), (NONE, (1, 2), 0), ((2, 2), (1, 0), 0), ((0, 2), NONE, 8),
        ((2, 3), NONE, 0), (NONE, (2, 2), 0), (NONE, (2, 0), 0), (NONE, NONE, 0), ((3, 0), (3, 2), 0),
        (SLASH, NONE, 0), ((3, 1), NONE, 0), (NONE, (0, 3), 0), (NONE, NONE, 0), (NONE, (0, OWN), 0),
        ((3, 2), (1, 3), 0), (NONE, (1, OWN), 0), (NONE, (2, OWN), 16), ((3, 3), (2, 3), 0), (NONE, (3, OWN), 0),
        (NONE, NONE, 0), (NONE, (3, 3), 0), (NONE, NONE, 0)]
    two = [((1, 0), (0, 2), 0), ((3, 0), (1, 2), 0), (NONE, (2, 2), 0), ((1, 3), (0, 1), 0), ((3, 1), (0, 3), 0),
        (NONE, (3, 2), 0), ((1, 1), (3, 1), 0), ((3, 2), (1, 3), 0), (NONE, NONE, 0), ((0, 0), (1, 1), 0),
        ((3, 3), (2, 3), 0), (NONE, NONE, 0), ((0, 3), (0, 0), 0), (NONE, (3, 3), 0), (NONE, NONE, 0),
        (NONE, (3, 0), 0), ((0, 1), NONE, 0), (QUEST, NONE, 0), (NONE, (4, 2), 0), ((1, 2), (4, GUEST), 0),
        (NONE, (4, 1), 0), (NONE, (4, 0), 0), (NONE, (1, 0), 0), ((0, 2), (2, 1), 2), (NONE, NONE, 0),
        (NONE, (2, 0), 0), (NONE, NONE, 0), (SLASH, NONE, 0), (NONE, (0, OWN), 0), (NONE, (1, OWN), 0),
        (NONE, (2, OWN), 16), (NONE, (3, OWN), 0), (NONE, NONE, 0)]
    three = [(NONE, (0, 3), 0), ((2, 0), (1, 3), 0), (NONE, (2, 3), 0), (NONE, (3, 3), 0), (NONE, (0, 2), 0),
        (SLASH, (3, ALONE), 0), (NONE, NONE, 0), (NONE, (0, OWN), 0), ((2, 1), (1, OWN), 0), (NONE, (2, OWN), 0),
        (NONE, NONE, 0), ((2, 2), (1, 2), 0), (NONE, NONE, 0), ((1, 0), NONE, 0), (NONE, (2, 2), 0), (NONE, NONE, 0),
        (NONE, (0, 1), 0), ((1, 1), NONE, 0), ((0, 0), NONE, 0), (NONE, (1, 1), 0), (NONE, NONE, 0),
        (NONE, (0, 0), 0), ((0, 1), NONE, 0), ((1, 2), NONE, 0), (NONE, (1, 0), 0), (NONE, NONE, 16),
        (NONE, (2, 1), 0), ((0, 2), NONE, 0), (NONE, (2, 0), 0), (NONE, NONE, 0)]

    def build(z, table):
        out, before, used = [], NONE, set()
        for recv, now, flags in table + [(NONE, NONE, 0)]:
            kind, message = (1, recv[0] * 4 + recv[1]) if recv[0] >= 0 else (-recv[0] if recv != NONE else 0, 0)
            slot, src = now
            h = slot if slot < heads else slot - GUESTS
            key = OWN if src == OWN else (src, h)
            first = now != NONE and key not in used and src not in (z, GUEST, ALONE)
            used.add(key)
            code = (slot + (8 if first else 0), src * 4 + h) if now != NONE else IDLE
            busy = now != NONE or before != NONE
            out.append((kind, message) + code + (int(busy) | flags,))
            before = now
        return out

    return [build(z, table) for z, table in enumerate((zero, one, two, three))]


def chain(n, q_hbm, nk_hbm, nv_hbm, ck_hbm, cv_hbm, vp_hbm, vl_hbm, sl_hbm, cnt_hbm, o_ref,
          vp_ref, vl_ref, sl_ref, cnt_ref,
          q_raw, nk_raw, nv_raw, ck_raw, cv_raw, q_ref, sort_kv, sort_q, ext,
          pool, acc, peak, total, mask, part_acc, part_stat, scores_a, scores_b, top_a, top_b, most, sort_o,
          send_sem, hop_recv, sib_recv, sl_sem, ends_sem, in_sem, ready):
    z = lax.axis_index("ctx")
    s = lax.axis_index("sub")
    heads = pool.shape[1]
    head_dim, rows = acc.shape[1:]
    groups = rows // BLK
    wide = heads * BLK
    last = n - 1
    stay = heads - GUESTS
    loads = [pltpu.make_async_copy(src, dst, in_sem.at[i]) for i, (src, dst) in enumerate(
        [(ck_hbm, ck_raw), (cv_hbm, cv_raw), (nk_hbm, nk_raw), (nv_hbm, nv_raw), (q_hbm, q_raw)])]
    tables = [pltpu.make_async_copy(src, dst, in_sem.at[2 + i]) for i, (src, dst) in enumerate(
        [(vp_hbm, vp_ref), (vl_hbm, vl_ref), (sl_hbm, sl_ref), (cnt_hbm, cnt_ref)])]
    loads[0].start()
    loads[1].start()
    for table in tables:
        table.start()
    c = math.log2(math.e) / math.sqrt(head_dim)
    has_left = z > 0
    has_right = z < last
    sib_id = {"sub": 1 - s}
    inner = has_left & has_right

    barrier = pltpu.get_barrier_semaphore()
    pl.semaphore_signal(barrier, inc=1, device_id=sib_id, device_id_type=MESH)

    @pl.when(has_right)
    def _():
        pl.semaphore_signal(barrier, inc=1, device_id={"ctx": z + 1}, device_id_type=MESH)

    def by_role(values):
        out = jnp.int32(values[-1])
        for i in reversed(range(len(values) - 1)):
            out = jnp.where(z == i, jnp.int32(values[i]), out)
        return out

    roles = plan(heads)
    lengths = [max(t for t, step in enumerate(role) if step[0] or step[4]) + 1 for role in roles]
    steps = -(-max(lengths) // PACK) * PACK
    roles = [(role + [(0, 0) + IDLE + (0,)] * steps)[:steps] for role in roles]
    ids = lax.broadcasted_iota(jnp.int32, (wide, wide), 0)
    at = lax.broadcasted_iota(jnp.int32, (wide, wide), 1)
    sort_kv[...] = jnp.where(at == (ids % BLK) * heads + ids // BLK, 1.0, 0.0).astype(jnp.bfloat16)

    pl.semaphore_wait(barrier, 1 + has_left.astype(jnp.int32))

    @pl.when(has_left)
    def _():
        pl.semaphore_signal(ready, inc=1, device_id={"ctx": z - 1}, device_id_type=MESH)

    def put_keys(raw, put, those=range(heads)):
        ordered = jnp.dot(sort_kv[those.start * BLK:those.stop * BLK], raw,
                          preferred_element_type=jnp.float32).astype(jnp.bfloat16)
        for i, h in enumerate(those):
            put(h, ordered[i * BLK:(i + 1) * BLK])

    def put_values(raw, put):
        ordered = lax.dot_general(raw, sort_kv[...], (((0,), (1,)), ((), ())),
                                  preferred_element_type=jnp.float32).astype(jnp.bfloat16)
        for h in range(heads):
            put(h, ordered[:, h * BLK:(h + 1) * BLK])

    def put_pool(b, kv):
        def put(h, block):
            pool[z, h, b, kv] = block
        return put

    def put_new(kv):
        def put(h, block):
            pool[OWN, h, 0, kv] = block
            pool[GUEST, h, 0, kv] = block
            pool[GUEST, h, 1, kv] = jnp.zeros_like(block)
        return put

    def hop(src, h, right):
        return pltpu.make_async_remote_copy(
            src_ref=pool.at[src, h, s], dst_ref=pool.at[src, h, s],
            send_sem=send_sem.at[int(right)], recv_sem=hop_recv.at[src if right else src - 1, h],
            device_id={"ctx": z + 1 if right else z - 1}, device_id_type=MESH)

    def first_hop(h, kv, right):
        return pltpu.make_async_remote_copy(
            src_ref=pool.at[z, h, s, kv], dst_ref=pool.at[z, h, s, kv],
            send_sem=send_sem.at[int(right)], recv_sem=hop_recv.at[z if right else z - 1, h],
            device_id={"ctx": z + 1 if right else z - 1}, device_id_type=MESH)

    def sib(src, h, part):
        return pltpu.make_async_remote_copy(
            src_ref=pool.at[src, h, part], dst_ref=pool.at[src, h, part],
            send_sem=send_sem.at[2], recv_sem=sib_recv.at[src - (src > z).astype(jnp.int32), h],
            device_id=sib_id, device_id_type=MESH)

    end = heads - 1

    def end_hop(kv):
        block = pool.at[last, end, s, kv]
        return pltpu.make_async_remote_copy(
            src_ref=block, dst_ref=block,
            send_sem=send_sem.at[0], recv_sem=ends_sem.at[1, 0] if kv else hop_recv.at[last - 1, end],
            device_id={"ctx": z - 1}, device_id_type=MESH)

    def end_across():
        block = pool.at[last, end, s, 1]
        return pltpu.make_async_remote_copy(
            src_ref=block, dst_ref=block, send_sem=ends_sem.at[0, 0], recv_sem=ends_sem.at[1, 1],
            device_id={"ctx": z - 1, "sub": 1 - s}, device_id_type=MESH)

    def end_sib(part):
        block = pool.at[last, end, part, 0]
        return pltpu.make_async_remote_copy(
            src_ref=block, dst_ref=block, send_sem=ends_sem.at[0, 1], recv_sem=sib_recv.at[last - 1, end],
            device_id=sib_id, device_id_type=MESH)

    def slash_hop(count):
        return pltpu.make_async_remote_copy(
            src_ref=pool.at[OWN, pl.ds(0, count), 0, s], dst_ref=pool.at[OWN, pl.ds(0, count), 1, s],
            send_sem=sl_sem.at[0], recv_sem=sl_sem.at[1],
            device_id={"ctx": z + 1}, device_id_type=MESH)

    def slash_sib(count, part):
        block = pool.at[OWN, pl.ds(0, count), 1, part]
        return pltpu.make_async_remote_copy(
            src_ref=block, dst_ref=block,
            send_sem=sl_sem.at[2], recv_sem=sl_sem.at[3],
            device_id=sib_id, device_id_type=MESH)

    def guest_q(g):
        return pltpu.make_async_remote_copy(
            src_ref=q_ref.at[stay + g, pl.ds(0, head_dim)], dst_ref=q_ref.at[heads + g, pl.ds(0, head_dim)],
            send_sem=ends_sem.at[0, g], recv_sem=ends_sem.at[1, g],
            device_id={"ctx": z - 1}, device_id_type=MESH)

    def guest_mask():
        return pltpu.make_async_remote_copy(
            src_ref=mask.at[0], dst_ref=mask.at[1],
            send_sem=ends_sem.at[0, GUESTS], recv_sem=ends_sem.at[1, GUESTS],
            device_id={"ctx": z - 1}, device_id_type=MESH)

    def guest_part(g):
        return [pltpu.make_async_remote_copy(
            src_ref=ref.at[g], dst_ref=ref.at[g],
            send_sem=ends_sem.at[0, 2 * g + i], recv_sem=ends_sem.at[1, 2 * g + i],
            device_id={"ctx": z + 1}, device_id_type=MESH)
            for i, ref in enumerate((part_acc, part_stat))]

    def leftward(*blocks):
        @pl.when(has_left)
        def _():
            for h, kv in blocks:
                first_hop(h, kv, False).start()

    for table in tables:
        table.wait()
    loads[0].wait()
    put_keys(ck_raw[vp_ref[s]], put_pool(s, 0), range(EARLY))
    leftward(*[(h, 0) for h in range(EARLY)])
    put_keys(ck_raw[vp_ref[s]], put_pool(s, 0), range(EARLY, heads))
    for load in loads[2:]:
        load.start()
    loads[1].wait()
    put_values(cv_raw[vp_ref[s]], put_pool(s, 1))
    leftward((0, 1), (1, 1), *[(h, kv) for h in range(2, heads) for kv in range(2)])

    @pl.when(has_right)
    def _():
        pl.semaphore_wait(ready, 1)

    @pl.when(z == 0)
    def _():
        for h in (0, 3, 1, 2):
            for kv in range(2):
                first_hop(h, kv, True).start()

    @pl.when(z == 1)
    def _():
        for h in (0, 3, 1):
            for kv in range(2):
                first_hop(h, kv, True).start()

    @pl.when(z == 2)
    def _():
        for kv in range(2):
            first_hop(0, kv, True).start()

    loads[2].wait()
    loads[3].wait()
    put_keys(nk_raw[...], put_new(0))
    put_values(nv_raw[...], put_new(1))

    @pl.when(z == 2)
    def _():
        slash_hop(stay).start()
        for h in range(1, stay):
            for kv in range(2):
                first_hop(h, kv, True).start()

    token = (ids % BLK) // groups
    sort_q[...] = jnp.where(at == (token * heads + ids // BLK) * groups + ids % groups,
                            1.0, 0.0).astype(jnp.bfloat16)
    half = EARLY * BLK
    ids = lax.broadcasted_iota(jnp.int32, (half, half), 0)
    at = lax.broadcasted_iota(jnp.int32, (half, half), 1)
    sort_o[...] = jnp.where(at == ((ids % BLK) // groups * EARLY + ids // BLK) * groups + ids % groups,
                            1.0, 0.0).astype(jnp.bfloat16)
    loads[4].wait()
    for part in range(rows // BLK):
        ordered = lax.dot_general(q_raw[part * wide:(part + 1) * wide], sort_q[...], (((0,), (1,)), ((), ())),
                                  preferred_element_type=jnp.float32).astype(jnp.bfloat16)
        for h in range(heads):
            q_ref[h, 0:head_dim, part * BLK:(part + 1) * BLK] = ordered[:, h * BLK:(h + 1) * BLK]

    def unseen(hit):
        return jnp.full((1, BLK), jnp.where(hit > 0, 0.0, jnp.inf), jnp.float32)

    for slot in range(2 * n):
        hit = jnp.int32(0)
        for i in range(vl_ref.shape[1]):
            hit = hit | jnp.where((vl_ref[0, i] == slot) & (i < cnt_ref[0, 0]), 1, 0)
        mask[0, slot:slot + 1] = unseen(hit)
    hit = jnp.int32(0)
    for i in range(sl_ref.shape[1]):
        hit = hit | jnp.where((sl_ref[0, i] == 1) & (i < cnt_ref[0, 1]), 1, 0)
    mask[0, 2 * OWN:2 * OWN + 2] = jnp.concatenate([jnp.zeros((1, BLK), jnp.float32), unseen(hit)], 0)
    mask[0, 2 * GUEST:2 * GUEST + 2] = jnp.concatenate([unseen(hit), jnp.full((1, BLK), jnp.inf, jnp.float32)], 0)
    mask[0, 2 * ALONE:2 * ALONE + 2] = jnp.concatenate(
        [jnp.zeros((1, BLK), jnp.float32), jnp.full((1, BLK), jnp.inf, jnp.float32)], 0)

    @pl.when(z == 0)
    def _():
        slash_hop(heads).start()

    @pl.when(z == last)
    def _():
        for g in range(GUESTS):
            guest_q(g).start()
        guest_mask().start()

    put_keys(ck_raw[vp_ref[1 - s]], put_pool(1 - s, 0))
    put_values(cv_raw[vp_ref[1 - s]], put_pool(1 - s, 1))

    key_id = lax.broadcasted_iota(jnp.int32, (BLK, rows), 0)
    row_id = lax.broadcasted_iota(jnp.int32, (BLK, rows), 1) // groups
    later = jnp.where(key_id > row_id, -1e30, 0.0).astype(jnp.bfloat16)
    slots = acc.shape[0]
    for slot in range(slots):
        q_ref[slot, head_dim:] = later if slot < heads else jnp.zeros_like(later)
        acc[slot] = jnp.zeros_like(acc[slot])
        total[slot] = jnp.zeros_like(total[slot])
        peak[slot] = jnp.full_like(peak[slot], -1e30)
    q_ref[slots - 1, 0:head_dim] = jnp.zeros_like(later)
    one_at = lax.broadcasted_iota(jnp.int32, (BLK, BLK), 0) == lax.broadcasted_iota(jnp.int32, (BLK, BLK), 1)
    ext[0] = jnp.zeros((BLK, BLK), jnp.bfloat16)
    ext[1] = jnp.where(one_at, 1.0, 0.0).astype(jnp.bfloat16)
    scores_b[...] = jnp.zeros_like(scores_b)
    top_b[...] = jnp.zeros_like(top_b)

    def spread(row):
        return jnp.concatenate([row] * groups, 1)

    def place(src):
        return src - src // ALONE

    def hidden(slot, src, b):
        return spread(mask[(slot // heads) % 2 * (1 - slot // (slots - 1)), pl.ds(2 * src + b, 1)])

    def ahead(unit, scores, top):
        slot, src, h = unit
        q = q_ref[slot]
        high = None
        for b in range(2):
            causal = (src // OWN) * (1 - src % 2) if b == 0 else 0
            keys = jnp.concatenate([pool[place(src), h, b, 0], ext[causal]], 1)
            found = jnp.dot(keys, q, preferred_element_type=jnp.float32)
            scores[b * BLK:(b + 1) * BLK] = found
            part = jnp.max(found, axis=0, keepdims=True) - hidden(slot, src, b)
            high = part if high is None else jnp.maximum(high, part)
        top[...] = high

    def behind(unit, scores, top):
        slot, src, h = unit
        old = peak[slot]
        high = jnp.maximum(old, top[...])
        factor = jnp.exp2((old - high) * c)
        peak[slot] = high
        weights = [jnp.exp2((scores[b * BLK:(b + 1) * BLK] - (high + hidden(slot, src, b))) * c)
                   .astype(jnp.bfloat16) for b in range(2)]
        values = jnp.concatenate([pool[place(src), h, b, 1] for b in range(2)], 1)
        values = jnp.concatenate([values, jnp.ones((16, 2 * BLK), jnp.bfloat16)], 0)
        add = jnp.dot(values, jnp.concatenate(weights, 0), preferred_element_type=jnp.float32)
        acc[slot] = acc[slot] * factor + add[:head_dim]
        total[slot] = total[slot] * factor + add[head_dim:head_dim + 1]

    def ordered(part, those):
        lanes = slice(part * BLK, (part + 1) * BLK)
        done = jnp.concatenate(
            [(acc[h, :, lanes] * (1.0 / total[h, :, lanes])).astype(jnp.bfloat16) for h in those], 1)
        return lax.dot_general(sort_o[...], done, (((0,), (1,)), ((), ())), preferred_element_type=jnp.float32)

    def early_output():
        for part in range(rows // BLK):
            most[part] = ordered(part, range(EARLY))

    def drain(index):
        def sent(kind, sources, count):
            blocks = pool.at[pl.ds(0, sources), pl.ds(0, count), s]
            pltpu.make_async_copy(blocks, blocks, send_sem.at[kind]).wait()

        right = heads if index < last - 1 else stay if index < last else 0
        if right:
            sent(1, index + 1, right)
            slash_hop(right).wait_send()
        if index > 0:
            sent(0, n - index, heads)
            slash_sib(heads if index < last else stay, s).wait_send()
            sent(2, n - 1, heads if index < last else stay)
        else:
            copied = q_ref.at[pl.ds(0, heads), pl.ds(0, ((n - 1) * heads - 1) * (2 * BLK * head_dim // rows) // heads)]
            pltpu.make_async_copy(copied, copied, send_sem.at[2]).wait()
        if index == 1:
            end_across().wait_send()
        if index == last:
            guest_mask().wait_send()
            for g in range(GUESTS):
                guest_q(g).wait_send()

    words = [[by_role([sum(step[field] << (BITS * i) for i, step in enumerate(role[start:start + PACK]))
                       for role in roles]) for start in range(0, steps, PACK)] for field in range(5)]

    def step(here, t, before, bufs, old_bufs):
        kind, message, code, block, flags = [(word >> (BITS * t)) & (2 ** BITS - 1) for word in here]
        src, h = message // 4, message % 4

        @pl.when(kind == 1)
        def _():
            block = pool.at[src, h, s]
            pltpu.make_async_copy(block, block, hop_recv.at[src - (src > z).astype(jnp.int32), h]).wait()

            split = (z == 1) & (message == last * 4 + end)

            @pl.when((src > z) & has_left & jnp.logical_not(split))
            def _():
                hop(src, h, False).start()

            @pl.when(split)
            def _():
                end_hop(0).start()
                end_hop(1).start()
                end_across().start()

            @pl.when((src < z) & ((z < last - 1) | ((z == last - 1) & (h < stay))))
            def _():
                hop(src, h, True).start()

            sib(src, h, s).start()

        @pl.when(kind > 1)
        def _():
            @pl.when(kind == 2)
            def _():
                guest_mask().wait_recv()
                for g in range(GUESTS):
                    guest_q(g).wait_recv()

            @pl.when((kind == 3) & has_right)
            def _():
                slash_hop(heads).wait_recv()
                slash_sib(heads, s).start()

            @pl.when((kind == 3) & (z == last))
            def _():
                slash_hop(stay).wait_recv()
                slash_sib(stay, s).start()

        unit = (code % 8, block // 4, block % 4)

        @pl.when(code > 7)
        def _():
            @pl.when(unit[1] < OWN)
            def _():
                sib(unit[1], unit[2], 1 - s).wait_recv()

            @pl.when((unit[1] == OWN) & has_right)
            def _():
                slash_sib(heads, 1 - s).wait_recv()

            @pl.when((unit[1] == OWN) & (z == last))
            def _():
                slash_sib(stay, 1 - s).wait_recv()

        @pl.when(flags % 2 == 1)
        def _():
            ahead(unit, *bufs)
            behind(before, *old_bufs)

        @pl.when(flags > 1)
        def _():
            @pl.when((flags // 4) % 2 == 1)
            def _():
                for kv in range(2):
                    first_hop(2, kv, True).start()

            @pl.when((flags // 8) % 2 == 1)
            def _():
                slash_hop(heads).start()

            @pl.when((flags // 2) % 2 == 1)
            def _():
                g = 0
                part_acc[g] = acc[heads + g].astype(jnp.bfloat16)
                part_stat[g, 0:1] = peak[heads + g]
                part_stat[g, 1:2] = total[heads + g]
                for copy in guest_part(g):
                    copy.start()

            @pl.when(flags // 16 == 1)
            def _():
                early_output()

        return unit

    pairs = by_role([(length + 1) // 2 for length in lengths])

    def some_steps(group, before):
        here = []
        for chunks in words:
            word = chunks[-1]
            for i in reversed(range(len(chunks) - 1)):
                word = jnp.where(group == i, chunks[i], word)
            here.append(word)

        def two_steps(i, before):
            mid = step(here, 2 * i, before, (scores_a, top_a), (scores_b, top_b))
            return step(here, 2 * i + 1, mid, (scores_b, top_b), (scores_a, top_a))

        return lax.fori_loop(0, jnp.minimum(PACK // 2, pairs - group * (PACK // 2)), two_steps, before)

    idle = (jnp.int32(IDLE[0]), jnp.int32(GUEST), jnp.int32(0))
    lax.fori_loop(0, by_role([-(-length // PACK) for length in lengths]), some_steps, idle)

    for index in range(1, n):
        @pl.when(z == index)
        def _():
            drain(index)

    @pl.when(z == 0)
    def _():
        end_hop(0).wait_recv()
        end_sib(s).start()
        early_output()
        sib(last, end - 1, 1 - s).wait_recv()
        unit = (end - 1, last, end - 1)
        ahead(unit, scores_a, top_a)
        behind(unit, scores_a, top_a)
        drain(0)
        end_sib(1 - s).wait_recv()
        unit = (end, last, end)
        ahead(unit, scores_b, top_b)
        end_hop(1).wait_recv()
        block = pool.at[last, end, 1 - s, 1]
        pltpu.make_async_copy(block, block, ends_sem.at[1, 1]).wait()
        behind(unit, scores_b, top_b)

    @pl.when(z == last)
    def _():
        for g in range(GUESTS):
            for copy in guest_part(g):
                copy.wait_recv()
            slot = stay + g
            old, new = peak[slot], part_stat[g, 0:1]
            high = jnp.maximum(old, new)
            mine, theirs = jnp.exp2((old - high) * c), jnp.exp2((new - high) * c)
            acc[slot] = acc[slot] * mine + part_acc[g].astype(jnp.float32) * theirs
            total[slot] = total[slot] * mine + part_stat[g, 1:2] * theirs

    tile = EARLY * groups
    for part in range(rows // BLK):
        pair = [half.reshape(-1, tile, head_dim) for half in (most[part], ordered(part, range(EARLY, heads)))]
        o_ref[part * wide:(part + 1) * wide] = jnp.concatenate(pair, 1).reshape(wide, head_dim).astype(o_ref.dtype)

    @pl.when(z == 0)
    def _():
        end_sib(s).wait_send()

    @pl.when(z == last - 1)
    def _():
        for g in range(GUESTS):
            for copy in guest_part(g):
                copy.wait_send()


def store(o_vmem, o_hbm, sem):
    copies = sem.shape[0]
    rows = o_vmem.shape[0] // copies
    for i in range(copies):
        lines = pl.ds(i * rows, rows)
        pltpu.make_async_copy(o_vmem.at[lines], o_hbm.at[lines], sem.at[i]).start()
    for i in range(copies):
        lines = pl.ds(i * rows, rows)
        pltpu.make_async_copy(o_vmem.at[lines], o_hbm.at[lines], sem.at[i]).wait()


def chain_call(n, q, nk, nv, ck, cv, tables, heads, rows, head_dim):
    def vmem(*shape):
        return pltpu.VMEM(shape, jnp.bfloat16)

    def wide_vmem(*shape):
        return pltpu.VMEM(shape, jnp.float32)

    hbm = pl.BlockSpec(memory_space=pltpu.HBM)
    in_vmem = pl.BlockSpec(memory_space=pltpu.VMEM)
    dma = pltpu.SemaphoreType.DMA
    cached, wide = ck.shape[:2]
    slots = 7
    out = pl.pallas_call(
        functools.partial(chain, n),
        out_shape=pltpu.VMEM((heads * rows, head_dim), jnp.bfloat16),
        in_specs=[hbm] * 9,
        out_specs=in_vmem,
        scratch_shapes=[
            *[pltpu.SMEM(table.shape, table.dtype) for table in tables],
            vmem(heads * rows, head_dim), vmem(wide, head_dim), vmem(wide, head_dim),
            vmem(cached, wide, head_dim), vmem(cached, wide, head_dim),
            vmem(slots, 2 * head_dim, rows), vmem(wide, wide), vmem(wide, wide), vmem(2, BLK, BLK),
            vmem(n + 2, heads, 2, 2, BLK, head_dim),
            wide_vmem(slots, head_dim, rows), wide_vmem(slots, 1, rows), wide_vmem(slots, 1, rows),
            wide_vmem(2, 16, BLK), vmem(GUESTS, head_dim, rows), wide_vmem(GUESTS, 8, rows),
            wide_vmem(2 * BLK, rows), wide_vmem(2 * BLK, rows), wide_vmem(1, rows), wide_vmem(1, rows),
            wide_vmem(rows // BLK, EARLY * BLK, head_dim), vmem(EARLY * BLK, EARLY * BLK),
            dma((3,)), dma((n - 1, heads)), dma((n - 1, heads)), dma((4,)),
            dma((2, 2 * GUESTS)), dma((6,)), pltpu.SemaphoreType.REGULAR,
        ],
        compiler_params=pltpu.CompilerParams(
            collective_id=0, has_side_effects=True, vmem_limit_bytes=60 * 2**20),
    )(*[pltpu.with_memory_space_constraint(x, pltpu.HBM) for x in (q, nk, nv, ck, cv, *tables)])
    return pl.pallas_call(
        store,
        out_shape=jax.ShapeDtypeStruct(out.shape, out.dtype),
        in_specs=[in_vmem],
        out_specs=hbm,
        scratch_shapes=[dma((4,))],
        compiler_params=pltpu.CompilerParams(vmem_limit_bytes=2**20),
    )(out)


def shards(n, queries, new_keys, new_values, cache_keys, cache_values,
           vertical_pool, vertical_lists, slash_lists, list_counts):
    tokens, heads, groups, head_dim = queries.shape
    rows = tokens * groups
    picked = vertical_pool.shape[0]

    def flat(x):
        return x.reshape(-1, head_dim)

    def vmem(*shape):
        return pltpu.VMEM(shape, jnp.bfloat16)

    hbm = pl.BlockSpec(memory_space=pltpu.HBM)
    smem = pl.BlockSpec(memory_space=pltpu.SMEM)
    dma = pltpu.SemaphoreType.DMA
    wide = heads * BLK
    cached = cache_keys.shape[0] // BLK
    if n == 4 and heads == 4 and picked == 2:
        out = chain_call(n, flat(queries), flat(new_keys), flat(new_values),
                         cache_keys.reshape(cached, wide, head_dim), cache_values.reshape(cached, wide, head_dim),
                         (vertical_pool, vertical_lists, slash_lists, list_counts), heads, rows, head_dim)
        return out.reshape(tokens, heads, groups, head_dim)
    out = pl.pallas_call(
        functools.partial(attend, n),
        out_shape=jax.ShapeDtypeStruct((tokens * heads * groups, head_dim), jnp.bfloat16),
        in_specs=[hbm] * 5 + [smem] * 4,
        out_specs=pl.BlockSpec(memory_space=pltpu.VMEM),
        scratch_shapes=[
            vmem(heads * rows, head_dim), vmem(wide, head_dim), vmem(wide, head_dim),
            vmem(cached, wide, head_dim), vmem(cached, wide, head_dim),
            vmem(heads, rows, head_dim), vmem(picked, 2, heads, BLK, head_dim),
            vmem(2, heads, BLK, head_dim), vmem(wide, wide), vmem(wide, wide),
            vmem(n, picked, 2, heads, BLK, head_dim),
            vmem(2, wide, head_dim), vmem(2, heads, BLK, head_dim),
            pltpu.VMEM((heads, head_dim, rows), jnp.float32),
            pltpu.VMEM((heads, 1, rows), jnp.float32),
            pltpu.VMEM((heads, 1, rows), jnp.float32),
            vmem(2, heads, 3 * BLK, rows), pltpu.VMEM((2, heads, 1, rows), jnp.float32),
            dma((n, 2, 2)), dma((n, 2)), dma((n, 2)), dma((n, 2)), dma((4,)), dma((5,)),
        ],
        compiler_params=pltpu.CompilerParams(
            collective_id=0, has_side_effects=True, vmem_limit_bytes=60 * 2**20),
    )(flat(queries), flat(new_keys), flat(new_values), cache_keys.reshape(cached, wide, head_dim),
      cache_values.reshape(cached, wide, head_dim),
      vertical_pool, vertical_lists, slash_lists, list_counts)
    return out.reshape(tokens, heads, groups, head_dim)


def solution(mesh):
    in_specs = (
        P(("grp", "ctx"), "kvh", "sub", None),
        P(("grp", "ctx"), "kvh", None),
        P(("grp", "ctx"), "kvh", None),
        P(("grp", "ctx"), "kvh", None),
        P(("grp", "ctx"), "kvh", None),
        P(("grp", "ctx")),
        P(("grp", "ctx"), None),
        P(("grp", "ctx"), None),
        P(("grp", "ctx"), None),
    )
    out_specs = P(("grp", "ctx"), "kvh", "sub", None)
    return jax.shard_map(functools.partial(shards, mesh.shape["ctx"]), mesh=mesh,
                         in_specs=in_specs, out_specs=out_specs, check_vma=False)
```

```python
import functools
import math

import jax
import jax.numpy as jnp
from jax import lax
from jax.experimental import pallas as pl
from jax.experimental.pallas import tpu as pltpu
from jax.sharding import PartitionSpec as P

BLK = 128
MESH = pl.DeviceIdType.MESH


def attend(n, q_hbm, nk_hbm, nv_hbm, ck_hbm, cv_hbm, vp_ref, vl_ref, sl_ref, cnt_ref, o_ref,
           q_raw, nk_raw, nv_raw, ck_raw, cv_raw, q_ref, own_ref, new_ref, sort_kv, sort_q,
           pool, slash_raw, slash, acc, peak, total, rounded, fade,
           hop_send, hop_recv, sib_send, sib_recv, sl_sem, in_sem):
    z = lax.axis_index("ctx")
    s = lax.axis_index("sub")
    heads, rows, head_dim = q_ref.shape
    groups = rows // BLK
    wide = heads * BLK
    loads = [pltpu.make_async_copy(src, dst, in_sem.at[i]) for i, (src, dst) in enumerate(
        [(ck_hbm, ck_raw), (cv_hbm, cv_raw), (nk_hbm, nk_raw), (nv_hbm, nv_raw), (q_hbm, q_raw)])]
    loads[0].start()
    c = math.log2(math.e) / math.sqrt(head_dim)
    has_left = z > 0
    has_right = z < n - 1
    sib_id = {"sub": 1 - s}

    barrier = pltpu.get_barrier_semaphore()
    pl.semaphore_signal(barrier, inc=1, device_id=sib_id, device_id_type=MESH)

    @pl.when(has_left)
    def _():
        pl.semaphore_signal(barrier, inc=1, device_id={"ctx": z - 1}, device_id_type=MESH)

    @pl.when(has_right)
    def _():
        pl.semaphore_signal(barrier, inc=1, device_id={"ctx": z + 1}, device_id_type=MESH)

    ids = lax.broadcasted_iota(jnp.int32, (wide, wide), 0)
    at = lax.broadcasted_iota(jnp.int32, (wide, wide), 1)
    sort_kv[...] = jnp.where(at == (ids % BLK) * heads + ids // BLK, 1.0, 0.0).astype(jnp.bfloat16)
    token = (ids % BLK) // groups
    sort_q[...] = jnp.where(at == (token * heads + ids // BLK) * groups + ids % groups,
                            1.0, 0.0).astype(jnp.bfloat16)

    def by_head(raw):
        return jnp.dot(sort_kv[...], raw, preferred_element_type=jnp.float32).astype(jnp.bfloat16)

    def put_keys(dst, raw):
        ordered = by_head(raw)
        for h in range(heads):
            dst[h] = ordered[h * BLK:(h + 1) * BLK]

    def put_values(dst, raw):
        ordered = lax.dot_general(raw, sort_kv[...], (((0,), (1,)), ((), ())),
                                  preferred_element_type=jnp.float32).astype(jnp.bfloat16)
        for h in range(heads):
            dst[h] = ordered[:, h * BLK:(h + 1) * BLK]

    def chosen(cache, b):
        return cache[vp_ref[b]]

    pl.semaphore_wait(barrier, 1 + has_left.astype(jnp.int32) + has_right.astype(jnp.int32))

    def hop(src_ref, src, kv, right):
        return pltpu.make_async_remote_copy(
            src_ref=src_ref, dst_ref=pool.at[src, s, kv],
            send_sem=hop_send.at[src, int(right), kv], recv_sem=hop_recv.at[src, kv],
            device_id={"ctx": z + 1 if right else z - 1}, device_id_type=MESH)

    def sib(src, kv):
        return pltpu.make_async_remote_copy(
            src_ref=pool.at[src, s, kv], dst_ref=pool.at[src, s, kv],
            send_sem=sib_send.at[src, kv], recv_sem=sib_recv.at[src, kv],
            device_id=sib_id, device_id_type=MESH)

    def sib_in(src, kv):
        return pltpu.make_async_remote_copy(
            src_ref=pool.at[src, 1 - s, kv], dst_ref=pool.at[src, 1 - s, kv],
            send_sem=sib_send.at[src, kv], recv_sem=sib_recv.at[src, kv],
            device_id=sib_id, device_id_type=MESH)

    def slash_hop(src_ref=nk_hbm):
        return pltpu.make_async_remote_copy(
            src_ref=src_ref, dst_ref=slash_raw.at[s],
            send_sem=sl_sem.at[0], recv_sem=sl_sem.at[1],
            device_id={"ctx": z + 1}, device_id_type=MESH)

    def slash_sib(part):
        return pltpu.make_async_remote_copy(
            src_ref=slash_raw.at[part], dst_ref=slash_raw.at[part],
            send_sem=sl_sem.at[2], recv_sem=sl_sem.at[3],
            device_id=sib_id, device_id_type=MESH)

    for part, src_ref in enumerate((nk_hbm, nv_hbm)):
        @pl.when(has_right & (s == part))
        def _():
            slash_hop(src_ref).start()

    def send_own(kv):
        @pl.when(has_right)
        def _():
            hop(own_ref.at[s, kv], z, kv, True).start()

        @pl.when(has_left)
        def _():
            hop(own_ref.at[s, kv], z, kv, False).start()

    loads[0].wait()
    loads[1].start()
    put_keys(own_ref.at[s, 0], chosen(ck_raw, s))
    for load in loads[2:]:
        load.start()
    send_own(0)
    loads[1].wait()
    put_values(own_ref.at[s, 1], chosen(cv_raw, s))
    send_own(1)
    loads[2].wait()
    loads[3].wait()
    put_keys(new_ref.at[0], nk_raw[...])
    put_values(new_ref.at[1], nv_raw[...])
    put_keys(own_ref.at[1 - s, 0], chosen(ck_raw, 1 - s))
    put_values(own_ref.at[1 - s, 1], chosen(cv_raw, 1 - s))
    loads[4].wait()
    for part in range(rows // BLK):
        ordered = jnp.dot(sort_q[...], q_raw[part * wide:(part + 1) * wide],
                          preferred_element_type=jnp.float32).astype(jnp.bfloat16)
        for h in range(heads):
            q_ref[h, part * BLK:(part + 1) * BLK] = ordered[h * BLK:(h + 1) * BLK]

    def listed(slot):
        count = cnt_ref[0, 0]
        width = vl_ref.shape[1]
        if width <= 8:
            hit = jnp.int32(0)
            for i in range(width):
                hit = hit | jnp.where((vl_ref[0, i] == slot) & (i < count), 1, 0)
            return hit

        def one(i, hit):
            return hit | jnp.where((vl_ref[0, i] == slot) & (i < count), 1, 0)

        return lax.fori_loop(0, width, one, jnp.int32(0))

    def score(keys, q):
        return lax.dot_general(keys, q, (((1,), (1,)), ((), ())),
                               preferred_element_type=jnp.float32)

    def take_keys(side, blocks, first=False):
        for h in range(heads):
            q = q_ref[h]
            raw = []
            tops = []
            for keys, seen in blocks:
                scores = score(keys[h], q)
                if seen is None:
                    key_id = lax.broadcasted_iota(jnp.int32, scores.shape, 0)
                    row_id = lax.broadcasted_iota(jnp.int32, scores.shape, 1) // groups
                    scores = jnp.where(key_id <= row_id, scores, -jnp.inf)
                top = jnp.max(scores, axis=0, keepdims=True)
                if seen is not None:
                    top = jnp.where(seen > 0, top, -jnp.inf)
                raw.append(scores)
                tops.append(top)
            high = functools.reduce(jnp.maximum, tops)
            if not first:
                old = peak[h]
                high = jnp.maximum(old, high)
                factor = jnp.exp2((old - high) * c)
                fade[side, h] = factor
            peak[h] = high
            sums = []
            for i, ((_, seen), scores) in enumerate(zip(blocks, raw)):
                base = high if seen is None else jnp.where(seen > 0, high, jnp.inf)
                weights = jnp.exp2((scores - base) * c)
                sums.append(jnp.sum(weights, axis=0, keepdims=True))
                rounded[side, h, i * BLK:(i + 1) * BLK] = weights.astype(jnp.bfloat16)
            add = sum(sums[1:], sums[0])
            total[h] = add if first else total[h] * fade[side, h] + add

    def take_values(side, blocks, first=False):
        depth = len(blocks) * BLK
        for h in range(heads):
            values = jnp.concatenate([values[h] for values in blocks], 1)
            add = jnp.dot(values, rounded[side, h, :depth], preferred_element_type=jnp.float32)
            acc[h] = add if first else acc[h] * fade[side, h] + add

    take_keys(0, [(new_ref.at[0], None)]
              + [(own_ref.at[b, 0], listed(2 * z + b)) for b in range(2)], first=True)
    take_values(0, [new_ref.at[1]] + [own_ref.at[b, 1] for b in range(2)], first=True)

    @pl.when(has_left)
    def _():
        slash_hop().wait_recv()
        slash_sib(s).start()

    def arrive(src, kv, right):
        hop(own_ref.at[s, kv], src, kv, right).wait_recv()

        @pl.when(has_right if right else has_left)
        def _():
            hop(pool.at[src, s, kv], src, kv, right).start()

        sib(src, kv).start()

    def step(d, carry):
        sides = ((z + d, z + d < n, False), (z - d, z - d >= 0, True))
        for kv in range(2):
            for src, there, right in sides:
                @pl.when(there)
                def _():
                    arrive(src, kv, right)

            for side, (src, there, right) in enumerate(sides):
                @pl.when(there)
                def _():
                    sib_in(src, kv).wait_recv()
                    if kv == 0:
                        take_keys(side, [(pool.at[src, b, 0], listed(2 * src + b))
                                         for b in range(2)])
                    else:
                        take_values(side, [pool.at[src, b, 1] for b in range(2)])

        @pl.when((d == 1) & has_left)
        def _():
            slash_sib(1 - s).wait_recv()
            put_keys(slash.at[0], slash_raw[0])
            put_values(slash.at[1], slash_raw[1])
            back = jnp.int32(0)
            for i in range(sl_ref.shape[1]):
                back = back | jnp.where((sl_ref[0, i] == 1) & (i < cnt_ref[0, 1]), 1, 0)
            take_keys(0, [(slash.at[0], back)])
            take_values(0, [slash.at[1]])

        return carry

    lax.fori_loop(1, n, step, 0)

    for part in range(rows // BLK):
        lanes = slice(part * BLK, (part + 1) * BLK)
        done = jnp.concatenate(
            [(acc[h, :, lanes] / total[h, :, lanes]).astype(jnp.bfloat16) for h in range(heads)], 1)
        o_ref[part * wide:(part + 1) * wide] = lax.dot_general(
            sort_q[...], done, (((0,), (1,)), ((), ())),
            preferred_element_type=jnp.float32).astype(o_ref.dtype)

    def drain(src, carry):
        for kv in range(2):
            @pl.when(has_right & (src <= z))
            def _():
                hop(own_ref.at[s, kv], src, kv, True).wait_send()

            @pl.when(has_left & (src >= z))
            def _():
                hop(own_ref.at[s, kv], src, kv, False).wait_send()

            @pl.when(src != z)
            def _():
                sib(src, kv).wait_send()
        return carry

    lax.fori_loop(0, n, drain, 0)

    @pl.when(has_right)
    def _():
        slash_hop().wait_send()

    @pl.when(has_left)
    def _():
        slash_sib(s).wait_send()

BITS = 5
OWN, GUEST, ALONE = 4, 5, 6
IDLE = (6, 4 * GUEST)
GUESTS = 1
EARLY = 2
PACK = 6


NONE = (-1, -1)
QUEST = (-2, 0)
SLASH = (-3, 0)


def plan(heads):
    zero = [(NONE, (0, 0), 0), (NONE, (0, ALONE), 0), (NONE, (1, 0), 0), ((1, 0), (1, ALONE), 0), (NONE, (2, 0), 0),
        (NONE, (2, ALONE), 0), ((1, 1), (0, 1), 0), (NONE, (3, 0), 0), (NONE, (3, ALONE), 0), ((1, 2), (1, 1), 0),
        (NONE, NONE, 0), ((1, 3), NONE, 0), (NONE, (2, 1), 0), (NONE, NONE, 0), (NONE, (3, 1), 0), ((2, 0), NONE, 0),
        ((2, 1), NONE, 0), (NONE, (0, 2), 0), (NONE, NONE, 0), (NONE, (1, 2), 0), ((2, 2), NONE, 0),
        ((2, 3), NONE, 0), (NONE, (2, 2), 0), (NONE, NONE, 0), (NONE, (3, 2), 0), ((3, 0), NONE, 0),
        ((3, 1), NONE, 0), (NONE, (0, 3), 0), (NONE, NONE, 0), (NONE, (1, 3), 0), ((3, 2), NONE, 0)]
    one = [((0, 0), (0, 1), 0), ((2, 0), (1, 1), 0), ((0, 3), (2, 1), 0), (NONE, (0, 0), 0), ((2, 1), (0, 2), 0),
        ((0, 1), (3, 0), 4), (NONE, (3, 1), 0), (NONE, (1, 2), 0), ((2, 2), (1, 0), 0), ((0, 2), NONE, 8),
        ((2, 3), NONE, 0), (NONE, (2, 2), 0), (NONE, (2, 0), 0), (NONE, NONE, 0), ((3, 0), (3, 2), 0),
        (SLASH, NONE, 0), ((3, 1), NONE, 0), (NONE, (0, 3), 0), (NONE, NONE, 0), (NONE, (0, OWN), 0),
        ((3, 2), (1, 3), 0), (NONE, (1, OWN), 0), (NONE, (2, OWN), 16), ((3, 3), (2, 3), 0), (NONE, (3, OWN), 0),
        (NONE, NONE, 0), (NONE, (3, 3), 0), (NONE, NONE, 0)]
    two = [((1, 0), (0, 2), 0), ((3, 0), (1, 2), 0), (NONE, (2, 2), 0), ((1, 3), (0, 1), 0), ((3, 1), (0, 3), 0),
        (NONE, (3, 2), 0), ((1, 1), (3, 1), 0), ((3, 2), (1, 3), 0), (NONE, NONE, 0), ((0, 0), (1, 1), 0),
        ((3, 3), (2, 3), 0), (NONE, NONE, 0), ((0, 3), (0, 0), 0), (NONE, (3, 3), 0), (NONE, NONE, 0),
        (NONE, (3, 0), 0), ((0, 1), NONE, 0), (QUEST, NONE, 0), (NONE, (4, 2), 0), ((1, 2), (4, GUEST), 0),
        (NONE, (4, 1), 0), (NONE, (4, 0), 0), (NONE, (1, 0), 0), ((0, 2), (2, 1), 2), (NONE, NONE, 0),
        (NONE, (2, 0), 0), (NONE, NONE, 0), (SLASH, NONE, 0), (NONE, (0, OWN), 0), (NONE, (1, OWN), 0),
        (NONE, (2, OWN), 16), (NONE, (3, OWN), 0), (NONE, NONE, 0)]
    three = [(NONE, (0, 3), 0), ((2, 0), (1, 3), 0), (NONE, (2, 3), 0), (NONE, (3, 3), 0), (NONE, (0, 2), 0),
        (SLASH, (3, ALONE), 0), (NONE, NONE, 0), (NONE, (0, OWN), 0), ((2, 1), (1, OWN), 0), (NONE, (2, OWN), 0),
        (NONE, NONE, 0), ((2, 2), (1, 2), 0), (NONE, NONE, 0), ((1, 0), NONE, 0), (NONE, (2, 2), 0), (NONE, NONE, 0),
        (NONE, (0, 1), 0), ((1, 1), NONE, 0), ((0, 0), NONE, 0), (NONE, (1, 1), 0), (NONE, NONE, 0),
        (NONE, (0, 0), 0), ((0, 1), NONE, 0), ((1, 2), NONE, 0), (NONE, (1, 0), 0), (NONE, NONE, 16),
        (NONE, (2, 1), 0), ((0, 2), NONE, 0), (NONE, (2, 0), 0), (NONE, NONE, 0)]

    def build(z, table):
        out, before, used = [], NONE, set()
        for recv, now, flags in table + [(NONE, NONE, 0)]:
            kind, message = (1, recv[0] * 4 + recv[1]) if recv[0] >= 0 else (-recv[0] if recv != NONE else 0, 0)
            slot, src = now
            h = slot if slot < heads else slot - GUESTS
            key = OWN if src == OWN else (src, h)
            first = now != NONE and key not in used and src not in (z, GUEST, ALONE)
            used.add(key)
            code = (slot + (8 if first else 0), src * 4 + h) if now != NONE else IDLE
            busy = now != NONE or before != NONE
            out.append((kind, message) + code + (int(busy) | flags,))
            before = now
        return out

    return [build(z, table) for z, table in enumerate((zero, one, two, three))]


def chain(n, q_hbm, nk_hbm, nv_hbm, ck_hbm, cv_hbm, vp_hbm, vl_hbm, sl_hbm, cnt_hbm, o_ref,
          vp_ref, vl_ref, sl_ref, cnt_ref,
          q_raw, nk_raw, nv_raw, ck_raw, cv_raw, q_ref, sort_kv, sort_q, ext,
          pool, acc, peak, total, mask, part_acc, part_stat, scores_a, scores_b, top_a, top_b, most, sort_o,
          send_sem, hop_recv, sib_recv, sl_sem, ends_sem, in_sem, ready):
    z = lax.axis_index("ctx")
    s = lax.axis_index("sub")
    heads = pool.shape[1]
    head_dim, rows = acc.shape[1:]
    groups = rows // BLK
    wide = heads * BLK
    last = n - 1
    stay = heads - GUESTS
    loads = [pltpu.make_async_copy(src, dst, in_sem.at[i]) for i, (src, dst) in enumerate(
        [(ck_hbm, ck_raw), (cv_hbm, cv_raw), (nk_hbm, nk_raw), (nv_hbm, nv_raw), (q_hbm, q_raw)])]
    tables = [pltpu.make_async_copy(src, dst, in_sem.at[2 + i]) for i, (src, dst) in enumerate(
        [(vp_hbm, vp_ref), (vl_hbm, vl_ref), (sl_hbm, sl_ref), (cnt_hbm, cnt_ref)])]
    loads[0].start()
    loads[1].start()
    for table in tables:
        table.start()
    c = math.log2(math.e) / math.sqrt(head_dim)
    has_left = z > 0
    has_right = z < last
    sib_id = {"sub": 1 - s}
    inner = has_left & has_right

    barrier = pltpu.get_barrier_semaphore()
    pl.semaphore_signal(barrier, inc=1, device_id=sib_id, device_id_type=MESH)

    @pl.when(has_right)
    def _():
        pl.semaphore_signal(barrier, inc=1, device_id={"ctx": z + 1}, device_id_type=MESH)

    def by_role(values):
        out = jnp.int32(values[-1])
        for i in reversed(range(len(values) - 1)):
            out = jnp.where(z == i, jnp.int32(values[i]), out)
        return out

    roles = plan(heads)
    lengths = [max(t for t, step in enumerate(role) if step[0] or step[4]) + 1 for role in roles]
    steps = -(-max(lengths) // PACK) * PACK
    roles = [(role + [(0, 0) + IDLE + (0,)] * steps)[:steps] for role in roles]
    ids = lax.broadcasted_iota(jnp.int32, (wide, wide), 0)
    at = lax.broadcasted_iota(jnp.int32, (wide, wide), 1)
    sort_kv[...] = jnp.where(at == (ids % BLK) * heads + ids // BLK, 1.0, 0.0).astype(jnp.bfloat16)

    pl.semaphore_wait(barrier, 1 + has_left.astype(jnp.int32))

    @pl.when(has_left)
    def _():
        pl.semaphore_signal(ready, inc=1, device_id={"ctx": z - 1}, device_id_type=MESH)

    def put_keys(raw, put, those=range(heads)):
        ordered = jnp.dot(sort_kv[those.start * BLK:those.stop * BLK], raw,
                          preferred_element_type=jnp.float32).astype(jnp.bfloat16)
        for i, h in enumerate(those):
            put(h, ordered[i * BLK:(i + 1) * BLK])

    def put_values(raw, put):
        ordered = lax.dot_general(raw, sort_kv[...], (((0,), (1,)), ((), ())),
                                  preferred_element_type=jnp.float32).astype(jnp.bfloat16)
        for h in range(heads):
            put(h, ordered[:, h * BLK:(h + 1) * BLK])

    def put_pool(b, kv):
        def put(h, block):
            pool[z, h, b, kv] = block
        return put

    def put_new(kv):
        def put(h, block):
            pool[OWN, h, 0, kv] = block
            pool[GUEST, h, 0, kv] = block
            pool[GUEST, h, 1, kv] = jnp.zeros_like(block)
        return put

    def hop(src, h, right):
        return pltpu.make_async_remote_copy(
            src_ref=pool.at[src, h, s], dst_ref=pool.at[src, h, s],
            send_sem=send_sem.at[int(right)], recv_sem=hop_recv.at[src if right else src - 1, h],
            device_id={"ctx": z + 1 if right else z - 1}, device_id_type=MESH)

    def first_hop(h, kv, right):
        return pltpu.make_async_remote_copy(
            src_ref=pool.at[z, h, s, kv], dst_ref=pool.at[z, h, s, kv],
            send_sem=send_sem.at[int(right)], recv_sem=hop_recv.at[z if right else z - 1, h],
            device_id={"ctx": z + 1 if right else z - 1}, device_id_type=MESH)

    def sib(src, h, part):
        return pltpu.make_async_remote_copy(
            src_ref=pool.at[src, h, part], dst_ref=pool.at[src, h, part],
            send_sem=send_sem.at[2], recv_sem=sib_recv.at[src - (src > z).astype(jnp.int32), h],
            device_id=sib_id, device_id_type=MESH)

    end = heads - 1

    def end_hop(kv):
        block = pool.at[last, end, s, kv]
        return pltpu.make_async_remote_copy(
            src_ref=block, dst_ref=block,
            send_sem=send_sem.at[0], recv_sem=ends_sem.at[1, 0] if kv else hop_recv.at[last - 1, end],
            device_id={"ctx": z - 1}, device_id_type=MESH)

    def end_across():
        block = pool.at[last, end, s, 1]
        return pltpu.make_async_remote_copy(
            src_ref=block, dst_ref=block, send_sem=ends_sem.at[0, 0], recv_sem=ends_sem.at[1, 1],
            device_id={"ctx": z - 1, "sub": 1 - s}, device_id_type=MESH)

    def end_sib(part):
        block = pool.at[last, end, part, 0]
        return pltpu.make_async_remote_copy(
            src_ref=block, dst_ref=block, send_sem=ends_sem.at[0, 1], recv_sem=sib_recv.at[last - 1, end],
            device_id=sib_id, device_id_type=MESH)

    def slash_hop(count):
        return pltpu.make_async_remote_copy(
            src_ref=pool.at[OWN, pl.ds(0, count), 0, s], dst_ref=pool.at[OWN, pl.ds(0, count), 1, s],
            send_sem=sl_sem.at[0], recv_sem=sl_sem.at[1],
            device_id={"ctx": z + 1}, device_id_type=MESH)

    def slash_sib(count, part):
        block = pool.at[OWN, pl.ds(0, count), 1, part]
        return pltpu.make_async_remote_copy(
            src_ref=block, dst_ref=block,
            send_sem=sl_sem.at[2], recv_sem=sl_sem.at[3],
            device_id=sib_id, device_id_type=MESH)

    def guest_q(g):
        return pltpu.make_async_remote_copy(
            src_ref=q_ref.at[stay + g, pl.ds(0, head_dim)], dst_ref=q_ref.at[heads + g, pl.ds(0, head_dim)],
            send_sem=ends_sem.at[0, g], recv_sem=ends_sem.at[1, g],
            device_id={"ctx": z - 1}, device_id_type=MESH)

    def guest_mask():
        return pltpu.make_async_remote_copy(
            src_ref=mask.at[0], dst_ref=mask.at[1],
            send_sem=ends_sem.at[0, GUESTS], recv_sem=ends_sem.at[1, GUESTS],
            device_id={"ctx": z - 1}, device_id_type=MESH)

    def guest_part(g):
        return [pltpu.make_async_remote_copy(
            src_ref=ref.at[g], dst_ref=ref.at[g],
            send_sem=ends_sem.at[0, 2 * g + i], recv_sem=ends_sem.at[1, 2 * g + i],
            device_id={"ctx": z + 1}, device_id_type=MESH)
            for i, ref in enumerate((part_acc, part_stat))]

    def leftward(*blocks):
        @pl.when(has_left)
        def _():
            for h, kv in blocks:
                first_hop(h, kv, False).start()

    for table in tables:
        table.wait()
    loads[0].wait()
    put_keys(ck_raw[vp_ref[s]], put_pool(s, 0), range(EARLY))
    leftward(*[(h, 0) for h in range(EARLY)])
    put_keys(ck_raw[vp_ref[s]], put_pool(s, 0), range(EARLY, heads))
    for load in loads[2:]:
        load.start()
    loads[1].wait()
    put_values(cv_raw[vp_ref[s]], put_pool(s, 1))
    leftward((0, 1), (1, 1), *[(h, kv) for h in range(2, heads) for kv in range(2)])

    @pl.when(has_right)
    def _():
        pl.semaphore_wait(ready, 1)

    @pl.when(z == 0)
    def _():
        for h in (0, 3, 1, 2):
            for kv in range(2):
                first_hop(h, kv, True).start()

    @pl.when(z == 1)
    def _():
        for h in (0, 3, 1):
            for kv in range(2):
                first_hop(h, kv, True).start()

    @pl.when(z == 2)
    def _():
        for kv in range(2):
            first_hop(0, kv, True).start()

    loads[2].wait()
    loads[3].wait()
    put_keys(nk_raw[...], put_new(0))
    put_values(nv_raw[...], put_new(1))

    @pl.when(z == 2)
    def _():
        slash_hop(stay).start()
        for h in range(1, stay):
            for kv in range(2):
                first_hop(h, kv, True).start()

    token = (ids % BLK) // groups
    sort_q[...] = jnp.where(at == (token * heads + ids // BLK) * groups + ids % groups,
                            1.0, 0.0).astype(jnp.bfloat16)
    half = EARLY * BLK
    ids = lax.broadcasted_iota(jnp.int32, (half, half), 0)
    at = lax.broadcasted_iota(jnp.int32, (half, half), 1)
    sort_o[...] = jnp.where(at == ((ids % BLK) // groups * EARLY + ids // BLK) * groups + ids % groups,
                            1.0, 0.0).astype(jnp.bfloat16)
    loads[4].wait()
    for part in range(rows // BLK):
        ordered = lax.dot_general(q_raw[part * wide:(part + 1) * wide], sort_q[...], (((0,), (1,)), ((), ())),
                                  preferred_element_type=jnp.float32).astype(jnp.bfloat16)
        for h in range(heads):
            q_ref[h, 0:head_dim, part * BLK:(part + 1) * BLK] = ordered[:, h * BLK:(h + 1) * BLK]

    def unseen(hit):
        return jnp.full((1, BLK), jnp.where(hit > 0, 0.0, jnp.inf), jnp.float32)

    for slot in range(2 * n):
        hit = jnp.int32(0)
        for i in range(vl_ref.shape[1]):
            hit = hit | jnp.where((vl_ref[0, i] == slot) & (i < cnt_ref[0, 0]), 1, 0)
        mask[0, slot:slot + 1] = unseen(hit)
    hit = jnp.int32(0)
    for i in range(sl_ref.shape[1]):
        hit = hit | jnp.where((sl_ref[0, i] == 1) & (i < cnt_ref[0, 1]), 1, 0)
    mask[0, 2 * OWN:2 * OWN + 2] = jnp.concatenate([jnp.zeros((1, BLK), jnp.float32), unseen(hit)], 0)
    mask[0, 2 * GUEST:2 * GUEST + 2] = jnp.concatenate([unseen(hit), jnp.full((1, BLK), jnp.inf, jnp.float32)], 0)
    mask[0, 2 * ALONE:2 * ALONE + 2] = jnp.concatenate(
        [jnp.zeros((1, BLK), jnp.float32), jnp.full((1, BLK), jnp.inf, jnp.float32)], 0)

    @pl.when(z == 0)
    def _():
        slash_hop(heads).start()

    @pl.when(z == last)
    def _():
        for g in range(GUESTS):
            guest_q(g).start()
        guest_mask().start()

    put_keys(ck_raw[vp_ref[1 - s]], put_pool(1 - s, 0))
    put_values(cv_raw[vp_ref[1 - s]], put_pool(1 - s, 1))

    key_id = lax.broadcasted_iota(jnp.int32, (BLK, rows), 0)
    row_id = lax.broadcasted_iota(jnp.int32, (BLK, rows), 1) // groups
    later = jnp.where(key_id > row_id, -3e38, 0.0).astype(jnp.bfloat16)
    slots = acc.shape[0]
    for slot in range(slots):
        q_ref[slot, head_dim:] = later if slot < heads else jnp.zeros_like(later)
        acc[slot] = jnp.zeros_like(acc[slot])
        total[slot] = jnp.zeros_like(total[slot])
        peak[slot] = jnp.full_like(peak[slot], jnp.finfo(jnp.float32).min)
    q_ref[slots - 1, 0:head_dim] = jnp.zeros_like(later)
    one_at = lax.broadcasted_iota(jnp.int32, (BLK, BLK), 0) == lax.broadcasted_iota(jnp.int32, (BLK, BLK), 1)
    ext[0] = jnp.zeros((BLK, BLK), jnp.bfloat16)
    ext[1] = jnp.where(one_at, 1.0, 0.0).astype(jnp.bfloat16)
    scores_b[...] = jnp.zeros_like(scores_b)
    top_b[...] = jnp.zeros_like(top_b)

    def spread(row):
        return jnp.concatenate([row] * groups, 1)

    def place(src):
        return src - src // ALONE

    def hidden(slot, src, b):
        return spread(mask[(slot // heads) % 2 * (1 - slot // (slots - 1)), pl.ds(2 * src + b, 1)])

    def ahead(unit, scores, top):
        slot, src, h = unit
        q = q_ref[slot]
        high = None
        for b in range(2):
            causal = (src // OWN) * (1 - src % 2) if b == 0 else 0
            keys = jnp.concatenate([pool[place(src), h, b, 0], ext[causal]], 1)
            found = jnp.dot(keys, q, preferred_element_type=jnp.float32)
            scores[b * BLK:(b + 1) * BLK] = found
            part = jnp.max(found, axis=0, keepdims=True) - hidden(slot, src, b)
            high = part if high is None else jnp.maximum(high, part)
        top[...] = high

    def behind(unit, scores, top):
        slot, src, h = unit
        old = peak[slot]
        high = jnp.maximum(old, top[...])
        factor = jnp.exp2((old - high) * c)
        peak[slot] = high
        weights = [jnp.exp2((scores[b * BLK:(b + 1) * BLK] - (high + hidden(slot, src, b))) * c)
                   .astype(jnp.bfloat16) for b in range(2)]
        values = jnp.concatenate([pool[place(src), h, b, 1] for b in range(2)], 1)
        values = jnp.concatenate([values, jnp.ones((16, 2 * BLK), jnp.bfloat16)], 0)
        add = jnp.dot(values, jnp.concatenate(weights, 0), preferred_element_type=jnp.float32)
        acc[slot] = acc[slot] * factor + add[:head_dim]
        total[slot] = total[slot] * factor + add[head_dim:head_dim + 1]

    def ordered(part, those):
        lanes = slice(part * BLK, (part + 1) * BLK)
        done = jnp.concatenate(
            [(acc[h, :, lanes] * (1.0 / total[h, :, lanes])).astype(jnp.bfloat16) for h in those], 1)
        return lax.dot_general(sort_o[...], done, (((0,), (1,)), ((), ())), preferred_element_type=jnp.float32)

    def early_output():
        for part in range(rows // BLK):
            most[part] = ordered(part, range(EARLY))

    def drain(index):
        def sent(kind, sources, count):
            blocks = pool.at[pl.ds(0, sources), pl.ds(0, count), s]
            pltpu.make_async_copy(blocks, blocks, send_sem.at[kind]).wait()

        right = heads if index < last - 1 else stay if index < last else 0
        if right:
            sent(1, index + 1, right)
            slash_hop(right).wait_send()
        if index > 0:
            sent(0, n - index, heads)
            slash_sib(heads if index < last else stay, s).wait_send()
            sent(2, n - 1, heads if index < last else stay)
        else:
            copied = q_ref.at[pl.ds(0, heads), pl.ds(0, ((n - 1) * heads - 1) * (2 * BLK * head_dim // rows) // heads)]
            pltpu.make_async_copy(copied, copied, send_sem.at[2]).wait()
        if index == 1:
            end_across().wait_send()
        if index == last:
            guest_mask().wait_send()
            for g in range(GUESTS):
                guest_q(g).wait_send()

    words = [[by_role([sum(step[field] << (BITS * i) for i, step in enumerate(role[start:start + PACK]))
                       for role in roles]) for start in range(0, steps, PACK)] for field in range(5)]

    def step(here, t, before, bufs, old_bufs):
        kind, message, code, block, flags = [(word >> (BITS * t)) & (2 ** BITS - 1) for word in here]
        src, h = message // 4, message % 4

        @pl.when(kind == 1)
        def _():
            block = pool.at[src, h, s]
            pltpu.make_async_copy(block, block, hop_recv.at[src - (src > z).astype(jnp.int32), h]).wait()

            split = (z == 1) & (message == last * 4 + end)

            @pl.when((src > z) & has_left & jnp.logical_not(split))
            def _():
                hop(src, h, False).start()

            @pl.when(split)
            def _():
                end_hop(0).start()
                end_hop(1).start()
                end_across().start()

            @pl.when((src < z) & ((z < last - 1) | ((z == last - 1) & (h < stay))))
            def _():
                hop(src, h, True).start()

            sib(src, h, s).start()

        @pl.when(kind > 1)
        def _():
            @pl.when(kind == 2)
            def _():
                guest_mask().wait_recv()
                for g in range(GUESTS):
                    guest_q(g).wait_recv()

            @pl.when((kind == 3) & has_right)
            def _():
                slash_hop(heads).wait_recv()
                slash_sib(heads, s).start()

            @pl.when((kind == 3) & (z == last))
            def _():
                slash_hop(stay).wait_recv()
                slash_sib(stay, s).start()

        unit = (code % 8, block // 4, block % 4)

        @pl.when(code > 7)
        def _():
            @pl.when(unit[1] < OWN)
            def _():
                sib(unit[1], unit[2], 1 - s).wait_recv()

            @pl.when((unit[1] == OWN) & has_right)
            def _():
                slash_sib(heads, 1 - s).wait_recv()

            @pl.when((unit[1] == OWN) & (z == last))
            def _():
                slash_sib(stay, 1 - s).wait_recv()

        @pl.when(flags % 2 == 1)
        def _():
            ahead(unit, *bufs)
            behind(before, *old_bufs)

        @pl.when(flags > 1)
        def _():
            @pl.when((flags // 4) % 2 == 1)
            def _():
                for kv in range(2):
                    first_hop(2, kv, True).start()

            @pl.when((flags // 8) % 2 == 1)
            def _():
                slash_hop(heads).start()

            @pl.when((flags // 2) % 2 == 1)
            def _():
                g = 0
                part_acc[g] = acc[heads + g].astype(jnp.bfloat16)
                part_stat[g, 0:1] = peak[heads + g]
                part_stat[g, 1:2] = total[heads + g]
                for copy in guest_part(g):
                    copy.start()

            @pl.when(flags // 16 == 1)
            def _():
                early_output()

        return unit

    pairs = by_role([(length + 1) // 2 for length in lengths])

    def some_steps(group, before):
        here = []
        for chunks in words:
            word = chunks[-1]
            for i in reversed(range(len(chunks) - 1)):
                word = jnp.where(group == i, chunks[i], word)
            here.append(word)

        def two_steps(i, before):
            mid = step(here, 2 * i, before, (scores_a, top_a), (scores_b, top_b))
            return step(here, 2 * i + 1, mid, (scores_b, top_b), (scores_a, top_a))

        return lax.fori_loop(0, jnp.minimum(PACK // 2, pairs - group * (PACK // 2)), two_steps, before)

    idle = (jnp.int32(IDLE[0]), jnp.int32(GUEST), jnp.int32(0))
    lax.fori_loop(0, by_role([-(-length // PACK) for length in lengths]), some_steps, idle)

    for index in range(1, n):
        @pl.when(z == index)
        def _():
            drain(index)

    @pl.when(z == 0)
    def _():
        end_hop(0).wait_recv()
        end_sib(s).start()
        early_output()
        sib(last, end - 1, 1 - s).wait_recv()
        unit = (end - 1, last, end - 1)
        ahead(unit, scores_a, top_a)
        behind(unit, scores_a, top_a)
        drain(0)
        end_sib(1 - s).wait_recv()
        unit = (end, last, end)
        ahead(unit, scores_b, top_b)
        end_hop(1).wait_recv()
        block = pool.at[last, end, 1 - s, 1]
        pltpu.make_async_copy(block, block, ends_sem.at[1, 1]).wait()
        behind(unit, scores_b, top_b)

    @pl.when(z == last)
    def _():
        for g in range(GUESTS):
            for copy in guest_part(g):
                copy.wait_recv()
            slot = stay + g
            old, new = peak[slot], part_stat[g, 0:1]
            high = jnp.maximum(old, new)
            mine, theirs = jnp.exp2((old - high) * c), jnp.exp2((new - high) * c)
            acc[slot] = acc[slot] * mine + part_acc[g].astype(jnp.float32) * theirs
            total[slot] = total[slot] * mine + part_stat[g, 1:2] * theirs

    tile = EARLY * groups
    for part in range(rows // BLK):
        pair = [half.reshape(-1, tile, head_dim) for half in (most[part], ordered(part, range(EARLY, heads)))]
        o_ref[part * wide:(part + 1) * wide] = jnp.concatenate(pair, 1).reshape(wide, head_dim).astype(o_ref.dtype)

    @pl.when(z == 0)
    def _():
        end_sib(s).wait_send()

    @pl.when(z == last - 1)
    def _():
        for g in range(GUESTS):
            for copy in guest_part(g):
                copy.wait_send()


def store(o_vmem, o_hbm, sem):
    copies = sem.shape[0]
    rows = o_vmem.shape[0] // copies
    for i in range(copies):
        lines = pl.ds(i * rows, rows)
        pltpu.make_async_copy(o_vmem.at[lines], o_hbm.at[lines], sem.at[i]).start()
    for i in range(copies):
        lines = pl.ds(i * rows, rows)
        pltpu.make_async_copy(o_vmem.at[lines], o_hbm.at[lines], sem.at[i]).wait()


def chain_call(n, q, nk, nv, ck, cv, tables, heads, rows, head_dim):
    def vmem(*shape):
        return pltpu.VMEM(shape, jnp.bfloat16)

    def wide_vmem(*shape):
        return pltpu.VMEM(shape, jnp.float32)

    hbm = pl.BlockSpec(memory_space=pltpu.HBM)
    in_vmem = pl.BlockSpec(memory_space=pltpu.VMEM)
    dma = pltpu.SemaphoreType.DMA
    cached, wide = ck.shape[:2]
    slots = 7
    out = pl.pallas_call(
        functools.partial(chain, n),
        out_shape=pltpu.VMEM((heads * rows, head_dim), jnp.bfloat16),
        in_specs=[hbm] * 9,
        out_specs=in_vmem,
        scratch_shapes=[
            *[pltpu.SMEM(table.shape, table.dtype) for table in tables],
            vmem(heads * rows, head_dim), vmem(wide, head_dim), vmem(wide, head_dim),
            vmem(cached, wide, head_dim), vmem(cached, wide, head_dim),
            vmem(slots, 2 * head_dim, rows), vmem(wide, wide), vmem(wide, wide), vmem(2, BLK, BLK),
            vmem(n + 2, heads, 2, 2, BLK, head_dim),
            wide_vmem(slots, head_dim, rows), wide_vmem(slots, 1, rows), wide_vmem(slots, 1, rows),
            wide_vmem(2, 16, BLK), vmem(GUESTS, head_dim, rows), wide_vmem(GUESTS, 8, rows),
            wide_vmem(2 * BLK, rows), wide_vmem(2 * BLK, rows), wide_vmem(1, rows), wide_vmem(1, rows),
            wide_vmem(rows // BLK, EARLY * BLK, head_dim), vmem(EARLY * BLK, EARLY * BLK),
            dma((3,)), dma((n - 1, heads)), dma((n - 1, heads)), dma((4,)),
            dma((2, 2 * GUESTS)), dma((6,)), pltpu.SemaphoreType.REGULAR,
        ],
        compiler_params=pltpu.CompilerParams(
            collective_id=0, has_side_effects=True, vmem_limit_bytes=60 * 2**20),
    )(*[pltpu.with_memory_space_constraint(x, pltpu.HBM) for x in (q, nk, nv, ck, cv, *tables)])
    return pl.pallas_call(
        store,
        out_shape=jax.ShapeDtypeStruct(out.shape, out.dtype),
        in_specs=[in_vmem],
        out_specs=hbm,
        scratch_shapes=[dma((4,))],
        compiler_params=pltpu.CompilerParams(vmem_limit_bytes=2**20),
    )(out)


def shards(n, queries, new_keys, new_values, cache_keys, cache_values,
           vertical_pool, vertical_lists, slash_lists, list_counts):
    tokens, heads, groups, head_dim = queries.shape
    rows = tokens * groups
    picked = vertical_pool.shape[0]

    def flat(x):
        return x.reshape(-1, head_dim)

    def vmem(*shape):
        return pltpu.VMEM(shape, jnp.bfloat16)

    hbm = pl.BlockSpec(memory_space=pltpu.HBM)
    smem = pl.BlockSpec(memory_space=pltpu.SMEM)
    dma = pltpu.SemaphoreType.DMA
    wide = heads * BLK
    cached = cache_keys.shape[0] // BLK
    if n == 4 and heads == 4 and picked == 2:
        out = chain_call(n, flat(queries), flat(new_keys), flat(new_values),
                         cache_keys.reshape(cached, wide, head_dim), cache_values.reshape(cached, wide, head_dim),
                         (vertical_pool, vertical_lists, slash_lists, list_counts), heads, rows, head_dim)
        return out.reshape(tokens, heads, groups, head_dim)
    out = pl.pallas_call(
        functools.partial(attend, n),
        out_shape=jax.ShapeDtypeStruct((tokens * heads * groups, head_dim), jnp.bfloat16),
        in_specs=[hbm] * 5 + [smem] * 4,
        out_specs=pl.BlockSpec(memory_space=pltpu.VMEM),
        scratch_shapes=[
            vmem(heads * rows, head_dim), vmem(wide, head_dim), vmem(wide, head_dim),
            vmem(cached, wide, head_dim), vmem(cached, wide, head_dim),
            vmem(heads, rows, head_dim), vmem(picked, 2, heads, BLK, head_dim),
            vmem(2, heads, BLK, head_dim), vmem(wide, wide), vmem(wide, wide),
            vmem(n, picked, 2, heads, BLK, head_dim),
            vmem(2, wide, head_dim), vmem(2, heads, BLK, head_dim),
            pltpu.VMEM((heads, head_dim, rows), jnp.float32),
            pltpu.VMEM((heads, 1, rows), jnp.float32),
            pltpu.VMEM((heads, 1, rows), jnp.float32),
            vmem(2, heads, 3 * BLK, rows), pltpu.VMEM((2, heads, 1, rows), jnp.float32),
            dma((n, 2, 2)), dma((n, 2)), dma((n, 2)), dma((n, 2)), dma((4,)), dma((5,)),
        ],
        compiler_params=pltpu.CompilerParams(
            collective_id=0, has_side_effects=True, vmem_limit_bytes=60 * 2**20),
    )(flat(queries), flat(new_keys), flat(new_values), cache_keys.reshape(cached, wide, head_dim),
      cache_values.reshape(cached, wide, head_dim),
      vertical_pool, vertical_lists, slash_lists, list_counts)
    return out.reshape(tokens, heads, groups, head_dim)


def solution(mesh):
    in_specs = (
        P(("grp", "ctx"), "kvh", "sub", None),
        P(("grp", "ctx"), "kvh", None),
        P(("grp", "ctx"), "kvh", None),
        P(("grp", "ctx"), "kvh", None),
        P(("grp", "ctx"), "kvh", None),
        P(("grp", "ctx")),
        P(("grp", "ctx"), None),
        P(("grp", "ctx"), None),
        P(("grp", "ctx"), None),
    )
    out_specs = P(("grp", "ctx"), "kvh", "sub", None)
    return jax.shard_map(functools.partial(shards, mesh.shape["ctx"]), mesh=mesh,
                         in_specs=in_specs, out_specs=out_specs, check_vma=False)
```

```python
import functools
import math

import jax
import jax.numpy as jnp
from jax import lax
from jax.experimental import pallas as pl
from jax.experimental.pallas import tpu as pltpu
from jax.sharding import PartitionSpec as P

BLK = 128
MESH = pl.DeviceIdType.MESH


def attend(n, q_hbm, nk_hbm, nv_hbm, ck_hbm, cv_hbm, vp_ref, vl_ref, sl_ref, cnt_ref, o_ref,
           q_raw, nk_raw, nv_raw, ck_raw, cv_raw, q_ref, own_ref, new_ref, sort_kv, sort_q,
           pool, slash_raw, slash, acc, peak, total, rounded, fade,
           hop_send, hop_recv, sib_send, sib_recv, sl_sem, in_sem):
    z = lax.axis_index("ctx")
    s = lax.axis_index("sub")
    heads, rows, head_dim = q_ref.shape
    groups = rows // BLK
    wide = heads * BLK
    loads = [pltpu.make_async_copy(src, dst, in_sem.at[i]) for i, (src, dst) in enumerate(
        [(ck_hbm, ck_raw), (cv_hbm, cv_raw), (nk_hbm, nk_raw), (nv_hbm, nv_raw), (q_hbm, q_raw)])]
    loads[0].start()
    c = math.log2(math.e) / math.sqrt(head_dim)
    has_left = z > 0
    has_right = z < n - 1
    sib_id = {"sub": 1 - s}

    barrier = pltpu.get_barrier_semaphore()
    pl.semaphore_signal(barrier, inc=1, device_id=sib_id, device_id_type=MESH)

    @pl.when(has_left)
    def _():
        pl.semaphore_signal(barrier, inc=1, device_id={"ctx": z - 1}, device_id_type=MESH)

    @pl.when(has_right)
    def _():
        pl.semaphore_signal(barrier, inc=1, device_id={"ctx": z + 1}, device_id_type=MESH)

    ids = lax.broadcasted_iota(jnp.int32, (wide, wide), 0)
    at = lax.broadcasted_iota(jnp.int32, (wide, wide), 1)
    sort_kv[...] = jnp.where(at == (ids % BLK) * heads + ids // BLK, 1.0, 0.0).astype(jnp.bfloat16)
    token = (ids % BLK) // groups
    sort_q[...] = jnp.where(at == (token * heads + ids // BLK) * groups + ids % groups,
                            1.0, 0.0).astype(jnp.bfloat16)

    def by_head(raw):
        return jnp.dot(sort_kv[...], raw, preferred_element_type=jnp.float32).astype(jnp.bfloat16)

    def put_keys(dst, raw):
        ordered = by_head(raw)
        for h in range(heads):
            dst[h] = ordered[h * BLK:(h + 1) * BLK]

    def put_values(dst, raw):
        ordered = lax.dot_general(raw, sort_kv[...], (((0,), (1,)), ((), ())),
                                  preferred_element_type=jnp.float32).astype(jnp.bfloat16)
        for h in range(heads):
            dst[h] = ordered[:, h * BLK:(h + 1) * BLK]

    def chosen(cache, b):
        return cache[vp_ref[b]]

    pl.semaphore_wait(barrier, 1 + has_left.astype(jnp.int32) + has_right.astype(jnp.int32))

    def hop(src_ref, src, kv, right):
        return pltpu.make_async_remote_copy(
            src_ref=src_ref, dst_ref=pool.at[src, s, kv],
            send_sem=hop_send.at[src, int(right), kv], recv_sem=hop_recv.at[src, kv],
            device_id={"ctx": z + 1 if right else z - 1}, device_id_type=MESH)

    def sib(src, kv):
        return pltpu.make_async_remote_copy(
            src_ref=pool.at[src, s, kv], dst_ref=pool.at[src, s, kv],
            send_sem=sib_send.at[src, kv], recv_sem=sib_recv.at[src, kv],
            device_id=sib_id, device_id_type=MESH)

    def sib_in(src, kv):
        return pltpu.make_async_remote_copy(
            src_ref=pool.at[src, 1 - s, kv], dst_ref=pool.at[src, 1 - s, kv],
            send_sem=sib_send.at[src, kv], recv_sem=sib_recv.at[src, kv],
            device_id=sib_id, device_id_type=MESH)

    def slash_hop(src_ref=nk_hbm):
        return pltpu.make_async_remote_copy(
            src_ref=src_ref, dst_ref=slash_raw.at[s],
            send_sem=sl_sem.at[0], recv_sem=sl_sem.at[1],
            device_id={"ctx": z + 1}, device_id_type=MESH)

    def slash_sib(part):
        return pltpu.make_async_remote_copy(
            src_ref=slash_raw.at[part], dst_ref=slash_raw.at[part],
            send_sem=sl_sem.at[2], recv_sem=sl_sem.at[3],
            device_id=sib_id, device_id_type=MESH)

    for part, src_ref in enumerate((nk_hbm, nv_hbm)):
        @pl.when(has_right & (s == part))
        def _():
            slash_hop(src_ref).start()

    def send_own(kv):
        @pl.when(has_right)
        def _():
            hop(own_ref.at[s, kv], z, kv, True).start()

        @pl.when(has_left)
        def _():
            hop(own_ref.at[s, kv], z, kv, False).start()

    loads[0].wait()
    loads[1].start()
    put_keys(own_ref.at[s, 0], chosen(ck_raw, s))
    for load in loads[2:]:
        load.start()
    send_own(0)
    loads[1].wait()
    put_values(own_ref.at[s, 1], chosen(cv_raw, s))
    send_own(1)
    loads[2].wait()
    loads[3].wait()
    put_keys(new_ref.at[0], nk_raw[...])
    put_values(new_ref.at[1], nv_raw[...])
    put_keys(own_ref.at[1 - s, 0], chosen(ck_raw, 1 - s))
    put_values(own_ref.at[1 - s, 1], chosen(cv_raw, 1 - s))
    loads[4].wait()
    for part in range(rows // BLK):
        ordered = jnp.dot(sort_q[...], q_raw[part * wide:(part + 1) * wide],
                          preferred_element_type=jnp.float32).astype(jnp.bfloat16)
        for h in range(heads):
            q_ref[h, part * BLK:(part + 1) * BLK] = ordered[h * BLK:(h + 1) * BLK]

    def listed(slot):
        count = cnt_ref[0, 0]
        width = vl_ref.shape[1]
        if width <= 8:
            hit = jnp.int32(0)
            for i in range(width):
                hit = hit | jnp.where((vl_ref[0, i] == slot) & (i < count), 1, 0)
            return hit

        def one(i, hit):
            return hit | jnp.where((vl_ref[0, i] == slot) & (i < count), 1, 0)

        return lax.fori_loop(0, width, one, jnp.int32(0))

    def score(keys, q):
        return lax.dot_general(keys, q, (((1,), (1,)), ((), ())),
                               preferred_element_type=jnp.float32)

    def take_keys(side, blocks, first=False):
        for h in range(heads):
            q = q_ref[h]
            raw = []
            tops = []
            for keys, seen in blocks:
                scores = score(keys[h], q)
                if seen is None:
                    key_id = lax.broadcasted_iota(jnp.int32, scores.shape, 0)
                    row_id = lax.broadcasted_iota(jnp.int32, scores.shape, 1) // groups
                    scores = jnp.where(key_id <= row_id, scores, -jnp.inf)
                top = jnp.max(scores, axis=0, keepdims=True)
                if seen is not None:
                    top = jnp.where(seen > 0, top, -jnp.inf)
                raw.append(scores)
                tops.append(top)
            high = functools.reduce(jnp.maximum, tops)
            if not first:
                old = peak[h]
                high = jnp.maximum(old, high)
                factor = jnp.exp2((old - high) * c)
                fade[side, h] = factor
            peak[h] = high
            sums = []
            for i, ((_, seen), scores) in enumerate(zip(blocks, raw)):
                base = high if seen is None else jnp.where(seen > 0, high, jnp.inf)
                weights = jnp.exp2((scores - base) * c)
                sums.append(jnp.sum(weights, axis=0, keepdims=True))
                rounded[side, h, i * BLK:(i + 1) * BLK] = weights.astype(jnp.bfloat16)
            add = sum(sums[1:], sums[0])
            total[h] = add if first else total[h] * fade[side, h] + add

    def take_values(side, blocks, first=False):
        depth = len(blocks) * BLK
        for h in range(heads):
            values = jnp.concatenate([values[h] for values in blocks], 1)
            add = jnp.dot(values, rounded[side, h, :depth], preferred_element_type=jnp.float32)
            acc[h] = add if first else acc[h] * fade[side, h] + add

    take_keys(0, [(new_ref.at[0], None)]
              + [(own_ref.at[b, 0], listed(2 * z + b)) for b in range(2)], first=True)
    take_values(0, [new_ref.at[1]] + [own_ref.at[b, 1] for b in range(2)], first=True)

    @pl.when(has_left)
    def _():
        slash_hop().wait_recv()
        slash_sib(s).start()

    def arrive(src, kv, right):
        hop(own_ref.at[s, kv], src, kv, right).wait_recv()

        @pl.when(has_right if right else has_left)
        def _():
            hop(pool.at[src, s, kv], src, kv, right).start()

        sib(src, kv).start()

    def step(d, carry):
        sides = ((z + d, z + d < n, False), (z - d, z - d >= 0, True))
        for kv in range(2):
            for src, there, right in sides:
                @pl.when(there)
                def _():
                    arrive(src, kv, right)

            for side, (src, there, right) in enumerate(sides):
                @pl.when(there)
                def _():
                    sib_in(src, kv).wait_recv()
                    if kv == 0:
                        take_keys(side, [(pool.at[src, b, 0], listed(2 * src + b))
                                         for b in range(2)])
                    else:
                        take_values(side, [pool.at[src, b, 1] for b in range(2)])

        @pl.when((d == 1) & has_left)
        def _():
            slash_sib(1 - s).wait_recv()
            put_keys(slash.at[0], slash_raw[0])
            put_values(slash.at[1], slash_raw[1])
            back = jnp.int32(0)
            for i in range(sl_ref.shape[1]):
                back = back | jnp.where((sl_ref[0, i] == 1) & (i < cnt_ref[0, 1]), 1, 0)
            take_keys(0, [(slash.at[0], back)])
            take_values(0, [slash.at[1]])

        return carry

    lax.fori_loop(1, n, step, 0)

    for part in range(rows // BLK):
        lanes = slice(part * BLK, (part + 1) * BLK)
        done = jnp.concatenate(
            [(acc[h, :, lanes] / total[h, :, lanes]).astype(jnp.bfloat16) for h in range(heads)], 1)
        o_ref[part * wide:(part + 1) * wide] = lax.dot_general(
            sort_q[...], done, (((0,), (1,)), ((), ())),
            preferred_element_type=jnp.float32).astype(o_ref.dtype)

    def drain(src, carry):
        for kv in range(2):
            @pl.when(has_right & (src <= z))
            def _():
                hop(own_ref.at[s, kv], src, kv, True).wait_send()

            @pl.when(has_left & (src >= z))
            def _():
                hop(own_ref.at[s, kv], src, kv, False).wait_send()

            @pl.when(src != z)
            def _():
                sib(src, kv).wait_send()
        return carry

    lax.fori_loop(0, n, drain, 0)

    @pl.when(has_right)
    def _():
        slash_hop().wait_send()

    @pl.when(has_left)
    def _():
        slash_sib(s).wait_send()

BITS = 5
OWN, GUEST, ALONE = 4, 5, 6
IDLE = (6, 4 * GUEST)
GUESTS = 1
EARLY = 2
PACK = 6


NONE = (-1, -1)
QUEST = (-2, 0)
SLASH = (-3, 0)


def plan(heads):
    zero = [(NONE, (0, 0), 0), (NONE, (0, ALONE), 0), (NONE, (1, 0), 0), ((1, 0), (1, ALONE), 0), (NONE, (2, 0), 0),
        (NONE, (2, ALONE), 0), ((1, 1), (0, 1), 0), (NONE, (3, 0), 0), (NONE, (3, ALONE), 0), ((1, 2), (1, 1), 0),
        (NONE, NONE, 0), ((1, 3), NONE, 0), (NONE, (2, 1), 0), (NONE, NONE, 0), (NONE, (3, 1), 0), ((2, 0), NONE, 0),
        ((2, 1), NONE, 0), (NONE, (0, 2), 0), (NONE, NONE, 0), (NONE, (1, 2), 0), ((2, 2), NONE, 0),
        ((2, 3), NONE, 0), (NONE, (2, 2), 0), (NONE, NONE, 0), (NONE, (3, 2), 0), ((3, 0), NONE, 0),
        ((3, 1), NONE, 0), (NONE, (0, 3), 0), (NONE, NONE, 0), (NONE, (1, 3), 0), ((3, 2), NONE, 0)]
    one = [((0, 0), (0, 1), 0), ((2, 0), (1, 1), 0), ((0, 3), (2, 1), 0), (NONE, (0, 0), 0), ((2, 1), (0, 2), 0),
        ((0, 1), (3, 0), 4), (NONE, (3, 1), 0), (NONE, (1, 2), 0), ((2, 2), (1, 0), 0), ((0, 2), NONE, 8),
        ((2, 3), NONE, 0), (NONE, (2, 2), 0), (NONE, (2, 0), 0), (NONE, NONE, 0), ((3, 0), (3, 2), 0),
        (SLASH, NONE, 0), ((3, 1), NONE, 0), (NONE, (0, 3), 0), (NONE, NONE, 0), (NONE, (0, OWN), 0),
        ((3, 2), (1, 3), 0), (NONE, (1, OWN), 0), (NONE, (2, OWN), 16), ((3, 3), (2, 3), 0), (NONE, (3, OWN), 0),
        (NONE, NONE, 0), (NONE, (3, 3), 0), (NONE, NONE, 0)]
    two = [((1, 0), (0, 2), 0), ((3, 0), (1, 2), 0), (NONE, (2, 2), 0), ((1, 3), (0, 1), 0), ((3, 1), (0, 3), 0),
        (NONE, (3, 2), 0), ((1, 1), (3, 1), 0), ((3, 2), (1, 3), 0), (NONE, NONE, 0), ((0, 0), (1, 1), 0),
        ((3, 3), (2, 3), 0), (NONE, NONE, 0), ((0, 3), (0, 0), 0), (NONE, (3, 3), 0), (NONE, NONE, 0),
        (NONE, (3, 0), 0), ((0, 1), NONE, 0), (QUEST, NONE, 0), (NONE, (4, 2), 0), ((1, 2), (4, GUEST), 0),
        (NONE, (4, 1), 0), (NONE, (4, 0), 0), (NONE, (1, 0), 0), ((0, 2), (2, 1), 2), (NONE, NONE, 0),
        (NONE, (2, 0), 0), (NONE, NONE, 0), (SLASH, NONE, 0), (NONE, (0, OWN), 0), (NONE, (1, OWN), 0),
        (NONE, (2, OWN), 16), (NONE, (3, OWN), 0), (NONE, NONE, 0)]
    three = [(NONE, (0, 3), 0), ((2, 0), (1, 3), 0), (NONE, (2, 3), 0), (NONE, (3, 3), 0), (NONE, (0, 2), 0),
        (SLASH, (3, ALONE), 0), (NONE, NONE, 0), (NONE, (0, OWN), 0), ((2, 1), (1, OWN), 0), (NONE, (2, OWN), 0),
        (NONE, NONE, 0), ((2, 2), (1, 2), 0), (NONE, NONE, 0), ((1, 0), NONE, 0), (NONE, (2, 2), 0), (NONE, NONE, 0),
        (NONE, (0, 1), 0), ((1, 1), NONE, 0), ((0, 0), NONE, 0), (NONE, (1, 1), 0), (NONE, NONE, 0),
        (NONE, (0, 0), 0), ((0, 1), NONE, 0), ((1, 2), NONE, 0), (NONE, (1, 0), 0), (NONE, NONE, 16),
        (NONE, (2, 1), 0), ((0, 2), NONE, 0), (NONE, (2, 0), 0), (NONE, NONE, 0)]

    def build(z, table):
        out, before, used = [], NONE, set()
        for recv, now, flags in table + [(NONE, NONE, 0)]:
            kind, message = (1, recv[0] * 4 + recv[1]) if recv[0] >= 0 else (-recv[0] if recv != NONE else 0, 0)
            slot, src = now
            h = slot if slot < heads else slot - GUESTS
            key = OWN if src == OWN else (src, h)
            first = now != NONE and key not in used and src not in (z, GUEST, ALONE)
            used.add(key)
            code = (slot + (8 if first else 0), src * 4 + h) if now != NONE else IDLE
            busy = now != NONE or before != NONE
            out.append((kind, message) + code + (int(busy) | flags,))
            before = now
        return out

    return [build(z, table) for z, table in enumerate((zero, one, two, three))]


def chain(n, q_hbm, nk_hbm, nv_hbm, ck_hbm, cv_hbm, vp_hbm, vl_hbm, sl_hbm, cnt_hbm, o_ref,
          vp_ref, vl_ref, sl_ref, cnt_ref,
          q_raw, nk_raw, nv_raw, ck_raw, cv_raw, q_ref, sort_kv, sort_q, ext,
          pool, acc, peak, total, mask, part_acc, part_stat, scores_a, scores_b, top_a, top_b, most, sort_o,
          send_sem, hop_recv, sib_recv, sl_sem, ends_sem, in_sem, ready):
    z = lax.axis_index("ctx")
    s = lax.axis_index("sub")
    heads = pool.shape[1]
    head_dim, rows = acc.shape[1:]
    groups = rows // BLK
    wide = heads * BLK
    last = n - 1
    stay = heads - GUESTS
    loads = [pltpu.make_async_copy(src, dst, in_sem.at[i]) for i, (src, dst) in enumerate(
        [(ck_hbm, ck_raw), (cv_hbm, cv_raw), (nk_hbm, nk_raw), (nv_hbm, nv_raw), (q_hbm, q_raw)])]
    tables = [pltpu.make_async_copy(src, dst, in_sem.at[2 + i]) for i, (src, dst) in enumerate(
        [(vp_hbm, vp_ref), (vl_hbm, vl_ref), (sl_hbm, sl_ref), (cnt_hbm, cnt_ref)])]
    half = ck_raw.shape[0] // 2
    for i in range(2):
        lines = pl.ds(i * half, half)
        pltpu.make_async_copy(ck_hbm.at[lines], ck_raw.at[lines], in_sem.at[0]).start()
    loads[1].start()
    for table in tables:
        table.start()
    c = math.log2(math.e) / math.sqrt(head_dim)
    has_left = z > 0
    has_right = z < last
    sib_id = {"sub": 1 - s}
    inner = has_left & has_right

    barrier = pltpu.get_barrier_semaphore()
    pl.semaphore_signal(barrier, inc=1, device_id=sib_id, device_id_type=MESH)

    @pl.when(has_right)
    def _():
        pl.semaphore_signal(barrier, inc=1, device_id={"ctx": z + 1}, device_id_type=MESH)

    def by_role(values):
        out = jnp.int32(values[-1])
        for i in reversed(range(len(values) - 1)):
            out = jnp.where(z == i, jnp.int32(values[i]), out)
        return out

    roles = plan(heads)
    lengths = [max(t for t, step in enumerate(role) if step[0] or step[4]) + 1 for role in roles]
    steps = -(-max(lengths) // PACK) * PACK
    roles = [(role + [(0, 0) + IDLE + (0,)] * steps)[:steps] for role in roles]
    ids = lax.broadcasted_iota(jnp.int32, (wide, wide), 0)
    at = lax.broadcasted_iota(jnp.int32, (wide, wide), 1)
    sort_kv[...] = jnp.where(at == (ids % BLK) * heads + ids // BLK, 1.0, 0.0).astype(jnp.bfloat16)

    pl.semaphore_wait(barrier, 1 + has_left.astype(jnp.int32))

    @pl.when(has_left)
    def _():
        pl.semaphore_signal(ready, inc=1, device_id={"ctx": z - 1}, device_id_type=MESH)

    def put_keys(raw, put, those=range(heads)):
        ordered = jnp.dot(sort_kv[those.start * BLK:those.stop * BLK], raw,
                          preferred_element_type=jnp.float32).astype(jnp.bfloat16)
        for i, h in enumerate(those):
            put(h, ordered[i * BLK:(i + 1) * BLK])

    def put_values(raw, put):
        ordered = lax.dot_general(raw, sort_kv[...], (((0,), (1,)), ((), ())),
                                  preferred_element_type=jnp.float32).astype(jnp.bfloat16)
        for h in range(heads):
            put(h, ordered[:, h * BLK:(h + 1) * BLK])

    def put_pool(b, kv):
        def put(h, block):
            pool[z, h, b, kv] = block
        return put

    def put_new(kv):
        def put(h, block):
            pool[OWN, h, 0, kv] = block
            pool[GUEST, h, 0, kv] = block
            pool[GUEST, h, 1, kv] = jnp.zeros_like(block)
        return put

    def hop(src, h, right):
        return pltpu.make_async_remote_copy(
            src_ref=pool.at[src, h, s], dst_ref=pool.at[src, h, s],
            send_sem=send_sem.at[int(right)], recv_sem=hop_recv.at[src if right else src - 1, h],
            device_id={"ctx": z + 1 if right else z - 1}, device_id_type=MESH)

    def first_hop(h, kv, right):
        return pltpu.make_async_remote_copy(
            src_ref=pool.at[z, h, s, kv], dst_ref=pool.at[z, h, s, kv],
            send_sem=send_sem.at[int(right)], recv_sem=hop_recv.at[z if right else z - 1, h],
            device_id={"ctx": z + 1 if right else z - 1}, device_id_type=MESH)

    def sib(src, h, part):
        return pltpu.make_async_remote_copy(
            src_ref=pool.at[src, h, part], dst_ref=pool.at[src, h, part],
            send_sem=send_sem.at[2], recv_sem=sib_recv.at[src - (src > z).astype(jnp.int32), h],
            device_id=sib_id, device_id_type=MESH)

    end = heads - 1

    def end_hop(kv):
        block = pool.at[last, end, s, kv]
        return pltpu.make_async_remote_copy(
            src_ref=block, dst_ref=block,
            send_sem=send_sem.at[0], recv_sem=ends_sem.at[1, 0] if kv else hop_recv.at[last - 1, end],
            device_id={"ctx": z - 1}, device_id_type=MESH)

    def end_across():
        block = pool.at[last, end, s, 1]
        return pltpu.make_async_remote_copy(
            src_ref=block, dst_ref=block, send_sem=ends_sem.at[0, 0], recv_sem=ends_sem.at[1, 1],
            device_id={"ctx": z - 1, "sub": 1 - s}, device_id_type=MESH)

    def end_sib(part):
        block = pool.at[last, end, part, 0]
        return pltpu.make_async_remote_copy(
            src_ref=block, dst_ref=block, send_sem=ends_sem.at[0, 1], recv_sem=sib_recv.at[last - 1, end],
            device_id=sib_id, device_id_type=MESH)

    def slash_hop(count):
        return pltpu.make_async_remote_copy(
            src_ref=pool.at[OWN, pl.ds(0, count), 0, s], dst_ref=pool.at[OWN, pl.ds(0, count), 1, s],
            send_sem=sl_sem.at[0], recv_sem=sl_sem.at[1],
            device_id={"ctx": z + 1}, device_id_type=MESH)

    def slash_sib(count, part):
        block = pool.at[OWN, pl.ds(0, count), 1, part]
        return pltpu.make_async_remote_copy(
            src_ref=block, dst_ref=block,
            send_sem=sl_sem.at[2], recv_sem=sl_sem.at[3],
            device_id=sib_id, device_id_type=MESH)

    def guest_q(g):
        return pltpu.make_async_remote_copy(
            src_ref=q_ref.at[stay + g, pl.ds(0, head_dim)], dst_ref=q_ref.at[heads + g, pl.ds(0, head_dim)],
            send_sem=ends_sem.at[0, g], recv_sem=ends_sem.at[1, g],
            device_id={"ctx": z - 1}, device_id_type=MESH)

    def guest_mask():
        return pltpu.make_async_remote_copy(
            src_ref=mask.at[0], dst_ref=mask.at[1],
            send_sem=ends_sem.at[0, GUESTS], recv_sem=ends_sem.at[1, GUESTS],
            device_id={"ctx": z - 1}, device_id_type=MESH)

    def guest_part(g):
        return [pltpu.make_async_remote_copy(
            src_ref=ref.at[g], dst_ref=ref.at[g],
            send_sem=ends_sem.at[0, 2 * g + i], recv_sem=ends_sem.at[1, 2 * g + i],
            device_id={"ctx": z + 1}, device_id_type=MESH)
            for i, ref in enumerate((part_acc, part_stat))]

    def leftward(*blocks):
        @pl.when(has_left)
        def _():
            for h, kv in blocks:
                first_hop(h, kv, False).start()

    for table in tables:
        table.wait()
    loads[0].wait()
    put_keys(ck_raw[vp_ref[s]], put_pool(s, 0), range(EARLY))
    leftward(*[(h, 0) for h in range(EARLY)])
    put_keys(ck_raw[vp_ref[s]], put_pool(s, 0), range(EARLY, heads))
    for load in loads[2:]:
        load.start()
    loads[1].wait()
    put_values(cv_raw[vp_ref[s]], put_pool(s, 1))
    leftward((0, 1), (1, 1), *[(h, kv) for h in range(2, heads) for kv in range(2)])

    @pl.when(has_right)
    def _():
        pl.semaphore_wait(ready, 1)

    @pl.when(z == 0)
    def _():
        for h in (0, 3, 1, 2):
            for kv in range(2):
                first_hop(h, kv, True).start()

    @pl.when(z == 1)
    def _():
        for h in (0, 3, 1):
            for kv in range(2):
                first_hop(h, kv, True).start()

    @pl.when(z == 2)
    def _():
        for kv in range(2):
            first_hop(0, kv, True).start()

    loads[2].wait()
    loads[3].wait()
    put_keys(nk_raw[...], put_new(0))
    put_values(nv_raw[...], put_new(1))

    @pl.when(z == 2)
    def _():
        slash_hop(stay).start()
        for h in range(1, stay):
            for kv in range(2):
                first_hop(h, kv, True).start()

    token = (ids % BLK) // groups
    sort_q[...] = jnp.where(at == (token * heads + ids // BLK) * groups + ids % groups,
                            1.0, 0.0).astype(jnp.bfloat16)
    half = EARLY * BLK
    ids = lax.broadcasted_iota(jnp.int32, (half, half), 0)
    at = lax.broadcasted_iota(jnp.int32, (half, half), 1)
    sort_o[...] = jnp.where(at == ((ids % BLK) // groups * EARLY + ids // BLK) * groups + ids % groups,
                            1.0, 0.0).astype(jnp.bfloat16)
    loads[4].wait()
    for part in range(rows // BLK):
        ordered = lax.dot_general(q_raw[part * wide:(part + 1) * wide], sort_q[...], (((0,), (1,)), ((), ())),
                                  preferred_element_type=jnp.float32).astype(jnp.bfloat16)
        for h in range(heads):
            q_ref[h, 0:head_dim, part * BLK:(part + 1) * BLK] = ordered[:, h * BLK:(h + 1) * BLK]

    def unseen(hit):
        return jnp.full((1, BLK), jnp.where(hit > 0, 0.0, jnp.inf), jnp.float32)

    for slot in range(2 * n):
        hit = jnp.int32(0)
        for i in range(vl_ref.shape[1]):
            hit = hit | jnp.where((vl_ref[0, i] == slot) & (i < cnt_ref[0, 0]), 1, 0)
        mask[0, slot:slot + 1] = unseen(hit)
    hit = jnp.int32(0)
    for i in range(sl_ref.shape[1]):
        hit = hit | jnp.where((sl_ref[0, i] == 1) & (i < cnt_ref[0, 1]), 1, 0)
    mask[0, 2 * OWN:2 * OWN + 2] = jnp.concatenate([jnp.zeros((1, BLK), jnp.float32), unseen(hit)], 0)
    mask[0, 2 * GUEST:2 * GUEST + 2] = jnp.concatenate([unseen(hit), jnp.full((1, BLK), jnp.inf, jnp.float32)], 0)
    mask[0, 2 * ALONE:2 * ALONE + 2] = jnp.concatenate(
        [jnp.zeros((1, BLK), jnp.float32), jnp.full((1, BLK), jnp.inf, jnp.float32)], 0)

    @pl.when(z == 0)
    def _():
        slash_hop(heads).start()

    @pl.when(z == last)
    def _():
        for g in range(GUESTS):
            guest_q(g).start()
        guest_mask().start()

    put_keys(ck_raw[vp_ref[1 - s]], put_pool(1 - s, 0))
    put_values(cv_raw[vp_ref[1 - s]], put_pool(1 - s, 1))

    key_id = lax.broadcasted_iota(jnp.int32, (BLK, rows), 0)
    row_id = lax.broadcasted_iota(jnp.int32, (BLK, rows), 1) // groups
    later = jnp.where(key_id > row_id, -3e38, 0.0).astype(jnp.bfloat16)
    slots = acc.shape[0]
    for slot in range(slots):
        q_ref[slot, head_dim:] = later if slot < heads else jnp.zeros_like(later)
        acc[slot] = jnp.zeros_like(acc[slot])
        total[slot] = jnp.zeros_like(total[slot])
        peak[slot] = jnp.full_like(peak[slot], jnp.finfo(jnp.float32).min)
    q_ref[slots - 1, 0:head_dim] = jnp.zeros_like(later)
    one_at = lax.broadcasted_iota(jnp.int32, (BLK, BLK), 0) == lax.broadcasted_iota(jnp.int32, (BLK, BLK), 1)
    ext[0] = jnp.zeros((BLK, BLK), jnp.bfloat16)
    ext[1] = jnp.where(one_at, 1.0, 0.0).astype(jnp.bfloat16)
    scores_b[...] = jnp.zeros_like(scores_b)
    top_b[...] = jnp.zeros_like(top_b)

    def spread(row):
        return jnp.concatenate([row] * groups, 1)

    def place(src):
        return src - src // ALONE

    def hidden(slot, src, b):
        return spread(mask[(slot // heads) % 2 * (1 - slot // (slots - 1)), pl.ds(2 * src + b, 1)])

    def ahead(unit, scores, top):
        slot, src, h = unit
        q = q_ref[slot]
        high = None
        for b in range(2):
            causal = (src // OWN) * (1 - src % 2) if b == 0 else 0
            keys = jnp.concatenate([pool[place(src), h, b, 0], ext[causal]], 1)
            found = jnp.dot(keys, q, preferred_element_type=jnp.float32)
            scores[b * BLK:(b + 1) * BLK] = found
            part = jnp.max(found, axis=0, keepdims=True) - hidden(slot, src, b)
            high = part if high is None else jnp.maximum(high, part)
        top[...] = high

    def behind(unit, scores, top):
        slot, src, h = unit
        old = peak[slot]
        high = jnp.maximum(old, top[...])
        factor = jnp.exp2((old - high) * c)
        peak[slot] = high
        weights = [jnp.exp2((scores[b * BLK:(b + 1) * BLK] - (high + hidden(slot, src, b))) * c)
                   .astype(jnp.bfloat16) for b in range(2)]
        values = jnp.concatenate([pool[place(src), h, b, 1] for b in range(2)], 1)
        values = jnp.concatenate([values, jnp.ones((16, 2 * BLK), jnp.bfloat16)], 0)
        add = jnp.dot(values, jnp.concatenate(weights, 0), preferred_element_type=jnp.float32)
        acc[slot] = acc[slot] * factor + add[:head_dim]
        total[slot] = total[slot] * factor + add[head_dim:head_dim + 1]

    def ordered(part, those):
        lanes = slice(part * BLK, (part + 1) * BLK)
        done = jnp.concatenate(
            [(acc[h, :, lanes] * (1.0 / total[h, :, lanes])).astype(jnp.bfloat16) for h in those], 1)
        return lax.dot_general(sort_o[...], done, (((0,), (1,)), ((), ())), preferred_element_type=jnp.float32)

    def early_output():
        for part in range(rows // BLK):
            most[part] = ordered(part, range(EARLY))

    def drain(index):
        def sent(kind, sources, count):
            blocks = pool.at[pl.ds(0, sources), pl.ds(0, count), s]
            pltpu.make_async_copy(blocks, blocks, send_sem.at[kind]).wait()

        right = heads if index < last - 1 else stay if index < last else 0
        if right:
            sent(1, index + 1, right)
            slash_hop(right).wait_send()
        if index > 0:
            sent(0, n - index, heads)
            slash_sib(heads if index < last else stay, s).wait_send()
            sent(2, n - 1, heads if index < last else stay)
        else:
            copied = q_ref.at[pl.ds(0, heads), pl.ds(0, ((n - 1) * heads - 1) * (2 * BLK * head_dim // rows) // heads)]
            pltpu.make_async_copy(copied, copied, send_sem.at[2]).wait()
        if index == 1:
            end_across().wait_send()
        if index == last:
            guest_mask().wait_send()
            for g in range(GUESTS):
                guest_q(g).wait_send()

    words = [[by_role([sum(step[field] << (BITS * i) for i, step in enumerate(role[start:start + PACK]))
                       for role in roles]) for start in range(0, steps, PACK)] for field in range(5)]

    def step(here, t, before, bufs, old_bufs):
        kind, message, code, block, flags = [(word >> (BITS * t)) & (2 ** BITS - 1) for word in here]
        src, h = message // 4, message % 4

        @pl.when(kind == 1)
        def _():
            block = pool.at[src, h, s]
            pltpu.make_async_copy(block, block, hop_recv.at[src - (src > z).astype(jnp.int32), h]).wait()

            split = (z == 1) & (message == last * 4 + end)

            @pl.when((src > z) & has_left & jnp.logical_not(split))
            def _():
                hop(src, h, False).start()

            @pl.when(split)
            def _():
                end_hop(0).start()
                end_hop(1).start()
                end_across().start()

            @pl.when((src < z) & ((z < last - 1) | ((z == last - 1) & (h < stay))))
            def _():
                hop(src, h, True).start()

            sib(src, h, s).start()

        @pl.when(kind > 1)
        def _():
            @pl.when(kind == 2)
            def _():
                guest_mask().wait_recv()
                for g in range(GUESTS):
                    guest_q(g).wait_recv()

            @pl.when((kind == 3) & has_right)
            def _():
                slash_hop(heads).wait_recv()
                slash_sib(heads, s).start()

            @pl.when((kind == 3) & (z == last))
            def _():
                slash_hop(stay).wait_recv()
                slash_sib(stay, s).start()

        unit = (code % 8, block // 4, block % 4)

        @pl.when(code > 7)
        def _():
            @pl.when(unit[1] < OWN)
            def _():
                sib(unit[1], unit[2], 1 - s).wait_recv()

            @pl.when((unit[1] == OWN) & has_right)
            def _():
                slash_sib(heads, 1 - s).wait_recv()

            @pl.when((unit[1] == OWN) & (z == last))
            def _():
                slash_sib(stay, 1 - s).wait_recv()

        @pl.when(flags % 2 == 1)
        def _():
            ahead(unit, *bufs)
            behind(before, *old_bufs)

        @pl.when(flags > 1)
        def _():
            @pl.when((flags // 4) % 2 == 1)
            def _():
                for kv in range(2):
                    first_hop(2, kv, True).start()

            @pl.when((flags // 8) % 2 == 1)
            def _():
                slash_hop(heads).start()

            @pl.when((flags // 2) % 2 == 1)
            def _():
                g = 0
                part_acc[g] = acc[heads + g].astype(jnp.bfloat16)
                part_stat[g, 0:1] = peak[heads + g]
                part_stat[g, 1:2] = total[heads + g]
                for copy in guest_part(g):
                    copy.start()

            @pl.when(flags // 16 == 1)
            def _():
                early_output()

        return unit

    pairs = by_role([(length + 1) // 2 for length in lengths])

    def some_steps(group, before):
        here = []
        for chunks in words:
            word = chunks[-1]
            for i in reversed(range(len(chunks) - 1)):
                word = jnp.where(group == i, chunks[i], word)
            here.append(word)

        def two_steps(i, before):
            mid = step(here, 2 * i, before, (scores_a, top_a), (scores_b, top_b))
            return step(here, 2 * i + 1, mid, (scores_b, top_b), (scores_a, top_a))

        return lax.fori_loop(0, jnp.minimum(PACK // 2, pairs - group * (PACK // 2)), two_steps, before)

    idle = (jnp.int32(IDLE[0]), jnp.int32(GUEST), jnp.int32(0))
    lax.fori_loop(0, by_role([-(-length // PACK) for length in lengths]), some_steps, idle)

    for index in range(1, n):
        @pl.when(z == index)
        def _():
            drain(index)

    @pl.when(z == 0)
    def _():
        end_hop(0).wait_recv()
        end_sib(s).start()
        early_output()
        sib(last, end - 1, 1 - s).wait_recv()
        unit = (end - 1, last, end - 1)
        ahead(unit, scores_a, top_a)
        behind(unit, scores_a, top_a)
        drain(0)
        end_sib(1 - s).wait_recv()
        unit = (end, last, end)
        ahead(unit, scores_b, top_b)
        end_hop(1).wait_recv()
        block = pool.at[last, end, 1 - s, 1]
        pltpu.make_async_copy(block, block, ends_sem.at[1, 1]).wait()
        behind(unit, scores_b, top_b)

    @pl.when(z == last)
    def _():
        for g in range(GUESTS):
            for copy in guest_part(g):
                copy.wait_recv()
            slot = stay + g
            old, new = peak[slot], part_stat[g, 0:1]
            high = jnp.maximum(old, new)
            mine, theirs = jnp.exp2((old - high) * c), jnp.exp2((new - high) * c)
            acc[slot] = acc[slot] * mine + part_acc[g].astype(jnp.float32) * theirs
            total[slot] = total[slot] * mine + part_stat[g, 1:2] * theirs

    tile = EARLY * groups
    for part in range(rows // BLK):
        pair = [half.reshape(-1, tile, head_dim) for half in (most[part], ordered(part, range(EARLY, heads)))]
        o_ref[part * wide:(part + 1) * wide] = jnp.concatenate(pair, 1).reshape(wide, head_dim).astype(o_ref.dtype)

    @pl.when(z == 0)
    def _():
        end_sib(s).wait_send()

    @pl.when(z == last - 1)
    def _():
        for g in range(GUESTS):
            for copy in guest_part(g):
                copy.wait_send()


def store(o_vmem, o_hbm, sem):
    copies = sem.shape[0]
    rows = o_vmem.shape[0] // copies
    for i in range(copies):
        lines = pl.ds(i * rows, rows)
        pltpu.make_async_copy(o_vmem.at[lines], o_hbm.at[lines], sem.at[i]).start()
    for i in range(copies):
        lines = pl.ds(i * rows, rows)
        pltpu.make_async_copy(o_vmem.at[lines], o_hbm.at[lines], sem.at[i]).wait()


def chain_call(n, q, nk, nv, ck, cv, tables, heads, rows, head_dim):
    def vmem(*shape):
        return pltpu.VMEM(shape, jnp.bfloat16)

    def wide_vmem(*shape):
        return pltpu.VMEM(shape, jnp.float32)

    hbm = pl.BlockSpec(memory_space=pltpu.HBM)
    in_vmem = pl.BlockSpec(memory_space=pltpu.VMEM)
    dma = pltpu.SemaphoreType.DMA
    cached, wide = ck.shape[:2]
    slots = 7
    out = pl.pallas_call(
        functools.partial(chain, n),
        out_shape=pltpu.VMEM((heads * rows, head_dim), jnp.bfloat16),
        in_specs=[hbm] * 9,
        out_specs=in_vmem,
        scratch_shapes=[
            *[pltpu.SMEM(table.shape, table.dtype) for table in tables],
            vmem(heads * rows, head_dim), vmem(wide, head_dim), vmem(wide, head_dim),
            vmem(cached, wide, head_dim), vmem(cached, wide, head_dim),
            vmem(slots, 2 * head_dim, rows), vmem(wide, wide), vmem(wide, wide), vmem(2, BLK, BLK),
            vmem(n + 2, heads, 2, 2, BLK, head_dim),
            wide_vmem(slots, head_dim, rows), wide_vmem(slots, 1, rows), wide_vmem(slots, 1, rows),
            wide_vmem(2, 16, BLK), vmem(GUESTS, head_dim, rows), wide_vmem(GUESTS, 8, rows),
            wide_vmem(2 * BLK, rows), wide_vmem(2 * BLK, rows), wide_vmem(1, rows), wide_vmem(1, rows),
            wide_vmem(rows // BLK, EARLY * BLK, head_dim), vmem(EARLY * BLK, EARLY * BLK),
            dma((3,)), dma((n - 1, heads)), dma((n - 1, heads)), dma((4,)),
            dma((2, 2 * GUESTS)), dma((6,)), pltpu.SemaphoreType.REGULAR,
        ],
        compiler_params=pltpu.CompilerParams(
            collective_id=0, has_side_effects=True, vmem_limit_bytes=60 * 2**20),
    )(*[pltpu.with_memory_space_constraint(x, pltpu.HBM) for x in (q, nk, nv, ck, cv, *tables)])
    return pl.pallas_call(
        store,
        out_shape=jax.ShapeDtypeStruct(out.shape, out.dtype),
        in_specs=[in_vmem],
        out_specs=hbm,
        scratch_shapes=[dma((4,))],
        compiler_params=pltpu.CompilerParams(vmem_limit_bytes=2**20),
    )(out)


def shards(n, queries, new_keys, new_values, cache_keys, cache_values,
           vertical_pool, vertical_lists, slash_lists, list_counts):
    tokens, heads, groups, head_dim = queries.shape
    rows = tokens * groups
    picked = vertical_pool.shape[0]

    def flat(x):
        return x.reshape(-1, head_dim)

    def vmem(*shape):
        return pltpu.VMEM(shape, jnp.bfloat16)

    hbm = pl.BlockSpec(memory_space=pltpu.HBM)
    smem = pl.BlockSpec(memory_space=pltpu.SMEM)
    dma = pltpu.SemaphoreType.DMA
    wide = heads * BLK
    cached = cache_keys.shape[0] // BLK
    if n == 4 and heads == 4 and picked == 2:
        out = chain_call(n, flat(queries), flat(new_keys), flat(new_values),
                         cache_keys.reshape(cached, wide, head_dim), cache_values.reshape(cached, wide, head_dim),
                         (vertical_pool, vertical_lists, slash_lists, list_counts), heads, rows, head_dim)
        return out.reshape(tokens, heads, groups, head_dim)
    out = pl.pallas_call(
        functools.partial(attend, n),
        out_shape=jax.ShapeDtypeStruct((tokens * heads * groups, head_dim), jnp.bfloat16),
        in_specs=[hbm] * 5 + [smem] * 4,
        out_specs=pl.BlockSpec(memory_space=pltpu.VMEM),
        scratch_shapes=[
            vmem(heads * rows, head_dim), vmem(wide, head_dim), vmem(wide, head_dim),
            vmem(cached, wide, head_dim), vmem(cached, wide, head_dim),
            vmem(heads, rows, head_dim), vmem(picked, 2, heads, BLK, head_dim),
            vmem(2, heads, BLK, head_dim), vmem(wide, wide), vmem(wide, wide),
            vmem(n, picked, 2, heads, BLK, head_dim),
            vmem(2, wide, head_dim), vmem(2, heads, BLK, head_dim),
            pltpu.VMEM((heads, head_dim, rows), jnp.float32),
            pltpu.VMEM((heads, 1, rows), jnp.float32),
            pltpu.VMEM((heads, 1, rows), jnp.float32),
            vmem(2, heads, 3 * BLK, rows), pltpu.VMEM((2, heads, 1, rows), jnp.float32),
            dma((n, 2, 2)), dma((n, 2)), dma((n, 2)), dma((n, 2)), dma((4,)), dma((5,)),
        ],
        compiler_params=pltpu.CompilerParams(
            collective_id=0, has_side_effects=True, vmem_limit_bytes=60 * 2**20),
    )(flat(queries), flat(new_keys), flat(new_values), cache_keys.reshape(cached, wide, head_dim),
      cache_values.reshape(cached, wide, head_dim),
      vertical_pool, vertical_lists, slash_lists, list_counts)
    return out.reshape(tokens, heads, groups, head_dim)


def solution(mesh):
    in_specs = (
        P(("grp", "ctx"), "kvh", "sub", None),
        P(("grp", "ctx"), "kvh", None),
        P(("grp", "ctx"), "kvh", None),
        P(("grp", "ctx"), "kvh", None),
        P(("grp", "ctx"), "kvh", None),
        P(("grp", "ctx")),
        P(("grp", "ctx"), None),
        P(("grp", "ctx"), None),
        P(("grp", "ctx"), None),
    )
    out_specs = P(("grp", "ctx"), "kvh", "sub", None)
    return jax.shard_map(functools.partial(shards, mesh.shape["ctx"]), mesh=mesh,
                         in_specs=in_specs, out_specs=out_specs, check_vma=False)
```
